32 devices in a mesh: grp: 2 (over x), head: 16 (over z, y, core).
Axes of the slice: x: 2, y: 2, z: 4, core: 2. Of those that a mesh axis runs over, the one named last changes fastest.
Arguments:
- queries: bfloat16 [2048, 2, 16, 256], P('head', 'grp'), parts along dimension 1, may hold values from -12 to 12
- new_kv: bfloat16 [2048, 2, 2, 512], P('head', 'grp'), parts along dimension 1, may hold values from -4 to 4
- cache: bfloat16 [32, 256, 512], P(('grp', 'head')), parts along dimension 0, may hold values from -12 to 12
- resid: bfloat16 [2048, 2, 2048], P('head', 'grp'), parts along dimension 1, may hold values from -6 to 6
- w_out: bfloat16 [16, 256, 2048], P(None, 'head'), may hold values from -0.375 to 0.375
- norm_gain: float32 [2048], replicated, may hold values from 0.1 to 1.9
- expert_ids: int32 [2048, 2, 2], P('head', 'grp'), parts along dimension 1, may hold values from 0 to 15, all different within a row; in each aligned block of 128 rows (0 to 127, 128 to 255, ..., all dimensions but the last counted through in order) at most 32 rows name the same one
- expert_gates: float32 [2048, 2, 2], P('head', 'grp'), parts along dimension 1, may hold values from 0.2 to 1
- w_in: bfloat16 [16, 2048, 1024], P('head'), may hold values from -0.125 to 0.125
- w_down: bfloat16 [16, 512, 2048], P('head'), may hold values from -0.25 to 0.25
Outputs:
- layer_out: bfloat16 [2048, 2, 2048], P('head', 'grp'), parts along dimension 1
The draws below stay inside these ranges and needn't reach their ends.
There are 2 independent parts, one for each index of `grp`. The reference program is written for one: setup_inputs(seed, part) draws one part's arguments, and reference() takes and returns one part's arrays. A program takes and returns all parts, laid end to end along the dimension named above; an argument that names none is the same for every part. Nothing has to cross between parts.
Inputs may be any that keep to these rules, and one draw needn't show every extreme that they name: `expert_ids`: rows are taken in order over positions and then sequences; in each aligned block of 128 such rows (the rows of one device) no expert is named by more than 32 rows, a bound that some block reaches. A row names 2 different experts.
All inputs are finite; a program needn't handle non-finite values.
Results may differ from the reference program's by a relative error of at most 0.009.
Values may be sent and summed in bfloat16 or wider, within the bound.
A program may use at most 128 MiB of HBM per device.

```python
import math
import jax
import jax.numpy as jnp
import numpy as np
from jax import lax

D = 2048
HEADS = 16
KV_HEADS = 2
HD = 256
FF_E = 512
TOP = 2
SPAN = 2048
CACHE = 2048
SEQS = 1
ROWS = 128
EXPERTS = 16
CAP = 32
N_HEAD = 16


def draw_queries(key, part):
    full_shape = (SPAN, SEQS, HEADS, HD)
    values = 2.0 * jnp.clip(jax.random.normal(jax.random.fold_in(key, 1), full_shape, jnp.float32), -4.0, 4.0)
    return values.astype(jnp.bfloat16)


def draw_cache(key, part):
    full_shape = (SEQS * KV_HEADS, CACHE, 2 * HD)
    values = jnp.clip(jax.random.normal(jax.random.fold_in(key, 2), full_shape, jnp.float32), -4.0, 4.0)
    paged = values.reshape(SEQS * HEADS, CACHE // (HEADS // KV_HEADS), 2 * HD)
    return paged.astype(jnp.bfloat16)


def level_of(own_key, extent, pieces, least, high):
    loudness, own = 1.0, jax.random.fold_in(own_key, 6)
    for dim, blocks in pieces:
        steps = jnp.exp(jax.random.uniform(jax.random.fold_in(own, dim), (blocks,), jnp.float32, least / len(pieces), high / len(pieces)))
        loudness = loudness * jnp.repeat(steps, extent[dim] // blocks).reshape([-1 if axis == dim else 1 for axis in range(len(extent))])
    return loudness


def routed_block(own_key, own, number, rows, number_of, top, bound, skew):
    order = jax.random.permutation(own_key, number_of)
    packed, ordinary = shares(number_of, rows * top, bound, skew, True), shares(number_of, rows * top, bound, skew, False)
    places = jnp.arange(number_of)

    def named(lengths, rotation):
        used = int((lengths > 0).sum())
        fixed = max(1, used // 4)
        passed = fixed + (places - fixed + rotation * (used - fixed)) % max(1, number_of - fixed)
        return jnp.zeros((number_of,), jnp.int32).at[order[jnp.where(places < fixed, places, passed)]].set(jnp.asarray(lengths, jnp.int32))

    lengths = jnp.where(number % 4 == 0, named(packed, number // 4), named(ordinary, number - number // 4 - 1))
    mixed = jax.random.permutation(jax.random.fold_in(own, 3), number_of)
    source_of, taker = mixed[0:number_of // 2 * 2:2], mixed[1:number_of // 2 * 2:2]
    slack = jnp.minimum(lengths[source_of] - 1, bound - lengths[taker]) // 2
    slack = jnp.where((source_of == order[0]) | (taker == order[0]) | (lengths[taker] == 0), 0, jnp.maximum(slack, 0))
    passed = jax.random.randint(jax.random.fold_in(own, 4), (number_of // 2,), 0, 1 << 20) % (slack + 1)
    lengths = lengths.at[source_of].add(-passed).at[taker].add(passed)
    members = jnp.searchsorted(jnp.cumsum(lengths), jnp.arange(rows * top), side="right").astype(jnp.int32)
    table = members.reshape(top, rows).T
    table = table[jax.random.permutation(jax.random.fold_in(own, 1), rows)]
    rotation = jax.random.randint(jax.random.fold_in(own, 2), (rows, 1), 0, top)
    return jnp.take_along_axis(table, (jnp.arange(top)[None, :] + rotation) % top, axis=1)


def shares(amount, total, reach, slope, full):
    weights = [(1 << 20) // math.isqrt(rank ** slope) + 1 for rank in range(1, amount + 1)]
    largest = reach if full else min(reach, max(-(-total // amount), total * weights[0] // sum(weights)))
    least = 1 if total - largest >= amount - 1 else 0
    counts, rest = [largest] + [least] * (amount - 1), total - largest - least * (amount - 1)
    while rest > 0:
        free = [i for i in range(1, amount) if counts[i] < largest] or [i for i in range(1, amount) if counts[i] < reach]
        pool, remaining = sum([weights[i] for i in free]), rest
        for i in free:
            extra = min(reach - counts[i], max(1, remaining * weights[i] // pool), rest)
            counts[i] = counts[i] + extra
            rest = rest - extra
    return np.array(counts)


def noise(stream_key, shape, deviation, reach, shards=(), kind=jnp.bfloat16):
    result = deviation * jax.random.normal(stream_key, shape, jnp.float32)
    if shards:
        result = result * level_of(stream_key, shape, shards, -0.22, 0.18)
    return jnp.clip(result, -reach, reach).astype(kind)


def setup_inputs(seed: int = 0, part: int = 0) -> dict:
    streams_of = jax.random.split(jax.random.key(seed), 11)
    own_keys = jax.random.split(jax.random.fold_in(streams_of[10], part), 11)
    queries = draw_queries(jax.random.fold_in(jax.random.fold_in(streams_of[10], part), 71), part)
    new_kv = noise(own_keys[1], (SPAN, SEQS, KV_HEADS, 2 * HD), 1.0, 4.0, ((0, 16),))
    cache = draw_cache(jax.random.fold_in(jax.random.fold_in(streams_of[10], part), 71), part)
    resid = noise(own_keys[3], (SPAN, SEQS, D), 1.0, 6.0, ((0, 16),))
    w_out = noise(streams_of[4], (HEADS, HD, D), HD ** -0.5, 0.375, ((1, 16),))
    norm_gain = jnp.clip(1.0 + 0.18 * jax.random.normal(streams_of[5], (D,), jnp.float32), 0.1, 1.9)
    expert_ids_keys = jax.random.split(jax.random.fold_in(own_keys[6], 1), SPAN * SEQS // ROWS)
    expert_ids_turns = jax.random.permutation(jax.random.fold_in(own_keys[6], 3), SPAN * SEQS // ROWS)
    expert_ids = jax.vmap(lambda own, number: routed_block(jax.random.fold_in(own_keys[6], 2), own, number, ROWS, EXPERTS, TOP, CAP, 0))(expert_ids_keys, expert_ids_turns).reshape((SPAN, SEQS, TOP))
    expert_gates = jnp.clip(0.2 + 0.8 * jax.random.uniform(own_keys[7], (SPAN, SEQS, TOP), jnp.float32) ** level_of(own_keys[7], (SPAN, SEQS, TOP), ((0, 16),), -0.2, 0.2), 0.2, 1.0)
    w_in = noise(streams_of[8], (EXPERTS, D, 2 * FF_E), D ** -0.5, 0.125, ((0, 16),))
    w_down = noise(streams_of[9], (EXPERTS, FF_E, D), FF_E ** -0.5, 0.25, ((0, 16),))
    return dict(queries=queries, new_kv=new_kv, cache=cache, resid=resid, w_out=w_out, norm_gain=norm_gain, expert_ids=expert_ids, expert_gates=expert_gates, w_in=w_in, w_down=w_down)


def attend_slot(query_rows_all, new_keys, new_values, cached):
    length = query_rows_all.shape[0]
    block_rows = min(512, length)
    score_scale = HD ** (-0.5)
    old_keys = cached[:, :HD]
    old_values = cached[:, HD:]
    key_positions = jnp.arange(length, dtype=jnp.int32)

    def one_block(first_row):
        query_rows = lax.dynamic_slice_in_dim(query_rows_all, first_row, block_rows, 0)
        old_scores = jnp.dot(query_rows, old_keys.T, preferred_element_type=jnp.float32) * score_scale
        new_scores = jnp.dot(query_rows, new_keys.T, preferred_element_type=jnp.float32) * score_scale
        row_positions = first_row + jnp.arange(block_rows, dtype=jnp.int32)
        allowed = key_positions[None, :] <= row_positions[:, None]
        new_scores = jnp.where(allowed, new_scores, -jnp.inf)
        row_max = jnp.maximum(lax.optimization_barrier(jnp.max(old_scores, 1)), lax.optimization_barrier(jnp.max(new_scores, 1)))[:, None]
        old_exp = jnp.exp(old_scores - row_max)
        new_exp = jnp.exp(new_scores - row_max)
        denominator = lax.optimization_barrier(jnp.sum(old_exp, 1)) + lax.optimization_barrier(jnp.sum(new_exp, 1))
        weighted_sum = jnp.dot(old_exp.astype(jnp.bfloat16), old_values, preferred_element_type=jnp.float32)
        weighted_sum = weighted_sum + jnp.dot(new_exp.astype(jnp.bfloat16), new_values, preferred_element_type=jnp.float32)
        return (weighted_sum / denominator[:, None]).astype(jnp.bfloat16)
    starts = (jnp.arange(length // block_rows) * block_rows).astype(jnp.int32)
    return lax.map(one_block, starts).reshape(length, HD)

def reference(queries, new_kv, cache, resid, w_out, norm_gain, expert_ids, expert_gates, w_in, w_down):
    group_size = HEADS // KV_HEADS
    slot_count = SEQS * HEADS
    query_slots = queries.reshape(SPAN, slot_count, HD).transpose(1, 0, 2)
    pair_slots = new_kv.reshape(SPAN, SEQS * KV_HEADS, 2 * HD).transpose(1, 0, 2)
    cached_slots = cache.reshape(SEQS * KV_HEADS, CACHE, 2 * HD)

    def per_slot(slot_index):
        pair_index = (slot_index // group_size).astype(jnp.int32)
        slot_queries = lax.dynamic_index_in_dim(query_slots, slot_index, 0, keepdims=False)
        slot_pairs = lax.dynamic_index_in_dim(pair_slots, pair_index, 0, keepdims=False)
        slot_cache = lax.dynamic_index_in_dim(cached_slots, pair_index, 0, keepdims=False)
        return attend_slot(slot_queries, slot_pairs[:, :HD], slot_pairs[:, HD:], slot_cache)
    outputs = lax.map(per_slot, jnp.arange(slot_count, dtype=jnp.int32))
    attended = outputs.transpose(1, 0, 2).reshape(SPAN * SEQS, HEADS * HD)
    stream = resid.reshape(SPAN * SEQS, D).astype(jnp.float32)
    stream = stream + jnp.dot(attended, w_out.reshape(HEADS * HD, D), preferred_element_type=jnp.float32)
    normed = stream * lax.rsqrt(lax.optimization_barrier(jnp.mean(stream * stream, 1, keepdims=True)) + 1e-06) * norm_gain
    normed = normed.astype(jnp.bfloat16)
    flat_ids = expert_ids.reshape(-1).astype(jnp.int32)
    assignments = flat_ids.shape[0]
    onehot = (flat_ids[:, None] == jnp.arange(EXPERTS, dtype=jnp.int32)[None, :]).astype(jnp.int32)
    earlier = jnp.cumsum(onehot, 0).astype(jnp.int32) - onehot
    slot_rank = lax.optimization_barrier(jnp.sum(earlier * onehot, 1)).astype(jnp.int32)
    limit = N_HEAD * CAP
    target = (flat_ids * limit + slot_rank).astype(jnp.int32)
    table = jnp.full((EXPERTS * limit,), assignments, jnp.int32)
    table = table.at[target].set(jnp.arange(assignments).astype(jnp.int32))
    repeated = jnp.concatenate([jnp.repeat(normed, TOP, axis=0), jnp.zeros((1, D), jnp.bfloat16)], 0)

    def per_expert(inputs):
        row_index, gate_up, down_weight = inputs
        expert_rows = repeated[row_index]
        inner_act = jnp.dot(expert_rows, gate_up, preferred_element_type=jnp.float32)
        hidden = (jax.nn.silu(inner_act[:, :FF_E]) * inner_act[:, FF_E:]).astype(jnp.bfloat16)
        return jnp.dot(hidden, down_weight, preferred_element_type=jnp.float32).astype(jnp.bfloat16)
    results = lax.map(per_expert, (table.reshape(EXPERTS, limit), w_in, w_down))
    picked = results.reshape(EXPERTS * limit, D)[target].astype(jnp.float32)
    weighted = picked * expert_gates.reshape(-1)[:, None]
    expert_sum = weighted.reshape(SPAN * SEQS, TOP, D).sum(1)
    return (stream + expert_sum).astype(jnp.bfloat16).reshape(SPAN, SEQS, D)
```

```python
import functools

import jax
import jax.numpy as jnp
from jax import lax
from jax.experimental import pallas as pl
from jax.experimental.pallas import tpu as pltpu
from jax.sharding import PartitionSpec as P

eps_norm = 1e-06
MESH = pl.DeviceIdType.MESH


def front_kernel(
    q_ref,
    kv_ref,
    cache_ref,
    w_ref,
    resid_ref,
    gain_ref,
    stream_ref,
    normed_ref,
    q_buf,
    kn,
    kc,
    wb,
    acc,
    top,
    total,
    att,
    part_out,
    part_in,
    local_sem,
    q_sem,
    kn_line,
    kn_up,
    kn_side,
    kn_side_s,
    kn_twin,
    kn_twin_s,
    kc_line,
    kc_up,
    kc_down,
    kc_side,
    kc_side_s,
    kc_twin,
    kc_twin_s,
    w_line,
    w_up,
    w_down,
    w_side,
    w_far,
    w_far_s,
    w_twin,
    w_twin_s,
    part_sem,
    part_sem_s,
):
    planes = kn.shape[1]
    group = q_buf.shape[1]
    rows, width = q_buf.shape[2:]
    model = w_ref.shape[2]
    half = model // 2
    g = lax.axis_index("grp")
    me = lax.axis_index("head")
    z, y, c = me // 4, (me // 2) % 2, me % 2
    up, down = (g, me + 4), (g, me - 4)
    side, twin, far = (g, me + 2 - 4 * y), (g, me + 1 - 2 * c), (1 - g, me)
    has_up, has_down = z < planes - 1, z > 0

    barrier = pltpu.get_barrier_semaphore()
    for peer in (side, twin, far):
        pl.semaphore_signal(barrier, inc=1, device_id=peer, device_id_type=MESH)

    @pl.when(has_up)
    def _():
        pl.semaphore_signal(barrier, inc=1, device_id=up, device_id_type=MESH)

    @pl.when(has_down)
    def _():
        pl.semaphore_signal(barrier, inc=1, device_id=down, device_id_type=MESH)

    pl.semaphore_wait(barrier, 3 + has_up.astype(jnp.int32) + has_down.astype(jnp.int32))

    def copy(src, dst, sent, got, peer):
        return pltpu.make_async_remote_copy(
            src_ref=src,
            dst_ref=dst,
            send_sem=sent,
            recv_sem=got,
            device_id=peer,
            device_id_type=MESH,
        )

    def arrived(dst, got):
        copy(dst, dst, got, got, twin).wait_recv()

    def left(src, sent):
        copy(src, src, sent, sent, twin).wait_send()

    def mine(plane):
        return plane // (planes // 2) == y

    cols_near = pl.ds(pl.multiple_of(g * half, half), half)
    cols_far = pl.ds(pl.multiple_of((1 - g) * half, half), half)
    own_heads = pl.ds(y * group, group)
    other_heads = pl.ds((1 - y) * group, group)


    @pl.when(has_up)
    def _():
        copy(cache_ref, kc.at[z, y, c], kc_up.at[z], kc_line.at[z], up).start()
        copy(kv_ref, kn.at[:, z, y, c], kn_up.at[z], kn_line.at[z], up).start()

    @pl.when(has_down)
    def _():
        copy(cache_ref, kc.at[z, y, c], kc_down.at[z], kc_line.at[z], down).start()

    copy(kv_ref.at[1 - y], kn.at[1 - y, z, y, c], kn_side_s.at[z], kn_side.at[z], side).start()
    copy(kv_ref.at[y], kn.at[y, z, y, c], kn_twin_s.at[z, y], kn_twin.at[z, y], twin).start()
    copy(q_ref.at[other_heads], q_buf.at[y], q_sem.at[0], q_sem.at[1], side).start()

    @pl.when(mine(z))
    def _():
        copy(cache_ref, kc.at[z, y, c], kc_twin_s.at[z, y], kc_twin.at[z, y], twin).start()

    @pl.when(jnp.logical_not(mine(z)))
    def _():
        copy(cache_ref, kc.at[z, y, c], kc_side_s.at[z], kc_side.at[z], side).start()

    locals_ = (
        pltpu.make_async_copy(q_ref.at[own_heads], q_buf.at[y], local_sem.at[0]),
        pltpu.make_async_copy(kv_ref.at[y], kn.at[y, z, y, c], local_sem.at[1]),
        pltpu.make_async_copy(cache_ref, kc.at[z, y, c], local_sem.at[2]),
        pltpu.make_async_copy(
            w_ref.at[own_heads, :, cols_near], wb.at[:, z, y, c, :, cols_near], local_sem.at[3]
        ),
    )
    for item in locals_:
        item.start()

    def from_side_new(plane):
        block = kn.at[y, plane, 1 - y, c]
        arrived(block, kn_side.at[plane])
        copy(block, block, kn_twin_s.at[plane, 1 - y], kn_twin.at[plane, 1 - y], twin).start()

    def from_side_old(plane):
        @pl.when(mine(plane))
        def _():
            block = kc.at[plane, 1 - y, c]
            arrived(block, kc_side.at[plane])
            copy(block, block, kc_twin_s.at[plane, 1 - y], kc_twin.at[plane, 1 - y], twin).start()

    def spread_old(plane):
        block = kc.at[plane, y, c]

        @pl.when(mine(plane))
        def _():
            copy(block, block, kc_twin_s.at[plane, y], kc_twin.at[plane, y], twin).start()

        @pl.when(jnp.logical_not(mine(plane)))
        def _():
            copy(block, block, kc_side_s.at[plane], kc_side.at[plane], side).start()

    def relay(step):
        low, high = z - step, z + step

        @pl.when(low >= 0)
        def _():
            old, new = kc.at[low, y, c], kn.at[:, low, y, c]
            arrived(old, kc_line.at[low])

            @pl.when(has_up)
            def _():
                copy(old, old, kc_up.at[low], kc_line.at[low], up).start()

            arrived(new, kn_line.at[low])

            @pl.when(has_up)
            def _():
                copy(new, new, kn_up.at[low], kn_line.at[low], up).start()

            spread_old(low)
            there, here = kn.at[1 - y, low, y, c], kn.at[y, low, y, c]
            copy(there, there, kn_side_s.at[low], kn_side.at[low], side).start()
            copy(here, here, kn_twin_s.at[low, y], kn_twin.at[low, y], twin).start()

        @pl.when(high < planes)
        def _():
            old = kc.at[high, y, c]
            arrived(old, kc_line.at[high])

            @pl.when(has_down)
            def _():
                copy(old, old, kc_down.at[high], kc_line.at[high], down).start()

            spread_old(high)

        @pl.when(low >= 0)
        def _():
            from_side_old(low)
            from_side_new(low)

        @pl.when(high < planes)
        def _():
            from_side_old(high)

    def w_block(plane, line, core, cols):
        return wb.at[:, plane, line, core, :, cols]

    def w_spread(src, plane, line):
        dst = w_block(plane, line, c, cols_near)
        copy(src, dst, w_far_s.at[plane, line], w_far.at[plane, line], far).start()
        copy(src, dst, w_twin_s.at[plane, line, 0], w_twin.at[plane, line, 0], twin).start()

    def w_send_up(src, plane, line):
        @pl.when(has_up)
        def _():
            dst = w_block(plane, line, c, cols_near)
            copy(src, dst, w_up.at[plane, line], w_line.at[plane, line], up).start()

    def w_send_down(src, plane, line):
        @pl.when(has_down)
        def _():
            dst = w_block(plane, line, c, cols_near)
            copy(src, dst, w_down.at[plane, line], w_line.at[plane, line], down).start()

    def w_start():
        mine_src = w_ref.at[own_heads, :, cols_near]
        copy(
            w_ref.at[other_heads, :, cols_near],
            w_block(z, y, c, cols_near),
            w_side.at[0],
            w_side.at[1],
            side,
        ).start()
        w_send_up(mine_src, z, y)
        w_send_down(mine_src, z, y)
        w_spread(mine_src, z, y)

    def w_side_relay():
        block = w_block(z, 1 - y, c, cols_near)
        arrived(block, w_side.at[1])
        w_send_up(block, z, 1 - y)
        w_send_down(block, z, 1 - y)
        w_spread(block, z, 1 - y)

    def w_relay(step):
        low, high = z - step, z + step
        for turn in range(2):
            line = y + turn - 2 * y * turn

            @pl.when(low >= 0)
            def _():
                block = w_block(low, line, c, cols_near)
                arrived(block, w_line.at[low, line])
                w_send_up(block, low, line)
                w_spread(block, low, line)

            @pl.when(high < planes)
            def _():
                block = w_block(high, line, c, cols_near)
                arrived(block, w_line.at[high, line])
                w_send_down(block, high, line)
                w_spread(block, high, line)

    def w_far_relay(plane):
        for line in range(2):
            block = w_block(plane, line, c, cols_far)
            arrived(block, w_far.at[plane, line])
            copy(
                block, block, w_twin_s.at[plane, line, 1], w_twin.at[plane, line, 1], twin
            ).start()

    def w_far_relays(step):
        low, high = z - step, z + step

        @pl.when(low >= 0)
        def _():
            w_far_relay(low)

        @pl.when((high < planes) & (step > 0))
        def _():
            w_far_relay(high)

    scale = width ** (-0.5)
    tile = group // 2
    tile_rows = tile * rows

    def fold(keys, values, diagonal):
        def lines(line, carry):
            for part in range(2):
                heads = pl.ds(part * tile, tile)
                queries = q_buf[line, heads].reshape(tile_rows, width)
                queries = queries * jnp.asarray(scale, queries.dtype)
                scores = lax.dot_general(
                    queries, keys(), (((1,), (1,)), ((), ())), preferred_element_type=jnp.float32
                )
                if diagonal:
                    row_at = lax.broadcasted_iota(jnp.int32, scores.shape, 0) % rows
                    col_at = lax.broadcasted_iota(jnp.int32, scores.shape, 1)
                    scores = jnp.where(
                        col_at <= row_at + (line * 2 + c) * rows, scores, -jnp.inf
                    )
                    new_top = jnp.max(scores, 1, keepdims=True)
                    exps = jnp.exp(scores - new_top)
                    new_total = jnp.sum(exps, 1, keepdims=True)
                    new_acc = jnp.dot(
                        exps.astype(jnp.bfloat16), values(), preferred_element_type=jnp.float32
                    )
                else:
                    old_top = top[line, heads].reshape(tile_rows, 128)[:, :1]
                    old_total = total[line, heads].reshape(tile_rows, 128)[:, :1]
                    new_top = jnp.maximum(old_top, jnp.max(scores, 1, keepdims=True))
                    exps = jnp.exp(scores - new_top)
                    shrink = jnp.exp(old_top - new_top)
                    new_total = old_total * shrink + jnp.sum(exps, 1, keepdims=True)
                    new_acc = acc[line, heads].reshape(tile_rows, width) * shrink + jnp.dot(
                        exps.astype(jnp.bfloat16), values(), preferred_element_type=jnp.float32
                    )
                top[line, heads] = jnp.broadcast_to(new_top, (tile_rows, 128)).reshape(
                    tile, rows, 128
                )
                total[line, heads] = jnp.broadcast_to(new_total, (tile_rows, 128)).reshape(
                    tile, rows, 128
                )
                acc[line, heads] = new_acc.reshape(tile, rows, width)
            return carry

        lax.fori_loop(0, 2, lines, 0)

    def new_part(plane, first):
        return lambda: kn[y, plane, :, :, :, first : first + width].reshape(4 * rows, width)

    page = kc.shape[3]

    def old_part(plane, line, first):
        return lambda: kc[plane, line, :, :, first : first + width].reshape(2 * page, width)

    def twins_new(plane):
        for line in range(2):
            arrived(kn.at[y, plane, line, 1 - c], kn_twin.at[plane, line])

    def twins_old(plane):
        for line in range(2):
            arrived(kc.at[plane, line, 1 - c], kc_twin.at[plane, line])

    from_side_new(z)
    from_side_old(z)
    relay(1)
    w_start()
    arrived(q_buf.at[1 - y], q_sem.at[1])
    for item in locals_:
        item.wait()
    twins_new(z)
    fold(new_part(z, 0), new_part(z, width), True)

    def step_body(step, carry):
        @pl.when((step >= 1) & (step + 1 < planes))
        def _():
            relay(step + 1)

        @pl.when(step == planes - 2)
        def _():
            w_side_relay()

        @pl.when(step == planes - 1)
        def _():
            w_relay(1)

        low, high = z - step, z + step

        @pl.when((step >= 1) & (low >= 0))
        def _():
            twins_new(low)
            fold(new_part(low, 0), new_part(low, width), False)

        def old_body(index, carry):
            plane = jnp.where(index == 0, low, high)
            valid = (plane >= 0) & (plane < planes) & ((index == 0) | (step > 0))

            @pl.when(valid & mine(plane))
            def _():
                twins_old(plane)

                def line_body(line, carry):
                    fold(old_part(plane, line, 0), old_part(plane, line, width), False)
                    return carry

                lax.fori_loop(0, 2, line_body, 0)

            return carry

        lax.fori_loop(0, 2, old_body, 0)
        return carry

    lax.fori_loop(0, planes, step_body, 0)

    for line in range(2):
        for head in range(group):
            att[line, :, head * width : (head + 1) * width] = (
                acc[line, head] / total[line, head][:, :1]
            ).astype(att.dtype)

    w_far_relays(0)

    def w_body(step, carry):
        w_relay(step)
        w_far_relays(step - 1)
        return carry

    lax.fori_loop(2, planes, w_body, 0)
    w_far_relays(planes - 1)
    for plane in range(planes):
        for line in range(2):
            arrived(w_block(plane, line, 1 - c, cols_near), w_twin.at[plane, line, 0])
            arrived(w_block(plane, line, 1 - c, cols_far), w_twin.at[plane, line, 1])

    chunk = half // 2
    chunks = model // chunk
    for index in range(chunks):
        cols = pl.ds(index * chunk, chunk)
        weights = wb[:, :, :, :, :, index * chunk : (index + 1) * chunk].reshape(
            group * width, chunk
        )
        there = jnp.dot(att[1 - y], weights, preferred_element_type=jnp.float32)
        part_out[:, cols] = there.astype(part_out.dtype)
        block = part_out.at[:, cols]
        copy(block, part_in.at[:, cols], part_sem_s.at[index], part_sem.at[index], side).start()
        here = jnp.dot(att[y], weights, preferred_element_type=jnp.float32)
        stream_ref[:, cols] = here + resid_ref[:, cols].astype(jnp.float32)
    square = jnp.zeros((rows, 1), jnp.float32)
    for index in range(chunks):
        cols = pl.ds(index * chunk, chunk)
        arrived(part_in.at[:, cols], part_sem.at[index])
        stream = stream_ref[:, cols] + part_in[:, cols].astype(jnp.float32)
        stream_ref[:, cols] = stream
        square = square + jnp.sum(stream * stream, 1, keepdims=True)
    inverse = lax.rsqrt(square / model + eps_norm)
    for index in range(chunks):
        cols = pl.ds(index * chunk, chunk)
        normed_ref[:, cols] = (stream_ref[:, cols] * inverse * gain_ref[:, cols]).astype(
            normed_ref.dtype
        )
        left(part_out.at[:, cols], part_sem_s.at[index])

    left(q_buf.at[y], q_sem.at[0])
    left(w_block(z, y, c, cols_near), w_side.at[0])

    def drain(plane, carry):
        reached = plane <= z

        @pl.when(reached)
        def _():
            left(kn.at[1 - y, plane, y, c], kn_side_s.at[plane])
            left(kn.at[y, plane, y, c], kn_twin_s.at[plane, y])
            left(kn.at[y, plane, 1 - y, c], kn_twin_s.at[plane, 1 - y])

        @pl.when(reached & has_up)
        def _():
            left(kn.at[:, plane, y, c], kn_up.at[plane])
            left(kc.at[plane, y, c], kc_up.at[plane])
            for line in range(2):
                left(w_block(plane, line, c, cols_near), w_up.at[plane, line])

        @pl.when((plane >= z) & has_down)
        def _():
            left(kc.at[plane, y, c], kc_down.at[plane])
            for line in range(2):
                left(w_block(plane, line, c, cols_near), w_down.at[plane, line])

        @pl.when(mine(plane))
        def _():
            for line in range(2):
                left(kc.at[plane, line, c], kc_twin_s.at[plane, line])

        @pl.when(jnp.logical_not(mine(plane)))
        def _():
            left(kc.at[plane, y, c], kc_side_s.at[plane])

        for line in range(2):
            left(w_block(plane, line, c, cols_near), w_far_s.at[plane, line])
            left(w_block(plane, line, c, cols_near), w_twin_s.at[plane, line, 0])
            left(w_block(plane, line, c, cols_far), w_twin_s.at[plane, line, 1])
        return carry

    lax.fori_loop(0, planes, drain, 0)


def front(queries, pairs, cached, w_out, resid, gain, axis_count):
    heads, rows, width = queries.shape
    group = heads // 2
    planes = axis_count // 4
    model = w_out.shape[2]
    slice_rows = w_out.shape[1]
    page = cached.shape[0]
    dma = pltpu.SemaphoreType.DMA
    anywhere = pl.BlockSpec(memory_space=pl.ANY)
    inside = pl.BlockSpec(memory_space=pltpu.VMEM)
    return pl.pallas_call(
        front_kernel,
        out_shape=(
            jax.ShapeDtypeStruct((rows, model), jnp.float32),
            jax.ShapeDtypeStruct((rows, model), jnp.bfloat16),
        ),
        in_specs=[anywhere] * 4 + [inside] * 2,
        out_specs=(inside, inside),
        scratch_shapes=[
            pltpu.VMEM((2, group, rows, width), jnp.bfloat16),
            pltpu.VMEM((2, planes, 2, 2, rows, 2 * width), jnp.bfloat16),
            pltpu.VMEM((planes, 2, 2, page, 2 * width), jnp.bfloat16),
            pltpu.VMEM((group, planes, 2, 2, slice_rows, model), jnp.bfloat16),
            pltpu.VMEM((2, group, rows, width), jnp.float32),
            pltpu.VMEM((2, group, rows, 128), jnp.float32),
            pltpu.VMEM((2, group, rows, 128), jnp.float32),
            pltpu.VMEM((2, rows, group * width), jnp.bfloat16),
            pltpu.VMEM((rows, model), jnp.bfloat16),
            pltpu.VMEM((rows, model), jnp.bfloat16),
            dma((4,)),
            dma((2,)),
            dma((planes,)),
            dma((planes,)),
            dma((planes,)),
            dma((planes,)),
            dma((planes, 2)),
            dma((planes, 2)),
            dma((planes,)),
            dma((planes,)),
            dma((planes,)),
            dma((planes,)),
            dma((planes,)),
            dma((planes, 2)),
            dma((planes, 2)),
            dma((planes, 2)),
            dma((planes, 2)),
            dma((planes, 2)),
            dma((2,)),
            dma((planes, 2)),
            dma((planes, 2)),
            dma((planes, 2, 2)),
            dma((planes, 2, 2)),
            dma((4,)),
            dma((4,)),
        ],
        compiler_params=pltpu.CompilerParams(
            collective_id=0, has_side_effects=True, vmem_limit_bytes=48 * 2**20
        ),
        cost_estimate=pl.CostEstimate(
            flops=4 * 2 * group * rows * width * 4 * axis_count * rows
            + 4 * rows * group * width * model,
            bytes_accessed=8 * 2**20,
            transcendentals=2 * group * rows * axis_count * rows,
        ),
    )(queries, pairs, cached, w_out, resid, gain)


def partner_2(value, stride):
    mask = 2**stride
    pairs = [(source, source ^ mask) for source in range(lax.axis_size("head"))]
    return lax.ppermute(value, "head", pairs)


def turn_grp(value, shift):
    count = lax.axis_size("grp")
    return lax.ppermute(value, "grp", [(i, (i + shift) % count) for i in range(count)])


def attend_kernel(
    me_ref, query_ref, cache_ref, other_ref, pairs_ref, out_ref, new_ref, *, block, old_block, order
):
    head_width = query_ref.shape[1]
    step = pl.program_id(0)
    members, slots, local_rows = pairs_ref.shape[:3]

    @pl.when(step == 0)
    def _():
        for slot in range(slots):
            for member in range(members):
                apart = member ^ me_ref[0]
                place = 0
                for rank, bit in enumerate(order):
                    place = place + ((apart >> bit) & 1) * 2**rank
                first = (slot * members + member) * local_rows
                new_ref[first : first + local_rows, :] = pairs_ref[place, slot]

    query_rows = query_ref[...] * jnp.asarray(head_width ** (-0.5), query_ref.dtype)

    def fold(carry, keys, values, mask):
        top, total, weighted = carry
        scores = lax.dot_general(
            query_rows, keys, (((1,), (1,)), ((), ())), preferred_element_type=jnp.float32
        )
        if mask is not None:
            scores = jnp.where(mask, scores, -jnp.inf)
        new_top = jnp.maximum(top, jnp.max(scores, 1, keepdims=True))
        exps = jnp.exp(scores - new_top)
        shrink = jnp.exp(top - new_top)
        total = total * shrink + jnp.sum(exps, 1, keepdims=True)
        weighted = weighted * shrink + jnp.dot(
            exps.astype(jnp.bfloat16), values, preferred_element_type=jnp.float32
        )
        return new_top, total, weighted

    rows = query_rows.shape[0]
    carry = (
        jnp.full((rows, 1), -jnp.inf, jnp.float32),
        jnp.zeros((rows, 1), jnp.float32),
        jnp.zeros((rows, head_width), jnp.float32),
    )
    row_at = lax.broadcasted_iota(jnp.int32, (rows, block), 0)
    col_at = lax.broadcasted_iota(jnp.int32, (rows, block), 1)
    here = pl.ds(step * block, block)
    carry = fold(
        carry, new_ref[here, :head_width], new_ref[here, head_width:], col_at <= row_at
    )
    for old_ref in (cache_ref, other_ref):
        for first in range(0, old_ref.shape[0], old_block):
            part = pl.ds(first, old_block)
            carry = fold(carry, old_ref[part, :head_width], old_ref[part, head_width:], None)

    def earlier(index, carry):
        part = pl.ds(index * block, block)
        return fold(carry, new_ref[part, :head_width], new_ref[part, head_width:], None)

    top, total, weighted = lax.fori_loop(0, step, earlier, carry)
    out_ref[...] = (weighted / total).astype(out_ref.dtype)


def attend(me, queries, new_pairs, cached, cached_other, order):
    length, head_width = queries.shape
    block = min(512, length)
    old_block = min(1024, cached.shape[0])
    return pl.pallas_call(
        functools.partial(attend_kernel, block=block, old_block=old_block, order=order),
        grid_spec=pltpu.PrefetchScalarGridSpec(
            num_scalar_prefetch=1,
            grid=(length // block,),
            in_specs=[
                pl.BlockSpec((block, head_width), lambda i, me: (i, 0)),
                pl.BlockSpec(cached.shape, lambda i, me: (0, 0)),
                pl.BlockSpec(cached_other.shape, lambda i, me: (0, 0)),
                pl.BlockSpec(new_pairs.shape, lambda i, me: (0, 0, 0, 0)),
            ],
            out_specs=pl.BlockSpec((block, head_width), lambda i, me: (i, 0)),
            scratch_shapes=[pltpu.VMEM((length, 2 * head_width), jnp.bfloat16)],
        ),
        out_shape=jax.ShapeDtypeStruct((length, head_width), jnp.bfloat16),
        cost_estimate=pl.CostEstimate(
            flops=4 * length * head_width * (length // 2 + 2 * cached.shape[0]),
            bytes_accessed=8 * length * head_width * 2,
            transcendentals=length * (length // 2 + 2 * cached.shape[0]),
        ),
    )(me, queries, cached, cached_other, new_pairs)


def front_general(queries, new_kv, cache, resid, w_out, norm_gain):
    axis_count = lax.axis_size("head")
    local_rows = queries.shape[0]
    seq_count = queries.shape[1]
    head_count = queries.shape[2]
    head_width = queries.shape[3]
    pair_heads = new_kv.shape[2]
    group_size = head_count // pair_heads
    model_width = resid.shape[2]
    row_count = local_rows * seq_count
    slots = seq_count * pair_heads
    across = [[c * group_size + j for c in range(slots)] for j in range(group_size)]
    query_slots = queries.reshape(local_rows, axis_count, head_width).transpose(1, 0, 2)
    pair_slots = new_kv.reshape(local_rows, slots, 2 * head_width).transpose(1, 0, 2)
    pair_slots = lax.all_to_all(
        pair_slots, "head", split_axis=0, concat_axis=0, axis_index_groups=across, tiled=True
    )
    grp_count = lax.axis_size("grp")
    grp_me = lax.axis_index("grp")
    part_width = model_width // grp_count
    w_part = lax.dynamic_slice_in_dim(w_out, grp_me * part_width, part_width, 2)
    bits = group_size.bit_length() - 1
    order = tuple(range(1, bits)) + (0,)
    cache_rows = cache[0]
    pairs = pair_slots[None]
    for bit in order[:-1]:
        cache_rows = jnp.concatenate([cache_rows, partner_2(cache_rows, bit)], 0)
    head_queries = lax.all_to_all(query_slots, "head", split_axis=0, concat_axis=0, tiled=True)
    for bit in order[:-1]:
        pairs = jnp.concatenate([pairs, partner_2(pairs, bit)], 0)
    w_part, pairs, cache_rows, head_queries = lax.optimization_barrier(
        (w_part, pairs, cache_rows, head_queries)
    )
    w_part = lax.all_gather(w_part, "head", axis=1, tiled=True)
    w_part = w_part.reshape(head_count * head_width, part_width)
    cache_other = partner_2(cache_rows, 0)
    pairs = jnp.concatenate([pairs, partner_2(pairs, 0)], 0)
    me = (lax.axis_index("head") % group_size).astype(jnp.int32).reshape(1)
    attended = attend(
        me, head_queries.reshape(-1, head_width), pairs, cache_rows, cache_other, order
    )
    returned = lax.all_to_all(
        attended.reshape(axis_count, local_rows, head_width),
        "head",
        split_axis=0,
        concat_axis=0,
        tiled=True,
    )
    attn_rows = returned.reshape(seq_count, head_count, local_rows, head_width)
    attn_rows = attn_rows.transpose(2, 0, 1, 3).reshape(row_count, head_count * head_width)
    parts = []
    for shift in range(1, grp_count):
        far_rows = turn_grp(attn_rows, shift)
        far_part = jnp.dot(far_rows, w_part, preferred_element_type=jnp.float32)
        parts.append(turn_grp(far_part.astype(jnp.bfloat16), -shift).astype(jnp.float32))
    projected = []
    near_part = jnp.dot(attn_rows, w_part, preferred_element_type=jnp.float32)
    for column in range(grp_count):
        piece = near_part
        for shift in range(1, grp_count):
            piece = jnp.where((grp_me + shift) % grp_count == column, parts[shift - 1], piece)
        projected.append(piece)
    projected = jnp.concatenate(projected, 1)
    stream = resid.reshape(row_count, model_width).astype(jnp.float32) + projected
    normed = stream * lax.rsqrt(jnp.mean(stream * stream, 1, keepdims=True) + eps_norm) * norm_gain
    normed = normed.astype(jnp.bfloat16)
    return stream, normed


def experts(stream, normed, expert_ids, expert_gates, w_in, w_down):
    row_count, model_width = stream.shape
    axis_count = lax.axis_size("head")
    top_count = expert_ids.shape[2]
    flat_ids = expert_ids.reshape(-1)
    local_experts = w_in.shape[0]
    experts = local_experts * axis_count
    capacity = max(2, 2 * row_count * top_count // experts)
    onehot = (flat_ids[:, None] == jnp.arange(experts, dtype=jnp.int32)[None, :]).astype(jnp.int32)
    before = jnp.tri(flat_ids.shape[0], k=-1, dtype=jnp.bfloat16)
    earlier = jnp.dot(
        before, onehot.astype(jnp.bfloat16), preferred_element_type=jnp.float32
    ).astype(jnp.int32)
    slot_rank = jnp.sum(earlier * onehot, 1)
    target = flat_ids * capacity + slot_rank
    target = target.reshape(row_count, top_count)
    places = jnp.arange(experts * capacity, dtype=jnp.int32)
    chosen = jnp.zeros((experts * capacity, row_count), jnp.bool_)
    gate_of = jnp.zeros((row_count, experts * capacity), jnp.float32)
    gates = expert_gates.reshape(row_count, top_count)
    for rank in range(top_count):
        chosen = chosen | (places[:, None] == target[None, :, rank])
        gate_of = jnp.where(
            target[:, rank, None] == places[None, :], gates[:, rank, None], gate_of
        )
    outgoing = jnp.dot(
        chosen.astype(jnp.bfloat16), normed, preferred_element_type=jnp.float32
    ).astype(jnp.bfloat16)
    outgoing = outgoing.reshape(axis_count, local_experts, capacity, model_width)
    hidden_width = w_down.shape[1]
    inner_act = jnp.einsum(
        "semd,edf->semf",
        lax.all_to_all(outgoing, "head", split_axis=0, concat_axis=0, tiled=True),
        w_in,
        preferred_element_type=jnp.float32,
    )
    hidden = (jax.nn.silu(inner_act[..., :hidden_width]) * inner_act[..., hidden_width:]).astype(
        jnp.bfloat16
    )
    answered = jnp.einsum(
        "semf,efd->semd", hidden, w_down, preferred_element_type=jnp.float32
    ).astype(jnp.bfloat16)
    returned_rows = lax.all_to_all(answered, "head", split_axis=0, concat_axis=0, tiled=True)
    picked = returned_rows.reshape(experts * capacity, model_width)
    expert_sum = jnp.zeros((row_count, model_width), jnp.float32)
    rest = gate_of
    for _ in range(3):
        term = lax.reduce_precision(rest, 8, 7)
        rest = rest - term
        expert_sum = expert_sum + jnp.dot(
            term.astype(jnp.bfloat16), picked, preferred_element_type=jnp.float32
        )
    return (stream + expert_sum).astype(jnp.bfloat16)


def local(queries, new_kv, cache, resid, w_out, norm_gain, expert_ids, expert_gates, w_in, w_down):
    axis_count = lax.axis_size("head")
    local_rows, seq_count, head_count, head_width = queries.shape
    pair_heads = new_kv.shape[2]
    fits = (
        seq_count == 1
        and pair_heads == 2
        and lax.axis_size("grp") == 2
        and axis_count % 8 == 0
        and cache.shape[0] == 1
        and w_out.shape[1] * axis_count == head_width
        and w_out.shape[1] % 16 == 0
        and local_rows % 16 == 0
        and head_count % 4 == 0
    )
    if fits:
        stream, normed = front(
            queries.reshape(local_rows, head_count, head_width).transpose(1, 0, 2),
            new_kv.reshape(local_rows, pair_heads, 2 * head_width).transpose(1, 0, 2),
            cache[0],
            w_out,
            resid.reshape(local_rows, -1),
            norm_gain.reshape(1, -1),
            axis_count,
        )
    else:
        stream, normed = front_general(queries, new_kv, cache, resid, w_out, norm_gain)
    out = experts(stream, normed, expert_ids, expert_gates, w_in, w_down)
    return out.reshape(resid.shape)


def solution(mesh):
    return jax.shard_map(
        local,
        mesh=mesh,
        in_specs=(
            P("head", "grp", None, None),
            P("head", "grp", None, None),
            P(("grp", "head"), None, None),
            P("head", "grp", None),
            P(None, "head", None),
            P(),
            P("head", "grp", None),
            P("head", "grp", None),
            P("head", None, None),
            P("head", None, None),
        ),
        out_specs=P("head", "grp", None),
        check_vma=False,
    )
```

```python
import functools

import jax
import jax.numpy as jnp
from jax import lax
from jax.experimental import pallas as pl
from jax.experimental.pallas import tpu as pltpu
from jax.sharding import PartitionSpec as P

eps_norm = 1e-06
MESH = pl.DeviceIdType.MESH


def front_kernel(
    q_ref,
    kv_ref,
    cache_ref,
    w_ref,
    resid_ref,
    gain_ref,
    stream_ref,
    normed_ref,
    q_buf,
    kn,
    kc,
    wb,
    acc,
    top,
    total,
    att,
    part_out,
    part_in,
    local_sem,
    q_sem,
    kn_line,
    kn_up,
    kn_side,
    kn_side_s,
    kn_twin,
    kn_twin_s,
    kc_line,
    kc_up,
    kc_down,
    kc_side,
    kc_side_s,
    kc_twin,
    kc_twin_s,
    w_line,
    w_up,
    w_down,
    w_side,
    w_side_s,
    w_far,
    w_far_s,
    w_twin,
    w_twin_s,
    part_sem,
    part_sem_s,
):
    planes = kn.shape[1]
    group = q_buf.shape[1]
    rows, width = q_buf.shape[2:]
    model = w_ref.shape[2]
    half, chunk = model // 2, model // 4
    g = lax.axis_index("grp")
    me = lax.axis_index("head")
    z, y, c = me // 4, (me // 2) % 2, me % 2
    up, down = (g, me + 4), (g, me - 4)
    side, twin, far = (g, me + 2 - 4 * y), (g, me + 1 - 2 * c), (1 - g, me)
    has_up, has_down = z < planes - 1, z > 0

    barrier = pltpu.get_barrier_semaphore()
    for peer in (side, twin, far):
        pl.semaphore_signal(barrier, inc=1, device_id=peer, device_id_type=MESH)

    @pl.when(has_up)
    def _():
        pl.semaphore_signal(barrier, inc=1, device_id=up, device_id_type=MESH)

    @pl.when(has_down)
    def _():
        pl.semaphore_signal(barrier, inc=1, device_id=down, device_id_type=MESH)

    pl.semaphore_wait(barrier, 3 + has_up.astype(jnp.int32) + has_down.astype(jnp.int32))

    def copy(src, dst, sent, got, peer):
        return pltpu.make_async_remote_copy(
            src_ref=src,
            dst_ref=dst,
            send_sem=sent,
            recv_sem=got,
            device_id=peer,
            device_id_type=MESH,
        )

    def arrived(dst, got):
        copy(dst, dst, got, got, twin).wait_recv()

    def left(src, sent):
        copy(src, src, sent, sent, twin).wait_send()

    def mine(plane):
        return plane // (planes // 2) == y

    cols_near = pl.ds(pl.multiple_of(g * half, half), half)
    own_heads = pl.ds(y * group, group)
    other_heads = pl.ds((1 - y) * group, group)

    def w_cols(quarter, near):
        first = jnp.where(near, g, 1 - g) * half + quarter * chunk
        return pl.ds(pl.multiple_of(first, chunk), chunk)

    def w_block(quarter, plane, line, core, near=True):
        return wb.at[:, plane, line, core, :, w_cols(quarter, near)]

    def w_spread(src, quarter, plane, line):
        dst = w_block(quarter, plane, line, c)
        at = (quarter, plane, line)
        copy(src, dst, w_far_s.at[at], w_far.at[at], far).start()
        copy(src, dst, w_twin_s.at[(*at, 0)], w_twin.at[(*at, 0)], twin).start()

    def w_send_up(src, quarter, plane, line):
        at = (quarter, plane, line)

        @pl.when(has_up)
        def _():
            copy(src, w_block(quarter, plane, line, c), w_up.at[at], w_line.at[at], up).start()

    def w_send_down(src, quarter, plane, line):
        at = (quarter, plane, line)

        @pl.when(has_down)
        def _():
            copy(src, w_block(quarter, plane, line, c), w_down.at[at], w_line.at[at], down).start()

    def w_own_side(quarter):
        src = w_ref.at[other_heads, :, w_cols(quarter, True)]
        dst = w_block(quarter, z, y, c)
        copy(src, dst, w_side_s.at[quarter], w_side.at[quarter], side).start()

    def w_own(quarter):
        src = w_ref.at[own_heads, :, w_cols(quarter, True)]
        w_send_up(src, quarter, z, y)
        w_send_down(src, quarter, z, y)
        w_spread(src, quarter, z, y)

    def w_side_relay(quarter):
        block = w_block(quarter, z, 1 - y, c)
        arrived(block, w_side.at[quarter])
        w_send_up(block, quarter, z, 1 - y)
        w_send_down(block, quarter, z, 1 - y)
        w_spread(block, quarter, z, 1 - y)

    def w_relay(quarter, step):
        low, high = z - step, z + step
        for turn in range(2):
            line = y + turn - 2 * y * turn

            @pl.when(low >= 0)
            def _():
                block = w_block(quarter, low, line, c)
                arrived(block, w_line.at[quarter, low, line])
                w_send_up(block, quarter, low, line)
                w_spread(block, quarter, low, line)

            @pl.when(high < planes)
            def _():
                block = w_block(quarter, high, line, c)
                arrived(block, w_line.at[quarter, high, line])
                w_send_down(block, quarter, high, line)
                w_spread(block, quarter, high, line)

    def w_far_relay(quarter, plane):
        for line in range(2):
            block = w_block(quarter, plane, line, c, False)
            arrived(block, w_far.at[quarter, plane, line])
            at = (quarter, plane, line, 1)
            copy(block, block, w_twin_s.at[at], w_twin.at[at], twin).start()

    def w_far_relays(quarter, step):
        low, high = z - step, z + step

        @pl.when(low >= 0)
        def _():
            w_far_relay(quarter, low)

        if step > 0:

            @pl.when(high < planes)
            def _():
                w_far_relay(quarter, high)

    @pl.when(has_up)
    def _():
        copy(cache_ref, kc.at[z, y, c], kc_up.at[z], kc_line.at[z], up).start()
        copy(kv_ref, kn.at[:, z, y, c], kn_up.at[z], kn_line.at[z], up).start()

    @pl.when(has_down)
    def _():
        copy(cache_ref, kc.at[z, y, c], kc_down.at[z], kc_line.at[z], down).start()

    copy(kv_ref.at[1 - y], kn.at[1 - y, z, y, c], kn_side_s.at[z], kn_side.at[z], side).start()
    w_own_side(0)
    copy(q_ref.at[other_heads], q_buf.at[y], q_sem.at[0], q_sem.at[1], side).start()
    copy(kv_ref.at[y], kn.at[y, z, y, c], kn_twin_s.at[z, y], kn_twin.at[z, y], twin).start()

    @pl.when(mine(z))
    def _():
        copy(cache_ref, kc.at[z, y, c], kc_twin_s.at[z, y], kc_twin.at[z, y], twin).start()

    @pl.when(jnp.logical_not(mine(z)))
    def _():
        copy(cache_ref, kc.at[z, y, c], kc_side_s.at[z], kc_side.at[z], side).start()

    w_own(0)
    w_own_side(1)
    locals_ = (
        pltpu.make_async_copy(q_ref.at[own_heads], q_buf.at[y], local_sem.at[0]),
        pltpu.make_async_copy(kv_ref.at[y], kn.at[y, z, y, c], local_sem.at[1]),
        pltpu.make_async_copy(cache_ref, kc.at[z, y, c], local_sem.at[2]),
        pltpu.make_async_copy(
            w_ref.at[own_heads, :, cols_near], wb.at[:, z, y, c, :, cols_near], local_sem.at[3]
        ),
    )
    for item in locals_:
        item.start()

    def from_side_new(plane):
        block = kn.at[y, plane, 1 - y, c]
        arrived(block, kn_side.at[plane])
        copy(block, block, kn_twin_s.at[plane, 1 - y], kn_twin.at[plane, 1 - y], twin).start()

    def from_side_old(plane):
        @pl.when(mine(plane))
        def _():
            block = kc.at[plane, 1 - y, c]
            arrived(block, kc_side.at[plane])
            copy(block, block, kc_twin_s.at[plane, 1 - y], kc_twin.at[plane, 1 - y], twin).start()

    def spread_old(plane):
        block = kc.at[plane, y, c]

        @pl.when(mine(plane))
        def _():
            copy(block, block, kc_twin_s.at[plane, y], kc_twin.at[plane, y], twin).start()

        @pl.when(jnp.logical_not(mine(plane)))
        def _():
            copy(block, block, kc_side_s.at[plane], kc_side.at[plane], side).start()

    def relay(step):
        low, high = z - step, z + step

        @pl.when(high < planes)
        def _():
            old = kc.at[high, y, c]
            arrived(old, kc_line.at[high])

            @pl.when(has_down)
            def _():
                copy(old, old, kc_down.at[high], kc_line.at[high], down).start()

            spread_old(high)

        @pl.when(low >= 0)
        def _():
            old, new = kc.at[low, y, c], kn.at[:, low, y, c]
            arrived(old, kc_line.at[low])

            @pl.when(has_up)
            def _():
                copy(old, old, kc_up.at[low], kc_line.at[low], up).start()

            arrived(new, kn_line.at[low])

            @pl.when(has_up)
            def _():
                copy(new, new, kn_up.at[low], kn_line.at[low], up).start()

            there, here = kn.at[1 - y, low, y, c], kn.at[y, low, y, c]
            copy(there, there, kn_side_s.at[low], kn_side.at[low], side).start()
            copy(here, here, kn_twin_s.at[low, y], kn_twin.at[low, y], twin).start()
            spread_old(low)

    def from_side(step):
        low, high = z - step, z + step

        @pl.when(low >= 0)
        def _():
            from_side_new(low)
            from_side_old(low)

        @pl.when(high < planes)
        def _():
            from_side_old(high)

    scale = width ** (-0.5)
    tile = 2
    tile_rows = tile * rows

    def fold(keys, values, diagonal):
        def lines(line, carry):
            for part in range(group // tile):
                heads = pl.ds(part * tile, tile)
                queries = q_buf[line, heads].reshape(tile_rows, width)
                queries = queries * jnp.asarray(scale, queries.dtype)
                scores = lax.dot_general(
                    queries, keys(), (((1,), (1,)), ((), ())), preferred_element_type=jnp.float32
                )
                pieces = [
                    scores[:, first : first + 128] for first in range(0, scores.shape[1], 128)
                ]
                if diagonal:
                    row_at = lax.broadcasted_iota(jnp.int32, (tile_rows, 128), 0) % rows
                    ahead = row_at - lax.broadcasted_iota(jnp.int32, (tile_rows, 128), 1)
                    ahead = ahead + (line * 2 + c) * rows
                    pieces = [
                        jnp.where(ahead >= index * 128, piece, -jnp.inf)
                        for index, piece in enumerate(pieces)
                    ]
                best = functools.reduce(jnp.maximum, pieces)
                best = jnp.max(best, 1, keepdims=True)
                if diagonal:
                    new_top = jnp.broadcast_to(best, (tile_rows, 128))
                else:
                    old_top = top[line, heads].reshape(tile_rows, 128)
                    new_top = jnp.maximum(old_top, best)
                exps = [jnp.exp(piece - new_top) for piece in pieces]
                new_total = functools.reduce(jnp.add, exps)
                weighted = jnp.dot(
                    jnp.concatenate([part_.astype(jnp.bfloat16) for part_ in exps], 1),
                    values(),
                    preferred_element_type=jnp.float32,
                )
                if not diagonal:
                    shrink = jnp.exp(old_top - new_top)
                    new_total = new_total + total[line, heads].reshape(tile_rows, 128) * shrink
                    weighted = weighted + acc[line, heads].reshape(
                        tile_rows, width
                    ) * jnp.concatenate([shrink] * (width // 128), 1)
                top[line, heads] = new_top.reshape(tile, rows, 128)
                total[line, heads] = new_total.reshape(tile, rows, 128)
                acc[line, heads] = weighted.reshape(tile, rows, width)
            return carry

        lax.fori_loop(0, 2, lines, 0, unroll=2)

    def new_part(plane, first):
        return lambda: kn[y, plane, :, :, :, first : first + width].reshape(4 * rows, width)

    page = kc.shape[3]

    def old_part(plane, line, first):
        return lambda: kc[plane, line, :, :, first : first + width].reshape(2 * page, width)

    def twins_new(plane):
        for line in range(2):
            arrived(kn.at[y, plane, line, 1 - c], kn_twin.at[plane, line])

    def twins_old(plane):
        for line in range(2):
            arrived(kc.at[plane, line, 1 - c], kc_twin.at[plane, line])

    from_side_new(z)
    w_side_relay(0)
    relay(1)
    w_own(1)
    arrived(q_buf.at[1 - y], q_sem.at[1])
    from_side_old(z)
    for item in locals_:
        item.wait()
    twins_new(z)
    fold(new_part(z, 0), new_part(z, width), True)
    w_side_relay(1)

    def step_body(step, carry):
        @pl.when((step >= 1) & (step + 1 < planes))
        def _():
            relay(step + 1)

        @pl.when(step >= 2)
        def _():
            w_relay(0, step - 1)

        @pl.when(step >= 1)
        def _():
            from_side(step)

        low, high = z - step, z + step

        @pl.when((step >= 1) & (low >= 0))
        def _():
            twins_new(low)
            fold(new_part(low, 0), new_part(low, width), False)

        def old_body(index, carry):
            plane = jnp.where(index == 0, low, high)
            valid = (plane >= 0) & (plane < planes) & ((index == 0) | (step > 0))

            @pl.when(valid & mine(plane))
            def _():
                twins_old(plane)

                def line_body(line, carry):
                    fold(old_part(plane, line, 0), old_part(plane, line, width), False)
                    return carry

                lax.fori_loop(0, 2, line_body, 0)

            return carry

        lax.fori_loop(0, 2, old_body, 0)
        return carry

    lax.fori_loop(0, planes, step_body, 0)

    for line in range(2):
        for head in range(group):
            att[line, :, head * width : (head + 1) * width] = (
                acc[line, head] / jnp.sum(total[line, head], 1, keepdims=True)
            ).astype(att.dtype)

    def project(quarter):
        for near in range(2):
            for plane in range(planes):
                for line in range(2):
                    arrived(
                        w_block(quarter, plane, line, 1 - c, near == 0),
                        w_twin.at[quarter, plane, line, near],
                    )
            cols = w_cols(quarter, near == 0)
            weights = wb[:, :, :, :, :, cols].reshape(group * width, chunk)
            there = jnp.dot(att[1 - y], weights, preferred_element_type=jnp.float32)
            part_out[:, cols] = there.astype(part_out.dtype)
            index = quarter * 2 + near
            block = part_out.at[:, cols]
            copy(block, part_in.at[:, cols], part_sem_s.at[index], part_sem.at[index], side).start()
            here = jnp.dot(att[y], weights, preferred_element_type=jnp.float32)
            stream_ref[:, cols] = here + resid_ref[:, cols].astype(jnp.float32)

    for step in range(planes - 1):
        w_far_relays(0, step)
    w_relay(0, planes - 1)
    for step in range(1, planes - 1):
        w_relay(1, step)
    w_far_relays(0, planes - 1)
    project(0)
    for step in range(planes - 1):
        w_far_relays(1, step)
    w_relay(1, planes - 1)
    w_far_relays(1, planes - 1)
    project(1)
    square = jnp.zeros((rows, 1), jnp.float32)
    for quarter in range(2):
        for near in range(2):
            cols = w_cols(quarter, near == 0)
            index = quarter * 2 + near
            arrived(part_in.at[:, cols], part_sem.at[index])
            stream = stream_ref[:, cols] + part_in[:, cols].astype(jnp.float32)
            stream_ref[:, cols] = stream
            square = square + jnp.sum(stream * stream, 1, keepdims=True)
            left(part_out.at[:, cols], part_sem_s.at[index])
    inverse = lax.rsqrt(square / model + eps_norm)
    for index in range(4):
        cols = slice(index * chunk, (index + 1) * chunk)
        normed_ref[:, cols] = (stream_ref[:, cols] * inverse * gain_ref[:, cols]).astype(
            normed_ref.dtype
        )

    left(q_buf.at[y], q_sem.at[0])
    for quarter in range(2):
        left(w_block(quarter, z, y, c), w_side_s.at[quarter])

    def drain(plane, carry):
        reached = plane <= z

        @pl.when(reached)
        def _():
            left(kn.at[1 - y, plane, y, c], kn_side_s.at[plane])
            left(kn.at[y, plane, y, c], kn_twin_s.at[plane, y])
            left(kn.at[y, plane, 1 - y, c], kn_twin_s.at[plane, 1 - y])

        @pl.when(reached & has_up)
        def _():
            left(kn.at[:, plane, y, c], kn_up.at[plane])
            left(kc.at[plane, y, c], kc_up.at[plane])
            for quarter in range(2):
                for line in range(2):
                    left(w_block(quarter, plane, line, c), w_up.at[quarter, plane, line])

        @pl.when((plane >= z) & has_down)
        def _():
            left(kc.at[plane, y, c], kc_down.at[plane])
            for quarter in range(2):
                for line in range(2):
                    left(w_block(quarter, plane, line, c), w_down.at[quarter, plane, line])

        @pl.when(mine(plane))
        def _():
            for line in range(2):
                left(kc.at[plane, line, c], kc_twin_s.at[plane, line])

        @pl.when(jnp.logical_not(mine(plane)))
        def _():
            left(kc.at[plane, y, c], kc_side_s.at[plane])

        for quarter in range(2):
            for line in range(2):
                at = (quarter, plane, line)
                left(w_block(quarter, plane, line, c), w_far_s.at[at])
                left(w_block(quarter, plane, line, c), w_twin_s.at[(*at, 0)])
                left(w_block(quarter, plane, line, c, False), w_twin_s.at[(*at, 1)])
        return carry

    lax.fori_loop(0, planes, drain, 0)


def front(queries, pairs, cached, w_out, resid, gain, axis_count):
    heads, rows, width = queries.shape
    group = heads // 2
    planes = axis_count // 4
    model = w_out.shape[2]
    slice_rows = w_out.shape[1]
    page = cached.shape[0]
    dma = pltpu.SemaphoreType.DMA
    anywhere = pl.BlockSpec(memory_space=pl.ANY)
    inside = pl.BlockSpec(memory_space=pltpu.VMEM)
    return pl.pallas_call(
        front_kernel,
        out_shape=(
            jax.ShapeDtypeStruct((rows, model), jnp.float32),
            jax.ShapeDtypeStruct((rows, model), jnp.bfloat16),
        ),
        in_specs=[anywhere] * 4 + [inside] * 2,
        out_specs=(inside, inside),
        scratch_shapes=[
            pltpu.VMEM((2, group, rows, width), jnp.bfloat16),
            pltpu.VMEM((2, planes, 2, 2, rows, 2 * width), jnp.bfloat16),
            pltpu.VMEM((planes, 2, 2, page, 2 * width), jnp.bfloat16),
            pltpu.VMEM((group, planes, 2, 2, slice_rows, model), jnp.bfloat16),
            pltpu.VMEM((2, group, rows, width), jnp.float32),
            pltpu.VMEM((2, group, rows, 128), jnp.float32),
            pltpu.VMEM((2, group, rows, 128), jnp.float32),
            pltpu.VMEM((2, rows, group * width), jnp.bfloat16),
            pltpu.VMEM((rows, model), jnp.bfloat16),
            pltpu.VMEM((rows, model), jnp.bfloat16),
            dma((4,)),
            dma((2,)),
            dma((planes,)),
            dma((planes,)),
            dma((planes,)),
            dma((planes,)),
            dma((planes, 2)),
            dma((planes, 2)),
            dma((planes,)),
            dma((planes,)),
            dma((planes,)),
            dma((planes,)),
            dma((planes,)),
            dma((planes, 2)),
            dma((planes, 2)),
            dma((2, planes, 2)),
            dma((2, planes, 2)),
            dma((2, planes, 2)),
            dma((2,)),
            dma((2,)),
            dma((2, planes, 2)),
            dma((2, planes, 2)),
            dma((2, planes, 2, 2)),
            dma((2, planes, 2, 2)),
            dma((4,)),
            dma((4,)),
        ],
        compiler_params=pltpu.CompilerParams(
            collective_id=0, has_side_effects=True, vmem_limit_bytes=60 * 2**20
        ),
        cost_estimate=pl.CostEstimate(
            flops=4 * 2 * group * rows * width * 4 * axis_count * rows
            + 4 * rows * group * width * model,
            bytes_accessed=8 * 2**20,
            transcendentals=2 * group * rows * axis_count * rows,
        ),
    )(queries, pairs, cached, w_out, resid, gain)


def partner_2(value, stride):
    mask = 2**stride
    pairs = [(source, source ^ mask) for source in range(lax.axis_size("head"))]
    return lax.ppermute(value, "head", pairs)


def turn_grp(value, shift):
    count = lax.axis_size("grp")
    return lax.ppermute(value, "grp", [(i, (i + shift) % count) for i in range(count)])


def attend_kernel(
    me_ref, query_ref, cache_ref, other_ref, pairs_ref, out_ref, new_ref, *, block, old_block, order
):
    head_width = query_ref.shape[1]
    step = pl.program_id(0)
    members, slots, local_rows = pairs_ref.shape[:3]

    @pl.when(step == 0)
    def _():
        for slot in range(slots):
            for member in range(members):
                apart = member ^ me_ref[0]
                place = 0
                for rank, bit in enumerate(order):
                    place = place + ((apart >> bit) & 1) * 2**rank
                first = (slot * members + member) * local_rows
                new_ref[first : first + local_rows, :] = pairs_ref[place, slot]

    query_rows = query_ref[...] * jnp.asarray(head_width ** (-0.5), query_ref.dtype)

    def fold(carry, keys, values, mask):
        top, total, weighted = carry
        scores = lax.dot_general(
            query_rows, keys, (((1,), (1,)), ((), ())), preferred_element_type=jnp.float32
        )
        if mask is not None:
            scores = jnp.where(mask, scores, -jnp.inf)
        new_top = jnp.maximum(top, jnp.max(scores, 1, keepdims=True))
        exps = jnp.exp(scores - new_top)
        shrink = jnp.exp(top - new_top)
        total = total * shrink + jnp.sum(exps, 1, keepdims=True)
        weighted = weighted * shrink + jnp.dot(
            exps.astype(jnp.bfloat16), values, preferred_element_type=jnp.float32
        )
        return new_top, total, weighted

    rows = query_rows.shape[0]
    carry = (
        jnp.full((rows, 1), -jnp.inf, jnp.float32),
        jnp.zeros((rows, 1), jnp.float32),
        jnp.zeros((rows, head_width), jnp.float32),
    )
    row_at = lax.broadcasted_iota(jnp.int32, (rows, block), 0)
    col_at = lax.broadcasted_iota(jnp.int32, (rows, block), 1)
    here = pl.ds(step * block, block)
    carry = fold(
        carry, new_ref[here, :head_width], new_ref[here, head_width:], col_at <= row_at
    )
    for old_ref in (cache_ref, other_ref):
        for first in range(0, old_ref.shape[0], old_block):
            part = pl.ds(first, old_block)
            carry = fold(carry, old_ref[part, :head_width], old_ref[part, head_width:], None)

    def earlier(index, carry):
        part = pl.ds(index * block, block)
        return fold(carry, new_ref[part, :head_width], new_ref[part, head_width:], None)

    top, total, weighted = lax.fori_loop(0, step, earlier, carry)
    out_ref[...] = (weighted / total).astype(out_ref.dtype)


def attend(me, queries, new_pairs, cached, cached_other, order):
    length, head_width = queries.shape
    block = min(512, length)
    old_block = min(1024, cached.shape[0])
    return pl.pallas_call(
        functools.partial(attend_kernel, block=block, old_block=old_block, order=order),
        grid_spec=pltpu.PrefetchScalarGridSpec(
            num_scalar_prefetch=1,
            grid=(length // block,),
            in_specs=[
                pl.BlockSpec((block, head_width), lambda i, me: (i, 0)),
                pl.BlockSpec(cached.shape, lambda i, me: (0, 0)),
                pl.BlockSpec(cached_other.shape, lambda i, me: (0, 0)),
                pl.BlockSpec(new_pairs.shape, lambda i, me: (0, 0, 0, 0)),
            ],
            out_specs=pl.BlockSpec((block, head_width), lambda i, me: (i, 0)),
            scratch_shapes=[pltpu.VMEM((length, 2 * head_width), jnp.bfloat16)],
        ),
        out_shape=jax.ShapeDtypeStruct((length, head_width), jnp.bfloat16),
        cost_estimate=pl.CostEstimate(
            flops=4 * length * head_width * (length // 2 + 2 * cached.shape[0]),
            bytes_accessed=8 * length * head_width * 2,
            transcendentals=length * (length // 2 + 2 * cached.shape[0]),
        ),
    )(me, queries, cached, cached_other, new_pairs)


def front_general(queries, new_kv, cache, resid, w_out, norm_gain):
    axis_count = lax.axis_size("head")
    local_rows = queries.shape[0]
    seq_count = queries.shape[1]
    head_count = queries.shape[2]
    head_width = queries.shape[3]
    pair_heads = new_kv.shape[2]
    group_size = head_count // pair_heads
    model_width = resid.shape[2]
    row_count = local_rows * seq_count
    slots = seq_count * pair_heads
    across = [[c * group_size + j for c in range(slots)] for j in range(group_size)]
    query_slots = queries.reshape(local_rows, axis_count, head_width).transpose(1, 0, 2)
    pair_slots = new_kv.reshape(local_rows, slots, 2 * head_width).transpose(1, 0, 2)
    pair_slots = lax.all_to_all(
        pair_slots, "head", split_axis=0, concat_axis=0, axis_index_groups=across, tiled=True
    )
    grp_count = lax.axis_size("grp")
    grp_me = lax.axis_index("grp")
    part_width = model_width // grp_count
    w_part = lax.dynamic_slice_in_dim(w_out, grp_me * part_width, part_width, 2)
    bits = group_size.bit_length() - 1
    order = tuple(range(1, bits)) + (0,)
    cache_rows = cache[0]
    pairs = pair_slots[None]
    for bit in order[:-1]:
        cache_rows = jnp.concatenate([cache_rows, partner_2(cache_rows, bit)], 0)
    head_queries = lax.all_to_all(query_slots, "head", split_axis=0, concat_axis=0, tiled=True)
    for bit in order[:-1]:
        pairs = jnp.concatenate([pairs, partner_2(pairs, bit)], 0)
    w_part, pairs, cache_rows, head_queries = lax.optimization_barrier(
        (w_part, pairs, cache_rows, head_queries)
    )
    w_part = lax.all_gather(w_part, "head", axis=1, tiled=True)
    w_part = w_part.reshape(head_count * head_width, part_width)
    cache_other = partner_2(cache_rows, 0)
    pairs = jnp.concatenate([pairs, partner_2(pairs, 0)], 0)
    me = (lax.axis_index("head") % group_size).astype(jnp.int32).reshape(1)
    attended = attend(
        me, head_queries.reshape(-1, head_width), pairs, cache_rows, cache_other, order
    )
    returned = lax.all_to_all(
        attended.reshape(axis_count, local_rows, head_width),
        "head",
        split_axis=0,
        concat_axis=0,
        tiled=True,
    )
    attn_rows = returned.reshape(seq_count, head_count, local_rows, head_width)
    attn_rows = attn_rows.transpose(2, 0, 1, 3).reshape(row_count, head_count * head_width)
    parts = []
    for shift in range(1, grp_count):
        far_rows = turn_grp(attn_rows, shift)
        far_part = jnp.dot(far_rows, w_part, preferred_element_type=jnp.float32)
        parts.append(turn_grp(far_part.astype(jnp.bfloat16), -shift).astype(jnp.float32))
    projected = []
    near_part = jnp.dot(attn_rows, w_part, preferred_element_type=jnp.float32)
    for column in range(grp_count):
        piece = near_part
        for shift in range(1, grp_count):
            piece = jnp.where((grp_me + shift) % grp_count == column, parts[shift - 1], piece)
        projected.append(piece)
    projected = jnp.concatenate(projected, 1)
    stream = resid.reshape(row_count, model_width).astype(jnp.float32) + projected
    normed = stream * lax.rsqrt(jnp.mean(stream * stream, 1, keepdims=True) + eps_norm) * norm_gain
    normed = normed.astype(jnp.bfloat16)
    return stream, normed


def experts(stream, normed, expert_ids, expert_gates, w_in, w_down):
    row_count, model_width = stream.shape
    axis_count = lax.axis_size("head")
    top_count = expert_ids.shape[2]
    flat_ids = expert_ids.reshape(-1)
    local_experts = w_in.shape[0]
    experts = local_experts * axis_count
    capacity = max(2, 2 * row_count * top_count // experts)
    onehot = (flat_ids[:, None] == jnp.arange(experts, dtype=jnp.int32)[None, :]).astype(jnp.int32)
    before = jnp.tri(flat_ids.shape[0], k=-1, dtype=jnp.bfloat16)
    earlier = jnp.dot(
        before, onehot.astype(jnp.bfloat16), preferred_element_type=jnp.float32
    ).astype(jnp.int32)
    slot_rank = jnp.sum(earlier * onehot, 1)
    target = flat_ids * capacity + slot_rank
    target = target.reshape(row_count, top_count)
    places = jnp.arange(experts * capacity, dtype=jnp.int32)
    chosen = jnp.zeros((experts * capacity, row_count), jnp.bool_)
    gate_of = jnp.zeros((row_count, experts * capacity), jnp.float32)
    gates = expert_gates.reshape(row_count, top_count)
    for rank in range(top_count):
        chosen = chosen | (places[:, None] == target[None, :, rank])
        gate_of = jnp.where(
            target[:, rank, None] == places[None, :], gates[:, rank, None], gate_of
        )
    outgoing = jnp.dot(
        chosen.astype(jnp.bfloat16), normed, preferred_element_type=jnp.float32
    ).astype(jnp.bfloat16)
    outgoing = outgoing.reshape(axis_count, local_experts, capacity, model_width)
    hidden_width = w_down.shape[1]
    inner_act = jnp.einsum(
        "semd,edf->semf",
        lax.all_to_all(outgoing, "head", split_axis=0, concat_axis=0, tiled=True),
        w_in,
        preferred_element_type=jnp.float32,
    )
    hidden = (jax.nn.silu(inner_act[..., :hidden_width]) * inner_act[..., hidden_width:]).astype(
        jnp.bfloat16
    )
    answered = jnp.einsum(
        "semf,efd->semd", hidden, w_down, preferred_element_type=jnp.float32
    ).astype(jnp.bfloat16)
    returned_rows = lax.all_to_all(answered, "head", split_axis=0, concat_axis=0, tiled=True)
    picked = returned_rows.reshape(experts * capacity, model_width)
    expert_sum = jnp.zeros((row_count, model_width), jnp.float32)
    rest = gate_of
    for _ in range(3):
        term = lax.reduce_precision(rest, 8, 7)
        rest = rest - term
        expert_sum = expert_sum + jnp.dot(
            term.astype(jnp.bfloat16), picked, preferred_element_type=jnp.float32
        )
    return (stream + expert_sum).astype(jnp.bfloat16)


def local(queries, new_kv, cache, resid, w_out, norm_gain, expert_ids, expert_gates, w_in, w_down):
    axis_count = lax.axis_size("head")
    local_rows, seq_count, head_count, head_width = queries.shape
    pair_heads = new_kv.shape[2]
    fits = (
        seq_count == 1
        and pair_heads == 2
        and lax.axis_size("grp") == 2
        and axis_count % 8 == 0
        and cache.shape[0] == 1
        and w_out.shape[1] * axis_count == head_width
        and w_out.shape[1] % 16 == 0
        and local_rows % 32 == 0
        and cache.shape[1] * 2 % 128 == 0
        and head_count % 4 == 0
    )
    if fits:
        stream, normed = front(
            queries.reshape(local_rows, head_count, head_width).transpose(1, 0, 2),
            new_kv.reshape(local_rows, pair_heads, 2 * head_width).transpose(1, 0, 2),
            cache[0],
            w_out,
            resid.reshape(local_rows, -1),
            norm_gain.reshape(1, -1),
            axis_count,
        )
    else:
        stream, normed = front_general(queries, new_kv, cache, resid, w_out, norm_gain)
    out = experts(stream, normed, expert_ids, expert_gates, w_in, w_down)
    return out.reshape(resid.shape)


def solution(mesh):
    return jax.shard_map(
        local,
        mesh=mesh,
        in_specs=(
            P("head", "grp", None, None),
            P("head", "grp", None, None),
            P(("grp", "head"), None, None),
            P("head", "grp", None),
            P(None, "head", None),
            P(),
            P("head", "grp", None),
            P("head", "grp", None),
            P("head", None, None),
            P("head", None, None),
        ),
        out_specs=P("head", "grp", None),
        check_vma=False,
    )
```

```python
import functools

import jax
import jax.numpy as jnp
from jax import lax
from jax.experimental import pallas as pl
from jax.experimental.pallas import tpu as pltpu
from jax.sharding import PartitionSpec as P

eps_norm = 1e-06
MESH = pl.DeviceIdType.MESH


def front_kernel(
    q_ref,
    kv_ref,
    cache_ref,
    w_ref,
    resid_ref,
    gain_ref,
    stream_ref,
    normed_ref,
    q_buf,
    kn,
    kc,
    wb,
    acc,
    top,
    total,
    att,
    part_out,
    part_in,
    local_sem,
    q_sem,
    kn_line,
    kn_up,
    kn_side,
    kn_side_s,
    kn_twin,
    kn_twin_s,
    kc_line,
    kc_up,
    kc_down,
    kc_side,
    kc_side_s,
    kc_twin,
    kc_twin_s,
    w_line,
    w_up,
    w_down,
    w_side,
    w_side_s,
    w_far,
    w_far_s,
    w_twin,
    w_twin_s,
    part_sem,
    part_sem_s,
):
    planes = kn.shape[1]
    group = q_buf.shape[1]
    rows, width = q_buf.shape[2:]
    model = w_ref.shape[2]
    half, chunk = model // 2, model // 4
    g = lax.axis_index("grp")
    me = lax.axis_index("head")
    z, y, c = me // 4, (me // 2) % 2, me % 2
    up, down = (g, me + 4), (g, me - 4)
    side, twin, far = (g, me + 2 - 4 * y), (g, me + 1 - 2 * c), (1 - g, me)
    has_up, has_down = z < planes - 1, z > 0

    barrier = pltpu.get_barrier_semaphore()
    for peer in (side, twin, far):
        pl.semaphore_signal(barrier, inc=1, device_id=peer, device_id_type=MESH)

    @pl.when(has_up)
    def _():
        pl.semaphore_signal(barrier, inc=1, device_id=up, device_id_type=MESH)

    @pl.when(has_down)
    def _():
        pl.semaphore_signal(barrier, inc=1, device_id=down, device_id_type=MESH)

    pl.semaphore_wait(barrier, 3 + has_up.astype(jnp.int32) + has_down.astype(jnp.int32))

    def copy(src, dst, sent, got, peer):
        return pltpu.make_async_remote_copy(
            src_ref=src,
            dst_ref=dst,
            send_sem=sent,
            recv_sem=got,
            device_id=peer,
            device_id_type=MESH,
        )

    def arrived(dst, got):
        copy(dst, dst, got, got, twin).wait_recv()

    def left(src, sent):
        copy(src, src, sent, sent, twin).wait_send()

    def mine(plane):
        return plane // (planes // 2) == y

    cols_near = pl.ds(pl.multiple_of(g * half, half), half)
    own_heads = pl.ds(y * group, group)
    other_heads = pl.ds((1 - y) * group, group)

    def w_cols(quarter, near):
        first = jnp.where(near, g, 1 - g) * half + quarter * chunk
        return pl.ds(pl.multiple_of(first, chunk), chunk)

    def w_block(quarter, plane, line, core, near=True):
        return wb.at[:, plane, line, core, :, w_cols(quarter, near)]

    def w_spread(src, quarter, plane, line):
        dst = w_block(quarter, plane, line, c)
        at = (quarter, plane, line)
        copy(src, dst, w_far_s.at[at], w_far.at[at], far).start()
        copy(src, dst, w_twin_s.at[(*at, 0)], w_twin.at[(*at, 0)], twin).start()

    def w_send_up(src, quarter, plane, line):
        at = (quarter, plane, line)

        @pl.when(has_up)
        def _():
            copy(src, w_block(quarter, plane, line, c), w_up.at[at], w_line.at[at], up).start()

    def w_send_down(src, quarter, plane, line):
        at = (quarter, plane, line)

        @pl.when(has_down)
        def _():
            copy(src, w_block(quarter, plane, line, c), w_down.at[at], w_line.at[at], down).start()

    def w_own_side(quarter):
        src = w_ref.at[other_heads, :, w_cols(quarter, True)]
        dst = w_block(quarter, z, y, c)
        copy(src, dst, w_side_s.at[quarter], w_side.at[quarter], side).start()

    def w_own(quarter):
        src = w_ref.at[own_heads, :, w_cols(quarter, True)]
        w_send_up(src, quarter, z, y)
        w_send_down(src, quarter, z, y)
        w_spread(src, quarter, z, y)

    def w_side_relay(quarter):
        block = w_block(quarter, z, 1 - y, c)
        arrived(block, w_side.at[quarter])
        w_send_up(block, quarter, z, 1 - y)
        w_send_down(block, quarter, z, 1 - y)
        w_spread(block, quarter, z, 1 - y)

    def w_relay(quarter, step):
        low, high = z - step, z + step
        for turn in range(2):
            line = y + turn - 2 * y * turn

            @pl.when(low >= 0)
            def _():
                block = w_block(quarter, low, line, c)
                arrived(block, w_line.at[quarter, low, line])
                w_send_up(block, quarter, low, line)
                w_spread(block, quarter, low, line)

            @pl.when(high < planes)
            def _():
                block = w_block(quarter, high, line, c)
                arrived(block, w_line.at[quarter, high, line])
                w_send_down(block, quarter, high, line)
                w_spread(block, quarter, high, line)

    def w_far_relay(quarter, plane):
        for line in range(2):
            block = w_block(quarter, plane, line, c, False)
            arrived(block, w_far.at[quarter, plane, line])
            at = (quarter, plane, line, 1)
            copy(block, block, w_twin_s.at[at], w_twin.at[at], twin).start()

    def w_far_relays(quarter, step):
        low, high = z - step, z + step

        @pl.when(low >= 0)
        def _():
            w_far_relay(quarter, low)

        if step > 0:

            @pl.when(high < planes)
            def _():
                w_far_relay(quarter, high)

    @pl.when(has_up)
    def _():
        copy(cache_ref, kc.at[z, y, c], kc_up.at[z], kc_line.at[z], up).start()
        copy(kv_ref, kn.at[:, z, y, c], kn_up.at[z], kn_line.at[z], up).start()

    @pl.when(has_down)
    def _():
        copy(cache_ref, kc.at[z, y, c], kc_down.at[z], kc_line.at[z], down).start()

    copy(kv_ref.at[1 - y], kn.at[1 - y, z, y, c], kn_side_s.at[z], kn_side.at[z], side).start()
    w_own_side(0)
    copy(q_ref.at[other_heads], q_buf.at[y], q_sem.at[0], q_sem.at[1], side).start()
    copy(kv_ref.at[y], kn.at[y, z, y, c], kn_twin_s.at[z, y], kn_twin.at[z, y], twin).start()

    @pl.when(mine(z))
    def _():
        copy(cache_ref, kc.at[z, y, c], kc_twin_s.at[z, y], kc_twin.at[z, y], twin).start()

    @pl.when(jnp.logical_not(mine(z)))
    def _():
        copy(cache_ref, kc.at[z, y, c], kc_side_s.at[z], kc_side.at[z], side).start()

    w_own(0)
    w_own_side(1)
    locals_ = (
        pltpu.make_async_copy(q_ref.at[own_heads], q_buf.at[y], local_sem.at[0]),
        pltpu.make_async_copy(kv_ref.at[y], kn.at[y, z, y, c], local_sem.at[1]),
        pltpu.make_async_copy(cache_ref, kc.at[z, y, c], local_sem.at[2]),
        pltpu.make_async_copy(
            w_ref.at[own_heads, :, cols_near], wb.at[:, z, y, c, :, cols_near], local_sem.at[3]
        ),
    )
    for item in locals_:
        item.start()

    def from_side_new(plane):
        block = kn.at[y, plane, 1 - y, c]
        arrived(block, kn_side.at[plane])
        copy(block, block, kn_twin_s.at[plane, 1 - y], kn_twin.at[plane, 1 - y], twin).start()

    def from_side_old(plane):
        @pl.when(mine(plane))
        def _():
            block = kc.at[plane, 1 - y, c]
            arrived(block, kc_side.at[plane])
            copy(block, block, kc_twin_s.at[plane, 1 - y], kc_twin.at[plane, 1 - y], twin).start()

    def spread_old(plane):
        block = kc.at[plane, y, c]

        @pl.when(mine(plane))
        def _():
            copy(block, block, kc_twin_s.at[plane, y], kc_twin.at[plane, y], twin).start()

        @pl.when(jnp.logical_not(mine(plane)))
        def _():
            copy(block, block, kc_side_s.at[plane], kc_side.at[plane], side).start()

    def relay(step):
        low, high = z - step, z + step

        @pl.when(high < planes)
        def _():
            old = kc.at[high, y, c]
            arrived(old, kc_line.at[high])

            @pl.when(has_down)
            def _():
                copy(old, old, kc_down.at[high], kc_line.at[high], down).start()

            spread_old(high)

        @pl.when(low >= 0)
        def _():
            old, new = kc.at[low, y, c], kn.at[:, low, y, c]
            arrived(old, kc_line.at[low])

            @pl.when(has_up)
            def _():
                copy(old, old, kc_up.at[low], kc_line.at[low], up).start()

            arrived(new, kn_line.at[low])

            @pl.when(has_up)
            def _():
                copy(new, new, kn_up.at[low], kn_line.at[low], up).start()

            there, here = kn.at[1 - y, low, y, c], kn.at[y, low, y, c]
            copy(there, there, kn_side_s.at[low], kn_side.at[low], side).start()
            copy(here, here, kn_twin_s.at[low, y], kn_twin.at[low, y], twin).start()
            spread_old(low)

    def from_side(step):
        low, high = z - step, z + step

        @pl.when(low >= 0)
        def _():
            from_side_new(low)
            from_side_old(low)

        @pl.when(high < planes)
        def _():
            from_side_old(high)

    scale = width ** (-0.5)
    tile = 2
    tile_rows = tile * rows

    def fold(keys, values, diagonal):
        def lines(line, carry):
            for part in range(group // tile):
                heads = pl.ds(part * tile, tile)
                queries = q_buf[line, heads].reshape(tile_rows, width)
                queries = queries * jnp.asarray(scale, queries.dtype)
                scores = lax.dot_general(
                    queries, keys(), (((1,), (1,)), ((), ())), preferred_element_type=jnp.float32
                )
                pieces = [
                    scores[:, first : first + 128] for first in range(0, scores.shape[1], 128)
                ]
                if diagonal:
                    row_at = lax.broadcasted_iota(jnp.int32, (tile_rows, 128), 0) % rows
                    ahead = row_at - lax.broadcasted_iota(jnp.int32, (tile_rows, 128), 1)
                    ahead = ahead + (line * 2 + c) * rows
                    pieces = [
                        jnp.where(ahead >= index * 128, piece, -jnp.inf)
                        for index, piece in enumerate(pieces)
                    ]
                best = functools.reduce(jnp.maximum, pieces)
                best = jnp.max(best, 1, keepdims=True)
                if diagonal:
                    new_top = jnp.broadcast_to(best, (tile_rows, 128))
                else:
                    old_top = top[line, heads].reshape(tile_rows, 128)
                    new_top = jnp.maximum(old_top, best)
                exps = [jnp.exp(piece - new_top) for piece in pieces]
                new_total = functools.reduce(jnp.add, exps)
                weighted = jnp.dot(
                    jnp.concatenate([part_.astype(jnp.bfloat16) for part_ in exps], 1),
                    values(),
                    preferred_element_type=jnp.float32,
                )
                if not diagonal:
                    shrink = jnp.exp(old_top - new_top)
                    new_total = new_total + total[line, heads].reshape(tile_rows, 128) * shrink
                    weighted = weighted + acc[line, heads].reshape(
                        tile_rows, width
                    ) * jnp.concatenate([shrink] * (width // 128), 1)
                top[line, heads] = new_top.reshape(tile, rows, 128)
                total[line, heads] = new_total.reshape(tile, rows, 128)
                acc[line, heads] = weighted.reshape(tile, rows, width)
            return carry

        lax.fori_loop(0, 2, lines, 0, unroll=2)

    def new_part(plane, first):
        return lambda: kn[y, plane, :, :, :, first : first + width].reshape(4 * rows, width)

    page = kc.shape[3]

    def old_part(plane, line, first):
        return lambda: kc[plane, line, :, :, first : first + width].reshape(2 * page, width)

    def twins_new(plane):
        for line in range(2):
            arrived(kn.at[y, plane, line, 1 - c], kn_twin.at[plane, line])

    def twins_old(plane):
        for line in range(2):
            arrived(kc.at[plane, line, 1 - c], kc_twin.at[plane, line])

    from_side_new(z)
    w_side_relay(0)
    relay(1)
    w_own(1)
    arrived(q_buf.at[1 - y], q_sem.at[1])
    from_side_old(z)
    for item in locals_:
        item.wait()
    twins_new(z)
    fold(new_part(z, 0), new_part(z, width), True)
    w_side_relay(1)

    def step_body(step, carry):
        @pl.when((step >= 1) & (step + 1 < planes))
        def _():
            relay(step + 1)

        @pl.when(step >= 2)
        def _():
            w_relay(0, step - 1)

        @pl.when(step >= 1)
        def _():
            from_side(step)

        low, high = z - step, z + step

        @pl.when((step >= 1) & (low >= 0))
        def _():
            twins_new(low)
            fold(new_part(low, 0), new_part(low, width), False)

        def old_body(index, carry):
            plane = jnp.where(index == 0, low, high)
            valid = (plane >= 0) & (plane < planes) & ((index == 0) | (step > 0))

            @pl.when(valid & mine(plane))
            def _():
                twins_old(plane)

                def line_body(line, carry):
                    fold(old_part(plane, line, 0), old_part(plane, line, width), False)
                    return carry

                lax.fori_loop(0, 2, line_body, 0)

            return carry

        lax.fori_loop(0, 2, old_body, 0)
        return carry

    lax.fori_loop(0, planes, step_body, 0)

    for line in range(2):
        for head in range(group):
            att[line, :, head * width : (head + 1) * width] = (
                acc[line, head] / jnp.sum(total[line, head], 1, keepdims=True)
            ).astype(att.dtype)

    def project(quarter):
        for near in range(2):
            for plane in range(planes):
                for line in range(2):
                    arrived(
                        w_block(quarter, plane, line, 1 - c, near == 0),
                        w_twin.at[quarter, plane, line, near],
                    )
            cols = w_cols(quarter, near == 0)
            weights = wb[:, :, :, :, :, cols].reshape(group * width, chunk)
            there = jnp.dot(att[1 - y], weights, preferred_element_type=jnp.float32)
            part_out[:, cols] = there.astype(part_out.dtype)
            index = quarter * 2 + near
            block = part_out.at[:, cols]
            copy(block, part_in.at[:, cols], part_sem_s.at[index], part_sem.at[index], side).start()
            here = jnp.dot(att[y], weights, preferred_element_type=jnp.float32)
            stream_ref[:, cols] = here + resid_ref[:, cols].astype(jnp.float32)

    for step in range(planes - 1):
        w_far_relays(0, step)
    w_relay(0, planes - 1)
    for step in range(1, planes - 1):
        w_relay(1, step)
    w_far_relays(0, planes - 1)
    project(0)
    for step in range(planes - 1):
        w_far_relays(1, step)
    w_relay(1, planes - 1)
    w_far_relays(1, planes - 1)
    project(1)
    square = jnp.zeros((rows, 1), jnp.float32)
    for quarter in range(2):
        for near in range(2):
            cols = w_cols(quarter, near == 0)
            index = quarter * 2 + near
            arrived(part_in.at[:, cols], part_sem.at[index])
            stream = stream_ref[:, cols] + part_in[:, cols].astype(jnp.float32)
            stream_ref[:, cols] = stream
            square = square + jnp.sum(stream * stream, 1, keepdims=True)
            left(part_out.at[:, cols], part_sem_s.at[index])
    inverse = lax.rsqrt(square / model + eps_norm)
    for index in range(4):
        cols = slice(index * chunk, (index + 1) * chunk)
        normed_ref[:, cols] = (stream_ref[:, cols] * inverse * gain_ref[:, cols]).astype(
            normed_ref.dtype
        )

    left(q_buf.at[y], q_sem.at[0])
    for quarter in range(2):
        left(w_block(quarter, z, y, c), w_side_s.at[quarter])

    def drain(plane, carry):
        reached = plane <= z

        @pl.when(reached)
        def _():
            left(kn.at[1 - y, plane, y, c], kn_side_s.at[plane])
            left(kn.at[y, plane, y, c], kn_twin_s.at[plane, y])
            left(kn.at[y, plane, 1 - y, c], kn_twin_s.at[plane, 1 - y])

        @pl.when(reached & has_up)
        def _():
            left(kn.at[:, plane, y, c], kn_up.at[plane])
            left(kc.at[plane, y, c], kc_up.at[plane])
            for quarter in range(2):
                for line in range(2):
                    left(w_block(quarter, plane, line, c), w_up.at[quarter, plane, line])

        @pl.when((plane >= z) & has_down)
        def _():
            left(kc.at[plane, y, c], kc_down.at[plane])
            for quarter in range(2):
                for line in range(2):
                    left(w_block(quarter, plane, line, c), w_down.at[quarter, plane, line])

        @pl.when(mine(plane))
        def _():
            for line in range(2):
                left(kc.at[plane, line, c], kc_twin_s.at[plane, line])

        @pl.when(jnp.logical_not(mine(plane)))
        def _():
            left(kc.at[plane, y, c], kc_side_s.at[plane])

        for quarter in range(2):
            for line in range(2):
                at = (quarter, plane, line)
                left(w_block(quarter, plane, line, c), w_far_s.at[at])
                left(w_block(quarter, plane, line, c), w_twin_s.at[(*at, 0)])
                left(w_block(quarter, plane, line, c, False), w_twin_s.at[(*at, 1)])
        return carry

    lax.fori_loop(0, planes, drain, 0)


def front(queries, pairs, cached, w_out, resid, gain, axis_count):
    heads, rows, width = queries.shape
    group = heads // 2
    planes = axis_count // 4
    model = w_out.shape[2]
    slice_rows = w_out.shape[1]
    page = cached.shape[0]
    dma = pltpu.SemaphoreType.DMA
    anywhere = pl.BlockSpec(memory_space=pl.ANY)
    inside = pl.BlockSpec(memory_space=pltpu.VMEM)
    return pl.pallas_call(
        front_kernel,
        out_shape=(
            jax.ShapeDtypeStruct((rows, model), jnp.float32),
            jax.ShapeDtypeStruct((rows, model), jnp.bfloat16),
        ),
        in_specs=[anywhere] * 4 + [inside] * 2,
        out_specs=(inside, inside),
        scratch_shapes=[
            pltpu.VMEM((2, group, rows, width), jnp.bfloat16),
            pltpu.VMEM((2, planes, 2, 2, rows, 2 * width), jnp.bfloat16),
            pltpu.VMEM((planes, 2, 2, page, 2 * width), jnp.bfloat16),
            pltpu.VMEM((group, planes, 2, 2, slice_rows, model), jnp.bfloat16),
            pltpu.VMEM((2, group, rows, width), jnp.float32),
            pltpu.VMEM((2, group, rows, 128), jnp.float32),
            pltpu.VMEM((2, group, rows, 128), jnp.float32),
            pltpu.VMEM((2, rows, group * width), jnp.bfloat16),
            pltpu.VMEM((rows, model), jnp.bfloat16),
            pltpu.VMEM((rows, model), jnp.bfloat16),
            dma((4,)),
            dma((2,)),
            dma((planes,)),
            dma((planes,)),
            dma((planes,)),
            dma((planes,)),
            dma((planes, 2)),
            dma((planes, 2)),
            dma((planes,)),
            dma((planes,)),
            dma((planes,)),
            dma((planes,)),
            dma((planes,)),
            dma((planes, 2)),
            dma((planes, 2)),
            dma((2, planes, 2)),
            dma((2, planes, 2)),
            dma((2, planes, 2)),
            dma((2,)),
            dma((2,)),
            dma((2, planes, 2)),
            dma((2, planes, 2)),
            dma((2, planes, 2, 2)),
            dma((2, planes, 2, 2)),
            dma((4,)),
            dma((4,)),
        ],
        compiler_params=pltpu.CompilerParams(
            collective_id=0, has_side_effects=True, vmem_limit_bytes=60 * 2**20
        ),
        cost_estimate=pl.CostEstimate(
            flops=4 * 2 * group * rows * width * 4 * axis_count * rows
            + 4 * rows * group * width * model,
            bytes_accessed=8 * 2**20,
            transcendentals=2 * group * rows * axis_count * rows,
        ),
    )(queries, pairs, cached, w_out, resid, gain)


def partner_2(value, stride):
    mask = 2**stride
    pairs = [(source, source ^ mask) for source in range(lax.axis_size("head"))]
    return lax.ppermute(value, "head", pairs)


def turn_grp(value, shift):
    count = lax.axis_size("grp")
    return lax.ppermute(value, "grp", [(i, (i + shift) % count) for i in range(count)])


def attend_kernel(
    me_ref, query_ref, cache_ref, other_ref, pairs_ref, out_ref, new_ref, *, block, old_block, order
):
    head_width = query_ref.shape[1]
    step = pl.program_id(0)
    members, slots, local_rows = pairs_ref.shape[:3]

    @pl.when(step == 0)
    def _():
        for slot in range(slots):
            for member in range(members):
                apart = member ^ me_ref[0]
                place = 0
                for rank, bit in enumerate(order):
                    place = place + ((apart >> bit) & 1) * 2**rank
                first = (slot * members + member) * local_rows
                new_ref[first : first + local_rows, :] = pairs_ref[place, slot]

    query_rows = query_ref[...] * jnp.asarray(head_width ** (-0.5), query_ref.dtype)

    def fold(carry, keys, values, mask):
        top, total, weighted = carry
        scores = lax.dot_general(
            query_rows, keys, (((1,), (1,)), ((), ())), preferred_element_type=jnp.float32
        )
        if mask is not None:
            scores = jnp.where(mask, scores, -jnp.inf)
        new_top = jnp.maximum(top, jnp.max(scores, 1, keepdims=True))
        exps = jnp.exp(scores - new_top)
        shrink = jnp.exp(top - new_top)
        total = total * shrink + jnp.sum(exps, 1, keepdims=True)
        weighted = weighted * shrink + jnp.dot(
            exps.astype(jnp.bfloat16), values, preferred_element_type=jnp.float32
        )
        return new_top, total, weighted

    rows = query_rows.shape[0]
    carry = (
        jnp.full((rows, 1), -jnp.inf, jnp.float32),
        jnp.zeros((rows, 1), jnp.float32),
        jnp.zeros((rows, head_width), jnp.float32),
    )
    row_at = lax.broadcasted_iota(jnp.int32, (rows, block), 0)
    col_at = lax.broadcasted_iota(jnp.int32, (rows, block), 1)
    here = pl.ds(step * block, block)
    carry = fold(
        carry, new_ref[here, :head_width], new_ref[here, head_width:], col_at <= row_at
    )
    for old_ref in (cache_ref, other_ref):
        for first in range(0, old_ref.shape[0], old_block):
            part = pl.ds(first, old_block)
            carry = fold(carry, old_ref[part, :head_width], old_ref[part, head_width:], None)

    def earlier(index, carry):
        part = pl.ds(index * block, block)
        return fold(carry, new_ref[part, :head_width], new_ref[part, head_width:], None)

    top, total, weighted = lax.fori_loop(0, step, earlier, carry)
    out_ref[...] = (weighted / total).astype(out_ref.dtype)


def attend(me, queries, new_pairs, cached, cached_other, order):
    length, head_width = queries.shape
    block = min(512, length)
    old_block = min(1024, cached.shape[0])
    return pl.pallas_call(
        functools.partial(attend_kernel, block=block, old_block=old_block, order=order),
        grid_spec=pltpu.PrefetchScalarGridSpec(
            num_scalar_prefetch=1,
            grid=(length // block,),
            in_specs=[
                pl.BlockSpec((block, head_width), lambda i, me: (i, 0)),
                pl.BlockSpec(cached.shape, lambda i, me: (0, 0)),
                pl.BlockSpec(cached_other.shape, lambda i, me: (0, 0)),
                pl.BlockSpec(new_pairs.shape, lambda i, me: (0, 0, 0, 0)),
            ],
            out_specs=pl.BlockSpec((block, head_width), lambda i, me: (i, 0)),
            scratch_shapes=[pltpu.VMEM((length, 2 * head_width), jnp.bfloat16)],
        ),
        out_shape=jax.ShapeDtypeStruct((length, head_width), jnp.bfloat16),
        cost_estimate=pl.CostEstimate(
            flops=4 * length * head_width * (length // 2 + 2 * cached.shape[0]),
            bytes_accessed=8 * length * head_width * 2,
            transcendentals=length * (length // 2 + 2 * cached.shape[0]),
        ),
    )(me, queries, cached, cached_other, new_pairs)


def front_general(queries, new_kv, cache, resid, w_out, norm_gain):
    axis_count = lax.axis_size("head")
    local_rows = queries.shape[0]
    seq_count = queries.shape[1]
    head_count = queries.shape[2]
    head_width = queries.shape[3]
    pair_heads = new_kv.shape[2]
    group_size = head_count // pair_heads
    model_width = resid.shape[2]
    row_count = local_rows * seq_count
    slots = seq_count * pair_heads
    across = [[c * group_size + j for c in range(slots)] for j in range(group_size)]
    query_slots = queries.reshape(local_rows, axis_count, head_width).transpose(1, 0, 2)
    pair_slots = new_kv.reshape(local_rows, slots, 2 * head_width).transpose(1, 0, 2)
    pair_slots = lax.all_to_all(
        pair_slots, "head", split_axis=0, concat_axis=0, axis_index_groups=across, tiled=True
    )
    grp_count = lax.axis_size("grp")
    grp_me = lax.axis_index("grp")
    part_width = model_width // grp_count
    w_part = lax.dynamic_slice_in_dim(w_out, grp_me * part_width, part_width, 2)
    bits = group_size.bit_length() - 1
    order = tuple(range(1, bits)) + (0,)
    cache_rows = cache[0]
    pairs = pair_slots[None]
    for bit in order[:-1]:
        cache_rows = jnp.concatenate([cache_rows, partner_2(cache_rows, bit)], 0)
    head_queries = lax.all_to_all(query_slots, "head", split_axis=0, concat_axis=0, tiled=True)
    for bit in order[:-1]:
        pairs = jnp.concatenate([pairs, partner_2(pairs, bit)], 0)
    w_part, pairs, cache_rows, head_queries = lax.optimization_barrier(
        (w_part, pairs, cache_rows, head_queries)
    )
    w_part = lax.all_gather(w_part, "head", axis=1, tiled=True)
    w_part = w_part.reshape(head_count * head_width, part_width)
    cache_other = partner_2(cache_rows, 0)
    pairs = jnp.concatenate([pairs, partner_2(pairs, 0)], 0)
    me = (lax.axis_index("head") % group_size).astype(jnp.int32).reshape(1)
    attended = attend(
        me, head_queries.reshape(-1, head_width), pairs, cache_rows, cache_other, order
    )
    returned = lax.all_to_all(
        attended.reshape(axis_count, local_rows, head_width),
        "head",
        split_axis=0,
        concat_axis=0,
        tiled=True,
    )
    attn_rows = returned.reshape(seq_count, head_count, local_rows, head_width)
    attn_rows = attn_rows.transpose(2, 0, 1, 3).reshape(row_count, head_count * head_width)
    parts = []
    for shift in range(1, grp_count):
        far_rows = turn_grp(attn_rows, shift)
        far_part = jnp.dot(far_rows, w_part, preferred_element_type=jnp.float32)
        parts.append(turn_grp(far_part.astype(jnp.bfloat16), -shift).astype(jnp.float32))
    projected = []
    near_part = jnp.dot(attn_rows, w_part, preferred_element_type=jnp.float32)
    for column in range(grp_count):
        piece = near_part
        for shift in range(1, grp_count):
            piece = jnp.where((grp_me + shift) % grp_count == column, parts[shift - 1], piece)
        projected.append(piece)
    projected = jnp.concatenate(projected, 1)
    stream = resid.reshape(row_count, model_width).astype(jnp.float32) + projected
    normed = stream * lax.rsqrt(jnp.mean(stream * stream, 1, keepdims=True) + eps_norm) * norm_gain
    normed = normed.astype(jnp.bfloat16)
    return stream, normed


def expert_kernel(
    normed_ref,
    stream_ref,
    info_ref,
    w_in_ref,
    w_down_ref,
    out_ref,
    w_in,
    w_down,
    rows_buf,
    info_buf,
    picked,
    inbox,
    outbox,
    answer,
    dense,
    summed,
    sums_in,
    sums_out,
    w_sem,
    row_line,
    row_up,
    row_down,
    info_line,
    info_up,
    info_down,
    in_sem,
    in_sem_s,
    ans_sem,
    ans_sem_s,
    sum_sem,
    sum_sem_s,
    *,
    top_count,
):
    planes, rows, model = rows_buf.shape
    near, cap = inbox.shape[1:3]
    hidden_width = w_down.shape[0]
    chunks = row_line.shape[1]
    chunk = model // chunks
    g = lax.axis_index("grp")
    me = lax.axis_index("head")
    z, own = me // near, me % near
    up, down = (g, me + near), (g, me - near)
    has_up, has_down = z < planes - 1, z > 0

    barrier = pltpu.get_barrier_semaphore()
    for mask in range(1, near):
        pl.semaphore_signal(barrier, inc=1, device_id=(g, me ^ mask), device_id_type=MESH)

    @pl.when(has_up)
    def _():
        pl.semaphore_signal(barrier, inc=1, device_id=up, device_id_type=MESH)

    @pl.when(has_down)
    def _():
        pl.semaphore_signal(barrier, inc=1, device_id=down, device_id_type=MESH)

    loads = (
        pltpu.make_async_copy(w_in_ref, w_in, w_sem.at[0]),
        pltpu.make_async_copy(w_down_ref, w_down, w_sem.at[1]),
    )
    for load in loads:
        load.start()
    pl.semaphore_wait(
        barrier, near - 1 + has_up.astype(jnp.int32) + has_down.astype(jnp.int32)
    )

    def copy(src, dst, sent, got, peer):
        return pltpu.make_async_remote_copy(
            src_ref=src,
            dst_ref=dst,
            send_sem=sent,
            recv_sem=got,
            device_id=peer,
            device_id_type=MESH,
        )

    def arrived(dst, got):
        copy(dst, dst, got, got, (g, me ^ 1)).wait_recv()

    def left(src, sent):
        copy(src, src, sent, sent, (g, me ^ 1)).wait_send()

    def cols(index):
        return slice(index * chunk, (index + 1) * chunk)

    def send_up(info, block, plane):
        @pl.when(has_up)
        def _():
            if info is not None:
                copy(info, info_buf.at[plane], info_up.at[plane], info_line.at[plane], up).start()
            else:
                src, index = block
                dst = rows_buf.at[plane, :, cols(index)]
                at = (plane, index)
                copy(src, dst, row_up.at[at], row_line.at[at], up).start()

    def send_down(info, block, plane):
        @pl.when(has_down)
        def _():
            if info is not None:
                copy(
                    info, info_buf.at[plane], info_down.at[plane], info_line.at[plane], down
                ).start()
            else:
                src, index = block
                dst = rows_buf.at[plane, :, cols(index)]
                at = (plane, index)
                copy(src, dst, row_down.at[at], row_line.at[at], down).start()

    def slots_of(info):
        at = lax.broadcasted_iota(jnp.int32, (near * cap, rows), 0) + z * (near * cap)
        at = at.astype(jnp.float32)
        return [at == info[rank : rank + 1, :] for rank in range(top_count)]

    def pick(plane, info, load):
        chosen = functools.reduce(jnp.logical_or, slots_of(info))
        chosen = jnp.where(chosen, 1.0, 0.0).astype(jnp.bfloat16)
        for index in range(chunks):
            part = jnp.dot(chosen, load(index), preferred_element_type=jnp.float32)
            picked[plane, :, :, cols(index)] = part.astype(jnp.bfloat16).reshape(near, cap, chunk)
            for mask in range(1, near):
                other = own ^ mask
                copy(
                    picked.at[plane, other, :, cols(index)],
                    inbox.at[plane, own, :, cols(index)],
                    in_sem_s.at[plane, other],
                    in_sem.at[plane, own],
                    (g, me ^ mask),
                ).start()
            inbox[plane, own, :, cols(index)] = picked[plane, own, :, cols(index)]

    def each(step, act):
        for turn in range(2):
            plane = z + step if turn == 0 else z - step
            valid = (plane < planes) & (step > 0) if turn == 0 else plane >= 0

            @pl.when(valid)
            def _():
                act(plane, turn)

    def each_loop(step, act):
        def body(turn, carry):
            plane = z + step * (1 - 2 * turn)
            valid = (plane < planes) & (plane >= 0) & ((turn == 1) | (step > 0))

            @pl.when(valid)
            def _():
                act(plane)

            return carry

        lax.fori_loop(0, 2, body, 0)

    def receive(plane, turn):
        onward = send_down if turn == 0 else send_up
        arrived(info_buf.at[plane], info_line.at[plane])
        onward(info_buf.at[plane], None, plane)

        def load(index):
            block = rows_buf.at[plane, :, cols(index)]
            arrived(block, row_line.at[plane, index])
            onward(None, (block, index), plane)
            return block[...]

        pick(plane, info_buf[plane], load)

    def run_expert(plane):
        for mask in range(1, near):
            arrived(inbox.at[plane, own ^ mask], in_sem.at[plane, own ^ mask])
        inner = jnp.dot(
            inbox[plane].reshape(near * cap, model), w_in[...], preferred_element_type=jnp.float32
        )
        gate, value = inner[:, :hidden_width], inner[:, hidden_width:]
        hidden = (gate / (1.0 + jnp.exp(-gate)) * value).astype(jnp.bfloat16)
        for index in range(chunks):
            part = jnp.dot(hidden, w_down[:, cols(index)], preferred_element_type=jnp.float32)
            outbox[plane, :, :, cols(index)] = part.astype(jnp.bfloat16).reshape(near, cap, chunk)
            for mask in range(1, near):
                other = own ^ mask
                copy(
                    outbox.at[plane, other, :, cols(index)],
                    answer.at[plane, own, :, cols(index)],
                    ans_sem_s.at[plane, other],
                    ans_sem.at[plane, own],
                    (g, me ^ mask),
                ).start()
            answer[plane, own, :, cols(index)] = outbox[plane, own, :, cols(index)]

    def combine(plane, info, store):
        for mask in range(1, near):
            arrived(answer.at[plane, own ^ mask], ans_sem.at[plane, own ^ mask])
        gates = jnp.zeros((near * cap, rows), jnp.float32)
        for rank, here in enumerate(slots_of(info)):
            gates = jnp.where(here, info[top_count + rank : top_count + rank + 1, :], gates)
        high = gates.astype(jnp.bfloat16)
        low = (gates - high.astype(jnp.float32)).astype(jnp.bfloat16)
        for index in range(chunks):
            values = answer[plane, :, :, cols(index)].reshape(near * cap, chunk)
            total = jnp.zeros((rows, chunk), jnp.float32)
            for term in (high, low):
                total = total + lax.dot_general(
                    term, values, (((0,), (0,)), ((), ())), preferred_element_type=jnp.float32
                )
            store(index, total)

    def combine_far(plane):
        def store(index, total):
            dense[plane, :, cols(index)] = total

        combine(plane, info_buf[plane], store)

    def pass_sums(length):
        def body(turn, carry):
            way = (turn + (z >= planes // 2).astype(jnp.int32)) % 2
            target = jnp.where(way == 0, length, planes - 1 - length)
            takes_part = jnp.where(way == 0, target - z, z - target) > 0
            has_in = jnp.where(way == 0, z, planes - 1 - z) > 0
            peer = (g, me + near - 2 * near * way)

            @pl.when(takes_part)
            def _():
                for index in range(chunks):
                    block = sums_in.at[way, target, :, cols(index)]
                    at = (way, target, index)

                    @pl.when(has_in)
                    def _():
                        arrived(block, sum_sem.at[at])
                        sums_out[target, :, cols(index)] = (
                            dense[target, :, cols(index)] + block[...].astype(jnp.float32)
                        ).astype(jnp.bfloat16)

                    @pl.when(jnp.logical_not(has_in))
                    def _():
                        sums_out[target, :, cols(index)] = dense[target, :, cols(index)].astype(
                            jnp.bfloat16
                        )

                    copy(
                        sums_out.at[target, :, cols(index)],
                        block,
                        sum_sem_s.at[at],
                        sum_sem.at[at],
                        peer,
                    ).start()

            return carry

        lax.fori_loop(0, 2, body, 0)

    send_up(info_ref, None, z)
    send_down(info_ref, None, z)
    for index in range(chunks):
        block = (normed_ref.at[:, cols(index)], index)
        send_up(None, block, z)
        send_down(None, block, z)
    pick(z, info_ref[...], lambda index: normed_ref[:, cols(index)])
    each(1, receive)
    for load in loads:
        load.wait()

    def step_body(step, carry):
        each_loop(step, run_expert)

        @pl.when((step >= 1) & (step + 1 < planes))
        def _():
            each(step + 1, receive)

        @pl.when(step == 0)
        def _():
            def store(index, total):
                summed[:, cols(index)] = stream_ref[:, cols(index)] + total

            combine(z, info_ref[...], store)

        @pl.when(step >= 1)
        def _():
            each_loop(step, combine_far)
            pass_sums(step)

        return carry

    lax.fori_loop(0, planes, step_body, 0)

    for index in range(chunks):

        @pl.when(has_down)
        def _():
            block = sums_in.at[0, z, :, cols(index)]
            arrived(block, sum_sem.at[0, z, index])
            summed[:, cols(index)] = summed[:, cols(index)] + block[...].astype(jnp.float32)

        @pl.when(has_up)
        def _():
            block = sums_in.at[1, z, :, cols(index)]
            arrived(block, sum_sem.at[1, z, index])
            summed[:, cols(index)] = summed[:, cols(index)] + block[...].astype(jnp.float32)

        out_ref[:, cols(index)] = summed[:, cols(index)].astype(out_ref.dtype)

    def drain(plane, carry):
        @pl.when((plane <= z) & has_up)
        def _():
            left(info_buf.at[plane], info_up.at[plane])
            for index in range(chunks):
                left(rows_buf.at[plane, :, cols(index)], row_up.at[plane, index])

        @pl.when((plane >= z) & has_down)
        def _():
            left(info_buf.at[plane], info_down.at[plane])
            for index in range(chunks):
                left(rows_buf.at[plane, :, cols(index)], row_down.at[plane, index])

        for mask in range(1, near):
            left(picked.at[plane, own ^ mask], in_sem_s.at[plane, own ^ mask])
            left(outbox.at[plane, own ^ mask], ans_sem_s.at[plane, own ^ mask])

        for index in range(chunks):

            @pl.when(plane > z)
            def _():
                left(sums_out.at[plane, :, cols(index)], sum_sem_s.at[0, plane, index])

            @pl.when(plane < z)
            def _():
                left(sums_out.at[plane, :, cols(index)], sum_sem_s.at[1, plane, index])

        return carry

    lax.fori_loop(0, planes, drain, 0)


def run_experts(normed, stream, info, w_in, w_down, axis_count, cap, top_count):
    rows, model = normed.shape
    near = 4
    planes = axis_count // near
    chunks = 4
    dma = pltpu.SemaphoreType.DMA
    anywhere = pl.BlockSpec(memory_space=pl.ANY)
    inside = pl.BlockSpec(memory_space=pltpu.VMEM)
    slots = pltpu.VMEM((planes, near, cap, model), jnp.bfloat16)
    blocks = pltpu.VMEM((planes, rows, model), jnp.bfloat16)
    return pl.pallas_call(
        functools.partial(expert_kernel, top_count=top_count),
        out_shape=jax.ShapeDtypeStruct((rows, model), jnp.bfloat16),
        in_specs=[inside] * 3 + [anywhere] * 2,
        out_specs=inside,
        scratch_shapes=[
            pltpu.VMEM(w_in.shape, jnp.bfloat16),
            pltpu.VMEM(w_down.shape, jnp.bfloat16),
            blocks,
            pltpu.VMEM((planes, *info.shape), jnp.float32),
            slots,
            slots,
            slots,
            slots,
            pltpu.VMEM((planes, rows, model), jnp.float32),
            pltpu.VMEM((rows, model), jnp.float32),
            pltpu.VMEM((2, planes, rows, model), jnp.bfloat16),
            blocks,
            dma((2,)),
            dma((planes, chunks)),
            dma((planes, chunks)),
            dma((planes, chunks)),
            dma((planes,)),
            dma((planes,)),
            dma((planes,)),
            dma((planes, near)),
            dma((planes, near)),
            dma((planes, near)),
            dma((planes, near)),
            dma((2, planes, chunks)),
            dma((2, planes, chunks)),
        ],
        compiler_params=pltpu.CompilerParams(
            collective_id=1, has_side_effects=True, vmem_limit_bytes=60 * 2**20
        ),
        cost_estimate=pl.CostEstimate(
            flops=6 * planes * near * cap * model * w_down.shape[0],
            bytes_accessed=8 * 2**20,
            transcendentals=planes * near * cap * w_down.shape[0],
        ),
    )(normed, stream, info, w_in, w_down)


def route(expert_ids, expert_gates, experts, row_count, top_count):
    flat_ids = expert_ids.reshape(-1)
    capacity = max(2, 2 * row_count * top_count // experts)
    onehot = (flat_ids[:, None] == jnp.arange(experts, dtype=jnp.int32)[None, :]).astype(
        jnp.float32
    )
    before = jnp.tri(flat_ids.shape[0], k=-1, dtype=jnp.bfloat16)
    earlier = jnp.dot(before, onehot.astype(jnp.bfloat16), preferred_element_type=jnp.float32)
    slot = flat_ids.astype(jnp.float32) * capacity + jnp.sum(earlier * onehot, 1)
    lines = jnp.concatenate(
        [slot.reshape(row_count, top_count), expert_gates.reshape(row_count, top_count)], 1
    ).T
    spare = -lines.shape[0] % 8
    return jnp.pad(lines, ((0, spare), (0, 0))), capacity


def experts(stream, normed, expert_ids, expert_gates, w_in, w_down):
    row_count, model_width = stream.shape
    axis_count = lax.axis_size("head")
    top_count = expert_ids.shape[2]
    flat_ids = expert_ids.reshape(-1)
    local_experts = w_in.shape[0]
    experts = local_experts * axis_count
    capacity = max(2, 2 * row_count * top_count // experts)
    onehot = (flat_ids[:, None] == jnp.arange(experts, dtype=jnp.int32)[None, :]).astype(jnp.int32)
    before = jnp.tri(flat_ids.shape[0], k=-1, dtype=jnp.bfloat16)
    earlier = jnp.dot(
        before, onehot.astype(jnp.bfloat16), preferred_element_type=jnp.float32
    ).astype(jnp.int32)
    slot_rank = jnp.sum(earlier * onehot, 1)
    target = flat_ids * capacity + slot_rank
    target = target.reshape(row_count, top_count)
    places = jnp.arange(experts * capacity, dtype=jnp.int32)
    chosen = jnp.zeros((experts * capacity, row_count), jnp.bool_)
    gate_of = jnp.zeros((row_count, experts * capacity), jnp.float32)
    gates = expert_gates.reshape(row_count, top_count)
    for rank in range(top_count):
        chosen = chosen | (places[:, None] == target[None, :, rank])
        gate_of = jnp.where(
            target[:, rank, None] == places[None, :], gates[:, rank, None], gate_of
        )
    outgoing = jnp.dot(
        chosen.astype(jnp.bfloat16), normed, preferred_element_type=jnp.float32
    ).astype(jnp.bfloat16)
    outgoing = outgoing.reshape(axis_count, local_experts, capacity, model_width)
    hidden_width = w_down.shape[1]
    inner_act = jnp.einsum(
        "semd,edf->semf",
        lax.all_to_all(outgoing, "head", split_axis=0, concat_axis=0, tiled=True),
        w_in,
        preferred_element_type=jnp.float32,
    )
    hidden = (jax.nn.silu(inner_act[..., :hidden_width]) * inner_act[..., hidden_width:]).astype(
        jnp.bfloat16
    )
    answered = jnp.einsum(
        "semf,efd->semd", hidden, w_down, preferred_element_type=jnp.float32
    ).astype(jnp.bfloat16)
    returned_rows = lax.all_to_all(answered, "head", split_axis=0, concat_axis=0, tiled=True)
    picked = returned_rows.reshape(experts * capacity, model_width)
    expert_sum = jnp.zeros((row_count, model_width), jnp.float32)
    rest = gate_of
    for _ in range(3):
        term = lax.reduce_precision(rest, 8, 7)
        rest = rest - term
        expert_sum = expert_sum + jnp.dot(
            term.astype(jnp.bfloat16), picked, preferred_element_type=jnp.float32
        )
    return (stream + expert_sum).astype(jnp.bfloat16)


def local(queries, new_kv, cache, resid, w_out, norm_gain, expert_ids, expert_gates, w_in, w_down):
    axis_count = lax.axis_size("head")
    local_rows, seq_count, head_count, head_width = queries.shape
    pair_heads = new_kv.shape[2]
    fits = (
        seq_count == 1
        and pair_heads == 2
        and lax.axis_size("grp") == 2
        and axis_count % 8 == 0
        and cache.shape[0] == 1
        and w_out.shape[1] * axis_count == head_width
        and w_out.shape[1] % 16 == 0
        and local_rows % 32 == 0
        and cache.shape[1] * 2 % 128 == 0
        and head_count % 4 == 0
    )
    if fits:
        info, capacity = route(
            expert_ids,
            expert_gates,
            w_in.shape[0] * axis_count,
            local_rows * seq_count,
            expert_ids.shape[2],
        )
        stream, normed = front(
            queries.reshape(local_rows, head_count, head_width).transpose(1, 0, 2),
            new_kv.reshape(local_rows, pair_heads, 2 * head_width).transpose(1, 0, 2),
            cache[0],
            w_out,
            resid.reshape(local_rows, -1),
            norm_gain.reshape(1, -1),
            axis_count,
        )
    else:
        stream, normed = front_general(queries, new_kv, cache, resid, w_out, norm_gain)
    top_count = expert_ids.shape[2]
    row_count = stream.shape[0]
    experts_count = w_in.shape[0] * axis_count
    if fits and w_in.shape[0] == 1 and row_count % 128 == 0 and (row_count * top_count * 2) % (
        16 * experts_count
    ) == 0:
        out = run_experts(
            normed, stream, info, w_in[0], w_down[0], axis_count, capacity, top_count
        )
    else:
        out = experts(stream, normed, expert_ids, expert_gates, w_in, w_down)
    return out.reshape(resid.shape)


def solution(mesh):
    return jax.shard_map(
        local,
        mesh=mesh,
        in_specs=(
            P("head", "grp", None, None),
            P("head", "grp", None, None),
            P(("grp", "head"), None, None),
            P("head", "grp", None),
            P(None, "head", None),
            P(),
            P("head", "grp", None),
            P("head", "grp", None),
            P("head", None, None),
            P("head", None, None),
        ),
        out_specs=P("head", "grp", None),
        check_vma=False,
    )
```

```python
import functools

import jax
import jax.numpy as jnp
from jax import lax
from jax.experimental import pallas as pl
from jax.experimental.pallas import tpu as pltpu
from jax.sharding import PartitionSpec as P

eps_norm = 1e-06
MESH = pl.DeviceIdType.MESH
front_order = (
    ("o0", "s0", "o1", "L1", "W01", "s1", "q", "S0", "o2", "o3", "D",),
    (
        ("L2", "W02", "s2", "W11", "S1", "F00", "s3",),
        ("W03", "W21", "F10", "F01", "S2", "L3", "W12", "W31",),
        ("W22", "F11", "F30", "S3", "F02", "F03", "F12", "W13",),
    ),
    ("W23", "J0", "F20", "F21", "F13", "W32", "F31", "F22", "J1", "F23", "W33", "J2", "F32", "F33", "J3",),
)


def front_kernel(
    q_ref,
    kv_ref,
    cache_ref,
    w_ref,
    resid_ref,
    gain_ref,
    stream_ref,
    normed_ref,
    q_buf,
    kn,
    kc,
    wb,
    acc,
    top,
    total,
    att,
    part_out,
    part_in,
    local_sem,
    q_sem,
    kn_line,
    kn_up,
    kn_side,
    kn_side_s,
    kn_twin,
    kn_twin_s,
    kc_line,
    kc_up,
    kc_down,
    kc_side,
    kc_side_s,
    kc_twin,
    kc_twin_s,
    w_line,
    w_up,
    w_down,
    w_side,
    w_side_s,
    w_far,
    w_far_s,
    w_twin,
    w_twin_s,
    part_sem,
    part_sem_s,
):
    planes = kn.shape[1]
    group = q_buf.shape[1]
    rows, width = q_buf.shape[2:]
    model = w_ref.shape[2]
    pieces = w_side.shape[0]
    half, chunk = model // 2, model // (2 * pieces)
    g = lax.axis_index("grp")
    me = lax.axis_index("head")
    z, y, c = me // 4, (me // 2) % 2, me % 2
    up, down = (g, me + 4), (g, me - 4)
    side, twin, far = (g, me + 2 - 4 * y), (g, me + 1 - 2 * c), (1 - g, me)
    has_up, has_down = z < planes - 1, z > 0

    barrier = pltpu.get_barrier_semaphore()
    for peer in (side, twin, far):
        pl.semaphore_signal(barrier, inc=1, device_id=peer, device_id_type=MESH)

    @pl.when(has_up)
    def _():
        pl.semaphore_signal(barrier, inc=1, device_id=up, device_id_type=MESH)

    @pl.when(has_down)
    def _():
        pl.semaphore_signal(barrier, inc=1, device_id=down, device_id_type=MESH)

    pl.semaphore_wait(barrier, 3 + has_up.astype(jnp.int32) + has_down.astype(jnp.int32))

    def copy(src, dst, sent, got, peer):
        return pltpu.make_async_remote_copy(
            src_ref=src,
            dst_ref=dst,
            send_sem=sent,
            recv_sem=got,
            device_id=peer,
            device_id_type=MESH,
        )

    def arrived(dst, got):
        copy(dst, dst, got, got, twin).wait_recv()

    def left(src, sent):
        copy(src, src, sent, sent, twin).wait_send()

    def mine(plane):
        return plane // (planes // 2) == y

    cols_near = pl.ds(pl.multiple_of(g * half, half), half)
    own_heads = pl.ds(y * group, group)
    other_heads = pl.ds((1 - y) * group, group)

    def w_cols(quarter, near):
        first = jnp.where(near, g, 1 - g) * half + quarter * chunk
        return pl.ds(pl.multiple_of(first, chunk), chunk)

    def w_block(quarter, plane, line, core, near=True):
        return wb.at[:, plane, line, core, :, w_cols(quarter, near)]

    def w_spread(src, quarter, plane, line):
        dst = w_block(quarter, plane, line, c)
        at = (quarter, plane, line)
        copy(src, dst, w_far_s.at[at], w_far.at[at], far).start()
        copy(src, dst, w_twin_s.at[(*at, 0)], w_twin.at[(*at, 0)], twin).start()

    def w_send_up(src, quarter, plane, line):
        at = (quarter, plane, line)

        @pl.when(has_up)
        def _():
            copy(src, w_block(quarter, plane, line, c), w_up.at[at], w_line.at[at], up).start()

    def w_send_down(src, quarter, plane, line):
        at = (quarter, plane, line)

        @pl.when(has_down)
        def _():
            copy(src, w_block(quarter, plane, line, c), w_down.at[at], w_line.at[at], down).start()

    def w_own_side(quarter):
        src = w_ref.at[other_heads, :, w_cols(quarter, True)]
        dst = w_block(quarter, z, y, c)
        copy(src, dst, w_side_s.at[quarter], w_side.at[quarter], side).start()

    def w_own(quarter):
        src = w_ref.at[own_heads, :, w_cols(quarter, True)]
        w_send_up(src, quarter, z, y)
        w_send_down(src, quarter, z, y)
        w_spread(src, quarter, z, y)

    def w_side_relay(quarter):
        block = w_block(quarter, z, 1 - y, c)
        arrived(block, w_side.at[quarter])
        w_send_up(block, quarter, z, 1 - y)
        w_send_down(block, quarter, z, 1 - y)
        w_spread(block, quarter, z, 1 - y)

    def w_relay(quarter, step):
        low, high = z - step, z + step
        for turn in range(2):
            line = y + turn - 2 * y * turn

            @pl.when(low >= 0)
            def _():
                block = w_block(quarter, low, line, c)
                arrived(block, w_line.at[quarter, low, line])
                w_send_up(block, quarter, low, line)
                w_spread(block, quarter, low, line)

            @pl.when(high < planes)
            def _():
                block = w_block(quarter, high, line, c)
                arrived(block, w_line.at[quarter, high, line])
                w_send_down(block, quarter, high, line)
                w_spread(block, quarter, high, line)

    def w_far_relay(quarter, plane):
        for line in range(2):
            block = w_block(quarter, plane, line, c, False)
            arrived(block, w_far.at[quarter, plane, line])
            at = (quarter, plane, line, 1)
            copy(block, block, w_twin_s.at[at], w_twin.at[at], twin).start()

    def w_far_relays(quarter, step):
        low, high = z - step, z + step

        @pl.when(low >= 0)
        def _():
            w_far_relay(quarter, low)

        if step > 0:

            @pl.when(high < planes)
            def _():
                w_far_relay(quarter, high)

    @pl.when(has_up)
    def _():
        copy(cache_ref, kc.at[z, y, c], kc_up.at[z], kc_line.at[z], up).start()
        copy(kv_ref, kn.at[:, z, y, c], kn_up.at[z], kn_line.at[z], up).start()

    @pl.when(has_down)
    def _():
        copy(cache_ref, kc.at[z, y, c], kc_down.at[z], kc_line.at[z], down).start()

    copy(kv_ref.at[1 - y], kn.at[1 - y, z, y, c], kn_side_s.at[z], kn_side.at[z], side).start()
    w_own_side(0)
    copy(q_ref.at[other_heads], q_buf.at[y], q_sem.at[0], q_sem.at[1], side).start()
    w_own_side(1)
    copy(kv_ref.at[y], kn.at[y, z, y, c], kn_twin_s.at[z, y], kn_twin.at[z, y], twin).start()

    @pl.when(mine(z))
    def _():
        copy(cache_ref, kc.at[z, y, c], kc_twin_s.at[z, y], kc_twin.at[z, y], twin).start()

    @pl.when(jnp.logical_not(mine(z)))
    def _():
        copy(cache_ref, kc.at[z, y, c], kc_side_s.at[z], kc_side.at[z], side).start()

    for piece in range(2, pieces):
        w_own_side(piece)
    locals_ = (
        pltpu.make_async_copy(q_ref.at[own_heads], q_buf.at[y], local_sem.at[0]),
        pltpu.make_async_copy(kv_ref.at[y], kn.at[y, z, y, c], local_sem.at[1]),
        pltpu.make_async_copy(cache_ref, kc.at[z, y, c], local_sem.at[2]),
        pltpu.make_async_copy(
            w_ref.at[own_heads, :, cols_near], wb.at[:, z, y, c, :, cols_near], local_sem.at[3]
        ),
    )
    for item in locals_:
        item.start()

    def from_side_new(plane):
        block = kn.at[y, plane, 1 - y, c]
        arrived(block, kn_side.at[plane])
        copy(block, block, kn_twin_s.at[plane, 1 - y], kn_twin.at[plane, 1 - y], twin).start()

    def from_side_old(plane):
        @pl.when(mine(plane))
        def _():
            block = kc.at[plane, 1 - y, c]
            arrived(block, kc_side.at[plane])
            copy(block, block, kc_twin_s.at[plane, 1 - y], kc_twin.at[plane, 1 - y], twin).start()

    def spread_old(plane):
        block = kc.at[plane, y, c]

        @pl.when(mine(plane))
        def _():
            copy(block, block, kc_twin_s.at[plane, y], kc_twin.at[plane, y], twin).start()

        @pl.when(jnp.logical_not(mine(plane)))
        def _():
            copy(block, block, kc_side_s.at[plane], kc_side.at[plane], side).start()

    def relay(step):
        low, high = z - step, z + step

        @pl.when(high < planes)
        def _():
            old = kc.at[high, y, c]
            arrived(old, kc_line.at[high])

            @pl.when(has_down)
            def _():
                copy(old, old, kc_down.at[high], kc_line.at[high], down).start()

            spread_old(high)

        @pl.when(low >= 0)
        def _():
            old, new = kc.at[low, y, c], kn.at[:, low, y, c]
            arrived(old, kc_line.at[low])

            @pl.when(has_up)
            def _():
                copy(old, old, kc_up.at[low], kc_line.at[low], up).start()

            arrived(new, kn_line.at[low])

            @pl.when(has_up)
            def _():
                copy(new, new, kn_up.at[low], kn_line.at[low], up).start()

            there, here = kn.at[1 - y, low, y, c], kn.at[y, low, y, c]
            copy(there, there, kn_side_s.at[low], kn_side.at[low], side).start()
            copy(here, here, kn_twin_s.at[low, y], kn_twin.at[low, y], twin).start()
            spread_old(low)

    def from_side(step):
        low, high = z - step, z + step

        @pl.when(low >= 0)
        def _():
            from_side_new(low)
            from_side_old(low)

        if step > 0:

            @pl.when(high < planes)
            def _():
                from_side_old(high)

    scale = width ** (-0.5)
    tile = 2
    tile_rows = tile * rows

    def fold(keys, values, diagonal):
        def lines(line, carry):
            for part in range(group // tile):
                heads = pl.ds(part * tile, tile)
                queries = q_buf[line, heads].reshape(tile_rows, width)
                queries = queries * jnp.asarray(scale, queries.dtype)
                scores = lax.dot_general(
                    queries, keys(), (((1,), (1,)), ((), ())), preferred_element_type=jnp.float32
                )
                pieces = [
                    scores[:, first : first + 128] for first in range(0, scores.shape[1], 128)
                ]
                if diagonal:
                    row_at = lax.broadcasted_iota(jnp.int32, (tile_rows, 128), 0) % rows
                    ahead = row_at - lax.broadcasted_iota(jnp.int32, (tile_rows, 128), 1)
                    ahead = ahead + (line * 2 + c) * rows
                    pieces = [
                        jnp.where(ahead >= index * 128, piece, -jnp.inf)
                        for index, piece in enumerate(pieces)
                    ]
                best = functools.reduce(jnp.maximum, pieces)
                best = jnp.max(best, 1, keepdims=True)
                if diagonal:
                    new_top = jnp.broadcast_to(best, (tile_rows, 128))
                else:
                    old_top = top[line, heads].reshape(tile_rows, 128)
                    new_top = jnp.maximum(old_top, best)
                exps = [jnp.exp(piece - new_top) for piece in pieces]
                new_total = functools.reduce(jnp.add, exps)
                weighted = jnp.dot(
                    jnp.concatenate([part_.astype(jnp.bfloat16) for part_ in exps], 1),
                    values(),
                    preferred_element_type=jnp.float32,
                )
                if not diagonal:
                    shrink = jnp.exp(old_top - new_top)
                    new_total = new_total + total[line, heads].reshape(tile_rows, 128) * shrink
                    weighted = weighted + acc[line, heads].reshape(
                        tile_rows, width
                    ) * jnp.concatenate([shrink] * (width // 128), 1)
                top[line, heads] = new_top.reshape(tile, rows, 128)
                total[line, heads] = new_total.reshape(tile, rows, 128)
                acc[line, heads] = weighted.reshape(tile, rows, width)
            return carry

        lax.fori_loop(0, 2, lines, 0, unroll=2)

    def new_part(plane, first):
        return lambda: kn[y, plane, :, :, :, first : first + width].reshape(4 * rows, width)

    page = kc.shape[3]

    def old_part(plane, line, first):
        return lambda: kc[plane, line, :, :, first : first + width].reshape(2 * page, width)

    def twins_new(plane):
        for line in range(2):
            arrived(kn.at[y, plane, line, 1 - c], kn_twin.at[plane, line])

    def twins_old(plane):
        for line in range(2):
            arrived(kc.at[plane, line, 1 - c], kc_twin.at[plane, line])

    def first_fold():
        twins_new(z)
        fold(new_part(z, 0), new_part(z, width), True)

    def queries_here():
        arrived(q_buf.at[1 - y], q_sem.at[1])
        for item in locals_:
            item.wait()

    def later_folds(step):
        low, high = z - step, z + step

        @pl.when((step >= 1) & (low >= 0))
        def _():
            twins_new(low)
            fold(new_part(low, 0), new_part(low, width), False)

        def old_body(index, carry):
            plane = jnp.where(index == 0, low, high)
            valid = (plane >= 0) & (plane < planes) & ((index == 0) | (step > 0))

            @pl.when(valid & mine(plane))
            def _():
                twins_old(plane)

                def line_body(line, carry):
                    fold(old_part(plane, line, 0), old_part(plane, line, width), False)
                    return carry

                lax.fori_loop(0, 2, line_body, 0)

            return carry

        lax.fori_loop(0, 2, old_body, 0)

    def finish():
        for line in range(2):
            for head in range(group):
                att[line, :, head * width : (head + 1) * width] = (
                    acc[line, head] / jnp.sum(total[line, head], 1, keepdims=True)
                ).astype(att.dtype)

    def project(quarter):
        for near in range(2):
            for plane in range(planes):
                for line in range(2):
                    arrived(
                        w_block(quarter, plane, line, 1 - c, near == 0),
                        w_twin.at[quarter, plane, line, near],
                    )
            cols = w_cols(quarter, near == 0)
            weights = wb[:, :, :, :, :, cols].reshape(group * width, chunk)
            both = jnp.dot(
                att[...].reshape(2 * rows, group * width),
                weights,
                preferred_element_type=jnp.float32,
            )
            there = jnp.where(y == 0, both[rows:], both[:rows])
            here = jnp.where(y == 0, both[:rows], both[rows:])
            part_out[:, cols] = there.astype(part_out.dtype)
            index = quarter * 2 + near
            block = part_out.at[:, cols]
            copy(block, part_in.at[:, cols], part_sem_s.at[index], part_sem.at[index], side).start()
            stream_ref[:, cols] = here + resid_ref[:, cols].astype(jnp.float32)

    acts = {
        "o": w_own,
        "s": w_side_relay,
        "L": relay,
        "S": from_side,
        "q": queries_here,
        "D": first_fold,
        "W": w_relay,
        "F": w_far_relays,
        "J": project,
    }

    def perform(segment):
        for word in segment:
            acts[word[0]](*(int(digit) for digit in word[1:]))

    before, between, after = front_order
    perform(before)

    def step_body(step, carry):
        for number, segment in enumerate(between):

            @pl.when(step == number + 1)
            def _():
                perform(segment)

        later_folds(step)
        return carry

    lax.fori_loop(0, planes, step_body, 0)
    finish()
    perform(after)
    square = jnp.zeros((rows, 1), jnp.float32)
    for quarter in range(pieces):
        for near in range(2):
            cols = w_cols(quarter, near == 0)
            index = quarter * 2 + near
            arrived(part_in.at[:, cols], part_sem.at[index])
            stream = stream_ref[:, cols] + part_in[:, cols].astype(jnp.float32)
            stream_ref[:, cols] = stream
            square = square + jnp.sum(stream * stream, 1, keepdims=True)
            left(part_out.at[:, cols], part_sem_s.at[index])
    inverse = lax.rsqrt(square / model + eps_norm)
    for index in range(2 * pieces):
        cols = slice(index * chunk, (index + 1) * chunk)
        normed_ref[:, cols] = (stream_ref[:, cols] * inverse * gain_ref[:, cols]).astype(
            normed_ref.dtype
        )

    left(q_buf.at[y], q_sem.at[0])
    for quarter in range(pieces):
        left(w_block(quarter, z, y, c), w_side_s.at[quarter])

    def drain(plane, carry):
        reached = plane <= z

        @pl.when(reached)
        def _():
            left(kn.at[1 - y, plane, y, c], kn_side_s.at[plane])
            left(kn.at[y, plane, y, c], kn_twin_s.at[plane, y])
            left(kn.at[y, plane, 1 - y, c], kn_twin_s.at[plane, 1 - y])

        @pl.when(reached & has_up)
        def _():
            left(kn.at[:, plane, y, c], kn_up.at[plane])
            left(kc.at[plane, y, c], kc_up.at[plane])
            for quarter in range(pieces):
                for line in range(2):
                    left(w_block(quarter, plane, line, c), w_up.at[quarter, plane, line])

        @pl.when((plane >= z) & has_down)
        def _():
            left(kc.at[plane, y, c], kc_down.at[plane])
            for quarter in range(pieces):
                for line in range(2):
                    left(w_block(quarter, plane, line, c), w_down.at[quarter, plane, line])

        @pl.when(mine(plane))
        def _():
            for line in range(2):
                left(kc.at[plane, line, c], kc_twin_s.at[plane, line])

        @pl.when(jnp.logical_not(mine(plane)))
        def _():
            left(kc.at[plane, y, c], kc_side_s.at[plane])

        for quarter in range(pieces):
            for line in range(2):
                at = (quarter, plane, line)
                left(w_block(quarter, plane, line, c), w_far_s.at[at])
                left(w_block(quarter, plane, line, c), w_twin_s.at[(*at, 0)])
                left(w_block(quarter, plane, line, c, False), w_twin_s.at[(*at, 1)])
        return carry

    lax.fori_loop(0, planes, drain, 0)


def front(queries, pairs, cached, w_out, resid, gain, axis_count):
    heads, rows, width = queries.shape
    group = heads // 2
    planes = axis_count // 4
    model = w_out.shape[2]
    slice_rows = w_out.shape[1]
    page = cached.shape[0]
    pieces = 4
    dma = pltpu.SemaphoreType.DMA
    anywhere = pl.BlockSpec(memory_space=pl.ANY)
    inside = pl.BlockSpec(memory_space=pltpu.VMEM)
    return pl.pallas_call(
        front_kernel,
        out_shape=(
            jax.ShapeDtypeStruct((rows, model), jnp.float32),
            jax.ShapeDtypeStruct((rows, model), jnp.bfloat16),
        ),
        in_specs=[anywhere] * 4 + [inside] * 2,
        out_specs=(inside, inside),
        scratch_shapes=[
            pltpu.VMEM((2, group, rows, width), jnp.bfloat16),
            pltpu.VMEM((2, planes, 2, 2, rows, 2 * width), jnp.bfloat16),
            pltpu.VMEM((planes, 2, 2, page, 2 * width), jnp.bfloat16),
            pltpu.VMEM((group, planes, 2, 2, slice_rows, model), jnp.bfloat16),
            pltpu.VMEM((2, group, rows, width), jnp.float32),
            pltpu.VMEM((2, group, rows, 128), jnp.float32),
            pltpu.VMEM((2, group, rows, 128), jnp.float32),
            pltpu.VMEM((2, rows, group * width), jnp.bfloat16),
            pltpu.VMEM((rows, model), jnp.bfloat16),
            pltpu.VMEM((rows, model), jnp.bfloat16),
            dma((4,)),
            dma((2,)),
            dma((planes,)),
            dma((planes,)),
            dma((planes,)),
            dma((planes,)),
            dma((planes, 2)),
            dma((planes, 2)),
            dma((planes,)),
            dma((planes,)),
            dma((planes,)),
            dma((planes,)),
            dma((planes,)),
            dma((planes, 2)),
            dma((planes, 2)),
            dma((pieces, planes, 2)),
            dma((pieces, planes, 2)),
            dma((pieces, planes, 2)),
            dma((pieces,)),
            dma((pieces,)),
            dma((pieces, planes, 2)),
            dma((pieces, planes, 2)),
            dma((pieces, planes, 2, 2)),
            dma((pieces, planes, 2, 2)),
            dma((2 * pieces,)),
            dma((2 * pieces,)),
        ],
        compiler_params=pltpu.CompilerParams(
            collective_id=0, has_side_effects=True, vmem_limit_bytes=60 * 2**20
        ),
        cost_estimate=pl.CostEstimate(
            flops=4 * 2 * group * rows * width * 4 * axis_count * rows
            + 4 * rows * group * width * model,
            bytes_accessed=8 * 2**20,
            transcendentals=2 * group * rows * axis_count * rows,
        ),
    )(queries, pairs, cached, w_out, resid, gain)


def partner_2(value, stride):
    mask = 2**stride
    pairs = [(source, source ^ mask) for source in range(lax.axis_size("head"))]
    return lax.ppermute(value, "head", pairs)


def turn_grp(value, shift):
    count = lax.axis_size("grp")
    return lax.ppermute(value, "grp", [(i, (i + shift) % count) for i in range(count)])


def attend_kernel(
    me_ref, query_ref, cache_ref, other_ref, pairs_ref, out_ref, new_ref, *, block, old_block, order
):
    head_width = query_ref.shape[1]
    step = pl.program_id(0)
    members, slots, local_rows = pairs_ref.shape[:3]

    @pl.when(step == 0)
    def _():
        for slot in range(slots):
            for member in range(members):
                apart = member ^ me_ref[0]
                place = 0
                for rank, bit in enumerate(order):
                    place = place + ((apart >> bit) & 1) * 2**rank
                first = (slot * members + member) * local_rows
                new_ref[first : first + local_rows, :] = pairs_ref[place, slot]

    query_rows = query_ref[...] * jnp.asarray(head_width ** (-0.5), query_ref.dtype)

    def fold(carry, keys, values, mask):
        top, total, weighted = carry
        scores = lax.dot_general(
            query_rows, keys, (((1,), (1,)), ((), ())), preferred_element_type=jnp.float32
        )
        if mask is not None:
            scores = jnp.where(mask, scores, -jnp.inf)
        new_top = jnp.maximum(top, jnp.max(scores, 1, keepdims=True))
        exps = jnp.exp(scores - new_top)
        shrink = jnp.exp(top - new_top)
        total = total * shrink + jnp.sum(exps, 1, keepdims=True)
        weighted = weighted * shrink + jnp.dot(
            exps.astype(jnp.bfloat16), values, preferred_element_type=jnp.float32
        )
        return new_top, total, weighted

    rows = query_rows.shape[0]
    carry = (
        jnp.full((rows, 1), -jnp.inf, jnp.float32),
        jnp.zeros((rows, 1), jnp.float32),
        jnp.zeros((rows, head_width), jnp.float32),
    )
    row_at = lax.broadcasted_iota(jnp.int32, (rows, block), 0)
    col_at = lax.broadcasted_iota(jnp.int32, (rows, block), 1)
    here = pl.ds(step * block, block)
    carry = fold(
        carry, new_ref[here, :head_width], new_ref[here, head_width:], col_at <= row_at
    )
    for old_ref in (cache_ref, other_ref):
        for first in range(0, old_ref.shape[0], old_block):
            part = pl.ds(first, old_block)
            carry = fold(carry, old_ref[part, :head_width], old_ref[part, head_width:], None)

    def earlier(index, carry):
        part = pl.ds(index * block, block)
        return fold(carry, new_ref[part, :head_width], new_ref[part, head_width:], None)

    top, total, weighted = lax.fori_loop(0, step, earlier, carry)
    out_ref[...] = (weighted / total).astype(out_ref.dtype)


def attend(me, queries, new_pairs, cached, cached_other, order):
    length, head_width = queries.shape
    block = min(512, length)
    old_block = min(1024, cached.shape[0])
    return pl.pallas_call(
        functools.partial(attend_kernel, block=block, old_block=old_block, order=order),
        grid_spec=pltpu.PrefetchScalarGridSpec(
            num_scalar_prefetch=1,
            grid=(length // block,),
            in_specs=[
                pl.BlockSpec((block, head_width), lambda i, me: (i, 0)),
                pl.BlockSpec(cached.shape, lambda i, me: (0, 0)),
                pl.BlockSpec(cached_other.shape, lambda i, me: (0, 0)),
                pl.BlockSpec(new_pairs.shape, lambda i, me: (0, 0, 0, 0)),
            ],
            out_specs=pl.BlockSpec((block, head_width), lambda i, me: (i, 0)),
            scratch_shapes=[pltpu.VMEM((length, 2 * head_width), jnp.bfloat16)],
        ),
        out_shape=jax.ShapeDtypeStruct((length, head_width), jnp.bfloat16),
        cost_estimate=pl.CostEstimate(
            flops=4 * length * head_width * (length // 2 + 2 * cached.shape[0]),
            bytes_accessed=8 * length * head_width * 2,
            transcendentals=length * (length // 2 + 2 * cached.shape[0]),
        ),
    )(me, queries, cached, cached_other, new_pairs)


def front_general(queries, new_kv, cache, resid, w_out, norm_gain):
    axis_count = lax.axis_size("head")
    local_rows = queries.shape[0]
    seq_count = queries.shape[1]
    head_count = queries.shape[2]
    head_width = queries.shape[3]
    pair_heads = new_kv.shape[2]
    group_size = head_count // pair_heads
    model_width = resid.shape[2]
    row_count = local_rows * seq_count
    slots = seq_count * pair_heads
    across = [[c * group_size + j for c in range(slots)] for j in range(group_size)]
    query_slots = queries.reshape(local_rows, axis_count, head_width).transpose(1, 0, 2)
    pair_slots = new_kv.reshape(local_rows, slots, 2 * head_width).transpose(1, 0, 2)
    pair_slots = lax.all_to_all(
        pair_slots, "head", split_axis=0, concat_axis=0, axis_index_groups=across, tiled=True
    )
    grp_count = lax.axis_size("grp")
    grp_me = lax.axis_index("grp")
    part_width = model_width // grp_count
    w_part = lax.dynamic_slice_in_dim(w_out, grp_me * part_width, part_width, 2)
    bits = group_size.bit_length() - 1
    order = tuple(range(1, bits)) + (0,)
    cache_rows = cache[0]
    pairs = pair_slots[None]
    for bit in order[:-1]:
        cache_rows = jnp.concatenate([cache_rows, partner_2(cache_rows, bit)], 0)
    head_queries = lax.all_to_all(query_slots, "head", split_axis=0, concat_axis=0, tiled=True)
    for bit in order[:-1]:
        pairs = jnp.concatenate([pairs, partner_2(pairs, bit)], 0)
    w_part, pairs, cache_rows, head_queries = lax.optimization_barrier(
        (w_part, pairs, cache_rows, head_queries)
    )
    w_part = lax.all_gather(w_part, "head", axis=1, tiled=True)
    w_part = w_part.reshape(head_count * head_width, part_width)
    cache_other = partner_2(cache_rows, 0)
    pairs = jnp.concatenate([pairs, partner_2(pairs, 0)], 0)
    me = (lax.axis_index("head") % group_size).astype(jnp.int32).reshape(1)
    attended = attend(
        me, head_queries.reshape(-1, head_width), pairs, cache_rows, cache_other, order
    )
    returned = lax.all_to_all(
        attended.reshape(axis_count, local_rows, head_width),
        "head",
        split_axis=0,
        concat_axis=0,
        tiled=True,
    )
    attn_rows = returned.reshape(seq_count, head_count, local_rows, head_width)
    attn_rows = attn_rows.transpose(2, 0, 1, 3).reshape(row_count, head_count * head_width)
    parts = []
    for shift in range(1, grp_count):
        far_rows = turn_grp(attn_rows, shift)
        far_part = jnp.dot(far_rows, w_part, preferred_element_type=jnp.float32)
        parts.append(turn_grp(far_part.astype(jnp.bfloat16), -shift).astype(jnp.float32))
    projected = []
    near_part = jnp.dot(attn_rows, w_part, preferred_element_type=jnp.float32)
    for column in range(grp_count):
        piece = near_part
        for shift in range(1, grp_count):
            piece = jnp.where((grp_me + shift) % grp_count == column, parts[shift - 1], piece)
        projected.append(piece)
    projected = jnp.concatenate(projected, 1)
    stream = resid.reshape(row_count, model_width).astype(jnp.float32) + projected
    normed = stream * lax.rsqrt(jnp.mean(stream * stream, 1, keepdims=True) + eps_norm) * norm_gain
    normed = normed.astype(jnp.bfloat16)
    return stream, normed


def expert_kernel(
    normed_ref,
    stream_ref,
    info_ref,
    w_in_ref,
    w_down_ref,
    out_ref,
    w_in,
    w_down,
    rows_buf,
    info_buf,
    picked,
    inbox,
    outbox,
    answer,
    dense,
    summed,
    sums_in,
    sums_out,
    w_sem,
    row_line,
    row_up,
    row_down,
    info_line,
    info_up,
    info_down,
    in_sem,
    in_sem_s,
    ans_sem,
    ans_sem_s,
    sum_sem,
    sum_sem_s,
    *,
    top_count,
):
    planes, rows, model = rows_buf.shape
    near, cap = inbox.shape[1:3]
    hidden_width = w_down.shape[0]
    chunks = row_line.shape[1]
    chunk = model // chunks
    g = lax.axis_index("grp")
    me = lax.axis_index("head")
    z, own = me // near, me % near
    up, down = (g, me + near), (g, me - near)
    has_up, has_down = z < planes - 1, z > 0

    barrier = pltpu.get_barrier_semaphore()
    for mask in range(1, near):
        pl.semaphore_signal(barrier, inc=1, device_id=(g, me ^ mask), device_id_type=MESH)

    @pl.when(has_up)
    def _():
        pl.semaphore_signal(barrier, inc=1, device_id=up, device_id_type=MESH)

    @pl.when(has_down)
    def _():
        pl.semaphore_signal(barrier, inc=1, device_id=down, device_id_type=MESH)

    loads = (
        pltpu.make_async_copy(w_in_ref, w_in, w_sem.at[0]),
        pltpu.make_async_copy(w_down_ref, w_down, w_sem.at[1]),
    )
    for load in loads:
        load.start()
    pl.semaphore_wait(
        barrier, near - 1 + has_up.astype(jnp.int32) + has_down.astype(jnp.int32)
    )

    def copy(src, dst, sent, got, peer):
        return pltpu.make_async_remote_copy(
            src_ref=src,
            dst_ref=dst,
            send_sem=sent,
            recv_sem=got,
            device_id=peer,
            device_id_type=MESH,
        )

    def arrived(dst, got):
        copy(dst, dst, got, got, (g, me ^ 1)).wait_recv()

    def left(src, sent):
        copy(src, src, sent, sent, (g, me ^ 1)).wait_send()

    def cols(index):
        return slice(index * chunk, (index + 1) * chunk)

    def send_up(info, block, plane):
        @pl.when(has_up)
        def _():
            if info is not None:
                copy(info, info_buf.at[plane], info_up.at[plane], info_line.at[plane], up).start()
            else:
                src, index = block
                dst = rows_buf.at[plane, :, cols(index)]
                at = (plane, index)
                copy(src, dst, row_up.at[at], row_line.at[at], up).start()

    def send_down(info, block, plane):
        @pl.when(has_down)
        def _():
            if info is not None:
                copy(
                    info, info_buf.at[plane], info_down.at[plane], info_line.at[plane], down
                ).start()
            else:
                src, index = block
                dst = rows_buf.at[plane, :, cols(index)]
                at = (plane, index)
                copy(src, dst, row_down.at[at], row_line.at[at], down).start()

    def slots_of(info):
        at = lax.broadcasted_iota(jnp.int32, (near * cap, rows), 0) + z * (near * cap)
        at = at.astype(jnp.float32)
        return [at == info[rank : rank + 1, :] for rank in range(top_count)]

    def pick(plane, info, load):
        chosen = functools.reduce(jnp.logical_or, slots_of(info))
        chosen = jnp.where(chosen, 1.0, 0.0).astype(jnp.bfloat16)
        for index in range(chunks):
            part = jnp.dot(chosen, load(index), preferred_element_type=jnp.float32)
            picked[plane, :, :, cols(index)] = part.astype(jnp.bfloat16).reshape(near, cap, chunk)
            for mask in range(1, near):
                other = own ^ mask
                copy(
                    picked.at[plane, other, :, cols(index)],
                    inbox.at[plane, own, :, cols(index)],
                    in_sem_s.at[plane, other],
                    in_sem.at[plane, own],
                    (g, me ^ mask),
                ).start()
            inbox[plane, own, :, cols(index)] = picked[plane, own, :, cols(index)]

    def each(step, act):
        for turn in range(2):
            plane = z + step if turn == 0 else z - step
            valid = (plane < planes) & (step > 0) if turn == 0 else plane >= 0

            @pl.when(valid)
            def _():
                act(plane, turn)

    def each_loop(step, act):
        def body(turn, carry):
            plane = z + step * (1 - 2 * turn)
            valid = (plane < planes) & (plane >= 0) & ((turn == 1) | (step > 0))

            @pl.when(valid)
            def _():
                act(plane)

            return carry

        lax.fori_loop(0, 2, body, 0)

    def receive(plane, turn):
        onward = send_down if turn == 0 else send_up
        arrived(info_buf.at[plane], info_line.at[plane])
        onward(info_buf.at[plane], None, plane)

        def load(index):
            block = rows_buf.at[plane, :, cols(index)]
            arrived(block, row_line.at[plane, index])
            onward(None, (block, index), plane)
            return block[...]

        pick(plane, info_buf[plane], load)

    def run_expert(plane):
        for mask in range(1, near):
            arrived(inbox.at[plane, own ^ mask], in_sem.at[plane, own ^ mask])
        inner = jnp.dot(
            inbox[plane].reshape(near * cap, model), w_in[...], preferred_element_type=jnp.float32
        )
        gate, value = inner[:, :hidden_width], inner[:, hidden_width:]
        hidden = (gate / (1.0 + jnp.exp(-gate)) * value).astype(jnp.bfloat16)
        for index in range(chunks):
            part = jnp.dot(hidden, w_down[:, cols(index)], preferred_element_type=jnp.float32)
            outbox[plane, :, :, cols(index)] = part.astype(jnp.bfloat16).reshape(near, cap, chunk)
            for mask in range(1, near):
                other = own ^ mask
                copy(
                    outbox.at[plane, other, :, cols(index)],
                    answer.at[plane, own, :, cols(index)],
                    ans_sem_s.at[plane, other],
                    ans_sem.at[plane, own],
                    (g, me ^ mask),
                ).start()
            answer[plane, own, :, cols(index)] = outbox[plane, own, :, cols(index)]

    def combine(plane, info, store):
        for mask in range(1, near):
            arrived(answer.at[plane, own ^ mask], ans_sem.at[plane, own ^ mask])
        gates = jnp.zeros((near * cap, rows), jnp.float32)
        for rank, here in enumerate(slots_of(info)):
            gates = jnp.where(here, info[top_count + rank : top_count + rank + 1, :], gates)
        high = gates.astype(jnp.bfloat16)
        low = (gates - high.astype(jnp.float32)).astype(jnp.bfloat16)
        for index in range(chunks):
            values = answer[plane, :, :, cols(index)].reshape(near * cap, chunk)
            total = jnp.zeros((rows, chunk), jnp.float32)
            for term in (high, low):
                total = total + lax.dot_general(
                    term, values, (((0,), (0,)), ((), ())), preferred_element_type=jnp.float32
                )
            store(index, total)

    def combine_far(plane):
        def store(index, total):
            dense[plane, :, cols(index)] = total

        combine(plane, info_buf[plane], store)

    def pass_sums(length):
        def body(turn, carry):
            way = (turn + (z >= planes // 2).astype(jnp.int32)) % 2
            target = jnp.where(way == 0, length, planes - 1 - length)
            takes_part = jnp.where(way == 0, target - z, z - target) > 0
            has_in = jnp.where(way == 0, z, planes - 1 - z) > 0
            peer = (g, me + near - 2 * near * way)

            @pl.when(takes_part)
            def _():
                for index in range(chunks):
                    block = sums_in.at[way, target, :, cols(index)]
                    at = (way, target, index)

                    @pl.when(has_in)
                    def _():
                        arrived(block, sum_sem.at[at])
                        sums_out[target, :, cols(index)] = (
                            dense[target, :, cols(index)] + block[...].astype(jnp.float32)
                        ).astype(jnp.bfloat16)

                    @pl.when(jnp.logical_not(has_in))
                    def _():
                        sums_out[target, :, cols(index)] = dense[target, :, cols(index)].astype(
                            jnp.bfloat16
                        )

                    copy(
                        sums_out.at[target, :, cols(index)],
                        block,
                        sum_sem_s.at[at],
                        sum_sem.at[at],
                        peer,
                    ).start()

            return carry

        lax.fori_loop(0, 2, body, 0)

    send_up(info_ref, None, z)
    send_down(info_ref, None, z)
    for index in range(chunks):
        block = (normed_ref.at[:, cols(index)], index)
        send_up(None, block, z)
        send_down(None, block, z)
    pick(z, info_ref[...], lambda index: normed_ref[:, cols(index)])
    each(1, receive)
    for load in loads:
        load.wait()

    def step_body(step, carry):
        each_loop(step, run_expert)

        @pl.when((step >= 1) & (step + 1 < planes))
        def _():
            each(step + 1, receive)

        @pl.when(step == 0)
        def _():
            def store(index, total):
                summed[:, cols(index)] = stream_ref[:, cols(index)] + total

            combine(z, info_ref[...], store)

        @pl.when(step >= 1)
        def _():
            each_loop(step, combine_far)
            pass_sums(step)

        return carry

    lax.fori_loop(0, planes, step_body, 0)

    for index in range(chunks):

        @pl.when(has_down)
        def _():
            block = sums_in.at[0, z, :, cols(index)]
            arrived(block, sum_sem.at[0, z, index])
            summed[:, cols(index)] = summed[:, cols(index)] + block[...].astype(jnp.float32)

        @pl.when(has_up)
        def _():
            block = sums_in.at[1, z, :, cols(index)]
            arrived(block, sum_sem.at[1, z, index])
            summed[:, cols(index)] = summed[:, cols(index)] + block[...].astype(jnp.float32)

        out_ref[:, cols(index)] = summed[:, cols(index)].astype(out_ref.dtype)

    def drain(plane, carry):
        @pl.when((plane <= z) & has_up)
        def _():
            left(info_buf.at[plane], info_up.at[plane])
            for index in range(chunks):
                left(rows_buf.at[plane, :, cols(index)], row_up.at[plane, index])

        @pl.when((plane >= z) & has_down)
        def _():
            left(info_buf.at[plane], info_down.at[plane])
            for index in range(chunks):
                left(rows_buf.at[plane, :, cols(index)], row_down.at[plane, index])

        for mask in range(1, near):
            left(picked.at[plane, own ^ mask], in_sem_s.at[plane, own ^ mask])
            left(outbox.at[plane, own ^ mask], ans_sem_s.at[plane, own ^ mask])

        for index in range(chunks):

            @pl.when(plane > z)
            def _():
                left(sums_out.at[plane, :, cols(index)], sum_sem_s.at[0, plane, index])

            @pl.when(plane < z)
            def _():
                left(sums_out.at[plane, :, cols(index)], sum_sem_s.at[1, plane, index])

        return carry

    lax.fori_loop(0, planes, drain, 0)


def run_experts(normed, stream, info, w_in, w_down, axis_count, cap, top_count):
    rows, model = normed.shape
    near = 4
    planes = axis_count // near
    chunks = 4
    dma = pltpu.SemaphoreType.DMA
    anywhere = pl.BlockSpec(memory_space=pl.ANY)
    inside = pl.BlockSpec(memory_space=pltpu.VMEM)
    slots = pltpu.VMEM((planes, near, cap, model), jnp.bfloat16)
    blocks = pltpu.VMEM((planes, rows, model), jnp.bfloat16)
    return pl.pallas_call(
        functools.partial(expert_kernel, top_count=top_count),
        out_shape=jax.ShapeDtypeStruct((rows, model), jnp.bfloat16),
        in_specs=[inside] * 3 + [anywhere] * 2,
        out_specs=inside,
        scratch_shapes=[
            pltpu.VMEM(w_in.shape, jnp.bfloat16),
            pltpu.VMEM(w_down.shape, jnp.bfloat16),
            blocks,
            pltpu.VMEM((planes, *info.shape), jnp.float32),
            slots,
            slots,
            slots,
            slots,
            pltpu.VMEM((planes, rows, model), jnp.float32),
            pltpu.VMEM((rows, model), jnp.float32),
            pltpu.VMEM((2, planes, rows, model), jnp.bfloat16),
            blocks,
            dma((2,)),
            dma((planes, chunks)),
            dma((planes, chunks)),
            dma((planes, chunks)),
            dma((planes,)),
            dma((planes,)),
            dma((planes,)),
            dma((planes, near)),
            dma((planes, near)),
            dma((planes, near)),
            dma((planes, near)),
            dma((2, planes, chunks)),
            dma((2, planes, chunks)),
        ],
        compiler_params=pltpu.CompilerParams(
            collective_id=1, has_side_effects=True, vmem_limit_bytes=60 * 2**20
        ),
        cost_estimate=pl.CostEstimate(
            flops=6 * planes * near * cap * model * w_down.shape[0],
            bytes_accessed=8 * 2**20,
            transcendentals=planes * near * cap * w_down.shape[0],
        ),
    )(normed, stream, info, w_in, w_down)


def route(expert_ids, expert_gates, experts, row_count, top_count):
    flat_ids = expert_ids.reshape(-1)
    capacity = max(2, 2 * row_count * top_count // experts)
    onehot = (flat_ids[:, None] == jnp.arange(experts, dtype=jnp.int32)[None, :]).astype(
        jnp.float32
    )
    before = jnp.tri(flat_ids.shape[0], k=-1, dtype=jnp.bfloat16)
    earlier = jnp.dot(before, onehot.astype(jnp.bfloat16), preferred_element_type=jnp.float32)
    slot = flat_ids.astype(jnp.float32) * capacity + jnp.sum(earlier * onehot, 1)
    lines = jnp.concatenate(
        [slot.reshape(row_count, top_count), expert_gates.reshape(row_count, top_count)], 1
    ).T
    spare = -lines.shape[0] % 8
    return jnp.pad(lines, ((0, spare), (0, 0))), capacity


def experts(stream, normed, expert_ids, expert_gates, w_in, w_down):
    row_count, model_width = stream.shape
    axis_count = lax.axis_size("head")
    top_count = expert_ids.shape[2]
    flat_ids = expert_ids.reshape(-1)
    local_experts = w_in.shape[0]
    experts = local_experts * axis_count
    capacity = max(2, 2 * row_count * top_count // experts)
    onehot = (flat_ids[:, None] == jnp.arange(experts, dtype=jnp.int32)[None, :]).astype(jnp.int32)
    before = jnp.tri(flat_ids.shape[0], k=-1, dtype=jnp.bfloat16)
    earlier = jnp.dot(
        before, onehot.astype(jnp.bfloat16), preferred_element_type=jnp.float32
    ).astype(jnp.int32)
    slot_rank = jnp.sum(earlier * onehot, 1)
    target = flat_ids * capacity + slot_rank
    target = target.reshape(row_count, top_count)
    places = jnp.arange(experts * capacity, dtype=jnp.int32)
    chosen = jnp.zeros((experts * capacity, row_count), jnp.bool_)
    gate_of = jnp.zeros((row_count, experts * capacity), jnp.float32)
    gates = expert_gates.reshape(row_count, top_count)
    for rank in range(top_count):
        chosen = chosen | (places[:, None] == target[None, :, rank])
        gate_of = jnp.where(
            target[:, rank, None] == places[None, :], gates[:, rank, None], gate_of
        )
    outgoing = jnp.dot(
        chosen.astype(jnp.bfloat16), normed, preferred_element_type=jnp.float32
    ).astype(jnp.bfloat16)
    outgoing = outgoing.reshape(axis_count, local_experts, capacity, model_width)
    hidden_width = w_down.shape[1]
    inner_act = jnp.einsum(
        "semd,edf->semf",
        lax.all_to_all(outgoing, "head", split_axis=0, concat_axis=0, tiled=True),
        w_in,
        preferred_element_type=jnp.float32,
    )
    hidden = (jax.nn.silu(inner_act[..., :hidden_width]) * inner_act[..., hidden_width:]).astype(
        jnp.bfloat16
    )
    answered = jnp.einsum(
        "semf,efd->semd", hidden, w_down, preferred_element_type=jnp.float32
    ).astype(jnp.bfloat16)
    returned_rows = lax.all_to_all(answered, "head", split_axis=0, concat_axis=0, tiled=True)
    picked = returned_rows.reshape(experts * capacity, model_width)
    expert_sum = jnp.zeros((row_count, model_width), jnp.float32)
    rest = gate_of
    for _ in range(3):
        term = lax.reduce_precision(rest, 8, 7)
        rest = rest - term
        expert_sum = expert_sum + jnp.dot(
            term.astype(jnp.bfloat16), picked, preferred_element_type=jnp.float32
        )
    return (stream + expert_sum).astype(jnp.bfloat16)


def local(queries, new_kv, cache, resid, w_out, norm_gain, expert_ids, expert_gates, w_in, w_down):
    axis_count = lax.axis_size("head")
    local_rows, seq_count, head_count, head_width = queries.shape
    pair_heads = new_kv.shape[2]
    fits = (
        seq_count == 1
        and pair_heads == 2
        and lax.axis_size("grp") == 2
        and axis_count == 4 * (len(front_order[1]) + 1)
        and w_out.shape[2] % 1024 == 0
        and cache.shape[0] == 1
        and w_out.shape[1] * axis_count == head_width
        and w_out.shape[1] % 16 == 0
        and local_rows % 32 == 0
        and cache.shape[1] * 2 % 128 == 0
        and head_count % 4 == 0
    )
    if fits:
        info, capacity = route(
            expert_ids,
            expert_gates,
            w_in.shape[0] * axis_count,
            local_rows * seq_count,
            expert_ids.shape[2],
        )
        stream, normed = front(
            queries.reshape(local_rows, head_count, head_width).transpose(1, 0, 2),
            new_kv.reshape(local_rows, pair_heads, 2 * head_width).transpose(1, 0, 2),
            cache[0],
            w_out,
            resid.reshape(local_rows, -1),
            norm_gain.reshape(1, -1),
            axis_count,
        )
    else:
        stream, normed = front_general(queries, new_kv, cache, resid, w_out, norm_gain)
    top_count = expert_ids.shape[2]
    row_count = stream.shape[0]
    experts_count = w_in.shape[0] * axis_count
    if fits and w_in.shape[0] == 1 and row_count % 128 == 0 and (row_count * top_count * 2) % (
        16 * experts_count
    ) == 0:
        out = run_experts(
            normed, stream, info, w_in[0], w_down[0], axis_count, capacity, top_count
        )
    else:
        out = experts(stream, normed, expert_ids, expert_gates, w_in, w_down)
    return out.reshape(resid.shape)


def solution(mesh):
    return jax.shard_map(
        local,
        mesh=mesh,
        in_specs=(
            P("head", "grp", None, None),
            P("head", "grp", None, None),
            P(("grp", "head"), None, None),
            P("head", "grp", None),
            P(None, "head", None),
            P(),
            P("head", "grp", None),
            P("head", "grp", None),
            P("head", None, None),
            P("head", None, None),
        ),
        out_specs=P("head", "grp", None),
        check_vma=False,
    )
```

```python
import functools

import jax
import jax.numpy as jnp
from jax import lax
from jax.experimental import pallas as pl
from jax.experimental.pallas import tpu as pltpu
from jax.sharding import PartitionSpec as P

eps_norm = 1e-06
MESH = pl.DeviceIdType.MESH
expert_order = (
    ("P0", "P1",),
    (),
    ("P2", "E0", "E1", "R00", "R01",),
    ("R02", "R03", "E2", "R20", "P3", "R21", "R22", "R23", "R10", "R11",),
    ("R12", "R13", "E3",),
)
visit_order = ((1, 2, 1, 2), (2, 0, 3, 1), (3, 3, 0, 0), (0, 1, 2, 3))
return_order = ((2, 2, 1, 1), (1, 0, 3, 2), (3, 3, 0, 0))
front_order = (
    ("o0", "s0", "o1", "L1", "W01", "s1", "q", "S0", "o2", "o3", "D",),
    (
        ("L2", "W02", "s2", "W11", "S1", "F00", "s3",),
        ("W03", "W21", "F10", "F01", "S2", "L3", "W12", "W31",),
        ("W22", "F11", "F30", "S3", "F02", "F03", "F12", "W13",),
    ),
    ("W23", "J0", "F20", "F21", "F13", "W32", "F31", "F22", "J1", "F23", "W33", "J2", "F32", "F33", "J3",),
)


def front_body(
    q_ref,
    kv_ref,
    cache_ref,
    w_ref,
    resid_ref,
    gain_ref,
    stream_ref,
    normed_ref,
    q_buf,
    kn,
    kc,
    wb,
    acc,
    top,
    total,
    att,
    part_out,
    part_in,
    local_sem,
    q_sem,
    kn_line,
    kn_up,
    kn_side,
    kn_side_s,
    kn_twin,
    kn_twin_s,
    kc_line,
    kc_up,
    kc_down,
    kc_side,
    kc_side_s,
    kc_twin,
    kc_twin_s,
    w_line,
    w_up,
    w_down,
    w_side,
    w_side_s,
    w_far,
    w_far_s,
    w_twin,
    w_twin_s,
    part_sem,
    part_sem_s,
):
    planes = kn.shape[1]
    group = q_buf.shape[1]
    rows, width = q_buf.shape[2:]
    model = w_ref.shape[2]
    pieces = w_side.shape[0]
    half, chunk = model // 2, model // (2 * pieces)
    g = lax.axis_index("grp")
    me = lax.axis_index("head")
    z, y, c = me // 4, (me // 2) % 2, me % 2
    up, down = (g, me + 4), (g, me - 4)
    side, twin, far = (g, me + 2 - 4 * y), (g, me + 1 - 2 * c), (1 - g, me)
    has_up, has_down = z < planes - 1, z > 0

    barrier = pltpu.get_barrier_semaphore()
    for peer in (side, twin, (g, me ^ 3), far):
        pl.semaphore_signal(barrier, inc=1, device_id=peer, device_id_type=MESH)

    @pl.when(has_up)
    def _():
        pl.semaphore_signal(barrier, inc=1, device_id=up, device_id_type=MESH)

    @pl.when(has_down)
    def _():
        pl.semaphore_signal(barrier, inc=1, device_id=down, device_id_type=MESH)

    pl.semaphore_wait(barrier, 4 + has_up.astype(jnp.int32) + has_down.astype(jnp.int32))

    def copy(src, dst, sent, got, peer):
        return pltpu.make_async_remote_copy(
            src_ref=src,
            dst_ref=dst,
            send_sem=sent,
            recv_sem=got,
            device_id=peer,
            device_id_type=MESH,
        )

    def arrived(dst, got):
        copy(dst, dst, got, got, twin).wait_recv()

    def left(src, sent):
        copy(src, src, sent, sent, twin).wait_send()

    def mine(plane):
        return plane // (planes // 2) == y

    cols_near = pl.ds(pl.multiple_of(g * half, half), half)
    own_heads = pl.ds(y * group, group)
    other_heads = pl.ds((1 - y) * group, group)

    def w_cols(quarter, near):
        first = jnp.where(near, g, 1 - g) * half + quarter * chunk
        return pl.ds(pl.multiple_of(first, chunk), chunk)

    def w_block(quarter, plane, line, core, near=True):
        return wb.at[:, plane, line, core, :, w_cols(quarter, near)]

    def w_spread(src, quarter, plane, line):
        dst = w_block(quarter, plane, line, c)
        at = (quarter, plane, line)
        copy(src, dst, w_far_s.at[at], w_far.at[at], far).start()
        copy(src, dst, w_twin_s.at[(*at, 0)], w_twin.at[(*at, 0)], twin).start()

    def w_send_up(src, quarter, plane, line):
        at = (quarter, plane, line)

        @pl.when(has_up)
        def _():
            copy(src, w_block(quarter, plane, line, c), w_up.at[at], w_line.at[at], up).start()

    def w_send_down(src, quarter, plane, line):
        at = (quarter, plane, line)

        @pl.when(has_down)
        def _():
            copy(src, w_block(quarter, plane, line, c), w_down.at[at], w_line.at[at], down).start()

    def w_own_side(quarter):
        src = w_ref.at[other_heads, :, w_cols(quarter, True)]
        dst = w_block(quarter, z, y, c)
        copy(src, dst, w_side_s.at[quarter], w_side.at[quarter], side).start()

    def w_own(quarter):
        src = w_ref.at[own_heads, :, w_cols(quarter, True)]
        w_send_up(src, quarter, z, y)
        w_send_down(src, quarter, z, y)
        w_spread(src, quarter, z, y)

    def w_side_relay(quarter):
        block = w_block(quarter, z, 1 - y, c)
        arrived(block, w_side.at[quarter])
        w_send_up(block, quarter, z, 1 - y)
        w_send_down(block, quarter, z, 1 - y)
        w_spread(block, quarter, z, 1 - y)

    def w_relay(quarter, step):
        low, high = z - step, z + step
        for turn in range(2):
            line = y + turn - 2 * y * turn

            @pl.when(low >= 0)
            def _():
                block = w_block(quarter, low, line, c)
                arrived(block, w_line.at[quarter, low, line])
                w_send_up(block, quarter, low, line)
                w_spread(block, quarter, low, line)

            @pl.when(high < planes)
            def _():
                block = w_block(quarter, high, line, c)
                arrived(block, w_line.at[quarter, high, line])
                w_send_down(block, quarter, high, line)
                w_spread(block, quarter, high, line)

    def w_far_relay(quarter, plane):
        for line in range(2):
            block = w_block(quarter, plane, line, c, False)
            arrived(block, w_far.at[quarter, plane, line])
            at = (quarter, plane, line, 1)
            copy(block, block, w_twin_s.at[at], w_twin.at[at], twin).start()

    def w_far_relays(quarter, step):
        low, high = z - step, z + step

        @pl.when(low >= 0)
        def _():
            w_far_relay(quarter, low)

        if step > 0:

            @pl.when(high < planes)
            def _():
                w_far_relay(quarter, high)

    @pl.when(has_up)
    def _():
        copy(cache_ref, kc.at[z, y, c], kc_up.at[z], kc_line.at[z], up).start()
        copy(kv_ref, kn.at[:, z, y, c], kn_up.at[z], kn_line.at[z], up).start()

    @pl.when(has_down)
    def _():
        copy(cache_ref, kc.at[z, y, c], kc_down.at[z], kc_line.at[z], down).start()

    copy(kv_ref.at[1 - y], kn.at[1 - y, z, y, c], kn_side_s.at[z], kn_side.at[z], side).start()
    w_own_side(0)
    copy(q_ref.at[other_heads], q_buf.at[y], q_sem.at[0], q_sem.at[1], side).start()
    w_own_side(1)
    copy(kv_ref.at[y], kn.at[y, z, y, c], kn_twin_s.at[z, y], kn_twin.at[z, y], twin).start()

    @pl.when(mine(z))
    def _():
        copy(cache_ref, kc.at[z, y, c], kc_twin_s.at[z, y], kc_twin.at[z, y], twin).start()

    @pl.when(jnp.logical_not(mine(z)))
    def _():
        copy(cache_ref, kc.at[z, y, c], kc_side_s.at[z], kc_side.at[z], side).start()

    for piece in range(2, pieces):
        w_own_side(piece)
    locals_ = (
        pltpu.make_async_copy(q_ref.at[own_heads], q_buf.at[y], local_sem.at[0]),
        pltpu.make_async_copy(kv_ref.at[y], kn.at[y, z, y, c], local_sem.at[1]),
        pltpu.make_async_copy(cache_ref, kc.at[z, y, c], local_sem.at[2]),
        pltpu.make_async_copy(
            w_ref.at[own_heads, :, cols_near], wb.at[:, z, y, c, :, cols_near], local_sem.at[3]
        ),
    )
    for item in locals_:
        item.start()

    def from_side_new(plane):
        block = kn.at[y, plane, 1 - y, c]
        arrived(block, kn_side.at[plane])
        copy(block, block, kn_twin_s.at[plane, 1 - y], kn_twin.at[plane, 1 - y], twin).start()

    def from_side_old(plane):
        @pl.when(mine(plane))
        def _():
            block = kc.at[plane, 1 - y, c]
            arrived(block, kc_side.at[plane])
            copy(block, block, kc_twin_s.at[plane, 1 - y], kc_twin.at[plane, 1 - y], twin).start()

    def spread_old(plane):
        block = kc.at[plane, y, c]

        @pl.when(mine(plane))
        def _():
            copy(block, block, kc_twin_s.at[plane, y], kc_twin.at[plane, y], twin).start()

        @pl.when(jnp.logical_not(mine(plane)))
        def _():
            copy(block, block, kc_side_s.at[plane], kc_side.at[plane], side).start()

    def relay(step):
        low, high = z - step, z + step

        @pl.when(high < planes)
        def _():
            old = kc.at[high, y, c]
            arrived(old, kc_line.at[high])

            @pl.when(has_down)
            def _():
                copy(old, old, kc_down.at[high], kc_line.at[high], down).start()

            spread_old(high)

        @pl.when(low >= 0)
        def _():
            old, new = kc.at[low, y, c], kn.at[:, low, y, c]
            arrived(old, kc_line.at[low])

            @pl.when(has_up)
            def _():
                copy(old, old, kc_up.at[low], kc_line.at[low], up).start()

            arrived(new, kn_line.at[low])

            @pl.when(has_up)
            def _():
                copy(new, new, kn_up.at[low], kn_line.at[low], up).start()

            there, here = kn.at[1 - y, low, y, c], kn.at[y, low, y, c]
            copy(there, there, kn_side_s.at[low], kn_side.at[low], side).start()
            copy(here, here, kn_twin_s.at[low, y], kn_twin.at[low, y], twin).start()
            spread_old(low)

    def from_side(step):
        low, high = z - step, z + step

        @pl.when(low >= 0)
        def _():
            from_side_new(low)
            from_side_old(low)

        if step > 0:

            @pl.when(high < planes)
            def _():
                from_side_old(high)

    scale = width ** (-0.5)
    tile = 2
    tile_rows = tile * rows

    def fold(keys, values, diagonal):
        def lines(line, carry):
            for part in range(group // tile):
                heads = pl.ds(part * tile, tile)
                queries = q_buf[line, heads].reshape(tile_rows, width)
                queries = queries * jnp.asarray(scale, queries.dtype)
                scores = lax.dot_general(
                    queries, keys(), (((1,), (1,)), ((), ())), preferred_element_type=jnp.float32
                )
                pieces = [
                    scores[:, first : first + 128] for first in range(0, scores.shape[1], 128)
                ]
                if diagonal:
                    row_at = lax.broadcasted_iota(jnp.int32, (tile_rows, 128), 0) % rows
                    ahead = row_at - lax.broadcasted_iota(jnp.int32, (tile_rows, 128), 1)
                    ahead = ahead + (line * 2 + c) * rows
                    pieces = [
                        jnp.where(ahead >= index * 128, piece, -jnp.inf)
                        for index, piece in enumerate(pieces)
                    ]
                best = functools.reduce(jnp.maximum, pieces)
                best = jnp.max(best, 1, keepdims=True)
                if diagonal:
                    new_top = jnp.broadcast_to(best, (tile_rows, 128))
                else:
                    old_top = top[line, heads].reshape(tile_rows, 128)
                    new_top = jnp.maximum(old_top, best)
                exps = [jnp.exp(piece - new_top) for piece in pieces]
                new_total = functools.reduce(jnp.add, exps)
                weighted = jnp.dot(
                    jnp.concatenate([part_.astype(jnp.bfloat16) for part_ in exps], 1),
                    values(),
                    preferred_element_type=jnp.float32,
                )
                if not diagonal:
                    shrink = jnp.exp(old_top - new_top)
                    new_total = new_total + total[line, heads].reshape(tile_rows, 128) * shrink
                    weighted = weighted + acc[line, heads].reshape(
                        tile_rows, width
                    ) * jnp.concatenate([shrink] * (width // 128), 1)
                top[line, heads] = new_top.reshape(tile, rows, 128)
                total[line, heads] = new_total.reshape(tile, rows, 128)
                acc[line, heads] = weighted.reshape(tile, rows, width)
            return carry

        lax.fori_loop(0, 2, lines, 0, unroll=2)

    def new_part(plane, first):
        return lambda: kn[y, plane, :, :, :, first : first + width].reshape(4 * rows, width)

    page = kc.shape[3]

    def old_part(plane, line, first):
        return lambda: kc[plane, line, :, :, first : first + width].reshape(2 * page, width)

    def twins_new(plane):
        for line in range(2):
            arrived(kn.at[y, plane, line, 1 - c], kn_twin.at[plane, line])

    def twins_old(plane):
        for line in range(2):
            arrived(kc.at[plane, line, 1 - c], kc_twin.at[plane, line])

    def first_fold():
        twins_new(z)
        fold(new_part(z, 0), new_part(z, width), True)

    def queries_here():
        arrived(q_buf.at[1 - y], q_sem.at[1])
        for item in locals_:
            item.wait()

    def later_folds(step):
        low, high = z - step, z + step

        @pl.when((step >= 1) & (low >= 0))
        def _():
            twins_new(low)
            fold(new_part(low, 0), new_part(low, width), False)

        def old_body(index, carry):
            plane = jnp.where(index == 0, low, high)
            valid = (plane >= 0) & (plane < planes) & ((index == 0) | (step > 0))

            @pl.when(valid & mine(plane))
            def _():
                twins_old(plane)

                def line_body(line, carry):
                    fold(old_part(plane, line, 0), old_part(plane, line, width), False)
                    return carry

                lax.fori_loop(0, 2, line_body, 0)

            return carry

        lax.fori_loop(0, 2, old_body, 0)

    def finish():
        for line in range(2):
            for head in range(group):
                att[line, :, head * width : (head + 1) * width] = (
                    acc[line, head] / jnp.sum(total[line, head], 1, keepdims=True)
                ).astype(att.dtype)

    def project(quarter):
        for near in range(2):
            for plane in range(planes):
                for line in range(2):
                    arrived(
                        w_block(quarter, plane, line, 1 - c, near == 0),
                        w_twin.at[quarter, plane, line, near],
                    )
            cols = w_cols(quarter, near == 0)
            weights = wb[:, :, :, :, :, cols].reshape(group * width, chunk)
            both = jnp.dot(
                att[...].reshape(2 * rows, group * width),
                weights,
                preferred_element_type=jnp.float32,
            )
            there = jnp.where(y == 0, both[rows:], both[:rows])
            here = jnp.where(y == 0, both[:rows], both[rows:])
            part_out[:, cols] = there.astype(part_out.dtype)
            index = quarter * 2 + near
            block = part_out.at[:, cols]
            copy(block, part_in.at[:, cols], part_sem_s.at[index], part_sem.at[index], side).start()
            stream_ref[:, cols] = here + resid_ref[:, cols].astype(jnp.float32)

    acts = {
        "o": w_own,
        "s": w_side_relay,
        "L": relay,
        "S": from_side,
        "q": queries_here,
        "D": first_fold,
        "W": w_relay,
        "F": w_far_relays,
        "J": project,
    }

    def perform(segment):
        for word in segment:
            acts[word[0]](*(int(digit) for digit in word[1:]))

    before, between, after = front_order
    perform(before)

    def step_body(step, carry):
        for number, segment in enumerate(between):

            @pl.when(step == number + 1)
            def _():
                perform(segment)

        later_folds(step)
        return carry

    lax.fori_loop(0, planes, step_body, 0)
    finish()
    perform(after)
    square = jnp.zeros((rows, 1), jnp.float32)
    for quarter in range(pieces):
        for near in range(2):
            cols = w_cols(quarter, near == 0)
            index = quarter * 2 + near
            arrived(part_in.at[:, cols], part_sem.at[index])
            stream = stream_ref[:, cols] + part_in[:, cols].astype(jnp.float32)
            stream_ref[:, cols] = stream
            square = square + jnp.sum(stream * stream, 1, keepdims=True)
            left(part_out.at[:, cols], part_sem_s.at[index])
    inverse = lax.rsqrt(square / model + eps_norm)
    for index in range(2 * pieces):
        cols = slice(index * chunk, (index + 1) * chunk)
        normed_ref[:, cols] = (stream_ref[:, cols] * inverse * gain_ref[:, cols]).astype(
            normed_ref.dtype
        )

    left(q_buf.at[y], q_sem.at[0])
    for quarter in range(pieces):
        left(w_block(quarter, z, y, c), w_side_s.at[quarter])

    def drain(plane, carry):
        reached = plane <= z

        @pl.when(reached)
        def _():
            left(kn.at[1 - y, plane, y, c], kn_side_s.at[plane])
            left(kn.at[y, plane, y, c], kn_twin_s.at[plane, y])
            left(kn.at[y, plane, 1 - y, c], kn_twin_s.at[plane, 1 - y])

        @pl.when(reached & has_up)
        def _():
            left(kn.at[:, plane, y, c], kn_up.at[plane])
            left(kc.at[plane, y, c], kc_up.at[plane])
            for quarter in range(pieces):
                for line in range(2):
                    left(w_block(quarter, plane, line, c), w_up.at[quarter, plane, line])

        @pl.when((plane >= z) & has_down)
        def _():
            left(kc.at[plane, y, c], kc_down.at[plane])
            for quarter in range(pieces):
                for line in range(2):
                    left(w_block(quarter, plane, line, c), w_down.at[quarter, plane, line])

        @pl.when(mine(plane))
        def _():
            for line in range(2):
                left(kc.at[plane, line, c], kc_twin_s.at[plane, line])

        @pl.when(jnp.logical_not(mine(plane)))
        def _():
            left(kc.at[plane, y, c], kc_side_s.at[plane])

        for quarter in range(pieces):
            for line in range(2):
                at = (quarter, plane, line)
                left(w_block(quarter, plane, line, c), w_far_s.at[at])
                left(w_block(quarter, plane, line, c), w_twin_s.at[(*at, 0)])
                left(w_block(quarter, plane, line, c, False), w_twin_s.at[(*at, 1)])
        return carry

    lax.fori_loop(0, planes, drain, 0)


def partner_2(value, stride):
    mask = 2**stride
    pairs = [(source, source ^ mask) for source in range(lax.axis_size("head"))]
    return lax.ppermute(value, "head", pairs)


def turn_grp(value, shift):
    count = lax.axis_size("grp")
    return lax.ppermute(value, "grp", [(i, (i + shift) % count) for i in range(count)])


def attend_kernel(
    me_ref, query_ref, cache_ref, other_ref, pairs_ref, out_ref, new_ref, *, block, old_block, order
):
    head_width = query_ref.shape[1]
    step = pl.program_id(0)
    members, slots, local_rows = pairs_ref.shape[:3]

    @pl.when(step == 0)
    def _():
        for slot in range(slots):
            for member in range(members):
                apart = member ^ me_ref[0]
                place = 0
                for rank, bit in enumerate(order):
                    place = place + ((apart >> bit) & 1) * 2**rank
                first = (slot * members + member) * local_rows
                new_ref[first : first + local_rows, :] = pairs_ref[place, slot]

    query_rows = query_ref[...] * jnp.asarray(head_width ** (-0.5), query_ref.dtype)

    def fold(carry, keys, values, mask):
        top, total, weighted = carry
        scores = lax.dot_general(
            query_rows, keys, (((1,), (1,)), ((), ())), preferred_element_type=jnp.float32
        )
        if mask is not None:
            scores = jnp.where(mask, scores, -jnp.inf)
        new_top = jnp.maximum(top, jnp.max(scores, 1, keepdims=True))
        exps = jnp.exp(scores - new_top)
        shrink = jnp.exp(top - new_top)
        total = total * shrink + jnp.sum(exps, 1, keepdims=True)
        weighted = weighted * shrink + jnp.dot(
            exps.astype(jnp.bfloat16), values, preferred_element_type=jnp.float32
        )
        return new_top, total, weighted

    rows = query_rows.shape[0]
    carry = (
        jnp.full((rows, 1), -jnp.inf, jnp.float32),
        jnp.zeros((rows, 1), jnp.float32),
        jnp.zeros((rows, head_width), jnp.float32),
    )
    row_at = lax.broadcasted_iota(jnp.int32, (rows, block), 0)
    col_at = lax.broadcasted_iota(jnp.int32, (rows, block), 1)
    here = pl.ds(step * block, block)
    carry = fold(
        carry, new_ref[here, :head_width], new_ref[here, head_width:], col_at <= row_at
    )
    for old_ref in (cache_ref, other_ref):
        for first in range(0, old_ref.shape[0], old_block):
            part = pl.ds(first, old_block)
            carry = fold(carry, old_ref[part, :head_width], old_ref[part, head_width:], None)

    def earlier(index, carry):
        part = pl.ds(index * block, block)
        return fold(carry, new_ref[part, :head_width], new_ref[part, head_width:], None)

    top, total, weighted = lax.fori_loop(0, step, earlier, carry)
    out_ref[...] = (weighted / total).astype(out_ref.dtype)


def attend(me, queries, new_pairs, cached, cached_other, order):
    length, head_width = queries.shape
    block = min(512, length)
    old_block = min(1024, cached.shape[0])
    return pl.pallas_call(
        functools.partial(attend_kernel, block=block, old_block=old_block, order=order),
        grid_spec=pltpu.PrefetchScalarGridSpec(
            num_scalar_prefetch=1,
            grid=(length // block,),
            in_specs=[
                pl.BlockSpec((block, head_width), lambda i, me: (i, 0)),
                pl.BlockSpec(cached.shape, lambda i, me: (0, 0)),
                pl.BlockSpec(cached_other.shape, lambda i, me: (0, 0)),
                pl.BlockSpec(new_pairs.shape, lambda i, me: (0, 0, 0, 0)),
            ],
            out_specs=pl.BlockSpec((block, head_width), lambda i, me: (i, 0)),
            scratch_shapes=[pltpu.VMEM((length, 2 * head_width), jnp.bfloat16)],
        ),
        out_shape=jax.ShapeDtypeStruct((length, head_width), jnp.bfloat16),
        cost_estimate=pl.CostEstimate(
            flops=4 * length * head_width * (length // 2 + 2 * cached.shape[0]),
            bytes_accessed=8 * length * head_width * 2,
            transcendentals=length * (length // 2 + 2 * cached.shape[0]),
        ),
    )(me, queries, cached, cached_other, new_pairs)


def front_general(queries, new_kv, cache, resid, w_out, norm_gain):
    axis_count = lax.axis_size("head")
    local_rows = queries.shape[0]
    seq_count = queries.shape[1]
    head_count = queries.shape[2]
    head_width = queries.shape[3]
    pair_heads = new_kv.shape[2]
    group_size = head_count // pair_heads
    model_width = resid.shape[2]
    row_count = local_rows * seq_count
    slots = seq_count * pair_heads
    across = [[c * group_size + j for c in range(slots)] for j in range(group_size)]
    query_slots = queries.reshape(local_rows, axis_count, head_width).transpose(1, 0, 2)
    pair_slots = new_kv.reshape(local_rows, slots, 2 * head_width).transpose(1, 0, 2)
    pair_slots = lax.all_to_all(
        pair_slots, "head", split_axis=0, concat_axis=0, axis_index_groups=across, tiled=True
    )
    grp_count = lax.axis_size("grp")
    grp_me = lax.axis_index("grp")
    part_width = model_width // grp_count
    w_part = lax.dynamic_slice_in_dim(w_out, grp_me * part_width, part_width, 2)
    bits = group_size.bit_length() - 1
    order = tuple(range(1, bits)) + (0,)
    cache_rows = cache[0]
    pairs = pair_slots[None]
    for bit in order[:-1]:
        cache_rows = jnp.concatenate([cache_rows, partner_2(cache_rows, bit)], 0)
    head_queries = lax.all_to_all(query_slots, "head", split_axis=0, concat_axis=0, tiled=True)
    for bit in order[:-1]:
        pairs = jnp.concatenate([pairs, partner_2(pairs, bit)], 0)
    w_part, pairs, cache_rows, head_queries = lax.optimization_barrier(
        (w_part, pairs, cache_rows, head_queries)
    )
    w_part = lax.all_gather(w_part, "head", axis=1, tiled=True)
    w_part = w_part.reshape(head_count * head_width, part_width)
    cache_other = partner_2(cache_rows, 0)
    pairs = jnp.concatenate([pairs, partner_2(pairs, 0)], 0)
    me = (lax.axis_index("head") % group_size).astype(jnp.int32).reshape(1)
    attended = attend(
        me, head_queries.reshape(-1, head_width), pairs, cache_rows, cache_other, order
    )
    returned = lax.all_to_all(
        attended.reshape(axis_count, local_rows, head_width),
        "head",
        split_axis=0,
        concat_axis=0,
        tiled=True,
    )
    attn_rows = returned.reshape(seq_count, head_count, local_rows, head_width)
    attn_rows = attn_rows.transpose(2, 0, 1, 3).reshape(row_count, head_count * head_width)
    parts = []
    for shift in range(1, grp_count):
        far_rows = turn_grp(attn_rows, shift)
        far_part = jnp.dot(far_rows, w_part, preferred_element_type=jnp.float32)
        parts.append(turn_grp(far_part.astype(jnp.bfloat16), -shift).astype(jnp.float32))
    projected = []
    near_part = jnp.dot(attn_rows, w_part, preferred_element_type=jnp.float32)
    for column in range(grp_count):
        piece = near_part
        for shift in range(1, grp_count):
            piece = jnp.where((grp_me + shift) % grp_count == column, parts[shift - 1], piece)
        projected.append(piece)
    projected = jnp.concatenate(projected, 1)
    stream = resid.reshape(row_count, model_width).astype(jnp.float32) + projected
    normed = stream * lax.rsqrt(jnp.mean(stream * stream, 1, keepdims=True) + eps_norm) * norm_gain
    normed = normed.astype(jnp.bfloat16)
    return stream, normed


def expert_body(
    normed_ref,
    stream_ref,
    info_ref,
    out_ref,
    top_count,
    w_in,
    w_down,
    rows_buf,
    info_buf,
    picked,
    inbox,
    outbox,
    answer,
    dense,
    summed,
    sums_in,
    sums_out,
    row_line,
    row_sent,
    info_line,
    info_sent,
    in_sem,
    in_sem_s,
    ans_sem,
    ans_sem_s,
    sum_sem,
    sum_sem_s,
):
    planes, rows, model = rows_buf.shape
    near, cap = inbox.shape[1:3]
    hidden_width = w_down.shape[0]
    chunks = row_line.shape[1]
    chunk = model // chunks
    g = lax.axis_index("grp")
    me = lax.axis_index("head")
    z, own = me // near, me % near
    up, down = (g, me + near), (g, me - near)
    has_up, has_down = z < planes - 1, z > 0

    def copy(src, dst, sent, got, peer):
        return pltpu.make_async_remote_copy(
            src_ref=src,
            dst_ref=dst,
            send_sem=sent,
            recv_sem=got,
            device_id=peer,
            device_id_type=MESH,
        )

    def arrived(dst, got):
        copy(dst, dst, got, got, (g, me ^ 1)).wait_recv()

    def left(src, sent):
        copy(src, src, sent, sent, (g, me ^ 1)).wait_send()

    def cols(index):
        return slice(index * chunk, (index + 1) * chunk)

    def by_plane(values):
        chosen = jnp.int32(values[0])
        for index, value in enumerate(values[1:], 1):
            chosen = jnp.where(z == index, value, chosen)
        return chosen

    def send_info(src, plane, way, peer):
        copy(src, info_buf.at[plane], info_sent.at[way, plane], info_line.at[plane], peer).start()

    def send_row(src, index, plane, way, peer):
        dst = rows_buf.at[plane, :, cols(index)]
        copy(src, dst, row_sent.at[way, plane, index], row_line.at[plane, index], peer).start()

    def slots_of(info):
        at = lax.broadcasted_iota(jnp.int32, (near * cap, rows), 0) + z * (near * cap)
        at = at.astype(jnp.float32)
        return [at == info[rank : rank + 1, :] for rank in range(top_count)]

    def pick(plane, info, load):
        chosen = functools.reduce(jnp.logical_or, slots_of(info))
        chosen = jnp.where(chosen, 1.0, 0.0).astype(jnp.bfloat16)
        for index in range(chunks):
            part = jnp.dot(chosen, load(index), preferred_element_type=jnp.float32)
            picked[plane, :, :, cols(index)] = part.astype(jnp.bfloat16).reshape(near, cap, chunk)
            for mask in range(1, near):
                other = own ^ mask
                copy(
                    picked.at[plane, other, :, cols(index)],
                    inbox.at[plane, own, :, cols(index)],
                    in_sem_s.at[plane, other],
                    in_sem.at[plane, own],
                    (g, me ^ mask),
                ).start()
            inbox[plane, own, :, cols(index)] = picked[plane, own, :, cols(index)]

    def receive(plane):
        way = (plane > z).astype(jnp.int32)
        onward = jnp.where(way == 0, planes - 1 - z, z) > 0
        peer = (g, me + near - 2 * near * way)
        arrived(info_buf.at[plane], info_line.at[plane])

        @pl.when(onward)
        def _():
            send_info(info_buf.at[plane], plane, way, peer)

        def load(index):
            block = rows_buf.at[plane, :, cols(index)]
            arrived(block, row_line.at[plane, index])

            @pl.when(onward)
            def _():
                send_row(block, index, plane, way, peer)

            return block[...]

        pick(plane, info_buf[plane], load)

    def run_expert(plane):
        for mask in range(1, near):
            arrived(inbox.at[plane, own ^ mask], in_sem.at[plane, own ^ mask])
        inner = jnp.dot(
            inbox[plane].reshape(near * cap, model), w_in[...], preferred_element_type=jnp.float32
        )
        gate, value = inner[:, :hidden_width], inner[:, hidden_width:]
        hidden = (gate / (1.0 + jnp.exp(-gate)) * value).astype(jnp.bfloat16)
        for index in range(chunks):
            part = jnp.dot(hidden, w_down[:, cols(index)], preferred_element_type=jnp.float32)
            outbox[plane, :, :, cols(index)] = part.astype(jnp.bfloat16).reshape(near, cap, chunk)
            for mask in range(1, near):
                other = own ^ mask
                copy(
                    outbox.at[plane, other, :, cols(index)],
                    answer.at[plane, own, :, cols(index)],
                    ans_sem_s.at[plane, other],
                    ans_sem.at[plane, own],
                    (g, me ^ mask),
                ).start()
            answer[plane, own, :, cols(index)] = outbox[plane, own, :, cols(index)]

    def combine(plane, info, store):
        for mask in range(1, near):
            arrived(answer.at[plane, own ^ mask], ans_sem.at[plane, own ^ mask])
        gates = jnp.zeros((near * cap, rows), jnp.float32)
        for rank, here in enumerate(slots_of(info)):
            gates = jnp.where(here, info[top_count + rank : top_count + rank + 1, :], gates)
        high = gates.astype(jnp.bfloat16)
        low = (gates - high.astype(jnp.float32)).astype(jnp.bfloat16)
        for index in range(chunks):
            values = answer[plane, :, :, cols(index)].reshape(near * cap, chunk)
            total = jnp.zeros((rows, chunk), jnp.float32)
            for term in (high, low):
                total = total + lax.dot_general(
                    term, values, (((0,), (0,)), ((), ())), preferred_element_type=jnp.float32
                )
            store(index, total)

    def combine_far(plane):
        def store(index, total):
            dense[plane, :, cols(index)] = total

        combine(plane, info_buf[plane], store)

    def pass_sum(target, index):
        way = (target < z).astype(jnp.int32)
        has_in = jnp.where(way == 0, z, planes - 1 - z) > 0
        peer = (g, me + near - 2 * near * way)
        block = sums_in.at[way, target, :, cols(index)]
        at = (way, target, index)

        @pl.when(has_in)
        def _():
            arrived(block, sum_sem.at[at])
            sums_out[target, :, cols(index)] = (
                dense[target, :, cols(index)] + block[...].astype(jnp.float32)
            ).astype(jnp.bfloat16)

        @pl.when(jnp.logical_not(has_in))
        def _():
            sums_out[target, :, cols(index)] = dense[target, :, cols(index)].astype(jnp.bfloat16)

        copy(
            sums_out.at[target, :, cols(index)], block, sum_sem_s.at[at], sum_sem.at[at], peer
        ).start()

    def combine_own():
        def store(index, total):
            summed[:, cols(index)] = stream_ref[:, cols(index)] + total

        combine(z, info_ref[...], store)

    @pl.when(has_up)
    def _():
        send_info(info_ref, z, 0, up)

    @pl.when(has_down)
    def _():
        send_info(info_ref, z, 1, down)

    for index in range(chunks):
        block = normed_ref.at[:, cols(index)]

        @pl.when(has_up)
        def _():
            send_row(block, index, z, 0, up)

        @pl.when(has_down)
        def _():
            send_row(block, index, z, 1, down)

    own_at = visit_order.index(tuple(range(planes)))
    plane_at = [by_plane(values) for values in visit_order]
    target_at = [by_plane(values) for values in return_order]

    def perform(segment):
        for word in segment:
            first = int(word[1])
            if word[0] == "P" and first == own_at:
                pick(z, info_ref[...], lambda index: normed_ref[:, cols(index)])
            elif word[0] == "P":
                receive(plane_at[first])
            elif word[0] == "E" and first == own_at:
                combine_own()
            elif word[0] == "E":
                combine_far(plane_at[first])
            else:
                pass_sum(target_at[first], int(word[2]))

    def step_body(step, carry):
        for number, segment in enumerate(expert_order[:-1]):

            @pl.when(step == number)
            def _():
                perform(segment)

        plane = plane_at[0]
        for number, value in enumerate(plane_at[1:], 1):
            plane = jnp.where(step == number, value, plane)
        run_expert(plane)
        return carry

    lax.fori_loop(0, planes, step_body, 0)
    perform(expert_order[-1])

    for index in range(chunks):

        @pl.when(has_down)
        def _():
            block = sums_in.at[0, z, :, cols(index)]
            arrived(block, sum_sem.at[0, z, index])
            summed[:, cols(index)] = summed[:, cols(index)] + block[...].astype(jnp.float32)

        @pl.when(has_up)
        def _():
            block = sums_in.at[1, z, :, cols(index)]
            arrived(block, sum_sem.at[1, z, index])
            summed[:, cols(index)] = summed[:, cols(index)] + block[...].astype(jnp.float32)

        out_ref[:, cols(index)] = summed[:, cols(index)].astype(out_ref.dtype)

    def drain(plane, carry):
        @pl.when((plane <= z) & has_up)
        def _():
            left(info_buf.at[plane], info_sent.at[0, plane])
            for index in range(chunks):
                left(rows_buf.at[plane, :, cols(index)], row_sent.at[0, plane, index])

        @pl.when((plane >= z) & has_down)
        def _():
            left(info_buf.at[plane], info_sent.at[1, plane])
            for index in range(chunks):
                left(rows_buf.at[plane, :, cols(index)], row_sent.at[1, plane, index])

        for mask in range(1, near):
            left(picked.at[plane, own ^ mask], in_sem_s.at[plane, own ^ mask])
            left(outbox.at[plane, own ^ mask], ans_sem_s.at[plane, own ^ mask])

        for index in range(chunks):

            @pl.when(plane > z)
            def _():
                left(sums_out.at[plane, :, cols(index)], sum_sem_s.at[0, plane, index])

            @pl.when(plane < z)
            def _():
                left(sums_out.at[plane, :, cols(index)], sum_sem_s.at[1, plane, index])

        return carry

    lax.fori_loop(0, planes, drain, 0)


def layer_kernel(*refs, top_count, front_count):
    inputs, out_ref, rest = refs[:9], refs[9], refs[10:]
    w_in_ref, w_down_ref = inputs[7:]
    stream, normed, w_in, w_down, load_sem = rest[:5]
    front_scratch, expert_scratch = rest[5 : 5 + front_count], rest[5 + front_count :]
    loads = (
        pltpu.make_async_copy(w_in_ref, w_in, load_sem.at[0]),
        pltpu.make_async_copy(w_down_ref, w_down, load_sem.at[1]),
    )
    for load in loads:
        load.start()
    front_body(*inputs[:6], stream, normed, *front_scratch)
    for load in loads:
        load.wait()
    expert_body(normed, stream, inputs[6], out_ref, top_count, w_in, w_down, *expert_scratch)


def layer(queries, pairs, cached, w_out, resid, gain, info, w_in, w_down, axis_count, cap, top_count):
    heads, rows, width = queries.shape
    group = heads // 2
    near = 4
    planes = axis_count // near
    model = w_out.shape[2]
    slice_rows = w_out.shape[1]
    page = cached.shape[0]
    pieces = 4
    chunks = 4
    dma = pltpu.SemaphoreType.DMA
    anywhere = pl.BlockSpec(memory_space=pl.ANY)
    inside = pl.BlockSpec(memory_space=pltpu.VMEM)

    def half(*shape):
        return pltpu.VMEM(shape, jnp.bfloat16)

    def full(*shape):
        return pltpu.VMEM(shape, jnp.float32)

    front_scratch = [
        half(2, group, rows, width),
        half(2, planes, 2, 2, rows, 2 * width),
        half(planes, 2, 2, page, 2 * width),
        half(group, planes, 2, 2, slice_rows, model),
        full(2, group, rows, width),
        full(2, group, rows, 128),
        full(2, group, rows, 128),
        half(2, rows, group * width),
        half(rows, model),
        half(rows, model),
        dma((4,)),
        dma((2,)),
        dma((planes,)),
        dma((planes,)),
        dma((planes,)),
        dma((planes,)),
        dma((planes, 2)),
        dma((planes, 2)),
        dma((planes,)),
        dma((planes,)),
        dma((planes,)),
        dma((planes,)),
        dma((planes,)),
        dma((planes, 2)),
        dma((planes, 2)),
        dma((pieces, planes, 2)),
        dma((pieces, planes, 2)),
        dma((pieces, planes, 2)),
        dma((pieces,)),
        dma((pieces,)),
        dma((pieces, planes, 2)),
        dma((pieces, planes, 2)),
        dma((pieces, planes, 2, 2)),
        dma((pieces, planes, 2, 2)),
        dma((2 * pieces,)),
        dma((2 * pieces,)),
    ]
    expert_scratch = [
        half(planes, rows, model),
        full(planes, *info.shape),
        half(planes, near, cap, model),
        half(planes, near, cap, model),
        half(planes, near, cap, model),
        half(planes, near, cap, model),
        full(planes, rows, model),
        full(rows, model),
        half(2, planes, rows, model),
        half(planes, rows, model),
        dma((planes, chunks)),
        dma((2, planes, chunks)),
        dma((planes,)),
        dma((2, planes)),
        dma((planes, near)),
        dma((planes, near)),
        dma((planes, near)),
        dma((planes, near)),
        dma((2, planes, chunks)),
        dma((2, planes, chunks)),
    ]
    return pl.pallas_call(
        functools.partial(
            layer_kernel, top_count=top_count, front_count=len(front_scratch)
        ),
        out_shape=jax.ShapeDtypeStruct((rows, model), jnp.bfloat16),
        in_specs=[anywhere] * 4 + [inside] * 3 + [anywhere] * 2,
        out_specs=inside,
        scratch_shapes=[
            full(rows, model),
            half(rows, model),
            half(*w_in.shape),
            half(*w_down.shape),
            dma((2,)),
            *front_scratch,
            *expert_scratch,
        ],
        compiler_params=pltpu.CompilerParams(
            collective_id=0, has_side_effects=True, vmem_limit_bytes=60 * 2**20
        ),
        cost_estimate=pl.CostEstimate(
            flops=4 * 2 * group * rows * width * 4 * axis_count * rows
            + 4 * rows * group * width * model
            + 6 * planes * near * cap * model * w_down.shape[0],
            bytes_accessed=12 * 2**20,
            transcendentals=2 * group * rows * axis_count * rows,
        ),
    )(queries, pairs, cached, w_out, resid, gain, info, w_in, w_down)


def route(expert_ids, expert_gates, experts, row_count, top_count):
    flat_ids = expert_ids.reshape(-1)
    capacity = max(2, 2 * row_count * top_count // experts)
    onehot = (flat_ids[:, None] == jnp.arange(experts, dtype=jnp.int32)[None, :]).astype(
        jnp.float32
    )
    before = jnp.tri(flat_ids.shape[0], k=-1, dtype=jnp.bfloat16)
    earlier = jnp.dot(before, onehot.astype(jnp.bfloat16), preferred_element_type=jnp.float32)
    slot = flat_ids.astype(jnp.float32) * capacity + jnp.sum(earlier * onehot, 1)
    lines = jnp.concatenate(
        [slot.reshape(row_count, top_count), expert_gates.reshape(row_count, top_count)], 1
    ).T
    spare = -lines.shape[0] % 8
    return jnp.pad(lines, ((0, spare), (0, 0))), capacity


def experts(stream, normed, expert_ids, expert_gates, w_in, w_down):
    row_count, model_width = stream.shape
    axis_count = lax.axis_size("head")
    top_count = expert_ids.shape[2]
    flat_ids = expert_ids.reshape(-1)
    local_experts = w_in.shape[0]
    experts = local_experts * axis_count
    capacity = max(2, 2 * row_count * top_count // experts)
    onehot = (flat_ids[:, None] == jnp.arange(experts, dtype=jnp.int32)[None, :]).astype(jnp.int32)
    before = jnp.tri(flat_ids.shape[0], k=-1, dtype=jnp.bfloat16)
    earlier = jnp.dot(
        before, onehot.astype(jnp.bfloat16), preferred_element_type=jnp.float32
    ).astype(jnp.int32)
    slot_rank = jnp.sum(earlier * onehot, 1)
    target = flat_ids * capacity + slot_rank
    target = target.reshape(row_count, top_count)
    places = jnp.arange(experts * capacity, dtype=jnp.int32)
    chosen = jnp.zeros((experts * capacity, row_count), jnp.bool_)
    gate_of = jnp.zeros((row_count, experts * capacity), jnp.float32)
    gates = expert_gates.reshape(row_count, top_count)
    for rank in range(top_count):
        chosen = chosen | (places[:, None] == target[None, :, rank])
        gate_of = jnp.where(
            target[:, rank, None] == places[None, :], gates[:, rank, None], gate_of
        )
    outgoing = jnp.dot(
        chosen.astype(jnp.bfloat16), normed, preferred_element_type=jnp.float32
    ).astype(jnp.bfloat16)
    outgoing = outgoing.reshape(axis_count, local_experts, capacity, model_width)
    hidden_width = w_down.shape[1]
    inner_act = jnp.einsum(
        "semd,edf->semf",
        lax.all_to_all(outgoing, "head", split_axis=0, concat_axis=0, tiled=True),
        w_in,
        preferred_element_type=jnp.float32,
    )
    hidden = (jax.nn.silu(inner_act[..., :hidden_width]) * inner_act[..., hidden_width:]).astype(
        jnp.bfloat16
    )
    answered = jnp.einsum(
        "semf,efd->semd", hidden, w_down, preferred_element_type=jnp.float32
    ).astype(jnp.bfloat16)
    returned_rows = lax.all_to_all(answered, "head", split_axis=0, concat_axis=0, tiled=True)
    picked = returned_rows.reshape(experts * capacity, model_width)
    expert_sum = jnp.zeros((row_count, model_width), jnp.float32)
    rest = gate_of
    for _ in range(3):
        term = lax.reduce_precision(rest, 8, 7)
        rest = rest - term
        expert_sum = expert_sum + jnp.dot(
            term.astype(jnp.bfloat16), picked, preferred_element_type=jnp.float32
        )
    return (stream + expert_sum).astype(jnp.bfloat16)


def local(queries, new_kv, cache, resid, w_out, norm_gain, expert_ids, expert_gates, w_in, w_down):
    axis_count = lax.axis_size("head")
    local_rows, seq_count, head_count, head_width = queries.shape
    pair_heads = new_kv.shape[2]
    fits = (
        seq_count == 1
        and pair_heads == 2
        and lax.axis_size("grp") == 2
        and axis_count == 4 * (len(front_order[1]) + 1)
        and w_out.shape[2] % 1024 == 0
        and cache.shape[0] == 1
        and w_out.shape[1] * axis_count == head_width
        and w_out.shape[1] % 16 == 0
        and local_rows % 32 == 0
        and cache.shape[1] * 2 % 128 == 0
        and head_count % 4 == 0
    )
    top_count = expert_ids.shape[2]
    experts_count = w_in.shape[0] * axis_count
    row_count = local_rows * seq_count
    fits = (
        fits
        and w_in.shape[0] == 1
        and row_count % 128 == 0
        and (row_count * top_count * 2) % (16 * experts_count) == 0
    )
    if fits:
        info, capacity = route(expert_ids, expert_gates, experts_count, row_count, top_count)
        out = layer(
            queries.reshape(local_rows, head_count, head_width).transpose(1, 0, 2),
            new_kv.reshape(local_rows, pair_heads, 2 * head_width).transpose(1, 0, 2),
            cache[0],
            w_out,
            resid.reshape(local_rows, -1),
            norm_gain.reshape(1, -1),
            info,
            w_in[0],
            w_down[0],
            axis_count,
            capacity,
            top_count,
        )
    else:
        stream, normed = front_general(queries, new_kv, cache, resid, w_out, norm_gain)
        out = experts(stream, normed, expert_ids, expert_gates, w_in, w_down)
    return out.reshape(resid.shape)


def solution(mesh):
    return jax.shard_map(
        local,
        mesh=mesh,
        in_specs=(
            P("head", "grp", None, None),
            P("head", "grp", None, None),
            P(("grp", "head"), None, None),
            P("head", "grp", None),
            P(None, "head", None),
            P(),
            P("head", "grp", None),
            P("head", "grp", None),
            P("head", None, None),
            P("head", None, None),
        ),
        out_specs=P("head", "grp", None),
        check_vma=False,
    )
```

```python
import functools

import jax
import jax.numpy as jnp
from jax import lax
from jax.experimental import pallas as pl
from jax.experimental.pallas import tpu as pltpu
from jax.sharding import PartitionSpec as P

eps_norm = 1e-06
MESH = pl.DeviceIdType.MESH
expert_order = (
    ("P0", "P1",),
    (),
    ("P2", "E0", "E1", "R00", "R01",),
    ("R02", "R03", "E2", "R20", "P3", "R21", "R22", "R23", "R10", "R11",),
    ("R12", "R13", "E3",),
)
visit_order = ((1, 2, 1, 2), (2, 0, 3, 1), (3, 3, 0, 0), (0, 1, 2, 3))
return_order = ((2, 2, 1, 1), (1, 0, 3, 2), (3, 3, 0, 0))
front_order = (
    ("o0", "s0", "o1", "L1", "W01", "s1", "q", "S0", "o2", "o3", "D",),
    (
        ("L2", "W02", "s2", "W11", "S1", "F00", "s3",),
        ("W03", "W21", "F10", "F01", "S2", "L3", "W12", "W31",),
        ("W22", "F11", "F30", "S3", "F02", "F03", "F12", "W13",),
    ),
    ("W23", "J0", "F20", "F21", "F13", "W32", "F31", "F22", "J1", "F23", "W33", "J2", "F32", "F33", "J3",),
)


def front_body(
    q_raw_ref,
    kv_raw_ref,
    cache_ref,
    w_ref,
    resid_ref,
    gain_ref,
    stream_ref,
    normed_ref,
    aside,
    q_raw,
    q_ref,
    kv_raw,
    kv_ref,
    q_buf,
    kn,
    kc,
    wb,
    acc,
    top,
    total,
    att,
    part_out,
    part_in,
    local_sem,
    q_sem,
    kn_line,
    kn_up,
    kn_side,
    kn_side_s,
    kn_twin,
    kn_twin_s,
    kc_line,
    kc_up,
    kc_down,
    kc_side,
    kc_side_s,
    kc_twin,
    kc_twin_s,
    w_line,
    w_up,
    w_down,
    w_side,
    w_side_s,
    w_far,
    w_far_s,
    w_twin,
    w_twin_s,
    part_sem,
    part_sem_s,
):
    planes = kn.shape[1]
    group = q_buf.shape[1]
    rows, width = q_buf.shape[2:]
    model = w_ref.shape[2]
    pieces = w_side.shape[0]
    half, chunk = model // 2, model // (2 * pieces)
    g = lax.axis_index("grp")
    me = lax.axis_index("head")
    z, y, c = me // 4, (me // 2) % 2, me % 2
    up, down = (g, me + 4), (g, me - 4)
    side, twin, far = (g, me + 2 - 4 * y), (g, me + 1 - 2 * c), (1 - g, me)
    has_up, has_down = z < planes - 1, z > 0

    raw = (
        pltpu.make_async_copy(kv_raw_ref, kv_raw, local_sem.at[0]),
        pltpu.make_async_copy(q_raw_ref, q_raw, local_sem.at[1]),
    )
    for item in raw:
        item.start()
    barrier = pltpu.get_barrier_semaphore()
    for peer in (side, twin, (g, me ^ 3), far):
        pl.semaphore_signal(barrier, inc=1, device_id=peer, device_id_type=MESH)

    @pl.when(has_up)
    def _():
        pl.semaphore_signal(barrier, inc=1, device_id=up, device_id_type=MESH)

    @pl.when(has_down)
    def _():
        pl.semaphore_signal(barrier, inc=1, device_id=down, device_id_type=MESH)

    pl.semaphore_wait(barrier, 4 + has_up.astype(jnp.int32) + has_down.astype(jnp.int32))

    def copy(src, dst, sent, got, peer):
        return pltpu.make_async_remote_copy(
            src_ref=src,
            dst_ref=dst,
            send_sem=sent,
            recv_sem=got,
            device_id=peer,
            device_id_type=MESH,
        )

    def arrived(dst, got):
        copy(dst, dst, got, got, twin).wait_recv()

    def left(src, sent):
        copy(src, src, sent, sent, twin).wait_send()

    def mine(plane):
        return plane // (planes // 2) == y

    cols_near = pl.ds(pl.multiple_of(g * half, half), half)
    raw[0].wait()
    kv_ref[...] = jnp.swapaxes(kv_raw[...], 0, 1)
    own_heads = pl.ds(y * group, group)
    other_heads = pl.ds((1 - y) * group, group)

    def w_cols(quarter, near):
        first = jnp.where(near, g, 1 - g) * half + quarter * chunk
        return pl.ds(pl.multiple_of(first, chunk), chunk)

    def w_block(quarter, plane, line, core, near=True):
        return wb.at[:, plane, line, core, :, w_cols(quarter, near)]

    def w_spread(src, quarter, plane, line):
        dst = w_block(quarter, plane, line, c)
        at = (quarter, plane, line)
        copy(src, dst, w_far_s.at[at], w_far.at[at], far).start()
        copy(src, dst, w_twin_s.at[(*at, 0)], w_twin.at[(*at, 0)], twin).start()

    def w_send_up(src, quarter, plane, line):
        at = (quarter, plane, line)

        @pl.when(has_up)
        def _():
            copy(src, w_block(quarter, plane, line, c), w_up.at[at], w_line.at[at], up).start()

    def w_send_down(src, quarter, plane, line):
        at = (quarter, plane, line)

        @pl.when(has_down)
        def _():
            copy(src, w_block(quarter, plane, line, c), w_down.at[at], w_line.at[at], down).start()

    def w_own_side(quarter):
        src = w_ref.at[other_heads, :, w_cols(quarter, True)]
        dst = w_block(quarter, z, y, c)
        copy(src, dst, w_side_s.at[quarter], w_side.at[quarter], side).start()

    def w_own(quarter):
        src = w_ref.at[own_heads, :, w_cols(quarter, True)]
        w_send_up(src, quarter, z, y)
        w_send_down(src, quarter, z, y)
        w_spread(src, quarter, z, y)

    def w_side_relay(quarter):
        block = w_block(quarter, z, 1 - y, c)
        arrived(block, w_side.at[quarter])
        w_send_up(block, quarter, z, 1 - y)
        w_send_down(block, quarter, z, 1 - y)
        w_spread(block, quarter, z, 1 - y)

    def w_relay(quarter, step):
        low, high = z - step, z + step
        for turn in range(2):
            line = y + turn - 2 * y * turn

            @pl.when(low >= 0)
            def _():
                block = w_block(quarter, low, line, c)
                arrived(block, w_line.at[quarter, low, line])
                w_send_up(block, quarter, low, line)
                w_spread(block, quarter, low, line)

            @pl.when(high < planes)
            def _():
                block = w_block(quarter, high, line, c)
                arrived(block, w_line.at[quarter, high, line])
                w_send_down(block, quarter, high, line)
                w_spread(block, quarter, high, line)

    def w_far_relay(quarter, plane):
        for line in range(2):
            block = w_block(quarter, plane, line, c, False)
            arrived(block, w_far.at[quarter, plane, line])
            at = (quarter, plane, line, 1)
            copy(block, block, w_twin_s.at[at], w_twin.at[at], twin).start()

    def w_far_relays(quarter, step):
        low, high = z - step, z + step

        @pl.when(low >= 0)
        def _():
            w_far_relay(quarter, low)

        if step > 0:

            @pl.when(high < planes)
            def _():
                w_far_relay(quarter, high)

    @pl.when(has_up)
    def _():
        copy(cache_ref, kc.at[z, y, c], kc_up.at[z], kc_line.at[z], up).start()
        copy(kv_ref, kn.at[:, z, y, c], kn_up.at[z], kn_line.at[z], up).start()

    @pl.when(has_down)
    def _():
        copy(cache_ref, kc.at[z, y, c], kc_down.at[z], kc_line.at[z], down).start()

    copy(kv_ref.at[1 - y], kn.at[1 - y, z, y, c], kn_side_s.at[z], kn_side.at[z], side).start()
    w_own_side(0)
    copy(kv_ref.at[y], kn.at[y, z, y, c], kn_twin_s.at[z, y], kn_twin.at[z, y], twin).start()

    @pl.when(mine(z))
    def _():
        copy(cache_ref, kc.at[z, y, c], kc_twin_s.at[z, y], kc_twin.at[z, y], twin).start()

    @pl.when(jnp.logical_not(mine(z)))
    def _():
        copy(cache_ref, kc.at[z, y, c], kc_side_s.at[z], kc_side.at[z], side).start()

    locals_ = (
        pltpu.make_async_copy(kv_ref.at[y], kn.at[y, z, y, c], local_sem.at[0]),
        pltpu.make_async_copy(cache_ref, kc.at[z, y, c], local_sem.at[2]),
        pltpu.make_async_copy(
            w_ref.at[own_heads, :, cols_near], wb.at[:, z, y, c, :, cols_near], local_sem.at[3]
        ),
    )
    for item in locals_:
        item.start()
    raw[1].wait()
    q_ref[...] = jnp.swapaxes(q_raw[...], 0, 1).reshape(q_ref.shape)
    copy(q_ref.at[1 - y], q_buf.at[y], q_sem.at[0], q_sem.at[1], side).start()
    for piece in range(1, pieces):
        w_own_side(piece)
    q_buf[y] = q_ref[y]
    aside()

    def from_side_new(plane):
        block = kn.at[y, plane, 1 - y, c]
        arrived(block, kn_side.at[plane])
        copy(block, block, kn_twin_s.at[plane, 1 - y], kn_twin.at[plane, 1 - y], twin).start()

    def from_side_old(plane):
        @pl.when(mine(plane))
        def _():
            block = kc.at[plane, 1 - y, c]
            arrived(block, kc_side.at[plane])
            copy(block, block, kc_twin_s.at[plane, 1 - y], kc_twin.at[plane, 1 - y], twin).start()

    def spread_old(plane):
        block = kc.at[plane, y, c]

        @pl.when(mine(plane))
        def _():
            copy(block, block, kc_twin_s.at[plane, y], kc_twin.at[plane, y], twin).start()

        @pl.when(jnp.logical_not(mine(plane)))
        def _():
            copy(block, block, kc_side_s.at[plane], kc_side.at[plane], side).start()

    def relay(step):
        low, high = z - step, z + step

        @pl.when(high < planes)
        def _():
            old = kc.at[high, y, c]
            arrived(old, kc_line.at[high])

            @pl.when(has_down)
            def _():
                copy(old, old, kc_down.at[high], kc_line.at[high], down).start()

            spread_old(high)

        @pl.when(low >= 0)
        def _():
            old, new = kc.at[low, y, c], kn.at[:, low, y, c]
            arrived(old, kc_line.at[low])

            @pl.when(has_up)
            def _():
                copy(old, old, kc_up.at[low], kc_line.at[low], up).start()

            arrived(new, kn_line.at[low])

            @pl.when(has_up)
            def _():
                copy(new, new, kn_up.at[low], kn_line.at[low], up).start()

            there, here = kn.at[1 - y, low, y, c], kn.at[y, low, y, c]
            copy(there, there, kn_side_s.at[low], kn_side.at[low], side).start()
            copy(here, here, kn_twin_s.at[low, y], kn_twin.at[low, y], twin).start()
            spread_old(low)

    def from_side(step):
        low, high = z - step, z + step

        @pl.when(low >= 0)
        def _():
            from_side_new(low)
            from_side_old(low)

        if step > 0:

            @pl.when(high < planes)
            def _():
                from_side_old(high)

    scale = width ** (-0.5)
    tile = 2
    tile_rows = tile * rows

    def fold(keys, values, diagonal):
        def lines(line, carry):
            for part in range(group // tile):
                heads = pl.ds(part * tile, tile)
                queries = q_buf[line, heads].reshape(tile_rows, width)
                queries = queries * jnp.asarray(scale, queries.dtype)
                scores = lax.dot_general(
                    queries, keys(), (((1,), (1,)), ((), ())), preferred_element_type=jnp.float32
                )
                pieces = [
                    scores[:, first : first + 128] for first in range(0, scores.shape[1], 128)
                ]
                if diagonal:
                    row_at = lax.broadcasted_iota(jnp.int32, (tile_rows, 128), 0) % rows
                    ahead = row_at - lax.broadcasted_iota(jnp.int32, (tile_rows, 128), 1)
                    ahead = ahead + (line * 2 + c) * rows
                    pieces = [
                        jnp.where(ahead >= index * 128, piece, -jnp.inf)
                        for index, piece in enumerate(pieces)
                    ]
                best = functools.reduce(jnp.maximum, pieces)
                best = jnp.max(best, 1, keepdims=True)
                if diagonal:
                    new_top = jnp.broadcast_to(best, (tile_rows, 128))
                else:
                    old_top = top[line, heads].reshape(tile_rows, 128)
                    new_top = jnp.maximum(old_top, best)
                exps = [jnp.exp(piece - new_top) for piece in pieces]
                new_total = functools.reduce(jnp.add, exps)
                weighted = jnp.dot(
                    jnp.concatenate([part_.astype(jnp.bfloat16) for part_ in exps], 1),
                    values(),
                    preferred_element_type=jnp.float32,
                )
                if not diagonal:
                    shrink = jnp.exp(old_top - new_top)
                    new_total = new_total + total[line, heads].reshape(tile_rows, 128) * shrink
                    weighted = weighted + acc[line, heads].reshape(
                        tile_rows, width
                    ) * jnp.concatenate([shrink] * (width // 128), 1)
                top[line, heads] = new_top.reshape(tile, rows, 128)
                total[line, heads] = new_total.reshape(tile, rows, 128)
                acc[line, heads] = weighted.reshape(tile, rows, width)
            return carry

        lax.fori_loop(0, 2, lines, 0, unroll=2)

    def new_part(plane, first):
        return lambda: kn[y, plane, :, :, :, first : first + width].reshape(4 * rows, width)

    page = kc.shape[3]

    def old_part(plane, line, first):
        return lambda: kc[plane, line, :, :, first : first + width].reshape(2 * page, width)

    def twins_new(plane):
        for line in range(2):
            arrived(kn.at[y, plane, line, 1 - c], kn_twin.at[plane, line])

    def twins_old(plane):
        for line in range(2):
            arrived(kc.at[plane, line, 1 - c], kc_twin.at[plane, line])

    def first_fold():
        twins_new(z)
        fold(new_part(z, 0), new_part(z, width), True)

    def queries_here():
        arrived(q_buf.at[1 - y], q_sem.at[1])
        for item in locals_:
            item.wait()

    def later_folds(step):
        low, high = z - step, z + step

        @pl.when((step >= 1) & (low >= 0))
        def _():
            twins_new(low)
            fold(new_part(low, 0), new_part(low, width), False)

        def old_body(index, carry):
            plane = jnp.where(index == 0, low, high)
            valid = (plane >= 0) & (plane < planes) & ((index == 0) | (step > 0))

            @pl.when(valid & mine(plane))
            def _():
                twins_old(plane)

                def line_body(line, carry):
                    fold(old_part(plane, line, 0), old_part(plane, line, width), False)
                    return carry

                lax.fori_loop(0, 2, line_body, 0)

            return carry

        lax.fori_loop(0, 2, old_body, 0)

    def finish():
        for line in range(2):
            for head in range(group):
                att[line, :, head * width : (head + 1) * width] = (
                    acc[line, head] / jnp.sum(total[line, head], 1, keepdims=True)
                ).astype(att.dtype)

    def project(quarter):
        for near in range(2):
            for plane in range(planes):
                for line in range(2):
                    arrived(
                        w_block(quarter, plane, line, 1 - c, near == 0),
                        w_twin.at[quarter, plane, line, near],
                    )
            cols = w_cols(quarter, near == 0)
            weights = wb[:, :, :, :, :, cols].reshape(group * width, chunk)
            both = jnp.dot(
                att[...].reshape(2 * rows, group * width),
                weights,
                preferred_element_type=jnp.float32,
            )
            there = jnp.where(y == 0, both[rows:], both[:rows])
            here = jnp.where(y == 0, both[:rows], both[rows:])
            part_out[:, cols] = there.astype(part_out.dtype)
            index = quarter * 2 + near
            block = part_out.at[:, cols]
            copy(block, part_in.at[:, cols], part_sem_s.at[index], part_sem.at[index], side).start()
            stream_ref[:, cols] = here + resid_ref[:, cols].astype(jnp.float32)

    acts = {
        "o": w_own,
        "s": w_side_relay,
        "L": relay,
        "S": from_side,
        "q": queries_here,
        "D": first_fold,
        "W": w_relay,
        "F": w_far_relays,
        "J": project,
    }

    def perform(segment):
        for word in segment:
            acts[word[0]](*(int(digit) for digit in word[1:]))

    before, between, after = front_order
    perform(before)

    def step_body(step, carry):
        for number, segment in enumerate(between):

            @pl.when(step == number + 1)
            def _():
                perform(segment)

        later_folds(step)
        return carry

    lax.fori_loop(0, planes, step_body, 0)
    finish()
    perform(after)
    square = jnp.zeros((rows, 1), jnp.float32)
    for quarter in range(pieces):
        for near in range(2):
            cols = w_cols(quarter, near == 0)
            index = quarter * 2 + near
            arrived(part_in.at[:, cols], part_sem.at[index])
            stream = stream_ref[:, cols] + part_in[:, cols].astype(jnp.float32)
            stream_ref[:, cols] = stream
            square = square + jnp.sum(stream * stream, 1, keepdims=True)
            left(part_out.at[:, cols], part_sem_s.at[index])
    inverse = lax.rsqrt(square / model + eps_norm)
    for index in range(2 * pieces):
        cols = slice(index * chunk, (index + 1) * chunk)
        normed_ref[:, cols] = (stream_ref[:, cols] * inverse * gain_ref[:, cols]).astype(
            normed_ref.dtype
        )

    left(q_buf.at[y], q_sem.at[0])
    for quarter in range(pieces):
        left(w_block(quarter, z, y, c), w_side_s.at[quarter])

    def drain(plane, carry):
        reached = plane <= z

        @pl.when(reached)
        def _():
            left(kn.at[1 - y, plane, y, c], kn_side_s.at[plane])
            left(kn.at[y, plane, y, c], kn_twin_s.at[plane, y])
            left(kn.at[y, plane, 1 - y, c], kn_twin_s.at[plane, 1 - y])

        @pl.when(reached & has_up)
        def _():
            left(kn.at[:, plane, y, c], kn_up.at[plane])
            left(kc.at[plane, y, c], kc_up.at[plane])
            for quarter in range(pieces):
                for line in range(2):
                    left(w_block(quarter, plane, line, c), w_up.at[quarter, plane, line])

        @pl.when((plane >= z) & has_down)
        def _():
            left(kc.at[plane, y, c], kc_down.at[plane])
            for quarter in range(pieces):
                for line in range(2):
                    left(w_block(quarter, plane, line, c), w_down.at[quarter, plane, line])

        @pl.when(mine(plane))
        def _():
            for line in range(2):
                left(kc.at[plane, line, c], kc_twin_s.at[plane, line])

        @pl.when(jnp.logical_not(mine(plane)))
        def _():
            left(kc.at[plane, y, c], kc_side_s.at[plane])

        for quarter in range(pieces):
            for line in range(2):
                at = (quarter, plane, line)
                left(w_block(quarter, plane, line, c), w_far_s.at[at])
                left(w_block(quarter, plane, line, c), w_twin_s.at[(*at, 0)])
                left(w_block(quarter, plane, line, c, False), w_twin_s.at[(*at, 1)])
        return carry

    lax.fori_loop(0, planes, drain, 0)


def partner_2(value, stride):
    mask = 2**stride
    pairs = [(source, source ^ mask) for source in range(lax.axis_size("head"))]
    return lax.ppermute(value, "head", pairs)


def turn_grp(value, shift):
    count = lax.axis_size("grp")
    return lax.ppermute(value, "grp", [(i, (i + shift) % count) for i in range(count)])


def attend_kernel(
    me_ref, query_ref, cache_ref, other_ref, pairs_ref, out_ref, new_ref, *, block, old_block, order
):
    head_width = query_ref.shape[1]
    step = pl.program_id(0)
    members, slots, local_rows = pairs_ref.shape[:3]

    @pl.when(step == 0)
    def _():
        for slot in range(slots):
            for member in range(members):
                apart = member ^ me_ref[0]
                place = 0
                for rank, bit in enumerate(order):
                    place = place + ((apart >> bit) & 1) * 2**rank
                first = (slot * members + member) * local_rows
                new_ref[first : first + local_rows, :] = pairs_ref[place, slot]

    query_rows = query_ref[...] * jnp.asarray(head_width ** (-0.5), query_ref.dtype)

    def fold(carry, keys, values, mask):
        top, total, weighted = carry
        scores = lax.dot_general(
            query_rows, keys, (((1,), (1,)), ((), ())), preferred_element_type=jnp.float32
        )
        if mask is not None:
            scores = jnp.where(mask, scores, -jnp.inf)
        new_top = jnp.maximum(top, jnp.max(scores, 1, keepdims=True))
        exps = jnp.exp(scores - new_top)
        shrink = jnp.exp(top - new_top)
        total = total * shrink + jnp.sum(exps, 1, keepdims=True)
        weighted = weighted * shrink + jnp.dot(
            exps.astype(jnp.bfloat16), values, preferred_element_type=jnp.float32
        )
        return new_top, total, weighted

    rows = query_rows.shape[0]
    carry = (
        jnp.full((rows, 1), -jnp.inf, jnp.float32),
        jnp.zeros((rows, 1), jnp.float32),
        jnp.zeros((rows, head_width), jnp.float32),
    )
    row_at = lax.broadcasted_iota(jnp.int32, (rows, block), 0)
    col_at = lax.broadcasted_iota(jnp.int32, (rows, block), 1)
    here = pl.ds(step * block, block)
    carry = fold(
        carry, new_ref[here, :head_width], new_ref[here, head_width:], col_at <= row_at
    )
    for old_ref in (cache_ref, other_ref):
        for first in range(0, old_ref.shape[0], old_block):
            part = pl.ds(first, old_block)
            carry = fold(carry, old_ref[part, :head_width], old_ref[part, head_width:], None)

    def earlier(index, carry):
        part = pl.ds(index * block, block)
        return fold(carry, new_ref[part, :head_width], new_ref[part, head_width:], None)

    top, total, weighted = lax.fori_loop(0, step, earlier, carry)
    out_ref[...] = (weighted / total).astype(out_ref.dtype)


def attend(me, queries, new_pairs, cached, cached_other, order):
    length, head_width = queries.shape
    block = min(512, length)
    old_block = min(1024, cached.shape[0])
    return pl.pallas_call(
        functools.partial(attend_kernel, block=block, old_block=old_block, order=order),
        grid_spec=pltpu.PrefetchScalarGridSpec(
            num_scalar_prefetch=1,
            grid=(length // block,),
            in_specs=[
                pl.BlockSpec((block, head_width), lambda i, me: (i, 0)),
                pl.BlockSpec(cached.shape, lambda i, me: (0, 0)),
                pl.BlockSpec(cached_other.shape, lambda i, me: (0, 0)),
                pl.BlockSpec(new_pairs.shape, lambda i, me: (0, 0, 0, 0)),
            ],
            out_specs=pl.BlockSpec((block, head_width), lambda i, me: (i, 0)),
            scratch_shapes=[pltpu.VMEM((length, 2 * head_width), jnp.bfloat16)],
        ),
        out_shape=jax.ShapeDtypeStruct((length, head_width), jnp.bfloat16),
        cost_estimate=pl.CostEstimate(
            flops=4 * length * head_width * (length // 2 + 2 * cached.shape[0]),
            bytes_accessed=8 * length * head_width * 2,
            transcendentals=length * (length // 2 + 2 * cached.shape[0]),
        ),
    )(me, queries, cached, cached_other, new_pairs)


def front_general(queries, new_kv, cache, resid, w_out, norm_gain):
    axis_count = lax.axis_size("head")
    local_rows = queries.shape[0]
    seq_count = queries.shape[1]
    head_count = queries.shape[2]
    head_width = queries.shape[3]
    pair_heads = new_kv.shape[2]
    group_size = head_count // pair_heads
    model_width = resid.shape[2]
    row_count = local_rows * seq_count
    slots = seq_count * pair_heads
    across = [[c * group_size + j for c in range(slots)] for j in range(group_size)]
    query_slots = queries.reshape(local_rows, axis_count, head_width).transpose(1, 0, 2)
    pair_slots = new_kv.reshape(local_rows, slots, 2 * head_width).transpose(1, 0, 2)
    pair_slots = lax.all_to_all(
        pair_slots, "head", split_axis=0, concat_axis=0, axis_index_groups=across, tiled=True
    )
    grp_count = lax.axis_size("grp")
    grp_me = lax.axis_index("grp")
    part_width = model_width // grp_count
    w_part = lax.dynamic_slice_in_dim(w_out, grp_me * part_width, part_width, 2)
    bits = group_size.bit_length() - 1
    order = tuple(range(1, bits)) + (0,)
    cache_rows = cache[0]
    pairs = pair_slots[None]
    for bit in order[:-1]:
        cache_rows = jnp.concatenate([cache_rows, partner_2(cache_rows, bit)], 0)
    head_queries = lax.all_to_all(query_slots, "head", split_axis=0, concat_axis=0, tiled=True)
    for bit in order[:-1]:
        pairs = jnp.concatenate([pairs, partner_2(pairs, bit)], 0)
    w_part, pairs, cache_rows, head_queries = lax.optimization_barrier(
        (w_part, pairs, cache_rows, head_queries)
    )
    w_part = lax.all_gather(w_part, "head", axis=1, tiled=True)
    w_part = w_part.reshape(head_count * head_width, part_width)
    cache_other = partner_2(cache_rows, 0)
    pairs = jnp.concatenate([pairs, partner_2(pairs, 0)], 0)
    me = (lax.axis_index("head") % group_size).astype(jnp.int32).reshape(1)
    attended = attend(
        me, head_queries.reshape(-1, head_width), pairs, cache_rows, cache_other, order
    )
    returned = lax.all_to_all(
        attended.reshape(axis_count, local_rows, head_width),
        "head",
        split_axis=0,
        concat_axis=0,
        tiled=True,
    )
    attn_rows = returned.reshape(seq_count, head_count, local_rows, head_width)
    attn_rows = attn_rows.transpose(2, 0, 1, 3).reshape(row_count, head_count * head_width)
    parts = []
    for shift in range(1, grp_count):
        far_rows = turn_grp(attn_rows, shift)
        far_part = jnp.dot(far_rows, w_part, preferred_element_type=jnp.float32)
        parts.append(turn_grp(far_part.astype(jnp.bfloat16), -shift).astype(jnp.float32))
    projected = []
    near_part = jnp.dot(attn_rows, w_part, preferred_element_type=jnp.float32)
    for column in range(grp_count):
        piece = near_part
        for shift in range(1, grp_count):
            piece = jnp.where((grp_me + shift) % grp_count == column, parts[shift - 1], piece)
        projected.append(piece)
    projected = jnp.concatenate(projected, 1)
    stream = resid.reshape(row_count, model_width).astype(jnp.float32) + projected
    normed = stream * lax.rsqrt(jnp.mean(stream * stream, 1, keepdims=True) + eps_norm) * norm_gain
    normed = normed.astype(jnp.bfloat16)
    return stream, normed


def expert_body(
    normed_ref,
    stream_ref,
    info_ref,
    out_ref,
    top_count,
    w_in,
    w_down,
    rows_buf,
    info_buf,
    picked,
    inbox,
    outbox,
    answer,
    dense,
    summed,
    sums_in,
    sums_out,
    row_line,
    row_sent,
    info_line,
    info_sent,
    in_sem,
    in_sem_s,
    ans_sem,
    ans_sem_s,
    sum_sem,
    sum_sem_s,
):
    planes, rows, model = rows_buf.shape
    near, cap = inbox.shape[1:3]
    hidden_width = w_down.shape[0]
    chunks = row_line.shape[1]
    chunk = model // chunks
    g = lax.axis_index("grp")
    me = lax.axis_index("head")
    z, own = me // near, me % near
    up, down = (g, me + near), (g, me - near)
    has_up, has_down = z < planes - 1, z > 0

    def copy(src, dst, sent, got, peer):
        return pltpu.make_async_remote_copy(
            src_ref=src,
            dst_ref=dst,
            send_sem=sent,
            recv_sem=got,
            device_id=peer,
            device_id_type=MESH,
        )

    def arrived(dst, got):
        copy(dst, dst, got, got, (g, me ^ 1)).wait_recv()

    def left(src, sent):
        copy(src, src, sent, sent, (g, me ^ 1)).wait_send()

    def cols(index):
        return slice(index * chunk, (index + 1) * chunk)

    def by_plane(values):
        chosen = jnp.int32(values[0])
        for index, value in enumerate(values[1:], 1):
            chosen = jnp.where(z == index, value, chosen)
        return chosen

    def send_info(src, plane, way, peer):
        copy(src, info_buf.at[plane], info_sent.at[way, plane], info_line.at[plane], peer).start()

    def send_row(src, index, plane, way, peer):
        dst = rows_buf.at[plane, :, cols(index)]
        copy(src, dst, row_sent.at[way, plane, index], row_line.at[plane, index], peer).start()

    def slots_of(info):
        at = lax.broadcasted_iota(jnp.int32, (near * cap, rows), 0) + z * (near * cap)
        at = at.astype(jnp.float32)
        return [at == info[rank : rank + 1, :] for rank in range(top_count)]

    def pick(plane, info, load):
        chosen = functools.reduce(jnp.logical_or, slots_of(info))
        chosen = jnp.where(chosen, 1.0, 0.0).astype(jnp.bfloat16)
        for index in range(chunks):
            part = jnp.dot(chosen, load(index), preferred_element_type=jnp.float32)
            picked[plane, :, :, cols(index)] = part.astype(jnp.bfloat16).reshape(near, cap, chunk)
            for mask in range(1, near):
                other = own ^ mask
                copy(
                    picked.at[plane, other, :, cols(index)],
                    inbox.at[plane, own, :, cols(index)],
                    in_sem_s.at[plane, other],
                    in_sem.at[plane, own],
                    (g, me ^ mask),
                ).start()
            inbox[plane, own, :, cols(index)] = picked[plane, own, :, cols(index)]

    def receive(plane):
        way = (plane > z).astype(jnp.int32)
        onward = jnp.where(way == 0, planes - 1 - z, z) > 0
        peer = (g, me + near - 2 * near * way)
        arrived(info_buf.at[plane], info_line.at[plane])

        @pl.when(onward)
        def _():
            send_info(info_buf.at[plane], plane, way, peer)

        def load(index):
            block = rows_buf.at[plane, :, cols(index)]
            arrived(block, row_line.at[plane, index])

            @pl.when(onward)
            def _():
                send_row(block, index, plane, way, peer)

            return block[...]

        pick(plane, info_buf[plane], load)

    def run_expert(plane):
        for mask in range(1, near):
            arrived(inbox.at[plane, own ^ mask], in_sem.at[plane, own ^ mask])
        inner = jnp.dot(
            inbox[plane].reshape(near * cap, model), w_in[...], preferred_element_type=jnp.float32
        )
        gate, value = inner[:, :hidden_width], inner[:, hidden_width:]
        hidden = (gate / (1.0 + jnp.exp(-gate)) * value).astype(jnp.bfloat16)
        for index in range(chunks):
            part = jnp.dot(hidden, w_down[:, cols(index)], preferred_element_type=jnp.float32)
            outbox[plane, :, :, cols(index)] = part.astype(jnp.bfloat16).reshape(near, cap, chunk)
            for mask in range(1, near):
                other = own ^ mask
                copy(
                    outbox.at[plane, other, :, cols(index)],
                    answer.at[plane, own, :, cols(index)],
                    ans_sem_s.at[plane, other],
                    ans_sem.at[plane, own],
                    (g, me ^ mask),
                ).start()
            answer[plane, own, :, cols(index)] = outbox[plane, own, :, cols(index)]

    def combine(plane, info, store):
        for mask in range(1, near):
            arrived(answer.at[plane, own ^ mask], ans_sem.at[plane, own ^ mask])
        gates = jnp.zeros((near * cap, rows), jnp.float32)
        for rank, here in enumerate(slots_of(info)):
            gates = jnp.where(here, info[top_count + rank : top_count + rank + 1, :], gates)
        high = gates.astype(jnp.bfloat16)
        low = (gates - high.astype(jnp.float32)).astype(jnp.bfloat16)
        for index in range(chunks):
            values = answer[plane, :, :, cols(index)].reshape(near * cap, chunk)
            total = jnp.zeros((rows, chunk), jnp.float32)
            for term in (high, low):
                total = total + lax.dot_general(
                    term, values, (((0,), (0,)), ((), ())), preferred_element_type=jnp.float32
                )
            store(index, total)

    def combine_far(plane):
        def store(index, total):
            dense[plane, :, cols(index)] = total

        combine(plane, info_buf[plane], store)

    def pass_sum(target, index):
        way = (target < z).astype(jnp.int32)
        has_in = jnp.where(way == 0, z, planes - 1 - z) > 0
        peer = (g, me + near - 2 * near * way)
        block = sums_in.at[way, target, :, cols(index)]
        at = (way, target, index)

        @pl.when(has_in)
        def _():
            arrived(block, sum_sem.at[at])
            sums_out[target, :, cols(index)] = (
                dense[target, :, cols(index)] + block[...].astype(jnp.float32)
            ).astype(jnp.bfloat16)

        @pl.when(jnp.logical_not(has_in))
        def _():
            sums_out[target, :, cols(index)] = dense[target, :, cols(index)].astype(jnp.bfloat16)

        copy(
            sums_out.at[target, :, cols(index)], block, sum_sem_s.at[at], sum_sem.at[at], peer
        ).start()

    def combine_own():
        def store(index, total):
            summed[:, cols(index)] = stream_ref[:, cols(index)] + total

        combine(z, info_ref[...], store)

    @pl.when(has_up)
    def _():
        send_info(info_ref, z, 0, up)

    @pl.when(has_down)
    def _():
        send_info(info_ref, z, 1, down)

    for index in range(chunks):
        block = normed_ref.at[:, cols(index)]

        @pl.when(has_up)
        def _():
            send_row(block, index, z, 0, up)

        @pl.when(has_down)
        def _():
            send_row(block, index, z, 1, down)

    own_at = visit_order.index(tuple(range(planes)))
    plane_at = [by_plane(values) for values in visit_order]
    target_at = [by_plane(values) for values in return_order]

    def perform(segment):
        for word in segment:
            first = int(word[1])
            if word[0] == "P" and first == own_at:
                pick(z, info_ref[...], lambda index: normed_ref[:, cols(index)])
            elif word[0] == "P":
                receive(plane_at[first])
            elif word[0] == "E" and first == own_at:
                combine_own()
            elif word[0] == "E":
                combine_far(plane_at[first])
            else:
                pass_sum(target_at[first], int(word[2]))

    def step_body(step, carry):
        for number, segment in enumerate(expert_order[:-1]):

            @pl.when(step == number)
            def _():
                perform(segment)

        plane = plane_at[0]
        for number, value in enumerate(plane_at[1:], 1):
            plane = jnp.where(step == number, value, plane)
        run_expert(plane)
        return carry

    lax.fori_loop(0, planes, step_body, 0)
    perform(expert_order[-1])

    for index in range(chunks):

        @pl.when(has_down)
        def _():
            block = sums_in.at[0, z, :, cols(index)]
            arrived(block, sum_sem.at[0, z, index])
            summed[:, cols(index)] = summed[:, cols(index)] + block[...].astype(jnp.float32)

        @pl.when(has_up)
        def _():
            block = sums_in.at[1, z, :, cols(index)]
            arrived(block, sum_sem.at[1, z, index])
            summed[:, cols(index)] = summed[:, cols(index)] + block[...].astype(jnp.float32)

        out_ref[:, cols(index)] = summed[:, cols(index)].astype(out_ref.dtype)

    def drain(plane, carry):
        @pl.when((plane <= z) & has_up)
        def _():
            left(info_buf.at[plane], info_sent.at[0, plane])
            for index in range(chunks):
                left(rows_buf.at[plane, :, cols(index)], row_sent.at[0, plane, index])

        @pl.when((plane >= z) & has_down)
        def _():
            left(info_buf.at[plane], info_sent.at[1, plane])
            for index in range(chunks):
                left(rows_buf.at[plane, :, cols(index)], row_sent.at[1, plane, index])

        for mask in range(1, near):
            left(picked.at[plane, own ^ mask], in_sem_s.at[plane, own ^ mask])
            left(outbox.at[plane, own ^ mask], ans_sem_s.at[plane, own ^ mask])

        for index in range(chunks):

            @pl.when(plane > z)
            def _():
                left(sums_out.at[plane, :, cols(index)], sum_sem_s.at[0, plane, index])

            @pl.when(plane < z)
            def _():
                left(sums_out.at[plane, :, cols(index)], sum_sem_s.at[1, plane, index])

        return carry

    lax.fori_loop(0, planes, drain, 0)


def layer_kernel(*refs, top_count, experts, cap, front_count):
    inputs, out_ref, rest = refs[:10], refs[10], refs[11:]
    ids_ref, gates_ref, w_in_ref, w_down_ref = inputs[6:]
    stream, normed, info, w_in, w_down, load_sem = rest[:6]
    front_scratch, expert_scratch = rest[6 : 6 + front_count], rest[6 + front_count :]

    def route():
        rows = ids_ref.shape[1]
        ids = ids_ref[...].astype(jnp.float32)
        named = lax.broadcasted_iota(jnp.int32, (experts, rows), 0).astype(jnp.float32)
        hits = [named == ids[rank : rank + 1] for rank in range(top_count)]
        onehot = sum(jnp.where(hit, 1.0, 0.0) for hit in hits).astype(jnp.bfloat16)
        first = lax.broadcasted_iota(jnp.int32, (rows, rows), 0)
        second = lax.broadcasted_iota(jnp.int32, (rows, rows), 1)
        before = jnp.where(first < second, 1.0, 0.0).astype(jnp.bfloat16)
        earlier = jnp.dot(onehot, before, preferred_element_type=jnp.float32)
        info[...] = jnp.zeros(info.shape, info.dtype)
        for rank, hit in enumerate(hits):
            place = jnp.sum(jnp.where(hit, earlier, 0.0), 0, keepdims=True)
            info[rank : rank + 1] = ids[rank : rank + 1] * cap + place
        info[top_count : 2 * top_count] = gates_ref[...]

    loads = (
        pltpu.make_async_copy(w_in_ref, w_in, load_sem.at[0]),
        pltpu.make_async_copy(w_down_ref, w_down, load_sem.at[1]),
    )
    for load in loads:
        load.start()
    front_body(*inputs[:6], stream, normed, route, *front_scratch)
    for load in loads:
        load.wait()
    expert_body(normed, stream, info, out_ref, top_count, w_in, w_down, *expert_scratch)


def layer(queries, pairs, cached, w_out, resid, gain, ids, gates, w_in, w_down, axis_count):
    rows, heads, width = queries.shape
    top_count = ids.shape[0]
    cap = 2 * rows * top_count // axis_count
    lines = -(-2 * top_count // 8) * 8
    group = heads // 2
    near = 4
    planes = axis_count // near
    model = w_out.shape[2]
    slice_rows = w_out.shape[1]
    page = cached.shape[0]
    pieces = 4
    chunks = 4
    dma = pltpu.SemaphoreType.DMA
    anywhere = pl.BlockSpec(memory_space=pl.ANY)
    inside = pl.BlockSpec(memory_space=pltpu.VMEM)

    def half(*shape):
        return pltpu.VMEM(shape, jnp.bfloat16)

    def full(*shape):
        return pltpu.VMEM(shape, jnp.float32)

    front_scratch = [
        half(rows, heads, width),
        half(2, group, rows, width),
        half(rows, 2, 2 * width),
        half(2, rows, 2 * width),
        half(2, group, rows, width),
        half(2, planes, 2, 2, rows, 2 * width),
        half(planes, 2, 2, page, 2 * width),
        half(group, planes, 2, 2, slice_rows, model),
        full(2, group, rows, width),
        full(2, group, rows, 128),
        full(2, group, rows, 128),
        half(2, rows, group * width),
        half(rows, model),
        half(rows, model),
        dma((4,)),
        dma((2,)),
        dma((planes,)),
        dma((planes,)),
        dma((planes,)),
        dma((planes,)),
        dma((planes, 2)),
        dma((planes, 2)),
        dma((planes,)),
        dma((planes,)),
        dma((planes,)),
        dma((planes,)),
        dma((planes,)),
        dma((planes, 2)),
        dma((planes, 2)),
        dma((pieces, planes, 2)),
        dma((pieces, planes, 2)),
        dma((pieces, planes, 2)),
        dma((pieces,)),
        dma((pieces,)),
        dma((pieces, planes, 2)),
        dma((pieces, planes, 2)),
        dma((pieces, planes, 2, 2)),
        dma((pieces, planes, 2, 2)),
        dma((2 * pieces,)),
        dma((2 * pieces,)),
    ]
    expert_scratch = [
        half(planes, rows, model),
        full(planes, lines, rows),
        half(planes, near, cap, model),
        half(planes, near, cap, model),
        half(planes, near, cap, model),
        half(planes, near, cap, model),
        full(planes, rows, model),
        full(rows, model),
        half(2, planes, rows, model),
        half(planes, rows, model),
        dma((planes, chunks)),
        dma((2, planes, chunks)),
        dma((planes,)),
        dma((2, planes)),
        dma((planes, near)),
        dma((planes, near)),
        dma((planes, near)),
        dma((planes, near)),
        dma((2, planes, chunks)),
        dma((2, planes, chunks)),
    ]
    return pl.pallas_call(
        functools.partial(
            layer_kernel,
            top_count=top_count,
            experts=axis_count,
            cap=cap,
            front_count=len(front_scratch),
        ),
        out_shape=jax.ShapeDtypeStruct((rows, model), jnp.bfloat16),
        in_specs=[anywhere] * 4 + [inside] * 4 + [anywhere] * 2,
        out_specs=inside,
        scratch_shapes=[
            full(rows, model),
            half(rows, model),
            full(lines, rows),
            half(*w_in.shape),
            half(*w_down.shape),
            dma((2,)),
            *front_scratch,
            *expert_scratch,
        ],
        compiler_params=pltpu.CompilerParams(
            collective_id=0, has_side_effects=True, vmem_limit_bytes=60 * 2**20
        ),
        cost_estimate=pl.CostEstimate(
            flops=4 * 2 * group * rows * width * 4 * axis_count * rows
            + 4 * rows * group * width * model
            + 6 * planes * near * cap * model * w_down.shape[0],
            bytes_accessed=12 * 2**20,
            transcendentals=2 * group * rows * axis_count * rows,
        ),
    )(queries, pairs, cached, w_out, resid, gain, ids, gates, w_in, w_down)


def experts(stream, normed, expert_ids, expert_gates, w_in, w_down):
    row_count, model_width = stream.shape
    axis_count = lax.axis_size("head")
    top_count = expert_ids.shape[2]
    flat_ids = expert_ids.reshape(-1)
    local_experts = w_in.shape[0]
    experts = local_experts * axis_count
    capacity = max(2, 2 * row_count * top_count // experts)
    onehot = (flat_ids[:, None] == jnp.arange(experts, dtype=jnp.int32)[None, :]).astype(jnp.int32)
    before = jnp.tri(flat_ids.shape[0], k=-1, dtype=jnp.bfloat16)
    earlier = jnp.dot(
        before, onehot.astype(jnp.bfloat16), preferred_element_type=jnp.float32
    ).astype(jnp.int32)
    slot_rank = jnp.sum(earlier * onehot, 1)
    target = flat_ids * capacity + slot_rank
    target = target.reshape(row_count, top_count)
    places = jnp.arange(experts * capacity, dtype=jnp.int32)
    chosen = jnp.zeros((experts * capacity, row_count), jnp.bool_)
    gate_of = jnp.zeros((row_count, experts * capacity), jnp.float32)
    gates = expert_gates.reshape(row_count, top_count)
    for rank in range(top_count):
        chosen = chosen | (places[:, None] == target[None, :, rank])
        gate_of = jnp.where(
            target[:, rank, None] == places[None, :], gates[:, rank, None], gate_of
        )
    outgoing = jnp.dot(
        chosen.astype(jnp.bfloat16), normed, preferred_element_type=jnp.float32
    ).astype(jnp.bfloat16)
    outgoing = outgoing.reshape(axis_count, local_experts, capacity, model_width)
    hidden_width = w_down.shape[1]
    inner_act = jnp.einsum(
        "semd,edf->semf",
        lax.all_to_all(outgoing, "head", split_axis=0, concat_axis=0, tiled=True),
        w_in,
        preferred_element_type=jnp.float32,
    )
    hidden = (jax.nn.silu(inner_act[..., :hidden_width]) * inner_act[..., hidden_width:]).astype(
        jnp.bfloat16
    )
    answered = jnp.einsum(
        "semf,efd->semd", hidden, w_down, preferred_element_type=jnp.float32
    ).astype(jnp.bfloat16)
    returned_rows = lax.all_to_all(answered, "head", split_axis=0, concat_axis=0, tiled=True)
    picked = returned_rows.reshape(experts * capacity, model_width)
    expert_sum = jnp.zeros((row_count, model_width), jnp.float32)
    rest = gate_of
    for _ in range(3):
        term = lax.reduce_precision(rest, 8, 7)
        rest = rest - term
        expert_sum = expert_sum + jnp.dot(
            term.astype(jnp.bfloat16), picked, preferred_element_type=jnp.float32
        )
    return (stream + expert_sum).astype(jnp.bfloat16)


def local(queries, new_kv, cache, resid, w_out, norm_gain, expert_ids, expert_gates, w_in, w_down):
    axis_count = lax.axis_size("head")
    local_rows, seq_count, head_count, head_width = queries.shape
    pair_heads = new_kv.shape[2]
    fits = (
        seq_count == 1
        and pair_heads == 2
        and lax.axis_size("grp") == 2
        and axis_count == 4 * (len(front_order[1]) + 1)
        and w_out.shape[2] % 1024 == 0
        and cache.shape[0] == 1
        and w_out.shape[1] * axis_count == head_width
        and w_out.shape[1] % 16 == 0
        and local_rows % 32 == 0
        and cache.shape[1] * 2 % 128 == 0
        and head_count % 4 == 0
    )
    top_count = expert_ids.shape[2]
    experts_count = w_in.shape[0] * axis_count
    row_count = local_rows * seq_count
    fits = (
        fits
        and w_in.shape[0] == 1
        and row_count % 128 == 0
        and (row_count * top_count * 2) % (16 * experts_count) == 0
    )
    if fits:
        out = layer(
            queries.reshape(local_rows, head_count, head_width),
            new_kv.reshape(local_rows, pair_heads, 2 * head_width),
            cache[0],
            w_out,
            resid.reshape(local_rows, -1),
            norm_gain.reshape(1, -1),
            expert_ids.reshape(local_rows, top_count).T,
            expert_gates.reshape(local_rows, top_count).T,
            w_in[0],
            w_down[0],
            axis_count,
        )
    else:
        stream, normed = front_general(queries, new_kv, cache, resid, w_out, norm_gain)
        out = experts(stream, normed, expert_ids, expert_gates, w_in, w_down)
    return out.reshape(resid.shape)


def solution(mesh):
    return jax.shard_map(
        local,
        mesh=mesh,
        in_specs=(
            P("head", "grp", None, None),
            P("head", "grp", None, None),
            P(("grp", "head"), None, None),
            P("head", "grp", None),
            P(None, "head", None),
            P(),
            P("head", "grp", None),
            P("head", "grp", None),
            P("head", None, None),
            P("head", None, None),
        ),
        out_specs=P("head", "grp", None),
        check_vma=False,
    )
```

```python
import functools

import jax
import jax.numpy as jnp
from jax import lax
from jax.experimental import pallas as pl
from jax.experimental.pallas import tpu as pltpu
from jax.sharding import PartitionSpec as P

eps_norm = 1e-06
MESH = pl.DeviceIdType.MESH
expert_order = (
    ("P301", "P000", "P200", "P011", "P211", "P022", "P222", "P033", "P233", "P100",),
    ("P113", "E0", "R10", "R11", "P322",),
    ("R12", "R13",),
    ("E1", "R20", "P333", "R21", "R22", "E2", "R00",),
    ("R23", "R01", "R02", "E3", "R03",),
)
visit_order = ((2, 2, 1, 1), (3, 3, 0, 0), (1, 0, 3, 2), (0, 1, 2, 3))
return_order = ((1, 0, 3, 2), (2, 2, 1, 1), (3, 3, 0, 0))
front_order = (
    ("o0", "s0", "o1", "L1", "W01", "s1", "q", "S0", "o2", "o3", "D",),
    (
        ("L2", "W02", "s2", "W11", "S1", "F00", "s3",),
        ("W03", "W21", "F10", "F01", "S2", "L3", "W12", "W31",),
        ("W22", "F11", "F30", "S3", "F02", "F03", "F12", "W13",),
    ),
    ("W23", "J0", "F20", "F21", "F13", "W32", "F31", "F22", "J1", "F23", "W33", "J2", "F32", "F33", "J3",),
)


def front_body(
    q_raw_ref,
    kv_raw_ref,
    cache_ref,
    w_ref,
    resid_ref,
    gain_ref,
    stream_ref,
    normed_ref,
    aside,
    q_raw,
    q_ref,
    kv_raw,
    kv_ref,
    q_buf,
    kn,
    kc,
    wb,
    acc,
    top,
    total,
    att,
    part_out,
    part_in,
    local_sem,
    q_sem,
    kn_line,
    kn_up,
    kn_side,
    kn_side_s,
    kn_twin,
    kn_twin_s,
    kc_line,
    kc_up,
    kc_down,
    kc_side,
    kc_side_s,
    kc_twin,
    kc_twin_s,
    w_line,
    w_up,
    w_down,
    w_side,
    w_side_s,
    w_far,
    w_far_s,
    w_twin,
    w_twin_s,
    part_sem,
    part_sem_s,
):
    planes = kn.shape[1]
    group = q_buf.shape[1]
    rows, width = q_buf.shape[2:]
    model = w_ref.shape[2]
    pieces = w_side.shape[0]
    half, chunk = model // 2, model // (2 * pieces)
    g = lax.axis_index("grp")
    me = lax.axis_index("head")
    z, y, c = me // 4, (me // 2) % 2, me % 2
    up, down = (g, me + 4), (g, me - 4)
    side, twin, far = (g, me + 2 - 4 * y), (g, me + 1 - 2 * c), (1 - g, me)
    has_up, has_down = z < planes - 1, z > 0

    raw = (
        pltpu.make_async_copy(kv_raw_ref, kv_raw, local_sem.at[0]),
        pltpu.make_async_copy(q_raw_ref, q_raw, local_sem.at[1]),
    )
    for item in raw:
        item.start()
    barrier = pltpu.get_barrier_semaphore()
    for peer in (side, twin, (g, me ^ 3), far):
        pl.semaphore_signal(barrier, inc=1, device_id=peer, device_id_type=MESH)

    @pl.when(has_up)
    def _():
        pl.semaphore_signal(barrier, inc=1, device_id=up, device_id_type=MESH)

    @pl.when(has_down)
    def _():
        pl.semaphore_signal(barrier, inc=1, device_id=down, device_id_type=MESH)

    pl.semaphore_wait(barrier, 4 + has_up.astype(jnp.int32) + has_down.astype(jnp.int32))

    def copy(src, dst, sent, got, peer):
        return pltpu.make_async_remote_copy(
            src_ref=src,
            dst_ref=dst,
            send_sem=sent,
            recv_sem=got,
            device_id=peer,
            device_id_type=MESH,
        )

    def arrived(dst, got):
        copy(dst, dst, got, got, twin).wait_recv()

    def left(src, sent):
        copy(src, src, sent, sent, twin).wait_send()

    def mine(plane):
        return plane // (planes // 2) == y

    cols_near = pl.ds(pl.multiple_of(g * half, half), half)
    raw[0].wait()
    kv_ref[...] = jnp.swapaxes(kv_raw[...], 0, 1)
    own_heads = pl.ds(y * group, group)
    other_heads = pl.ds((1 - y) * group, group)

    def w_cols(quarter, near):
        first = jnp.where(near, g, 1 - g) * half + quarter * chunk
        return pl.ds(pl.multiple_of(first, chunk), chunk)

    def w_block(quarter, plane, line, core, near=True):
        return wb.at[:, plane, line, core, :, w_cols(quarter, near)]

    def w_spread(src, quarter, plane, line):
        dst = w_block(quarter, plane, line, c)
        at = (quarter, plane, line)
        copy(src, dst, w_far_s.at[at], w_far.at[at], far).start()
        copy(src, dst, w_twin_s.at[(*at, 0)], w_twin.at[(*at, 0)], twin).start()

    def w_send_up(src, quarter, plane, line):
        at = (quarter, plane, line)

        @pl.when(has_up)
        def _():
            copy(src, w_block(quarter, plane, line, c), w_up.at[at], w_line.at[at], up).start()

    def w_send_down(src, quarter, plane, line):
        at = (quarter, plane, line)

        @pl.when(has_down)
        def _():
            copy(src, w_block(quarter, plane, line, c), w_down.at[at], w_line.at[at], down).start()

    def w_own_side(quarter):
        src = w_ref.at[other_heads, :, w_cols(quarter, True)]
        dst = w_block(quarter, z, y, c)
        copy(src, dst, w_side_s.at[quarter], w_side.at[quarter], side).start()

    def w_own(quarter):
        src = w_ref.at[own_heads, :, w_cols(quarter, True)]
        w_send_up(src, quarter, z, y)
        w_send_down(src, quarter, z, y)
        w_spread(src, quarter, z, y)

    def w_side_relay(quarter):
        block = w_block(quarter, z, 1 - y, c)
        arrived(block, w_side.at[quarter])
        w_send_up(block, quarter, z, 1 - y)
        w_send_down(block, quarter, z, 1 - y)
        w_spread(block, quarter, z, 1 - y)

    def w_relay(quarter, step):
        low, high = z - step, z + step
        for turn in range(2):
            line = y + turn - 2 * y * turn

            @pl.when(low >= 0)
            def _():
                block = w_block(quarter, low, line, c)
                arrived(block, w_line.at[quarter, low, line])
                w_send_up(block, quarter, low, line)
                w_spread(block, quarter, low, line)

            @pl.when(high < planes)
            def _():
                block = w_block(quarter, high, line, c)
                arrived(block, w_line.at[quarter, high, line])
                w_send_down(block, quarter, high, line)
                w_spread(block, quarter, high, line)

    def w_far_relay(quarter, plane):
        for line in range(2):
            block = w_block(quarter, plane, line, c, False)
            arrived(block, w_far.at[quarter, plane, line])
            at = (quarter, plane, line, 1)
            copy(block, block, w_twin_s.at[at], w_twin.at[at], twin).start()

    def w_far_relays(quarter, step):
        low, high = z - step, z + step

        @pl.when(low >= 0)
        def _():
            w_far_relay(quarter, low)

        if step > 0:

            @pl.when(high < planes)
            def _():
                w_far_relay(quarter, high)

    @pl.when(has_up)
    def _():
        copy(cache_ref, kc.at[z, y, c], kc_up.at[z], kc_line.at[z], up).start()
        copy(kv_ref, kn.at[:, z, y, c], kn_up.at[z], kn_line.at[z], up).start()

    @pl.when(has_down)
    def _():
        copy(cache_ref, kc.at[z, y, c], kc_down.at[z], kc_line.at[z], down).start()

    copy(kv_ref.at[1 - y], kn.at[1 - y, z, y, c], kn_side_s.at[z], kn_side.at[z], side).start()
    w_own_side(0)
    copy(kv_ref.at[y], kn.at[y, z, y, c], kn_twin_s.at[z, y], kn_twin.at[z, y], twin).start()

    @pl.when(mine(z))
    def _():
        copy(cache_ref, kc.at[z, y, c], kc_twin_s.at[z, y], kc_twin.at[z, y], twin).start()

    @pl.when(jnp.logical_not(mine(z)))
    def _():
        copy(cache_ref, kc.at[z, y, c], kc_side_s.at[z], kc_side.at[z], side).start()

    locals_ = (
        pltpu.make_async_copy(kv_ref.at[y], kn.at[y, z, y, c], local_sem.at[0]),
        pltpu.make_async_copy(cache_ref, kc.at[z, y, c], local_sem.at[2]),
        pltpu.make_async_copy(
            w_ref.at[own_heads, :, cols_near], wb.at[:, z, y, c, :, cols_near], local_sem.at[3]
        ),
    )
    for item in locals_:
        item.start()
    raw[1].wait()
    q_ref[...] = jnp.swapaxes(q_raw[...], 0, 1).reshape(q_ref.shape)
    copy(q_ref.at[1 - y], q_buf.at[y], q_sem.at[0], q_sem.at[1], side).start()
    for piece in range(1, pieces):
        w_own_side(piece)
    q_buf[y] = q_ref[y]
    aside()

    def from_side_new(plane):
        block = kn.at[y, plane, 1 - y, c]
        arrived(block, kn_side.at[plane])
        copy(block, block, kn_twin_s.at[plane, 1 - y], kn_twin.at[plane, 1 - y], twin).start()

    def from_side_old(plane):
        @pl.when(mine(plane))
        def _():
            block = kc.at[plane, 1 - y, c]
            arrived(block, kc_side.at[plane])
            copy(block, block, kc_twin_s.at[plane, 1 - y], kc_twin.at[plane, 1 - y], twin).start()

    def spread_old(plane):
        block = kc.at[plane, y, c]

        @pl.when(mine(plane))
        def _():
            copy(block, block, kc_twin_s.at[plane, y], kc_twin.at[plane, y], twin).start()

        @pl.when(jnp.logical_not(mine(plane)))
        def _():
            copy(block, block, kc_side_s.at[plane], kc_side.at[plane], side).start()

    def relay(step):
        low, high = z - step, z + step

        @pl.when(high < planes)
        def _():
            old = kc.at[high, y, c]
            arrived(old, kc_line.at[high])

            @pl.when(has_down)
            def _():
                copy(old, old, kc_down.at[high], kc_line.at[high], down).start()

            spread_old(high)

        @pl.when(low >= 0)
        def _():
            old, new = kc.at[low, y, c], kn.at[:, low, y, c]
            arrived(old, kc_line.at[low])

            @pl.when(has_up)
            def _():
                copy(old, old, kc_up.at[low], kc_line.at[low], up).start()

            arrived(new, kn_line.at[low])

            @pl.when(has_up)
            def _():
                copy(new, new, kn_up.at[low], kn_line.at[low], up).start()

            there, here = kn.at[1 - y, low, y, c], kn.at[y, low, y, c]
            copy(there, there, kn_side_s.at[low], kn_side.at[low], side).start()
            copy(here, here, kn_twin_s.at[low, y], kn_twin.at[low, y], twin).start()
            spread_old(low)

    def from_side(step):
        low, high = z - step, z + step

        @pl.when(low >= 0)
        def _():
            from_side_new(low)
            from_side_old(low)

        if step > 0:

            @pl.when(high < planes)
            def _():
                from_side_old(high)

    scale = width ** (-0.5)
    tile = 2
    tile_rows = tile * rows

    def fold(keys, values, diagonal):
        def lines(line, carry):
            for part in range(group // tile):
                heads = pl.ds(part * tile, tile)
                queries = q_buf[line, heads].reshape(tile_rows, width)
                queries = queries * jnp.asarray(scale, queries.dtype)
                scores = lax.dot_general(
                    queries, keys(), (((1,), (1,)), ((), ())), preferred_element_type=jnp.float32
                )
                pieces = [
                    scores[:, first : first + 128] for first in range(0, scores.shape[1], 128)
                ]
                if diagonal:
                    row_at = lax.broadcasted_iota(jnp.int32, (tile_rows, 128), 0) % rows
                    ahead = row_at - lax.broadcasted_iota(jnp.int32, (tile_rows, 128), 1)
                    ahead = ahead + (line * 2 + c) * rows
                    pieces = [
                        jnp.where(ahead >= index * 128, piece, -jnp.inf)
                        for index, piece in enumerate(pieces)
                    ]
                best = functools.reduce(jnp.maximum, pieces)
                best = jnp.max(best, 1, keepdims=True)
                if diagonal:
                    new_top = jnp.broadcast_to(best, (tile_rows, 128))
                else:
                    old_top = top[line, heads].reshape(tile_rows, 128)
                    new_top = jnp.maximum(old_top, best)
                exps = [jnp.exp(piece - new_top) for piece in pieces]
                new_total = functools.reduce(jnp.add, exps)
                weighted = jnp.dot(
                    jnp.concatenate([part_.astype(jnp.bfloat16) for part_ in exps], 1),
                    values(),
                    preferred_element_type=jnp.float32,
                )
                if not diagonal:
                    shrink = jnp.exp(old_top - new_top)
                    new_total = new_total + total[line, heads].reshape(tile_rows, 128) * shrink
                    weighted = weighted + acc[line, heads].reshape(
                        tile_rows, width
                    ) * jnp.concatenate([shrink] * (width // 128), 1)
                top[line, heads] = new_top.reshape(tile, rows, 128)
                total[line, heads] = new_total.reshape(tile, rows, 128)
                acc[line, heads] = weighted.reshape(tile, rows, width)
            return carry

        lax.fori_loop(0, 2, lines, 0, unroll=2)

    def new_part(plane, first):
        return lambda: kn[y, plane, :, :, :, first : first + width].reshape(4 * rows, width)

    page = kc.shape[3]

    def old_part(plane, line, first):
        return lambda: kc[plane, line, :, :, first : first + width].reshape(2 * page, width)

    def twins_new(plane):
        for line in range(2):
            arrived(kn.at[y, plane, line, 1 - c], kn_twin.at[plane, line])

    def twins_old(plane):
        for line in range(2):
            arrived(kc.at[plane, line, 1 - c], kc_twin.at[plane, line])

    def first_fold():
        twins_new(z)
        fold(new_part(z, 0), new_part(z, width), True)

    def queries_here():
        arrived(q_buf.at[1 - y], q_sem.at[1])
        for item in locals_:
            item.wait()

    def later_folds(step):
        low, high = z - step, z + step

        @pl.when((step >= 1) & (low >= 0))
        def _():
            twins_new(low)
            fold(new_part(low, 0), new_part(low, width), False)

        def old_body(index, carry):
            plane = jnp.where(index == 0, low, high)
            valid = (plane >= 0) & (plane < planes) & ((index == 0) | (step > 0))

            @pl.when(valid & mine(plane))
            def _():
                twins_old(plane)

                def line_body(line, carry):
                    fold(old_part(plane, line, 0), old_part(plane, line, width), False)
                    return carry

                lax.fori_loop(0, 2, line_body, 0)

            return carry

        lax.fori_loop(0, 2, old_body, 0)

    def finish():
        for line in range(2):
            for head in range(group):
                att[line, :, head * width : (head + 1) * width] = (
                    acc[line, head] / jnp.sum(total[line, head], 1, keepdims=True)
                ).astype(att.dtype)

    def project(quarter):
        for near in range(2):
            for plane in range(planes):
                for line in range(2):
                    arrived(
                        w_block(quarter, plane, line, 1 - c, near == 0),
                        w_twin.at[quarter, plane, line, near],
                    )
            cols = w_cols(quarter, near == 0)
            weights = wb[:, :, :, :, :, cols].reshape(group * width, chunk)
            both = jnp.dot(
                att[...].reshape(2 * rows, group * width),
                weights,
                preferred_element_type=jnp.float32,
            )
            there = jnp.where(y == 0, both[rows:], both[:rows])
            here = jnp.where(y == 0, both[:rows], both[rows:])
            part_out[:, cols] = there.astype(part_out.dtype)
            index = quarter * 2 + near
            block = part_out.at[:, cols]
            copy(block, part_in.at[:, cols], part_sem_s.at[index], part_sem.at[index], side).start()
            stream_ref[:, cols] = here + resid_ref[:, cols].astype(jnp.float32)

    acts = {
        "o": w_own,
        "s": w_side_relay,
        "L": relay,
        "S": from_side,
        "q": queries_here,
        "D": first_fold,
        "W": w_relay,
        "F": w_far_relays,
        "J": project,
    }

    def perform(segment):
        for word in segment:
            acts[word[0]](*(int(digit) for digit in word[1:]))

    before, between, after = front_order
    perform(before)

    def step_body(step, carry):
        for number, segment in enumerate(between):

            @pl.when(step == number + 1)
            def _():
                perform(segment)

        later_folds(step)
        return carry

    lax.fori_loop(0, planes, step_body, 0)
    finish()
    perform(after)
    square = jnp.zeros((rows, 1), jnp.float32)
    for quarter in range(pieces):
        for near in range(2):
            cols = w_cols(quarter, near == 0)
            index = quarter * 2 + near
            arrived(part_in.at[:, cols], part_sem.at[index])
            stream = stream_ref[:, cols] + part_in[:, cols].astype(jnp.float32)
            stream_ref[:, cols] = stream
            square = square + jnp.sum(stream * stream, 1, keepdims=True)
            left(part_out.at[:, cols], part_sem_s.at[index])
    inverse = lax.rsqrt(square / model + eps_norm)
    for index in range(2 * pieces):
        cols = slice(index * chunk, (index + 1) * chunk)
        normed_ref[:, cols] = (stream_ref[:, cols] * inverse * gain_ref[:, cols]).astype(
            normed_ref.dtype
        )

    left(q_buf.at[y], q_sem.at[0])
    for quarter in range(pieces):
        left(w_block(quarter, z, y, c), w_side_s.at[quarter])

    def drain(plane, carry):
        reached = plane <= z

        @pl.when(reached)
        def _():
            left(kn.at[1 - y, plane, y, c], kn_side_s.at[plane])
            left(kn.at[y, plane, y, c], kn_twin_s.at[plane, y])
            left(kn.at[y, plane, 1 - y, c], kn_twin_s.at[plane, 1 - y])

        @pl.when(reached & has_up)
        def _():
            left(kn.at[:, plane, y, c], kn_up.at[plane])
            left(kc.at[plane, y, c], kc_up.at[plane])
            for quarter in range(pieces):
                for line in range(2):
                    left(w_block(quarter, plane, line, c), w_up.at[quarter, plane, line])

        @pl.when((plane >= z) & has_down)
        def _():
            left(kc.at[plane, y, c], kc_down.at[plane])
            for quarter in range(pieces):
                for line in range(2):
                    left(w_block(quarter, plane, line, c), w_down.at[quarter, plane, line])

        @pl.when(mine(plane))
        def _():
            for line in range(2):
                left(kc.at[plane, line, c], kc_twin_s.at[plane, line])

        @pl.when(jnp.logical_not(mine(plane)))
        def _():
            left(kc.at[plane, y, c], kc_side_s.at[plane])

        for quarter in range(pieces):
            for line in range(2):
                at = (quarter, plane, line)
                left(w_block(quarter, plane, line, c), w_far_s.at[at])
                left(w_block(quarter, plane, line, c), w_twin_s.at[(*at, 0)])
                left(w_block(quarter, plane, line, c, False), w_twin_s.at[(*at, 1)])
        return carry

    lax.fori_loop(0, planes, drain, 0)


def partner_2(value, stride):
    mask = 2**stride
    pairs = [(source, source ^ mask) for source in range(lax.axis_size("head"))]
    return lax.ppermute(value, "head", pairs)


def turn_grp(value, shift):
    count = lax.axis_size("grp")
    return lax.ppermute(value, "grp", [(i, (i + shift) % count) for i in range(count)])


def attend_kernel(
    me_ref, query_ref, cache_ref, other_ref, pairs_ref, out_ref, new_ref, *, block, old_block, order
):
    head_width = query_ref.shape[1]
    step = pl.program_id(0)
    members, slots, local_rows = pairs_ref.shape[:3]

    @pl.when(step == 0)
    def _():
        for slot in range(slots):
            for member in range(members):
                apart = member ^ me_ref[0]
                place = 0
                for rank, bit in enumerate(order):
                    place = place + ((apart >> bit) & 1) * 2**rank
                first = (slot * members + member) * local_rows
                new_ref[first : first + local_rows, :] = pairs_ref[place, slot]

    query_rows = query_ref[...] * jnp.asarray(head_width ** (-0.5), query_ref.dtype)

    def fold(carry, keys, values, mask):
        top, total, weighted = carry
        scores = lax.dot_general(
            query_rows, keys, (((1,), (1,)), ((), ())), preferred_element_type=jnp.float32
        )
        if mask is not None:
            scores = jnp.where(mask, scores, -jnp.inf)
        new_top = jnp.maximum(top, jnp.max(scores, 1, keepdims=True))
        exps = jnp.exp(scores - new_top)
        shrink = jnp.exp(top - new_top)
        total = total * shrink + jnp.sum(exps, 1, keepdims=True)
        weighted = weighted * shrink + jnp.dot(
            exps.astype(jnp.bfloat16), values, preferred_element_type=jnp.float32
        )
        return new_top, total, weighted

    rows = query_rows.shape[0]
    carry = (
        jnp.full((rows, 1), -jnp.inf, jnp.float32),
        jnp.zeros((rows, 1), jnp.float32),
        jnp.zeros((rows, head_width), jnp.float32),
    )
    row_at = lax.broadcasted_iota(jnp.int32, (rows, block), 0)
    col_at = lax.broadcasted_iota(jnp.int32, (rows, block), 1)
    here = pl.ds(step * block, block)
    carry = fold(
        carry, new_ref[here, :head_width], new_ref[here, head_width:], col_at <= row_at
    )
    for old_ref in (cache_ref, other_ref):
        for first in range(0, old_ref.shape[0], old_block):
            part = pl.ds(first, old_block)
            carry = fold(carry, old_ref[part, :head_width], old_ref[part, head_width:], None)

    def earlier(index, carry):
        part = pl.ds(index * block, block)
        return fold(carry, new_ref[part, :head_width], new_ref[part, head_width:], None)

    top, total, weighted = lax.fori_loop(0, step, earlier, carry)
    out_ref[...] = (weighted / total).astype(out_ref.dtype)


def attend(me, queries, new_pairs, cached, cached_other, order):
    length, head_width = queries.shape
    block = min(512, length)
    old_block = min(1024, cached.shape[0])
    return pl.pallas_call(
        functools.partial(attend_kernel, block=block, old_block=old_block, order=order),
        grid_spec=pltpu.PrefetchScalarGridSpec(
            num_scalar_prefetch=1,
            grid=(length // block,),
            in_specs=[
                pl.BlockSpec((block, head_width), lambda i, me: (i, 0)),
                pl.BlockSpec(cached.shape, lambda i, me: (0, 0)),
                pl.BlockSpec(cached_other.shape, lambda i, me: (0, 0)),
                pl.BlockSpec(new_pairs.shape, lambda i, me: (0, 0, 0, 0)),
            ],
            out_specs=pl.BlockSpec((block, head_width), lambda i, me: (i, 0)),
            scratch_shapes=[pltpu.VMEM((length, 2 * head_width), jnp.bfloat16)],
        ),
        out_shape=jax.ShapeDtypeStruct((length, head_width), jnp.bfloat16),
        cost_estimate=pl.CostEstimate(
            flops=4 * length * head_width * (length // 2 + 2 * cached.shape[0]),
            bytes_accessed=8 * length * head_width * 2,
            transcendentals=length * (length // 2 + 2 * cached.shape[0]),
        ),
    )(me, queries, cached, cached_other, new_pairs)


def front_general(queries, new_kv, cache, resid, w_out, norm_gain):
    axis_count = lax.axis_size("head")
    local_rows = queries.shape[0]
    seq_count = queries.shape[1]
    head_count = queries.shape[2]
    head_width = queries.shape[3]
    pair_heads = new_kv.shape[2]
    group_size = head_count // pair_heads
    model_width = resid.shape[2]
    row_count = local_rows * seq_count
    slots = seq_count * pair_heads
    across = [[c * group_size + j for c in range(slots)] for j in range(group_size)]
    query_slots = queries.reshape(local_rows, axis_count, head_width).transpose(1, 0, 2)
    pair_slots = new_kv.reshape(local_rows, slots, 2 * head_width).transpose(1, 0, 2)
    pair_slots = lax.all_to_all(
        pair_slots, "head", split_axis=0, concat_axis=0, axis_index_groups=across, tiled=True
    )
    grp_count = lax.axis_size("grp")
    grp_me = lax.axis_index("grp")
    part_width = model_width // grp_count
    w_part = lax.dynamic_slice_in_dim(w_out, grp_me * part_width, part_width, 2)
    bits = group_size.bit_length() - 1
    order = tuple(range(1, bits)) + (0,)
    cache_rows = cache[0]
    pairs = pair_slots[None]
    for bit in order[:-1]:
        cache_rows = jnp.concatenate([cache_rows, partner_2(cache_rows, bit)], 0)
    head_queries = lax.all_to_all(query_slots, "head", split_axis=0, concat_axis=0, tiled=True)
    for bit in order[:-1]:
        pairs = jnp.concatenate([pairs, partner_2(pairs, bit)], 0)
    w_part, pairs, cache_rows, head_queries = lax.optimization_barrier(
        (w_part, pairs, cache_rows, head_queries)
    )
    w_part = lax.all_gather(w_part, "head", axis=1, tiled=True)
    w_part = w_part.reshape(head_count * head_width, part_width)
    cache_other = partner_2(cache_rows, 0)
    pairs = jnp.concatenate([pairs, partner_2(pairs, 0)], 0)
    me = (lax.axis_index("head") % group_size).astype(jnp.int32).reshape(1)
    attended = attend(
        me, head_queries.reshape(-1, head_width), pairs, cache_rows, cache_other, order
    )
    returned = lax.all_to_all(
        attended.reshape(axis_count, local_rows, head_width),
        "head",
        split_axis=0,
        concat_axis=0,
        tiled=True,
    )
    attn_rows = returned.reshape(seq_count, head_count, local_rows, head_width)
    attn_rows = attn_rows.transpose(2, 0, 1, 3).reshape(row_count, head_count * head_width)
    parts = []
    for shift in range(1, grp_count):
        far_rows = turn_grp(attn_rows, shift)
        far_part = jnp.dot(far_rows, w_part, preferred_element_type=jnp.float32)
        parts.append(turn_grp(far_part.astype(jnp.bfloat16), -shift).astype(jnp.float32))
    projected = []
    near_part = jnp.dot(attn_rows, w_part, preferred_element_type=jnp.float32)
    for column in range(grp_count):
        piece = near_part
        for shift in range(1, grp_count):
            piece = jnp.where((grp_me + shift) % grp_count == column, parts[shift - 1], piece)
        projected.append(piece)
    projected = jnp.concatenate(projected, 1)
    stream = resid.reshape(row_count, model_width).astype(jnp.float32) + projected
    normed = stream * lax.rsqrt(jnp.mean(stream * stream, 1, keepdims=True) + eps_norm) * norm_gain
    normed = normed.astype(jnp.bfloat16)
    return stream, normed


def expert_body(
    normed_ref,
    stream_ref,
    info_ref,
    out_ref,
    top_count,
    w_in,
    w_down,
    rows_buf,
    info_buf,
    picked,
    inbox,
    outbox,
    answer,
    dense,
    summed,
    sums_in,
    sums_out,
    row_line,
    row_sent,
    info_line,
    info_sent,
    in_sem,
    in_sem_s,
    ans_sem,
    ans_sem_s,
    sum_sem,
    sum_sem_s,
):
    planes, rows, model = rows_buf.shape
    near, cap = inbox.shape[1:3]
    hidden_width = w_down.shape[0]
    chunks = row_line.shape[1]
    chunk = model // chunks
    g = lax.axis_index("grp")
    me = lax.axis_index("head")
    z, own = me // near, me % near
    up, down = (g, me + near), (g, me - near)
    has_up, has_down = z < planes - 1, z > 0

    def copy(src, dst, sent, got, peer):
        return pltpu.make_async_remote_copy(
            src_ref=src,
            dst_ref=dst,
            send_sem=sent,
            recv_sem=got,
            device_id=peer,
            device_id_type=MESH,
        )

    def arrived(dst, got):
        copy(dst, dst, got, got, (g, me ^ 1)).wait_recv()

    def left(src, sent):
        copy(src, src, sent, sent, (g, me ^ 1)).wait_send()

    def cols(index):
        return slice(index * chunk, (index + 1) * chunk)

    def by_plane(values):
        chosen = jnp.int32(values[0])
        for index, value in enumerate(values[1:], 1):
            chosen = jnp.where(z == index, value, chosen)
        return chosen

    def send_info(src, plane, way, peer):
        copy(src, info_buf.at[plane], info_sent.at[way, plane], info_line.at[plane], peer).start()

    def send_row(src, index, plane, way, peer):
        dst = rows_buf.at[plane, :, cols(index)]
        copy(src, dst, row_sent.at[way, plane, index], row_line.at[plane, index], peer).start()

    def slots_of(info):
        at = lax.broadcasted_iota(jnp.int32, (near * cap, rows), 0) + z * (near * cap)
        at = at.astype(jnp.float32)
        return [at == info[rank : rank + 1, :] for rank in range(top_count)]

    def pick(plane, info, load, indices):
        chosen = functools.reduce(jnp.logical_or, slots_of(info))
        chosen = jnp.where(chosen, 1.0, 0.0).astype(jnp.bfloat16)
        for index in indices:
            part = jnp.dot(chosen, load(index), preferred_element_type=jnp.float32)
            picked[plane, :, :, cols(index)] = part.astype(jnp.bfloat16).reshape(near, cap, chunk)
            for mask in range(1, near):
                other = own ^ mask
                copy(
                    picked.at[plane, other, :, cols(index)],
                    inbox.at[plane, own, :, cols(index)],
                    in_sem_s.at[plane, other],
                    in_sem.at[plane, own],
                    (g, me ^ mask),
                ).start()
            inbox[plane, own, :, cols(index)] = picked[plane, own, :, cols(index)]

    def receive(plane, indices):
        way = (plane > z).astype(jnp.int32)
        onward = jnp.where(way == 0, planes - 1 - z, z) > 0
        peer = (g, me + near - 2 * near * way)
        if indices[0] == 0:
            arrived(info_buf.at[plane], info_line.at[plane])

            @pl.when(onward)
            def _():
                send_info(info_buf.at[plane], plane, way, peer)

        def load(index):
            block = rows_buf.at[plane, :, cols(index)]
            arrived(block, row_line.at[plane, index])

            @pl.when(onward)
            def _():
                send_row(block, index, plane, way, peer)

            return block[...]

        pick(plane, info_buf[plane], load, indices)

    def run_expert(plane):
        for mask in range(1, near):
            arrived(inbox.at[plane, own ^ mask], in_sem.at[plane, own ^ mask])
        inner = jnp.dot(
            inbox[plane].reshape(near * cap, model), w_in[...], preferred_element_type=jnp.float32
        )
        gate, value = inner[:, :hidden_width], inner[:, hidden_width:]
        hidden = (gate / (1.0 + jnp.exp(-gate)) * value).astype(jnp.bfloat16)
        for index in range(chunks):
            part = jnp.dot(hidden, w_down[:, cols(index)], preferred_element_type=jnp.float32)
            outbox[plane, :, :, cols(index)] = part.astype(jnp.bfloat16).reshape(near, cap, chunk)
            for mask in range(1, near):
                other = own ^ mask
                copy(
                    outbox.at[plane, other, :, cols(index)],
                    answer.at[plane, own, :, cols(index)],
                    ans_sem_s.at[plane, other],
                    ans_sem.at[plane, own],
                    (g, me ^ mask),
                ).start()
            answer[plane, own, :, cols(index)] = outbox[plane, own, :, cols(index)]

    def combine(plane, info, store):
        for mask in range(1, near):
            arrived(answer.at[plane, own ^ mask], ans_sem.at[plane, own ^ mask])
        gates = jnp.zeros((near * cap, rows), jnp.float32)
        for rank, here in enumerate(slots_of(info)):
            gates = jnp.where(here, info[top_count + rank : top_count + rank + 1, :], gates)
        high = gates.astype(jnp.bfloat16)
        low = (gates - high.astype(jnp.float32)).astype(jnp.bfloat16)
        for index in range(chunks):
            values = answer[plane, :, :, cols(index)].reshape(near * cap, chunk)
            total = jnp.zeros((rows, chunk), jnp.float32)
            for term in (high, low):
                total = total + lax.dot_general(
                    term, values, (((0,), (0,)), ((), ())), preferred_element_type=jnp.float32
                )
            store(index, total)

    def combine_far(plane):
        def store(index, total):
            dense[plane, :, cols(index)] = total

        combine(plane, info_buf[plane], store)

    def pass_sum(target, index):
        way = (target < z).astype(jnp.int32)
        has_in = jnp.where(way == 0, z, planes - 1 - z) > 0
        peer = (g, me + near - 2 * near * way)
        block = sums_in.at[way, target, :, cols(index)]
        at = (way, target, index)

        @pl.when(has_in)
        def _():
            arrived(block, sum_sem.at[at])
            sums_out[target, :, cols(index)] = (
                dense[target, :, cols(index)] + block[...].astype(jnp.float32)
            ).astype(jnp.bfloat16)

        @pl.when(jnp.logical_not(has_in))
        def _():
            sums_out[target, :, cols(index)] = dense[target, :, cols(index)].astype(jnp.bfloat16)

        copy(
            sums_out.at[target, :, cols(index)], block, sum_sem_s.at[at], sum_sem.at[at], peer
        ).start()

    def combine_own():
        def store(index, total):
            summed[:, cols(index)] = stream_ref[:, cols(index)] + total

        combine(z, info_ref[...], store)

    @pl.when(has_up)
    def _():
        send_info(info_ref, z, 0, up)

    @pl.when(has_down)
    def _():
        send_info(info_ref, z, 1, down)

    for index in range(chunks):
        block = normed_ref.at[:, cols(index)]

        @pl.when(has_up)
        def _():
            send_row(block, index, z, 0, up)

        @pl.when(has_down)
        def _():
            send_row(block, index, z, 1, down)

    own_at = visit_order.index(tuple(range(planes)))
    plane_at = [by_plane(values) for values in visit_order]
    target_at = [by_plane(values) for values in return_order]

    def perform(segment):
        for word in segment:
            first = int(word[1])
            if word[0] == "P":
                indices = range(int(word[2]), int(word[3]) + 1)
                if first == own_at:
                    pick(z, info_ref[...], lambda index: normed_ref[:, cols(index)], indices)
                else:
                    receive(plane_at[first], indices)
            elif word[0] == "E" and first == own_at:
                combine_own()
            elif word[0] == "E":
                combine_far(plane_at[first])
            else:
                pass_sum(target_at[first], int(word[2]))

    def step_body(step, carry):
        for number, segment in enumerate(expert_order[:-1]):

            @pl.when(step == number)
            def _():
                perform(segment)

        plane = plane_at[0]
        for number, value in enumerate(plane_at[1:], 1):
            plane = jnp.where(step == number, value, plane)
        run_expert(plane)
        return carry

    lax.fori_loop(0, planes, step_body, 0)
    perform(expert_order[-1])

    for index in range(chunks):

        @pl.when(has_down)
        def _():
            block = sums_in.at[0, z, :, cols(index)]
            arrived(block, sum_sem.at[0, z, index])
            summed[:, cols(index)] = summed[:, cols(index)] + block[...].astype(jnp.float32)

        @pl.when(has_up)
        def _():
            block = sums_in.at[1, z, :, cols(index)]
            arrived(block, sum_sem.at[1, z, index])
            summed[:, cols(index)] = summed[:, cols(index)] + block[...].astype(jnp.float32)

        out_ref[:, cols(index)] = summed[:, cols(index)].astype(out_ref.dtype)

    def drain(plane, carry):
        @pl.when((plane <= z) & has_up)
        def _():
            left(info_buf.at[plane], info_sent.at[0, plane])
            for index in range(chunks):
                left(rows_buf.at[plane, :, cols(index)], row_sent.at[0, plane, index])

        @pl.when((plane >= z) & has_down)
        def _():
            left(info_buf.at[plane], info_sent.at[1, plane])
            for index in range(chunks):
                left(rows_buf.at[plane, :, cols(index)], row_sent.at[1, plane, index])

        for mask in range(1, near):
            left(picked.at[plane, own ^ mask], in_sem_s.at[plane, own ^ mask])
            left(outbox.at[plane, own ^ mask], ans_sem_s.at[plane, own ^ mask])

        for index in range(chunks):

            @pl.when(plane > z)
            def _():
                left(sums_out.at[plane, :, cols(index)], sum_sem_s.at[0, plane, index])

            @pl.when(plane < z)
            def _():
                left(sums_out.at[plane, :, cols(index)], sum_sem_s.at[1, plane, index])

        return carry

    lax.fori_loop(0, planes, drain, 0)


def layer_kernel(*refs, top_count, experts, cap, front_count):
    inputs, out_ref, rest = refs[:10], refs[10], refs[11:]
    ids_ref, gates_ref, w_in_ref, w_down_ref = inputs[6:]
    stream, normed, info, w_in, w_down, load_sem = rest[:6]
    front_scratch, expert_scratch = rest[6 : 6 + front_count], rest[6 + front_count :]

    def route():
        rows = ids_ref.shape[1]
        ids = ids_ref[...].astype(jnp.float32)
        named = lax.broadcasted_iota(jnp.int32, (experts, rows), 0).astype(jnp.float32)
        hits = [named == ids[rank : rank + 1] for rank in range(top_count)]
        onehot = sum(jnp.where(hit, 1.0, 0.0) for hit in hits).astype(jnp.bfloat16)
        first = lax.broadcasted_iota(jnp.int32, (rows, rows), 0)
        second = lax.broadcasted_iota(jnp.int32, (rows, rows), 1)
        before = jnp.where(first < second, 1.0, 0.0).astype(jnp.bfloat16)
        earlier = jnp.dot(onehot, before, preferred_element_type=jnp.float32)
        info[...] = jnp.zeros(info.shape, info.dtype)
        for rank, hit in enumerate(hits):
            place = jnp.sum(jnp.where(hit, earlier, 0.0), 0, keepdims=True)
            info[rank : rank + 1] = ids[rank : rank + 1] * cap + place
        info[top_count : 2 * top_count] = gates_ref[...]

    loads = (
        pltpu.make_async_copy(w_in_ref, w_in, load_sem.at[0]),
        pltpu.make_async_copy(w_down_ref, w_down, load_sem.at[1]),
    )
    for load in loads:
        load.start()
    front_body(*inputs[:6], stream, normed, route, *front_scratch)
    for load in loads:
        load.wait()
    expert_body(normed, stream, info, out_ref, top_count, w_in, w_down, *expert_scratch)


def layer(queries, pairs, cached, w_out, resid, gain, ids, gates, w_in, w_down, axis_count):
    rows, heads, width = queries.shape
    top_count = ids.shape[0]
    cap = 2 * rows * top_count // axis_count
    lines = -(-2 * top_count // 8) * 8
    group = heads // 2
    near = 4
    planes = axis_count // near
    model = w_out.shape[2]
    slice_rows = w_out.shape[1]
    page = cached.shape[0]
    pieces = 4
    chunks = 4
    dma = pltpu.SemaphoreType.DMA
    anywhere = pl.BlockSpec(memory_space=pl.ANY)
    inside = pl.BlockSpec(memory_space=pltpu.VMEM)

    def half(*shape):
        return pltpu.VMEM(shape, jnp.bfloat16)

    def full(*shape):
        return pltpu.VMEM(shape, jnp.float32)

    front_scratch = [
        half(rows, heads, width),
        half(2, group, rows, width),
        half(rows, 2, 2 * width),
        half(2, rows, 2 * width),
        half(2, group, rows, width),
        half(2, planes, 2, 2, rows, 2 * width),
        half(planes, 2, 2, page, 2 * width),
        half(group, planes, 2, 2, slice_rows, model),
        full(2, group, rows, width),
        full(2, group, rows, 128),
        full(2, group, rows, 128),
        half(2, rows, group * width),
        half(rows, model),
        half(rows, model),
        dma((4,)),
        dma((2,)),
        dma((planes,)),
        dma((planes,)),
        dma((planes,)),
        dma((planes,)),
        dma((planes, 2)),
        dma((planes, 2)),
        dma((planes,)),
        dma((planes,)),
        dma((planes,)),
        dma((planes,)),
        dma((planes,)),
        dma((planes, 2)),
        dma((planes, 2)),
        dma((pieces, planes, 2)),
        dma((pieces, planes, 2)),
        dma((pieces, planes, 2)),
        dma((pieces,)),
        dma((pieces,)),
        dma((pieces, planes, 2)),
        dma((pieces, planes, 2)),
        dma((pieces, planes, 2, 2)),
        dma((pieces, planes, 2, 2)),
        dma((2 * pieces,)),
        dma((2 * pieces,)),
    ]
    expert_scratch = [
        half(planes, rows, model),
        full(planes, lines, rows),
        half(planes, near, cap, model),
        half(planes, near, cap, model),
        half(planes, near, cap, model),
        half(planes, near, cap, model),
        full(planes, rows, model),
        full(rows, model),
        half(2, planes, rows, model),
        half(planes, rows, model),
        dma((planes, chunks)),
        dma((2, planes, chunks)),
        dma((planes,)),
        dma((2, planes)),
        dma((planes, near)),
        dma((planes, near)),
        dma((planes, near)),
        dma((planes, near)),
        dma((2, planes, chunks)),
        dma((2, planes, chunks)),
    ]
    return pl.pallas_call(
        functools.partial(
            layer_kernel,
            top_count=top_count,
            experts=axis_count,
            cap=cap,
            front_count=len(front_scratch),
        ),
        out_shape=jax.ShapeDtypeStruct((rows, model), jnp.bfloat16),
        in_specs=[anywhere] * 4 + [inside] * 4 + [anywhere] * 2,
        out_specs=inside,
        scratch_shapes=[
            full(rows, model),
            half(rows, model),
            full(lines, rows),
            half(*w_in.shape),
            half(*w_down.shape),
            dma((2,)),
            *front_scratch,
            *expert_scratch,
        ],
        compiler_params=pltpu.CompilerParams(
            collective_id=0, has_side_effects=True, vmem_limit_bytes=60 * 2**20
        ),
        cost_estimate=pl.CostEstimate(
            flops=4 * 2 * group * rows * width * 4 * axis_count * rows
            + 4 * rows * group * width * model
            + 6 * planes * near * cap * model * w_down.shape[0],
            bytes_accessed=12 * 2**20,
            transcendentals=2 * group * rows * axis_count * rows,
        ),
    )(queries, pairs, cached, w_out, resid, gain, ids, gates, w_in, w_down)


def experts(stream, normed, expert_ids, expert_gates, w_in, w_down):
    row_count, model_width = stream.shape
    axis_count = lax.axis_size("head")
    top_count = expert_ids.shape[2]
    flat_ids = expert_ids.reshape(-1)
    local_experts = w_in.shape[0]
    experts = local_experts * axis_count
    capacity = max(2, 2 * row_count * top_count // experts)
    onehot = (flat_ids[:, None] == jnp.arange(experts, dtype=jnp.int32)[None, :]).astype(jnp.int32)
    before = jnp.tri(flat_ids.shape[0], k=-1, dtype=jnp.bfloat16)
    earlier = jnp.dot(
        before, onehot.astype(jnp.bfloat16), preferred_element_type=jnp.float32
    ).astype(jnp.int32)
    slot_rank = jnp.sum(earlier * onehot, 1)
    target = flat_ids * capacity + slot_rank
    target = target.reshape(row_count, top_count)
    places = jnp.arange(experts * capacity, dtype=jnp.int32)
    chosen = jnp.zeros((experts * capacity, row_count), jnp.bool_)
    gate_of = jnp.zeros((row_count, experts * capacity), jnp.float32)
    gates = expert_gates.reshape(row_count, top_count)
    for rank in range(top_count):
        chosen = chosen | (places[:, None] == target[None, :, rank])
        gate_of = jnp.where(
            target[:, rank, None] == places[None, :], gates[:, rank, None], gate_of
        )
    outgoing = jnp.dot(
        chosen.astype(jnp.bfloat16), normed, preferred_element_type=jnp.float32
    ).astype(jnp.bfloat16)
    outgoing = outgoing.reshape(axis_count, local_experts, capacity, model_width)
    hidden_width = w_down.shape[1]
    inner_act = jnp.einsum(
        "semd,edf->semf",
        lax.all_to_all(outgoing, "head", split_axis=0, concat_axis=0, tiled=True),
        w_in,
        preferred_element_type=jnp.float32,
    )
    hidden = (jax.nn.silu(inner_act[..., :hidden_width]) * inner_act[..., hidden_width:]).astype(
        jnp.bfloat16
    )
    answered = jnp.einsum(
        "semf,efd->semd", hidden, w_down, preferred_element_type=jnp.float32
    ).astype(jnp.bfloat16)
    returned_rows = lax.all_to_all(answered, "head", split_axis=0, concat_axis=0, tiled=True)
    picked = returned_rows.reshape(experts * capacity, model_width)
    expert_sum = jnp.zeros((row_count, model_width), jnp.float32)
    rest = gate_of
    for _ in range(3):
        term = lax.reduce_precision(rest, 8, 7)
        rest = rest - term
        expert_sum = expert_sum + jnp.dot(
            term.astype(jnp.bfloat16), picked, preferred_element_type=jnp.float32
        )
    return (stream + expert_sum).astype(jnp.bfloat16)


def local(queries, new_kv, cache, resid, w_out, norm_gain, expert_ids, expert_gates, w_in, w_down):
    axis_count = lax.axis_size("head")
    local_rows, seq_count, head_count, head_width = queries.shape
    pair_heads = new_kv.shape[2]
    fits = (
        seq_count == 1
        and pair_heads == 2
        and lax.axis_size("grp") == 2
        and axis_count == 4 * (len(front_order[1]) + 1)
        and w_out.shape[2] % 1024 == 0
        and cache.shape[0] == 1
        and w_out.shape[1] * axis_count == head_width
        and w_out.shape[1] % 16 == 0
        and local_rows % 32 == 0
        and cache.shape[1] * 2 % 128 == 0
        and head_count % 4 == 0
    )
    top_count = expert_ids.shape[2]
    experts_count = w_in.shape[0] * axis_count
    row_count = local_rows * seq_count
    fits = (
        fits
        and w_in.shape[0] == 1
        and row_count % 128 == 0
        and (row_count * top_count * 2) % (16 * experts_count) == 0
    )
    if fits:
        out = layer(
            queries.reshape(local_rows, head_count, head_width),
            new_kv.reshape(local_rows, pair_heads, 2 * head_width),
            cache[0],
            w_out,
            resid.reshape(local_rows, -1),
            norm_gain.reshape(1, -1),
            expert_ids.reshape(local_rows, top_count).T,
            expert_gates.reshape(local_rows, top_count).T,
            w_in[0],
            w_down[0],
            axis_count,
        )
    else:
        stream, normed = front_general(queries, new_kv, cache, resid, w_out, norm_gain)
        out = experts(stream, normed, expert_ids, expert_gates, w_in, w_down)
    return out.reshape(resid.shape)


def solution(mesh):
    return jax.shard_map(
        local,
        mesh=mesh,
        in_specs=(
            P("head", "grp", None, None),
            P("head", "grp", None, None),
            P(("grp", "head"), None, None),
            P("head", "grp", None),
            P(None, "head", None),
            P(),
            P("head", "grp", None),
            P("head", "grp", None),
            P("head", None, None),
            P("head", None, None),
        ),
        out_specs=P("head", "grp", None),
        check_vma=False,
    )
```

```python
import functools

import jax
import jax.numpy as jnp
from jax import lax
from jax.experimental import pallas as pl
from jax.experimental.pallas import tpu as pltpu
from jax.sharding import PartitionSpec as P

eps_norm = 1e-06
MESH = pl.DeviceIdType.MESH
expert_order = (
    ("P301", "P000", "P200", "P011", "P211", "P022", "P222", "P033", "P233", "P100",),
    ("P113", "E0", "R10", "R11", "P322",),
    ("R12", "R13",),
    ("E1", "R20", "P333", "R21", "R22", "E2", "R00",),
    ("R23", "R01", "R02", "E3", "R03",),
)
visit_order = ((2, 2, 1, 1), (3, 3, 0, 0), (1, 0, 3, 2), (0, 1, 2, 3))
return_order = ((1, 0, 3, 2), (2, 2, 1, 1), (3, 3, 0, 0))
front_order = (
    ("o0", "o1", "L1", "s0", "s1", "o2", "F00", "W01", "q", "s2", "L2", "W11", "o3", "F01", "S0", "F20", "D",),
    (
        ("W21", "W02", "S1",),
        ("F10", "L3", "s3", "S2", "W12",),
        ("W03", "F30", "W22", "S3", "W31",),
    ),
    ("W13", "F21", "F11", "F02", "W23", "F12", "F22", "F03", "J0", "W32", "F13", "J1", "W33", "F23", "F31", "J2", "F32", "F33", "J3",),
)


def front_body(
    q_raw_ref,
    kv_raw_ref,
    cache_ref,
    w_ref,
    resid_ref,
    gain_ref,
    stream_ref,
    normed_ref,
    aside,
    q_raw,
    q_ref,
    kv_raw,
    kv_ref,
    q_buf,
    kn,
    kc,
    wb,
    acc,
    top,
    total,
    att,
    part_out,
    part_in,
    local_sem,
    q_sem,
    kn_line,
    kn_up,
    kn_side,
    kn_side_s,
    kn_twin,
    kn_twin_s,
    kc_line,
    kc_up,
    kc_down,
    kc_side,
    kc_side_s,
    kc_twin,
    kc_twin_s,
    w_line,
    w_up,
    w_down,
    w_side,
    w_side_s,
    w_far,
    w_far_s,
    w_twin,
    w_twin_s,
    part_sem,
    part_sem_s,
):
    planes = kn.shape[1]
    group = q_buf.shape[1]
    rows, width = q_buf.shape[2:]
    model = w_ref.shape[2]
    pieces = w_side.shape[0]
    half, chunk = model // 2, model // (2 * pieces)
    g = lax.axis_index("grp")
    me = lax.axis_index("head")
    z, y, c = me // 4, (me // 2) % 2, me % 2
    up, down = (g, me + 4), (g, me - 4)
    side, twin, far = (g, me + 2 - 4 * y), (g, me + 1 - 2 * c), (1 - g, me)
    has_up, has_down = z < planes - 1, z > 0

    raw = (
        pltpu.make_async_copy(kv_raw_ref, kv_raw, local_sem.at[0]),
        pltpu.make_async_copy(q_raw_ref, q_raw, local_sem.at[1]),
    )
    for item in raw:
        item.start()
    barrier = pltpu.get_barrier_semaphore()
    for peer in (side, twin, (g, me ^ 3), far):
        pl.semaphore_signal(barrier, inc=1, device_id=peer, device_id_type=MESH)

    @pl.when(has_up)
    def _():
        pl.semaphore_signal(barrier, inc=1, device_id=up, device_id_type=MESH)

    @pl.when(has_down)
    def _():
        pl.semaphore_signal(barrier, inc=1, device_id=down, device_id_type=MESH)

    pl.semaphore_wait(barrier, 4 + has_up.astype(jnp.int32) + has_down.astype(jnp.int32))

    def copy(src, dst, sent, got, peer):
        return pltpu.make_async_remote_copy(
            src_ref=src,
            dst_ref=dst,
            send_sem=sent,
            recv_sem=got,
            device_id=peer,
            device_id_type=MESH,
        )

    def arrived(dst, got):
        copy(dst, dst, got, got, twin).wait_recv()

    def left(src, sent):
        copy(src, src, sent, sent, twin).wait_send()

    def mine(plane):
        return plane // (planes // 2) == y

    cols_near = pl.ds(pl.multiple_of(g * half, half), half)
    raw[0].wait()
    kv_ref[...] = jnp.swapaxes(kv_raw[...], 0, 1)
    own_heads = pl.ds(y * group, group)
    other_heads = pl.ds((1 - y) * group, group)

    def w_cols(quarter, near):
        first = jnp.where(near, g, 1 - g) * half + quarter * chunk
        return pl.ds(pl.multiple_of(first, chunk), chunk)

    def w_block(quarter, plane, line, core, near=True):
        return wb.at[:, plane, line, core, :, w_cols(quarter, near)]

    def w_spread(src, quarter, plane, line):
        dst = w_block(quarter, plane, line, c)
        at = (quarter, plane, line)
        copy(src, dst, w_far_s.at[at], w_far.at[at], far).start()
        copy(src, dst, w_twin_s.at[(*at, 0)], w_twin.at[(*at, 0)], twin).start()

    def w_send_up(src, quarter, plane, line):
        at = (quarter, plane, line)

        @pl.when(has_up)
        def _():
            copy(src, w_block(quarter, plane, line, c), w_up.at[at], w_line.at[at], up).start()

    def w_send_down(src, quarter, plane, line):
        at = (quarter, plane, line)

        @pl.when(has_down)
        def _():
            copy(src, w_block(quarter, plane, line, c), w_down.at[at], w_line.at[at], down).start()

    def w_own_side(quarter):
        src = w_ref.at[other_heads, :, w_cols(quarter, True)]
        dst = w_block(quarter, z, y, c)
        copy(src, dst, w_side_s.at[quarter], w_side.at[quarter], side).start()

    def w_own(quarter):
        src = w_ref.at[own_heads, :, w_cols(quarter, True)]
        w_send_up(src, quarter, z, y)
        w_send_down(src, quarter, z, y)
        w_spread(src, quarter, z, y)

    def w_side_relay(quarter):
        block = w_block(quarter, z, 1 - y, c)
        arrived(block, w_side.at[quarter])
        w_send_up(block, quarter, z, 1 - y)
        w_send_down(block, quarter, z, 1 - y)
        w_spread(block, quarter, z, 1 - y)

    def w_relay(quarter, step):
        low, high = z - step, z + step
        for turn in range(2):
            line = y + turn - 2 * y * turn

            @pl.when(low >= 0)
            def _():
                block = w_block(quarter, low, line, c)
                arrived(block, w_line.at[quarter, low, line])
                w_send_up(block, quarter, low, line)
                w_spread(block, quarter, low, line)

            @pl.when(high < planes)
            def _():
                block = w_block(quarter, high, line, c)
                arrived(block, w_line.at[quarter, high, line])
                w_send_down(block, quarter, high, line)
                w_spread(block, quarter, high, line)

    def w_far_relay(quarter, plane):
        for line in range(2):
            block = w_block(quarter, plane, line, c, False)
            arrived(block, w_far.at[quarter, plane, line])
            at = (quarter, plane, line, 1)
            copy(block, block, w_twin_s.at[at], w_twin.at[at], twin).start()

    def w_far_relays(quarter, step):
        low, high = z - step, z + step

        @pl.when(low >= 0)
        def _():
            w_far_relay(quarter, low)

        if step > 0:

            @pl.when(high < planes)
            def _():
                w_far_relay(quarter, high)

    @pl.when(has_up)
    def _():
        copy(cache_ref, kc.at[z, y, c], kc_up.at[z], kc_line.at[z], up).start()
        copy(kv_ref, kn.at[:, z, y, c], kn_up.at[z], kn_line.at[z], up).start()

    @pl.when(has_down)
    def _():
        copy(cache_ref, kc.at[z, y, c], kc_down.at[z], kc_line.at[z], down).start()

    copy(kv_ref.at[1 - y], kn.at[1 - y, z, y, c], kn_side_s.at[z], kn_side.at[z], side).start()
    w_own_side(0)
    copy(kv_ref.at[y], kn.at[y, z, y, c], kn_twin_s.at[z, y], kn_twin.at[z, y], twin).start()

    @pl.when(mine(z))
    def _():
        copy(cache_ref, kc.at[z, y, c], kc_twin_s.at[z, y], kc_twin.at[z, y], twin).start()

    @pl.when(jnp.logical_not(mine(z)))
    def _():
        copy(cache_ref, kc.at[z, y, c], kc_side_s.at[z], kc_side.at[z], side).start()

    locals_ = (
        pltpu.make_async_copy(kv_ref.at[y], kn.at[y, z, y, c], local_sem.at[0]),
        pltpu.make_async_copy(cache_ref, kc.at[z, y, c], local_sem.at[2]),
        pltpu.make_async_copy(
            w_ref.at[own_heads, :, cols_near], wb.at[:, z, y, c, :, cols_near], local_sem.at[3]
        ),
    )
    for item in locals_:
        item.start()
    raw[1].wait()
    scale = jnp.asarray(width ** (-0.5), q_ref.dtype)
    q_ref[...] = (jnp.swapaxes(q_raw[...], 0, 1) * scale).reshape(q_ref.shape)
    copy(q_ref.at[1 - y], q_buf.at[y], q_sem.at[0], q_sem.at[1], side).start()
    for piece in range(1, pieces):
        w_own_side(piece)
    q_buf[y] = q_ref[y]
    aside()

    def from_side_new(plane):
        block = kn.at[y, plane, 1 - y, c]
        arrived(block, kn_side.at[plane])
        copy(block, block, kn_twin_s.at[plane, 1 - y], kn_twin.at[plane, 1 - y], twin).start()

    def from_side_old(plane):
        @pl.when(mine(plane))
        def _():
            block = kc.at[plane, 1 - y, c]
            arrived(block, kc_side.at[plane])
            copy(block, block, kc_twin_s.at[plane, 1 - y], kc_twin.at[plane, 1 - y], twin).start()

    def spread_old(plane):
        block = kc.at[plane, y, c]

        @pl.when(mine(plane))
        def _():
            copy(block, block, kc_twin_s.at[plane, y], kc_twin.at[plane, y], twin).start()

        @pl.when(jnp.logical_not(mine(plane)))
        def _():
            copy(block, block, kc_side_s.at[plane], kc_side.at[plane], side).start()

    def relay(step):
        low, high = z - step, z + step

        @pl.when(high < planes)
        def _():
            old = kc.at[high, y, c]
            arrived(old, kc_line.at[high])

            @pl.when(has_down)
            def _():
                copy(old, old, kc_down.at[high], kc_line.at[high], down).start()

            spread_old(high)

        @pl.when(low >= 0)
        def _():
            old, new = kc.at[low, y, c], kn.at[:, low, y, c]
            arrived(old, kc_line.at[low])

            @pl.when(has_up)
            def _():
                copy(old, old, kc_up.at[low], kc_line.at[low], up).start()

            arrived(new, kn_line.at[low])

            @pl.when(has_up)
            def _():
                copy(new, new, kn_up.at[low], kn_line.at[low], up).start()

            there, here = kn.at[1 - y, low, y, c], kn.at[y, low, y, c]
            copy(there, there, kn_side_s.at[low], kn_side.at[low], side).start()
            copy(here, here, kn_twin_s.at[low, y], kn_twin.at[low, y], twin).start()
            spread_old(low)

    def from_side(step):
        low, high = z - step, z + step

        @pl.when(low >= 0)
        def _():
            from_side_new(low)
            from_side_old(low)

        if step > 0:

            @pl.when(high < planes)
            def _():
                from_side_old(high)

    tile = 2
    tile_rows = tile * rows

    def fold(keys, values, diagonal):
        def lines(line, carry):
            for part in range(group // tile):
                heads = pl.ds(part * tile, tile)
                queries = q_buf[line, heads].reshape(tile_rows, width)
                scores = lax.dot_general(
                    queries, keys(), (((1,), (1,)), ((), ())), preferred_element_type=jnp.float32
                )
                pieces = [
                    scores[:, first : first + 128] for first in range(0, scores.shape[1], 128)
                ]
                if diagonal:
                    row_at = lax.broadcasted_iota(jnp.int32, (tile_rows, 128), 0) % rows
                    ahead = row_at - lax.broadcasted_iota(jnp.int32, (tile_rows, 128), 1)
                    ahead = ahead + (line * 2 + c) * rows
                    pieces = [
                        jnp.where(ahead >= index * 128, piece, -jnp.inf)
                        for index, piece in enumerate(pieces)
                    ]
                best = functools.reduce(jnp.maximum, pieces)
                best = jnp.max(best, 1, keepdims=True)
                if diagonal:
                    new_top = jnp.broadcast_to(best, (tile_rows, 128))
                else:
                    old_top = top[line, heads].reshape(tile_rows, 128)
                    new_top = jnp.maximum(old_top, best)
                exps = [jnp.exp(piece - new_top) for piece in pieces]
                new_total = functools.reduce(jnp.add, exps)
                weighted = jnp.dot(
                    jnp.concatenate([part_.astype(jnp.bfloat16) for part_ in exps], 1),
                    values(),
                    preferred_element_type=jnp.float32,
                )
                if not diagonal:
                    shrink = jnp.exp(old_top - new_top)
                    new_total = new_total + total[line, heads].reshape(tile_rows, 128) * shrink
                    weighted = weighted + acc[line, heads].reshape(
                        tile_rows, width
                    ) * jnp.concatenate([shrink] * (width // 128), 1)
                top[line, heads] = new_top.reshape(tile, rows, 128)
                total[line, heads] = new_total.reshape(tile, rows, 128)
                acc[line, heads] = weighted.reshape(tile, rows, width)
            return carry

        lax.fori_loop(0, 2, lines, 0, unroll=2)

    def new_part(plane, first):
        return lambda: kn[y, plane, :, :, :, first : first + width].reshape(4 * rows, width)

    page = kc.shape[3]

    def old_part(plane, line, first):
        return lambda: kc[plane, line, :, :, first : first + width].reshape(2 * page, width)

    def twins_new(plane):
        for line in range(2):
            arrived(kn.at[y, plane, line, 1 - c], kn_twin.at[plane, line])

    def twins_old(plane):
        for line in range(2):
            arrived(kc.at[plane, line, 1 - c], kc_twin.at[plane, line])

    def first_fold():
        twins_new(z)
        fold(new_part(z, 0), new_part(z, width), True)

    def queries_here():
        arrived(q_buf.at[1 - y], q_sem.at[1])
        for item in locals_:
            item.wait()

    def later_folds(step):
        low, high = z - step, z + step

        @pl.when((step >= 1) & (low >= 0))
        def _():
            twins_new(low)
            fold(new_part(low, 0), new_part(low, width), False)

        def old_body(index, carry):
            plane = jnp.where(index == 0, low, high)
            valid = (plane >= 0) & (plane < planes) & ((index == 0) | (step > 0))

            @pl.when(valid & mine(plane))
            def _():
                twins_old(plane)

                def line_body(line, carry):
                    fold(old_part(plane, line, 0), old_part(plane, line, width), False)
                    return carry

                lax.fori_loop(0, 2, line_body, 0)

            return carry

        lax.fori_loop(0, 2, old_body, 0)

    def finish():
        for line in range(2):
            for head in range(group):
                att[line, :, head * width : (head + 1) * width] = (
                    acc[line, head] * (1.0 / jnp.sum(total[line, head], 1, keepdims=True))
                ).astype(att.dtype)

    def project(quarter):
        for near in range(2):
            for plane in range(planes):
                for line in range(2):
                    arrived(
                        w_block(quarter, plane, line, 1 - c, near == 0),
                        w_twin.at[quarter, plane, line, near],
                    )
            cols = w_cols(quarter, near == 0)
            weights = wb[:, :, :, :, :, cols].reshape(group * width, chunk)
            both = jnp.dot(
                att[...].reshape(2 * rows, group * width),
                weights,
                preferred_element_type=jnp.float32,
            )
            there = jnp.where(y == 0, both[rows:], both[:rows])
            here = jnp.where(y == 0, both[:rows], both[rows:])
            part_out[:, cols] = there.astype(part_out.dtype)
            index = quarter * 2 + near
            block = part_out.at[:, cols]
            copy(block, part_in.at[:, cols], part_sem_s.at[index], part_sem.at[index], side).start()
            stream_ref[:, cols] = here + resid_ref[:, cols].astype(jnp.float32)

    acts = {
        "o": w_own,
        "s": w_side_relay,
        "L": relay,
        "S": from_side,
        "q": queries_here,
        "D": first_fold,
        "W": w_relay,
        "F": w_far_relays,
        "J": project,
    }

    def perform(segment):
        for word in segment:
            acts[word[0]](*(int(digit) for digit in word[1:]))

    before, between, after = front_order
    perform(before)

    def step_body(step, carry):
        for number, segment in enumerate(between):

            @pl.when(step == number + 1)
            def _():
                perform(segment)

        later_folds(step)
        return carry

    lax.fori_loop(0, planes, step_body, 0)
    finish()
    perform(after)
    square = jnp.zeros((rows, 1), jnp.float32)
    for quarter in range(pieces):
        for near in range(2):
            cols = w_cols(quarter, near == 0)
            index = quarter * 2 + near
            arrived(part_in.at[:, cols], part_sem.at[index])
            stream = stream_ref[:, cols] + part_in[:, cols].astype(jnp.float32)
            stream_ref[:, cols] = stream
            square = square + jnp.sum(stream * stream, 1, keepdims=True)
            left(part_out.at[:, cols], part_sem_s.at[index])
    inverse = lax.rsqrt(square / model + eps_norm)
    for index in range(2 * pieces):
        cols = slice(index * chunk, (index + 1) * chunk)
        normed_ref[:, cols] = (stream_ref[:, cols] * inverse * gain_ref[:, cols]).astype(
            normed_ref.dtype
        )

    left(q_buf.at[y], q_sem.at[0])
    for quarter in range(pieces):
        left(w_block(quarter, z, y, c), w_side_s.at[quarter])

    def drain(plane, carry):
        reached = plane <= z

        @pl.when(reached)
        def _():
            left(kn.at[1 - y, plane, y, c], kn_side_s.at[plane])
            left(kn.at[y, plane, y, c], kn_twin_s.at[plane, y])
            left(kn.at[y, plane, 1 - y, c], kn_twin_s.at[plane, 1 - y])

        @pl.when(reached & has_up)
        def _():
            left(kn.at[:, plane, y, c], kn_up.at[plane])
            left(kc.at[plane, y, c], kc_up.at[plane])
            for quarter in range(pieces):
                for line in range(2):
                    left(w_block(quarter, plane, line, c), w_up.at[quarter, plane, line])

        @pl.when((plane >= z) & has_down)
        def _():
            left(kc.at[plane, y, c], kc_down.at[plane])
            for quarter in range(pieces):
                for line in range(2):
                    left(w_block(quarter, plane, line, c), w_down.at[quarter, plane, line])

        @pl.when(mine(plane))
        def _():
            for line in range(2):
                left(kc.at[plane, line, c], kc_twin_s.at[plane, line])

        @pl.when(jnp.logical_not(mine(plane)))
        def _():
            left(kc.at[plane, y, c], kc_side_s.at[plane])

        for quarter in range(pieces):
            for line in range(2):
                at = (quarter, plane, line)
                left(w_block(quarter, plane, line, c), w_far_s.at[at])
                left(w_block(quarter, plane, line, c), w_twin_s.at[(*at, 0)])
                left(w_block(quarter, plane, line, c, False), w_twin_s.at[(*at, 1)])
        return carry

    lax.fori_loop(0, planes, drain, 0)


def partner_2(value, stride):
    mask = 2**stride
    pairs = [(source, source ^ mask) for source in range(lax.axis_size("head"))]
    return lax.ppermute(value, "head", pairs)


def turn_grp(value, shift):
    count = lax.axis_size("grp")
    return lax.ppermute(value, "grp", [(i, (i + shift) % count) for i in range(count)])


def attend_kernel(
    me_ref, query_ref, cache_ref, other_ref, pairs_ref, out_ref, new_ref, *, block, old_block, order
):
    head_width = query_ref.shape[1]
    step = pl.program_id(0)
    members, slots, local_rows = pairs_ref.shape[:3]

    @pl.when(step == 0)
    def _():
        for slot in range(slots):
            for member in range(members):
                apart = member ^ me_ref[0]
                place = 0
                for rank, bit in enumerate(order):
                    place = place + ((apart >> bit) & 1) * 2**rank
                first = (slot * members + member) * local_rows
                new_ref[first : first + local_rows, :] = pairs_ref[place, slot]

    query_rows = query_ref[...] * jnp.asarray(head_width ** (-0.5), query_ref.dtype)

    def fold(carry, keys, values, mask):
        top, total, weighted = carry
        scores = lax.dot_general(
            query_rows, keys, (((1,), (1,)), ((), ())), preferred_element_type=jnp.float32
        )
        if mask is not None:
            scores = jnp.where(mask, scores, -jnp.inf)
        new_top = jnp.maximum(top, jnp.max(scores, 1, keepdims=True))
        exps = jnp.exp(scores - new_top)
        shrink = jnp.exp(top - new_top)
        total = total * shrink + jnp.sum(exps, 1, keepdims=True)
        weighted = weighted * shrink + jnp.dot(
            exps.astype(jnp.bfloat16), values, preferred_element_type=jnp.float32
        )
        return new_top, total, weighted

    rows = query_rows.shape[0]
    carry = (
        jnp.full((rows, 1), -jnp.inf, jnp.float32),
        jnp.zeros((rows, 1), jnp.float32),
        jnp.zeros((rows, head_width), jnp.float32),
    )
    row_at = lax.broadcasted_iota(jnp.int32, (rows, block), 0)
    col_at = lax.broadcasted_iota(jnp.int32, (rows, block), 1)
    here = pl.ds(step * block, block)
    carry = fold(
        carry, new_ref[here, :head_width], new_ref[here, head_width:], col_at <= row_at
    )
    for old_ref in (cache_ref, other_ref):
        for first in range(0, old_ref.shape[0], old_block):
            part = pl.ds(first, old_block)
            carry = fold(carry, old_ref[part, :head_width], old_ref[part, head_width:], None)

    def earlier(index, carry):
        part = pl.ds(index * block, block)
        return fold(carry, new_ref[part, :head_width], new_ref[part, head_width:], None)

    top, total, weighted = lax.fori_loop(0, step, earlier, carry)
    out_ref[...] = (weighted / total).astype(out_ref.dtype)


def attend(me, queries, new_pairs, cached, cached_other, order):
    length, head_width = queries.shape
    block = min(512, length)
    old_block = min(1024, cached.shape[0])
    return pl.pallas_call(
        functools.partial(attend_kernel, block=block, old_block=old_block, order=order),
        grid_spec=pltpu.PrefetchScalarGridSpec(
            num_scalar_prefetch=1,
            grid=(length // block,),
            in_specs=[
                pl.BlockSpec((block, head_width), lambda i, me: (i, 0)),
                pl.BlockSpec(cached.shape, lambda i, me: (0, 0)),
                pl.BlockSpec(cached_other.shape, lambda i, me: (0, 0)),
                pl.BlockSpec(new_pairs.shape, lambda i, me: (0, 0, 0, 0)),
            ],
            out_specs=pl.BlockSpec((block, head_width), lambda i, me: (i, 0)),
            scratch_shapes=[pltpu.VMEM((length, 2 * head_width), jnp.bfloat16)],
        ),
        out_shape=jax.ShapeDtypeStruct((length, head_width), jnp.bfloat16),
        cost_estimate=pl.CostEstimate(
            flops=4 * length * head_width * (length // 2 + 2 * cached.shape[0]),
            bytes_accessed=8 * length * head_width * 2,
            transcendentals=length * (length // 2 + 2 * cached.shape[0]),
        ),
    )(me, queries, cached, cached_other, new_pairs)


def front_general(queries, new_kv, cache, resid, w_out, norm_gain):
    axis_count = lax.axis_size("head")
    local_rows = queries.shape[0]
    seq_count = queries.shape[1]
    head_count = queries.shape[2]
    head_width = queries.shape[3]
    pair_heads = new_kv.shape[2]
    group_size = head_count // pair_heads
    model_width = resid.shape[2]
    row_count = local_rows * seq_count
    slots = seq_count * pair_heads
    across = [[c * group_size + j for c in range(slots)] for j in range(group_size)]
    query_slots = queries.reshape(local_rows, axis_count, head_width).transpose(1, 0, 2)
    pair_slots = new_kv.reshape(local_rows, slots, 2 * head_width).transpose(1, 0, 2)
    pair_slots = lax.all_to_all(
        pair_slots, "head", split_axis=0, concat_axis=0, axis_index_groups=across, tiled=True
    )
    grp_count = lax.axis_size("grp")
    grp_me = lax.axis_index("grp")
    part_width = model_width // grp_count
    w_part = lax.dynamic_slice_in_dim(w_out, grp_me * part_width, part_width, 2)
    bits = group_size.bit_length() - 1
    order = tuple(range(1, bits)) + (0,)
    cache_rows = cache[0]
    pairs = pair_slots[None]
    for bit in order[:-1]:
        cache_rows = jnp.concatenate([cache_rows, partner_2(cache_rows, bit)], 0)
    head_queries = lax.all_to_all(query_slots, "head", split_axis=0, concat_axis=0, tiled=True)
    for bit in order[:-1]:
        pairs = jnp.concatenate([pairs, partner_2(pairs, bit)], 0)
    w_part, pairs, cache_rows, head_queries = lax.optimization_barrier(
        (w_part, pairs, cache_rows, head_queries)
    )
    w_part = lax.all_gather(w_part, "head", axis=1, tiled=True)
    w_part = w_part.reshape(head_count * head_width, part_width)
    cache_other = partner_2(cache_rows, 0)
    pairs = jnp.concatenate([pairs, partner_2(pairs, 0)], 0)
    me = (lax.axis_index("head") % group_size).astype(jnp.int32).reshape(1)
    attended = attend(
        me, head_queries.reshape(-1, head_width), pairs, cache_rows, cache_other, order
    )
    returned = lax.all_to_all(
        attended.reshape(axis_count, local_rows, head_width),
        "head",
        split_axis=0,
        concat_axis=0,
        tiled=True,
    )
    attn_rows = returned.reshape(seq_count, head_count, local_rows, head_width)
    attn_rows = attn_rows.transpose(2, 0, 1, 3).reshape(row_count, head_count * head_width)
    parts = []
    for shift in range(1, grp_count):
        far_rows = turn_grp(attn_rows, shift)
        far_part = jnp.dot(far_rows, w_part, preferred_element_type=jnp.float32)
        parts.append(turn_grp(far_part.astype(jnp.bfloat16), -shift).astype(jnp.float32))
    projected = []
    near_part = jnp.dot(attn_rows, w_part, preferred_element_type=jnp.float32)
    for column in range(grp_count):
        piece = near_part
        for shift in range(1, grp_count):
            piece = jnp.where((grp_me + shift) % grp_count == column, parts[shift - 1], piece)
        projected.append(piece)
    projected = jnp.concatenate(projected, 1)
    stream = resid.reshape(row_count, model_width).astype(jnp.float32) + projected
    normed = stream * lax.rsqrt(jnp.mean(stream * stream, 1, keepdims=True) + eps_norm) * norm_gain
    normed = normed.astype(jnp.bfloat16)
    return stream, normed


def expert_body(
    normed_ref,
    stream_ref,
    info_ref,
    out_ref,
    top_count,
    w_in,
    w_down,
    rows_buf,
    info_buf,
    picked,
    inbox,
    outbox,
    answer,
    dense,
    summed,
    sums_in,
    sums_out,
    row_line,
    row_sent,
    info_line,
    info_sent,
    in_sem,
    in_sem_s,
    ans_sem,
    ans_sem_s,
    sum_sem,
    sum_sem_s,
):
    planes, rows, model = rows_buf.shape
    near, cap = inbox.shape[1:3]
    hidden_width = w_down.shape[0]
    chunks = row_line.shape[1]
    chunk = model // chunks
    g = lax.axis_index("grp")
    me = lax.axis_index("head")
    z, own = me // near, me % near
    up, down = (g, me + near), (g, me - near)
    has_up, has_down = z < planes - 1, z > 0

    def copy(src, dst, sent, got, peer):
        return pltpu.make_async_remote_copy(
            src_ref=src,
            dst_ref=dst,
            send_sem=sent,
            recv_sem=got,
            device_id=peer,
            device_id_type=MESH,
        )

    def arrived(dst, got):
        copy(dst, dst, got, got, (g, me ^ 1)).wait_recv()

    def left(src, sent):
        copy(src, src, sent, sent, (g, me ^ 1)).wait_send()

    def cols(index):
        return slice(index * chunk, (index + 1) * chunk)

    def by_plane(values):
        chosen = jnp.int32(values[0])
        for index, value in enumerate(values[1:], 1):
            chosen = jnp.where(z == index, value, chosen)
        return chosen

    def send_info(src, plane, way, peer):
        copy(src, info_buf.at[plane], info_sent.at[way, plane], info_line.at[plane], peer).start()

    def send_row(src, index, plane, way, peer):
        dst = rows_buf.at[plane, :, cols(index)]
        copy(src, dst, row_sent.at[way, plane, index], row_line.at[plane, index], peer).start()

    def slots_of(info):
        at = lax.broadcasted_iota(jnp.int32, (near * cap, rows), 0) + z * (near * cap)
        at = at.astype(jnp.float32)
        return [at == info[rank : rank + 1, :] for rank in range(top_count)]

    def pick(plane, info, load, indices):
        chosen = functools.reduce(jnp.logical_or, slots_of(info))
        chosen = jnp.where(chosen, 1.0, 0.0).astype(jnp.bfloat16)
        for index in indices:
            part = jnp.dot(chosen, load(index), preferred_element_type=jnp.float32)
            picked[plane, :, :, cols(index)] = part.astype(jnp.bfloat16).reshape(near, cap, chunk)
            for mask in range(1, near):
                other = own ^ mask
                copy(
                    picked.at[plane, other, :, cols(index)],
                    inbox.at[plane, own, :, cols(index)],
                    in_sem_s.at[plane, other],
                    in_sem.at[plane, own],
                    (g, me ^ mask),
                ).start()
            inbox[plane, own, :, cols(index)] = picked[plane, own, :, cols(index)]

    def receive(plane, indices):
        way = (plane > z).astype(jnp.int32)
        onward = jnp.where(way == 0, planes - 1 - z, z) > 0
        peer = (g, me + near - 2 * near * way)
        if indices[0] == 0:
            arrived(info_buf.at[plane], info_line.at[plane])

            @pl.when(onward)
            def _():
                send_info(info_buf.at[plane], plane, way, peer)

        def load(index):
            block = rows_buf.at[plane, :, cols(index)]
            arrived(block, row_line.at[plane, index])

            @pl.when(onward)
            def _():
                send_row(block, index, plane, way, peer)

            return block[...]

        pick(plane, info_buf[plane], load, indices)

    def run_expert(plane):
        for mask in range(1, near):
            arrived(inbox.at[plane, own ^ mask], in_sem.at[plane, own ^ mask])
        inner = jnp.dot(
            inbox[plane].reshape(near * cap, model), w_in[...], preferred_element_type=jnp.float32
        )
        gate, value = inner[:, :hidden_width], inner[:, hidden_width:]
        hidden = (gate / (1.0 + jnp.exp(-gate)) * value).astype(jnp.bfloat16)
        for index in range(chunks):
            part = jnp.dot(hidden, w_down[:, cols(index)], preferred_element_type=jnp.float32)
            outbox[plane, :, :, cols(index)] = part.astype(jnp.bfloat16).reshape(near, cap, chunk)
            for mask in range(1, near):
                other = own ^ mask
                copy(
                    outbox.at[plane, other, :, cols(index)],
                    answer.at[plane, own, :, cols(index)],
                    ans_sem_s.at[plane, other],
                    ans_sem.at[plane, own],
                    (g, me ^ mask),
                ).start()
            answer[plane, own, :, cols(index)] = outbox[plane, own, :, cols(index)]

    def combine(plane, info, store):
        for mask in range(1, near):
            arrived(answer.at[plane, own ^ mask], ans_sem.at[plane, own ^ mask])
        gates = jnp.zeros((near * cap, rows), jnp.float32)
        for rank, here in enumerate(slots_of(info)):
            gates = jnp.where(here, info[top_count + rank : top_count + rank + 1, :], gates)
        high = gates.astype(jnp.bfloat16)
        low = (gates - high.astype(jnp.float32)).astype(jnp.bfloat16)
        for index in range(chunks):
            values = answer[plane, :, :, cols(index)].reshape(near * cap, chunk)
            total = jnp.zeros((rows, chunk), jnp.float32)
            for term in (high, low):
                total = total + lax.dot_general(
                    term, values, (((0,), (0,)), ((), ())), preferred_element_type=jnp.float32
                )
            store(index, total)

    def combine_far(plane):
        def store(index, total):
            dense[plane, :, cols(index)] = total

        combine(plane, info_buf[plane], store)

    def pass_sum(target, index):
        way = (target < z).astype(jnp.int32)
        has_in = jnp.where(way == 0, z, planes - 1 - z) > 0
        peer = (g, me + near - 2 * near * way)
        block = sums_in.at[way, target, :, cols(index)]
        at = (way, target, index)

        @pl.when(has_in)
        def _():
            arrived(block, sum_sem.at[at])
            sums_out[target, :, cols(index)] = (
                dense[target, :, cols(index)] + block[...].astype(jnp.float32)
            ).astype(jnp.bfloat16)

        @pl.when(jnp.logical_not(has_in))
        def _():
            sums_out[target, :, cols(index)] = dense[target, :, cols(index)].astype(jnp.bfloat16)

        copy(
            sums_out.at[target, :, cols(index)], block, sum_sem_s.at[at], sum_sem.at[at], peer
        ).start()

    def combine_own():
        def store(index, total):
            summed[:, cols(index)] = stream_ref[:, cols(index)] + total

        combine(z, info_ref[...], store)

    @pl.when(has_up)
    def _():
        send_info(info_ref, z, 0, up)

    @pl.when(has_down)
    def _():
        send_info(info_ref, z, 1, down)

    for index in range(chunks):
        block = normed_ref.at[:, cols(index)]

        @pl.when(has_up)
        def _():
            send_row(block, index, z, 0, up)

        @pl.when(has_down)
        def _():
            send_row(block, index, z, 1, down)

    own_at = visit_order.index(tuple(range(planes)))
    plane_at = [by_plane(values) for values in visit_order]
    target_at = [by_plane(values) for values in return_order]

    def perform(segment):
        for word in segment:
            first = int(word[1])
            if word[0] == "P":
                indices = range(int(word[2]), int(word[3]) + 1)
                if first == own_at:
                    pick(z, info_ref[...], lambda index: normed_ref[:, cols(index)], indices)
                else:
                    receive(plane_at[first], indices)
            elif word[0] == "E" and first == own_at:
                combine_own()
            elif word[0] == "E":
                combine_far(plane_at[first])
            else:
                pass_sum(target_at[first], int(word[2]))

    def step_body(step, carry):
        for number, segment in enumerate(expert_order[:-1]):

            @pl.when(step == number)
            def _():
                perform(segment)

        plane = plane_at[0]
        for number, value in enumerate(plane_at[1:], 1):
            plane = jnp.where(step == number, value, plane)
        run_expert(plane)
        return carry

    lax.fori_loop(0, planes, step_body, 0)
    perform(expert_order[-1])

    for index in range(chunks):

        @pl.when(has_down)
        def _():
            block = sums_in.at[0, z, :, cols(index)]
            arrived(block, sum_sem.at[0, z, index])
            summed[:, cols(index)] = summed[:, cols(index)] + block[...].astype(jnp.float32)

        @pl.when(has_up)
        def _():
            block = sums_in.at[1, z, :, cols(index)]
            arrived(block, sum_sem.at[1, z, index])
            summed[:, cols(index)] = summed[:, cols(index)] + block[...].astype(jnp.float32)

        out_ref[:, cols(index)] = summed[:, cols(index)].astype(out_ref.dtype)

    def drain(plane, carry):
        @pl.when((plane <= z) & has_up)
        def _():
            left(info_buf.at[plane], info_sent.at[0, plane])
            for index in range(chunks):
                left(rows_buf.at[plane, :, cols(index)], row_sent.at[0, plane, index])

        @pl.when((plane >= z) & has_down)
        def _():
            left(info_buf.at[plane], info_sent.at[1, plane])
            for index in range(chunks):
                left(rows_buf.at[plane, :, cols(index)], row_sent.at[1, plane, index])

        for mask in range(1, near):
            left(picked.at[plane, own ^ mask], in_sem_s.at[plane, own ^ mask])
            left(outbox.at[plane, own ^ mask], ans_sem_s.at[plane, own ^ mask])

        for index in range(chunks):

            @pl.when(plane > z)
            def _():
                left(sums_out.at[plane, :, cols(index)], sum_sem_s.at[0, plane, index])

            @pl.when(plane < z)
            def _():
                left(sums_out.at[plane, :, cols(index)], sum_sem_s.at[1, plane, index])

        return carry

    lax.fori_loop(0, planes, drain, 0)


def layer_kernel(*refs, top_count, experts, cap, front_count):
    inputs, out_ref, rest = refs[:10], refs[10], refs[11:]
    ids_ref, gates_ref, w_in_ref, w_down_ref = inputs[6:]
    stream, normed, info, w_in, w_down, load_sem = rest[:6]
    front_scratch, expert_scratch = rest[6 : 6 + front_count], rest[6 + front_count :]

    def route():
        rows = ids_ref.shape[1]
        ids = ids_ref[...].astype(jnp.float32)
        named = lax.broadcasted_iota(jnp.int32, (experts, rows), 0).astype(jnp.float32)
        hits = [named == ids[rank : rank + 1] for rank in range(top_count)]
        onehot = sum(jnp.where(hit, 1.0, 0.0) for hit in hits).astype(jnp.bfloat16)
        first = lax.broadcasted_iota(jnp.int32, (rows, rows), 0)
        second = lax.broadcasted_iota(jnp.int32, (rows, rows), 1)
        before = jnp.where(first < second, 1.0, 0.0).astype(jnp.bfloat16)
        earlier = jnp.dot(onehot, before, preferred_element_type=jnp.float32)
        info[...] = jnp.zeros(info.shape, info.dtype)
        for rank, hit in enumerate(hits):
            place = jnp.sum(jnp.where(hit, earlier, 0.0), 0, keepdims=True)
            info[rank : rank + 1] = ids[rank : rank + 1] * cap + place
        info[top_count : 2 * top_count] = gates_ref[...]

    loads = (
        pltpu.make_async_copy(w_in_ref, w_in, load_sem.at[0]),
        pltpu.make_async_copy(w_down_ref, w_down, load_sem.at[1]),
    )
    for load in loads:
        load.start()
    front_body(*inputs[:6], stream, normed, route, *front_scratch)
    for load in loads:
        load.wait()
    expert_body(normed, stream, info, out_ref, top_count, w_in, w_down, *expert_scratch)


def layer(queries, pairs, cached, w_out, resid, gain, ids, gates, w_in, w_down, axis_count):
    rows, heads, width = queries.shape
    top_count = ids.shape[0]
    cap = 2 * rows * top_count // axis_count
    lines = -(-2 * top_count // 8) * 8
    group = heads // 2
    near = 4
    planes = axis_count // near
    model = w_out.shape[2]
    slice_rows = w_out.shape[1]
    page = cached.shape[0]
    pieces = 4
    chunks = 4
    dma = pltpu.SemaphoreType.DMA
    anywhere = pl.BlockSpec(memory_space=pl.ANY)
    inside = pl.BlockSpec(memory_space=pltpu.VMEM)

    def half(*shape):
        return pltpu.VMEM(shape, jnp.bfloat16)

    def full(*shape):
        return pltpu.VMEM(shape, jnp.float32)

    front_scratch = [
        half(rows, heads, width),
        half(2, group, rows, width),
        half(rows, 2, 2 * width),
        half(2, rows, 2 * width),
        half(2, group, rows, width),
        half(2, planes, 2, 2, rows, 2 * width),
        half(planes, 2, 2, page, 2 * width),
        half(group, planes, 2, 2, slice_rows, model),
        full(2, group, rows, width),
        full(2, group, rows, 128),
        full(2, group, rows, 128),
        half(2, rows, group * width),
        half(rows, model),
        half(rows, model),
        dma((4,)),
        dma((2,)),
        dma((planes,)),
        dma((planes,)),
        dma((planes,)),
        dma((planes,)),
        dma((planes, 2)),
        dma((planes, 2)),
        dma((planes,)),
        dma((planes,)),
        dma((planes,)),
        dma((planes,)),
        dma((planes,)),
        dma((planes, 2)),
        dma((planes, 2)),
        dma((pieces, planes, 2)),
        dma((pieces, planes, 2)),
        dma((pieces, planes, 2)),
        dma((pieces,)),
        dma((pieces,)),
        dma((pieces, planes, 2)),
        dma((pieces, planes, 2)),
        dma((pieces, planes, 2, 2)),
        dma((pieces, planes, 2, 2)),
        dma((2 * pieces,)),
        dma((2 * pieces,)),
    ]
    expert_scratch = [
        half(planes, rows, model),
        full(planes, lines, rows),
        half(planes, near, cap, model),
        half(planes, near, cap, model),
        half(planes, near, cap, model),
        half(planes, near, cap, model),
        full(planes, rows, model),
        full(rows, model),
        half(2, planes, rows, model),
        half(planes, rows, model),
        dma((planes, chunks)),
        dma((2, planes, chunks)),
        dma((planes,)),
        dma((2, planes)),
        dma((planes, near)),
        dma((planes, near)),
        dma((planes, near)),
        dma((planes, near)),
        dma((2, planes, chunks)),
        dma((2, planes, chunks)),
    ]
    return pl.pallas_call(
        functools.partial(
            layer_kernel,
            top_count=top_count,
            experts=axis_count,
            cap=cap,
            front_count=len(front_scratch),
        ),
        out_shape=jax.ShapeDtypeStruct((rows, model), jnp.bfloat16),
        in_specs=[anywhere] * 4 + [inside] * 4 + [anywhere] * 2,
        out_specs=inside,
        scratch_shapes=[
            full(rows, model),
            half(rows, model),
            full(lines, rows),
            half(*w_in.shape),
            half(*w_down.shape),
            dma((2,)),
            *front_scratch,
            *expert_scratch,
        ],
        compiler_params=pltpu.CompilerParams(
            collective_id=0, has_side_effects=True, vmem_limit_bytes=60 * 2**20
        ),
        cost_estimate=pl.CostEstimate(
            flops=4 * 2 * group * rows * width * 4 * axis_count * rows
            + 4 * rows * group * width * model
            + 6 * planes * near * cap * model * w_down.shape[0],
            bytes_accessed=12 * 2**20,
            transcendentals=2 * group * rows * axis_count * rows,
        ),
    )(queries, pairs, cached, w_out, resid, gain, ids, gates, w_in, w_down)


def experts(stream, normed, expert_ids, expert_gates, w_in, w_down):
    row_count, model_width = stream.shape
    axis_count = lax.axis_size("head")
    top_count = expert_ids.shape[2]
    flat_ids = expert_ids.reshape(-1)
    local_experts = w_in.shape[0]
    experts = local_experts * axis_count
    capacity = max(2, 2 * row_count * top_count // experts)
    onehot = (flat_ids[:, None] == jnp.arange(experts, dtype=jnp.int32)[None, :]).astype(jnp.int32)
    before = jnp.tri(flat_ids.shape[0], k=-1, dtype=jnp.bfloat16)
    earlier = jnp.dot(
        before, onehot.astype(jnp.bfloat16), preferred_element_type=jnp.float32
    ).astype(jnp.int32)
    slot_rank = jnp.sum(earlier * onehot, 1)
    target = flat_ids * capacity + slot_rank
    target = target.reshape(row_count, top_count)
    places = jnp.arange(experts * capacity, dtype=jnp.int32)
    chosen = jnp.zeros((experts * capacity, row_count), jnp.bool_)
    gate_of = jnp.zeros((row_count, experts * capacity), jnp.float32)
    gates = expert_gates.reshape(row_count, top_count)
    for rank in range(top_count):
        chosen = chosen | (places[:, None] == target[None, :, rank])
        gate_of = jnp.where(
            target[:, rank, None] == places[None, :], gates[:, rank, None], gate_of
        )
    outgoing = jnp.dot(
        chosen.astype(jnp.bfloat16), normed, preferred_element_type=jnp.float32
    ).astype(jnp.bfloat16)
    outgoing = outgoing.reshape(axis_count, local_experts, capacity, model_width)
    hidden_width = w_down.shape[1]
    inner_act = jnp.einsum(
        "semd,edf->semf",
        lax.all_to_all(outgoing, "head", split_axis=0, concat_axis=0, tiled=True),
        w_in,
        preferred_element_type=jnp.float32,
    )
    hidden = (jax.nn.silu(inner_act[..., :hidden_width]) * inner_act[..., hidden_width:]).astype(
        jnp.bfloat16
    )
    answered = jnp.einsum(
        "semf,efd->semd", hidden, w_down, preferred_element_type=jnp.float32
    ).astype(jnp.bfloat16)
    returned_rows = lax.all_to_all(answered, "head", split_axis=0, concat_axis=0, tiled=True)
    picked = returned_rows.reshape(experts * capacity, model_width)
    expert_sum = jnp.zeros((row_count, model_width), jnp.float32)
    rest = gate_of
    for _ in range(3):
        term = lax.reduce_precision(rest, 8, 7)
        rest = rest - term
        expert_sum = expert_sum + jnp.dot(
            term.astype(jnp.bfloat16), picked, preferred_element_type=jnp.float32
        )
    return (stream + expert_sum).astype(jnp.bfloat16)


def local(queries, new_kv, cache, resid, w_out, norm_gain, expert_ids, expert_gates, w_in, w_down):
    axis_count = lax.axis_size("head")
    local_rows, seq_count, head_count, head_width = queries.shape
    pair_heads = new_kv.shape[2]
    fits = (
        seq_count == 1
        and pair_heads == 2
        and lax.axis_size("grp") == 2
        and axis_count == 4 * (len(front_order[1]) + 1)
        and w_out.shape[2] % 1024 == 0
        and cache.shape[0] == 1
        and w_out.shape[1] * axis_count == head_width
        and w_out.shape[1] % 16 == 0
        and local_rows % 32 == 0
        and cache.shape[1] * 2 % 128 == 0
        and head_count % 4 == 0
    )
    top_count = expert_ids.shape[2]
    experts_count = w_in.shape[0] * axis_count
    row_count = local_rows * seq_count
    fits = (
        fits
        and w_in.shape[0] == 1
        and row_count % 128 == 0
        and (row_count * top_count * 2) % (16 * experts_count) == 0
    )
    if fits:
        out = layer(
            queries.reshape(local_rows, head_count, head_width),
            new_kv.reshape(local_rows, pair_heads, 2 * head_width),
            cache[0],
            w_out,
            resid.reshape(local_rows, -1),
            norm_gain.reshape(1, -1),
            expert_ids.reshape(local_rows, top_count).T,
            expert_gates.reshape(local_rows, top_count).T,
            w_in[0],
            w_down[0],
            axis_count,
        )
    else:
        stream, normed = front_general(queries, new_kv, cache, resid, w_out, norm_gain)
        out = experts(stream, normed, expert_ids, expert_gates, w_in, w_down)
    return out.reshape(resid.shape)


def solution(mesh):
    return jax.shard_map(
        local,
        mesh=mesh,
        in_specs=(
            P("head", "grp", None, None),
            P("head", "grp", None, None),
            P(("grp", "head"), None, None),
            P("head", "grp", None),
            P(None, "head", None),
            P(),
            P("head", "grp", None),
            P("head", "grp", None),
            P("head", None, None),
            P("head", None, None),
        ),
        out_specs=P("head", "grp", None),
        check_vma=False,
    )
```

```python
import functools

import jax
import jax.numpy as jnp
from jax import lax
from jax.experimental import pallas as pl
from jax.experimental.pallas import tpu as pltpu
from jax.sharding import PartitionSpec as P

eps_norm = 1e-06
MESH = pl.DeviceIdType.MESH
expert_order = (
    ("P301", "P000", "P200", "P011", "P211", "P022", "P222", "P033", "P233", "P100",),
    ("P113", "E0", "R10", "R11", "P322",),
    ("R12", "R13",),
    ("E1", "R20", "P333", "R21", "R22", "E2", "R00",),
    ("R23", "R01", "R02", "E3", "R03",),
)
visit_order = ((2, 2, 1, 1), (3, 3, 0, 0), (1, 0, 3, 2), (0, 1, 2, 3))
return_order = ((1, 0, 3, 2), (2, 2, 1, 1), (3, 3, 0, 0))
front_order = (
    ("o0", "o1", "L1", "s0", "s1", "o2", "F00", "W01", "q", "s2", "L2", "W11", "o3", "F01", "S0", "F20", "D",),
    (
        ("W21", "W02", "S1",),
        ("F10", "L3", "s3", "S2", "W12",),
        ("W03", "F30", "W22", "S3", "W31",),
    ),
    ("W13", "F21", "F11", "F02", "W23", "F12", "F22", "F03", "J0", "W32", "F13", "J1", "W33", "F23", "F31", "J2", "F32", "F33", "J3",),
)


def front_body(
    q_raw_ref,
    kv_raw_ref,
    cache_ref,
    w_ref,
    resid_ref,
    gain_ref,
    stream_ref,
    normed_ref,
    aside,
    q_raw,
    q_ref,
    kv_raw,
    kv_ref,
    q_buf,
    kn,
    kc,
    wb,
    acc,
    top,
    total,
    att,
    part_out,
    part_in,
    local_sem,
    q_sem,
    kn_line,
    kn_up,
    kn_side,
    kn_side_s,
    kn_twin,
    kn_twin_s,
    kc_line,
    kc_up,
    kc_down,
    kc_side,
    kc_side_s,
    kc_twin,
    kc_twin_s,
    w_line,
    w_up,
    w_down,
    w_side,
    w_side_s,
    w_far,
    w_far_s,
    w_twin,
    w_twin_s,
    part_sem,
    part_sem_s,
):
    planes = kn.shape[1]
    group = q_buf.shape[1]
    rows, width = q_buf.shape[2:]
    model = w_ref.shape[2]
    pieces = w_side.shape[0]
    half, chunk = model // 2, model // (2 * pieces)
    g = lax.axis_index("grp")
    me = lax.axis_index("head")
    z, y, c = me // 4, (me // 2) % 2, me % 2
    up, down = (g, me + 4), (g, me - 4)
    side, twin, far = (g, me + 2 - 4 * y), (g, me + 1 - 2 * c), (1 - g, me)
    has_up, has_down = z < planes - 1, z > 0

    raw = (
        pltpu.make_async_copy(kv_raw_ref, kv_raw, local_sem.at[0]),
        pltpu.make_async_copy(q_raw_ref, q_raw, local_sem.at[1]),
    )
    for item in raw:
        item.start()
    barrier = pltpu.get_barrier_semaphore()
    for peer in (side, twin, (g, me ^ 3), far):
        pl.semaphore_signal(barrier, inc=1, device_id=peer, device_id_type=MESH)

    @pl.when(has_up)
    def _():
        pl.semaphore_signal(barrier, inc=1, device_id=up, device_id_type=MESH)

    @pl.when(has_down)
    def _():
        pl.semaphore_signal(barrier, inc=1, device_id=down, device_id_type=MESH)

    pl.semaphore_wait(barrier, 4 + has_up.astype(jnp.int32) + has_down.astype(jnp.int32))

    def copy(src, dst, sent, got, peer):
        return pltpu.make_async_remote_copy(
            src_ref=src,
            dst_ref=dst,
            send_sem=sent,
            recv_sem=got,
            device_id=peer,
            device_id_type=MESH,
        )

    def arrived(dst, got):
        copy(dst, dst, got, got, twin).wait_recv()

    def left(src, sent):
        copy(src, src, sent, sent, twin).wait_send()

    def mine(plane):
        return plane // (planes // 2) == y

    cols_near = pl.ds(pl.multiple_of(g * half, half), half)
    raw[0].wait()
    kv_ref[...] = jnp.swapaxes(kv_raw[...], 0, 1)
    own_heads = pl.ds(y * group, group)
    other_heads = pl.ds((1 - y) * group, group)

    def w_cols(quarter, near):
        first = jnp.where(near, g, 1 - g) * half + quarter * chunk
        return pl.ds(pl.multiple_of(first, chunk), chunk)

    def w_block(quarter, plane, line, core, near=True):
        return wb.at[:, plane, line, core, :, w_cols(quarter, near)]

    def w_spread(src, quarter, plane, line):
        dst = w_block(quarter, plane, line, c)
        at = (quarter, plane, line)
        copy(src, dst, w_far_s.at[at], w_far.at[at], far).start()
        copy(src, dst, w_twin_s.at[(*at, 0)], w_twin.at[(*at, 0)], twin).start()

    def w_send_up(src, quarter, plane, line):
        at = (quarter, plane, line)

        @pl.when(has_up)
        def _():
            copy(src, w_block(quarter, plane, line, c), w_up.at[at], w_line.at[at], up).start()

    def w_send_down(src, quarter, plane, line):
        at = (quarter, plane, line)

        @pl.when(has_down)
        def _():
            copy(src, w_block(quarter, plane, line, c), w_down.at[at], w_line.at[at], down).start()

    def w_own_side(quarter):
        src = w_ref.at[other_heads, :, w_cols(quarter, True)]
        dst = w_block(quarter, z, y, c)
        copy(src, dst, w_side_s.at[quarter], w_side.at[quarter], side).start()

    def w_own(quarter):
        src = w_ref.at[own_heads, :, w_cols(quarter, True)]
        w_send_up(src, quarter, z, y)
        w_send_down(src, quarter, z, y)
        w_spread(src, quarter, z, y)

    def w_side_relay(quarter):
        block = w_block(quarter, z, 1 - y, c)
        arrived(block, w_side.at[quarter])
        w_send_up(block, quarter, z, 1 - y)
        w_send_down(block, quarter, z, 1 - y)
        w_spread(block, quarter, z, 1 - y)

    def w_relay(quarter, step):
        low, high = z - step, z + step
        for turn in range(2):
            line = y + turn - 2 * y * turn

            @pl.when(low >= 0)
            def _():
                block = w_block(quarter, low, line, c)
                arrived(block, w_line.at[quarter, low, line])
                w_send_up(block, quarter, low, line)
                w_spread(block, quarter, low, line)

            @pl.when(high < planes)
            def _():
                block = w_block(quarter, high, line, c)
                arrived(block, w_line.at[quarter, high, line])
                w_send_down(block, quarter, high, line)
                w_spread(block, quarter, high, line)

    def w_far_relay(quarter, plane):
        for line in range(2):
            block = w_block(quarter, plane, line, c, False)
            arrived(block, w_far.at[quarter, plane, line])
            at = (quarter, plane, line, 1)
            copy(block, block, w_twin_s.at[at], w_twin.at[at], twin).start()

    def w_far_relays(quarter, step):
        low, high = z - step, z + step

        @pl.when(low >= 0)
        def _():
            w_far_relay(quarter, low)

        if step > 0:

            @pl.when(high < planes)
            def _():
                w_far_relay(quarter, high)

    @pl.when(has_up)
    def _():
        copy(cache_ref, kc.at[z, y, c], kc_up.at[z], kc_line.at[z], up).start()
        copy(kv_ref, kn.at[:, z, y, c], kn_up.at[z], kn_line.at[z], up).start()

    @pl.when(has_down)
    def _():
        copy(cache_ref, kc.at[z, y, c], kc_down.at[z], kc_line.at[z], down).start()

    copy(kv_ref.at[1 - y], kn.at[1 - y, z, y, c], kn_side_s.at[z], kn_side.at[z], side).start()
    w_own_side(0)
    copy(kv_ref.at[y], kn.at[y, z, y, c], kn_twin_s.at[z, y], kn_twin.at[z, y], twin).start()

    @pl.when(mine(z))
    def _():
        copy(cache_ref, kc.at[z, y, c], kc_twin_s.at[z, y], kc_twin.at[z, y], twin).start()

    @pl.when(jnp.logical_not(mine(z)))
    def _():
        copy(cache_ref, kc.at[z, y, c], kc_side_s.at[z], kc_side.at[z], side).start()

    locals_ = (
        pltpu.make_async_copy(kv_ref.at[y], kn.at[y, z, y, c], local_sem.at[0]),
        pltpu.make_async_copy(cache_ref, kc.at[z, y, c], local_sem.at[2]),
        pltpu.make_async_copy(
            w_ref.at[own_heads, :, cols_near], wb.at[:, z, y, c, :, cols_near], local_sem.at[3]
        ),
    )
    for item in locals_:
        item.start()
    w_own_side(1)
    raw[1].wait()
    scale = jnp.asarray(width ** (-0.5), q_ref.dtype)
    q_ref[...] = (jnp.swapaxes(q_raw[...], 0, 1) * scale).reshape(q_ref.shape)
    copy(q_ref.at[1 - y], q_buf.at[y], q_sem.at[0], q_sem.at[1], side).start()
    for piece in range(2, pieces):
        w_own_side(piece)
    q_buf[y] = q_ref[y]
    aside()

    def from_side_new(plane):
        block = kn.at[y, plane, 1 - y, c]
        arrived(block, kn_side.at[plane])
        copy(block, block, kn_twin_s.at[plane, 1 - y], kn_twin.at[plane, 1 - y], twin).start()

    def from_side_old(plane):
        @pl.when(mine(plane))
        def _():
            block = kc.at[plane, 1 - y, c]
            arrived(block, kc_side.at[plane])
            copy(block, block, kc_twin_s.at[plane, 1 - y], kc_twin.at[plane, 1 - y], twin).start()

    def spread_old(plane):
        block = kc.at[plane, y, c]

        @pl.when(mine(plane))
        def _():
            copy(block, block, kc_twin_s.at[plane, y], kc_twin.at[plane, y], twin).start()

        @pl.when(jnp.logical_not(mine(plane)))
        def _():
            copy(block, block, kc_side_s.at[plane], kc_side.at[plane], side).start()

    def relay(step):
        low, high = z - step, z + step

        @pl.when(high < planes)
        def _():
            old = kc.at[high, y, c]
            arrived(old, kc_line.at[high])

            @pl.when(has_down)
            def _():
                copy(old, old, kc_down.at[high], kc_line.at[high], down).start()

            spread_old(high)

        @pl.when(low >= 0)
        def _():
            old, new = kc.at[low, y, c], kn.at[:, low, y, c]
            arrived(old, kc_line.at[low])

            @pl.when(has_up)
            def _():
                copy(old, old, kc_up.at[low], kc_line.at[low], up).start()

            arrived(new, kn_line.at[low])

            @pl.when(has_up)
            def _():
                copy(new, new, kn_up.at[low], kn_line.at[low], up).start()

            there, here = kn.at[1 - y, low, y, c], kn.at[y, low, y, c]
            copy(there, there, kn_side_s.at[low], kn_side.at[low], side).start()
            copy(here, here, kn_twin_s.at[low, y], kn_twin.at[low, y], twin).start()
            spread_old(low)

    def from_side(step):
        low, high = z - step, z + step

        @pl.when(low >= 0)
        def _():
            from_side_new(low)
            from_side_old(low)

        if step > 0:

            @pl.when(high < planes)
            def _():
                from_side_old(high)

    tile = 2
    tile_rows = tile * rows

    def fold(keys, values, diagonal):
        def lines(line, carry):
            for part in range(group // tile):
                heads = pl.ds(part * tile, tile)
                queries = q_buf[line, heads].reshape(tile_rows, width)
                scores = lax.dot_general(
                    queries, keys(), (((1,), (1,)), ((), ())), preferred_element_type=jnp.float32
                )
                pieces = [
                    scores[:, first : first + 128] for first in range(0, scores.shape[1], 128)
                ]
                if diagonal:
                    row_at = lax.broadcasted_iota(jnp.int32, (tile_rows, 128), 0) % rows
                    ahead = row_at - lax.broadcasted_iota(jnp.int32, (tile_rows, 128), 1)
                    ahead = ahead + (line * 2 + c) * rows
                    pieces = [
                        jnp.where(ahead >= index * 128, piece, -jnp.inf)
                        for index, piece in enumerate(pieces)
                    ]
                best = functools.reduce(jnp.maximum, pieces)
                best = jnp.max(best, 1, keepdims=True)
                if diagonal:
                    new_top = jnp.broadcast_to(best, (tile_rows, 128))
                else:
                    old_top = top[line, heads].reshape(tile_rows, 128)
                    new_top = jnp.maximum(old_top, best)
                exps = [jnp.exp(piece - new_top) for piece in pieces]
                new_total = functools.reduce(jnp.add, exps)
                weighted = jnp.dot(
                    jnp.concatenate([part_.astype(jnp.bfloat16) for part_ in exps], 1),
                    values(),
                    preferred_element_type=jnp.float32,
                )
                if not diagonal:
                    shrink = jnp.exp(old_top - new_top)
                    new_total = new_total + total[line, heads].reshape(tile_rows, 128) * shrink
                    weighted = weighted + acc[line, heads].reshape(
                        tile_rows, width
                    ) * jnp.concatenate([shrink] * (width // 128), 1)
                top[line, heads] = new_top.reshape(tile, rows, 128)
                total[line, heads] = new_total.reshape(tile, rows, 128)
                acc[line, heads] = weighted.reshape(tile, rows, width)
            return carry

        lax.fori_loop(0, 2, lines, 0, unroll=2)

    def new_part(plane, first):
        return lambda: kn[y, plane, :, :, :, first : first + width].reshape(4 * rows, width)

    page = kc.shape[3]

    def old_part(plane, line, first):
        return lambda: kc[plane, line, :, :, first : first + width].reshape(2 * page, width)

    def twins_new(plane):
        for line in range(2):
            arrived(kn.at[y, plane, line, 1 - c], kn_twin.at[plane, line])

    def twins_old(plane):
        for line in range(2):
            arrived(kc.at[plane, line, 1 - c], kc_twin.at[plane, line])

    def first_fold():
        twins_new(z)
        fold(new_part(z, 0), new_part(z, width), True)

    def queries_here():
        arrived(q_buf.at[1 - y], q_sem.at[1])
        for item in locals_:
            item.wait()

    def later_folds(step):
        low, high = z - step, z + step

        @pl.when((step >= 1) & (low >= 0))
        def _():
            twins_new(low)
            fold(new_part(low, 0), new_part(low, width), False)

        def old_body(index, carry):
            plane = jnp.where(index == 0, low, high)
            valid = (plane >= 0) & (plane < planes) & ((index == 0) | (step > 0))

            @pl.when(valid & mine(plane))
            def _():
                twins_old(plane)

                def line_body(line, carry):
                    fold(old_part(plane, line, 0), old_part(plane, line, width), False)
                    return carry

                lax.fori_loop(0, 2, line_body, 0)

            return carry

        lax.fori_loop(0, 2, old_body, 0)

    def finish():
        for line in range(2):
            for head in range(group):
                att[line, :, head * width : (head + 1) * width] = (
                    acc[line, head] * (1.0 / jnp.sum(total[line, head], 1, keepdims=True))
                ).astype(att.dtype)

    def project(quarter):
        for near in range(2):
            for plane in range(planes):
                for line in range(2):
                    arrived(
                        w_block(quarter, plane, line, 1 - c, near == 0),
                        w_twin.at[quarter, plane, line, near],
                    )
            cols = w_cols(quarter, near == 0)
            weights = wb[:, :, :, :, :, cols].reshape(group * width, chunk)
            both = jnp.dot(
                att[...].reshape(2 * rows, group * width),
                weights,
                preferred_element_type=jnp.float32,
            )
            there = jnp.where(y == 0, both[rows:], both[:rows])
            here = jnp.where(y == 0, both[:rows], both[rows:])
            part_out[:, cols] = there.astype(part_out.dtype)
            index = quarter * 2 + near
            block = part_out.at[:, cols]
            copy(block, part_in.at[:, cols], part_sem_s.at[index], part_sem.at[index], side).start()
            stream_ref[:, cols] = here + resid_ref[:, cols].astype(jnp.float32)

    acts = {
        "o": w_own,
        "s": w_side_relay,
        "L": relay,
        "S": from_side,
        "q": queries_here,
        "D": first_fold,
        "W": w_relay,
        "F": w_far_relays,
        "J": project,
    }

    def perform(segment):
        for word in segment:
            acts[word[0]](*(int(digit) for digit in word[1:]))

    before, between, after = front_order
    perform(before)

    def step_body(step, carry):
        for number, segment in enumerate(between):

            @pl.when(step == number + 1)
            def _():
                perform(segment)

        later_folds(step)
        return carry

    lax.fori_loop(0, planes, step_body, 0)
    finish()
    perform(after)
    square = jnp.zeros((rows, 1), jnp.float32)
    for quarter in range(pieces):
        for near in range(2):
            cols = w_cols(quarter, near == 0)
            index = quarter * 2 + near
            arrived(part_in.at[:, cols], part_sem.at[index])
            stream = stream_ref[:, cols] + part_in[:, cols].astype(jnp.float32)
            stream_ref[:, cols] = stream
            square = square + jnp.sum(stream * stream, 1, keepdims=True)
            left(part_out.at[:, cols], part_sem_s.at[index])
    inverse = lax.rsqrt(square / model + eps_norm)
    for index in range(2 * pieces):
        cols = slice(index * chunk, (index + 1) * chunk)
        normed_ref[:, cols] = (stream_ref[:, cols] * inverse * gain_ref[:, cols]).astype(
            normed_ref.dtype
        )

    left(q_buf.at[y], q_sem.at[0])
    for quarter in range(pieces):
        left(w_block(quarter, z, y, c), w_side_s.at[quarter])

    def drain(plane, carry):
        reached = plane <= z

        @pl.when(reached)
        def _():
            left(kn.at[1 - y, plane, y, c], kn_side_s.at[plane])
            left(kn.at[y, plane, y, c], kn_twin_s.at[plane, y])
            left(kn.at[y, plane, 1 - y, c], kn_twin_s.at[plane, 1 - y])

        @pl.when(reached & has_up)
        def _():
            left(kn.at[:, plane, y, c], kn_up.at[plane])
            left(kc.at[plane, y, c], kc_up.at[plane])
            for quarter in range(pieces):
                for line in range(2):
                    left(w_block(quarter, plane, line, c), w_up.at[quarter, plane, line])

        @pl.when((plane >= z) & has_down)
        def _():
            left(kc.at[plane, y, c], kc_down.at[plane])
            for quarter in range(pieces):
                for line in range(2):
                    left(w_block(quarter, plane, line, c), w_down.at[quarter, plane, line])

        @pl.when(mine(plane))
        def _():
            for line in range(2):
                left(kc.at[plane, line, c], kc_twin_s.at[plane, line])

        @pl.when(jnp.logical_not(mine(plane)))
        def _():
            left(kc.at[plane, y, c], kc_side_s.at[plane])

        for quarter in range(pieces):
            for line in range(2):
                at = (quarter, plane, line)
                left(w_block(quarter, plane, line, c), w_far_s.at[at])
                left(w_block(quarter, plane, line, c), w_twin_s.at[(*at, 0)])
                left(w_block(quarter, plane, line, c, False), w_twin_s.at[(*at, 1)])
        return carry

    lax.fori_loop(0, planes, drain, 0)


def partner_2(value, stride):
    mask = 2**stride
    pairs = [(source, source ^ mask) for source in range(lax.axis_size("head"))]
    return lax.ppermute(value, "head", pairs)


def turn_grp(value, shift):
    count = lax.axis_size("grp")
    return lax.ppermute(value, "grp", [(i, (i + shift) % count) for i in range(count)])


def attend_kernel(
    me_ref, query_ref, cache_ref, other_ref, pairs_ref, out_ref, new_ref, *, block, old_block, order
):
    head_width = query_ref.shape[1]
    step = pl.program_id(0)
    members, slots, local_rows = pairs_ref.shape[:3]

    @pl.when(step == 0)
    def _():
        for slot in range(slots):
            for member in range(members):
                apart = member ^ me_ref[0]
                place = 0
                for rank, bit in enumerate(order):
                    place = place + ((apart >> bit) & 1) * 2**rank
                first = (slot * members + member) * local_rows
                new_ref[first : first + local_rows, :] = pairs_ref[place, slot]

    query_rows = query_ref[...] * jnp.asarray(head_width ** (-0.5), query_ref.dtype)

    def fold(carry, keys, values, mask):
        top, total, weighted = carry
        scores = lax.dot_general(
            query_rows, keys, (((1,), (1,)), ((), ())), preferred_element_type=jnp.float32
        )
        if mask is not None:
            scores = jnp.where(mask, scores, -jnp.inf)
        new_top = jnp.maximum(top, jnp.max(scores, 1, keepdims=True))
        exps = jnp.exp(scores - new_top)
        shrink = jnp.exp(top - new_top)
        total = total * shrink + jnp.sum(exps, 1, keepdims=True)
        weighted = weighted * shrink + jnp.dot(
            exps.astype(jnp.bfloat16), values, preferred_element_type=jnp.float32
        )
        return new_top, total, weighted

    rows = query_rows.shape[0]
    carry = (
        jnp.full((rows, 1), -jnp.inf, jnp.float32),
        jnp.zeros((rows, 1), jnp.float32),
        jnp.zeros((rows, head_width), jnp.float32),
    )
    row_at = lax.broadcasted_iota(jnp.int32, (rows, block), 0)
    col_at = lax.broadcasted_iota(jnp.int32, (rows, block), 1)
    here = pl.ds(step * block, block)
    carry = fold(
        carry, new_ref[here, :head_width], new_ref[here, head_width:], col_at <= row_at
    )
    for old_ref in (cache_ref, other_ref):
        for first in range(0, old_ref.shape[0], old_block):
            part = pl.ds(first, old_block)
            carry = fold(carry, old_ref[part, :head_width], old_ref[part, head_width:], None)

    def earlier(index, carry):
        part = pl.ds(index * block, block)
        return fold(carry, new_ref[part, :head_width], new_ref[part, head_width:], None)

    top, total, weighted = lax.fori_loop(0, step, earlier, carry)
    out_ref[...] = (weighted / total).astype(out_ref.dtype)


def attend(me, queries, new_pairs, cached, cached_other, order):
    length, head_width = queries.shape
    block = min(512, length)
    old_block = min(1024, cached.shape[0])
    return pl.pallas_call(
        functools.partial(attend_kernel, block=block, old_block=old_block, order=order),
        grid_spec=pltpu.PrefetchScalarGridSpec(
            num_scalar_prefetch=1,
            grid=(length // block,),
            in_specs=[
                pl.BlockSpec((block, head_width), lambda i, me: (i, 0)),
                pl.BlockSpec(cached.shape, lambda i, me: (0, 0)),
                pl.BlockSpec(cached_other.shape, lambda i, me: (0, 0)),
                pl.BlockSpec(new_pairs.shape, lambda i, me: (0, 0, 0, 0)),
            ],
            out_specs=pl.BlockSpec((block, head_width), lambda i, me: (i, 0)),
            scratch_shapes=[pltpu.VMEM((length, 2 * head_width), jnp.bfloat16)],
        ),
        out_shape=jax.ShapeDtypeStruct((length, head_width), jnp.bfloat16),
        cost_estimate=pl.CostEstimate(
            flops=4 * length * head_width * (length // 2 + 2 * cached.shape[0]),
            bytes_accessed=8 * length * head_width * 2,
            transcendentals=length * (length // 2 + 2 * cached.shape[0]),
        ),
    )(me, queries, cached, cached_other, new_pairs)


def front_general(queries, new_kv, cache, resid, w_out, norm_gain):
    axis_count = lax.axis_size("head")
    local_rows = queries.shape[0]
    seq_count = queries.shape[1]
    head_count = queries.shape[2]
    head_width = queries.shape[3]
    pair_heads = new_kv.shape[2]
    group_size = head_count // pair_heads
    model_width = resid.shape[2]
    row_count = local_rows * seq_count
    slots = seq_count * pair_heads
    across = [[c * group_size + j for c in range(slots)] for j in range(group_size)]
    query_slots = queries.reshape(local_rows, axis_count, head_width).transpose(1, 0, 2)
    pair_slots = new_kv.reshape(local_rows, slots, 2 * head_width).transpose(1, 0, 2)
    pair_slots = lax.all_to_all(
        pair_slots, "head", split_axis=0, concat_axis=0, axis_index_groups=across, tiled=True
    )
    grp_count = lax.axis_size("grp")
    grp_me = lax.axis_index("grp")
    part_width = model_width // grp_count
    w_part = lax.dynamic_slice_in_dim(w_out, grp_me * part_width, part_width, 2)
    bits = group_size.bit_length() - 1
    order = tuple(range(1, bits)) + (0,)
    cache_rows = cache[0]
    pairs = pair_slots[None]
    for bit in order[:-1]:
        cache_rows = jnp.concatenate([cache_rows, partner_2(cache_rows, bit)], 0)
    head_queries = lax.all_to_all(query_slots, "head", split_axis=0, concat_axis=0, tiled=True)
    for bit in order[:-1]:
        pairs = jnp.concatenate([pairs, partner_2(pairs, bit)], 0)
    w_part, pairs, cache_rows, head_queries = lax.optimization_barrier(
        (w_part, pairs, cache_rows, head_queries)
    )
    w_part = lax.all_gather(w_part, "head", axis=1, tiled=True)
    w_part = w_part.reshape(head_count * head_width, part_width)
    cache_other = partner_2(cache_rows, 0)
    pairs = jnp.concatenate([pairs, partner_2(pairs, 0)], 0)
    me = (lax.axis_index("head") % group_size).astype(jnp.int32).reshape(1)
    attended = attend(
        me, head_queries.reshape(-1, head_width), pairs, cache_rows, cache_other, order
    )
    returned = lax.all_to_all(
        attended.reshape(axis_count, local_rows, head_width),
        "head",
        split_axis=0,
        concat_axis=0,
        tiled=True,
    )
    attn_rows = returned.reshape(seq_count, head_count, local_rows, head_width)
    attn_rows = attn_rows.transpose(2, 0, 1, 3).reshape(row_count, head_count * head_width)
    parts = []
    for shift in range(1, grp_count):
        far_rows = turn_grp(attn_rows, shift)
        far_part = jnp.dot(far_rows, w_part, preferred_element_type=jnp.float32)
        parts.append(turn_grp(far_part.astype(jnp.bfloat16), -shift).astype(jnp.float32))
    projected = []
    near_part = jnp.dot(attn_rows, w_part, preferred_element_type=jnp.float32)
    for column in range(grp_count):
        piece = near_part
        for shift in range(1, grp_count):
            piece = jnp.where((grp_me + shift) % grp_count == column, parts[shift - 1], piece)
        projected.append(piece)
    projected = jnp.concatenate(projected, 1)
    stream = resid.reshape(row_count, model_width).astype(jnp.float32) + projected
    normed = stream * lax.rsqrt(jnp.mean(stream * stream, 1, keepdims=True) + eps_norm) * norm_gain
    normed = normed.astype(jnp.bfloat16)
    return stream, normed


def expert_body(
    normed_ref,
    stream_ref,
    info_ref,
    out_ref,
    top_count,
    w_in,
    w_down,
    rows_buf,
    info_buf,
    picked,
    inbox,
    outbox,
    answer,
    dense,
    summed,
    sums_in,
    sums_out,
    row_line,
    row_sent,
    info_line,
    info_sent,
    in_sem,
    in_sem_s,
    ans_sem,
    ans_sem_s,
    sum_sem,
    sum_sem_s,
):
    planes, rows, model = rows_buf.shape
    near, cap = inbox.shape[1:3]
    hidden_width = w_down.shape[0]
    chunks = row_line.shape[1]
    chunk = model // chunks
    g = lax.axis_index("grp")
    me = lax.axis_index("head")
    z, own = me // near, me % near
    up, down = (g, me + near), (g, me - near)
    has_up, has_down = z < planes - 1, z > 0

    def copy(src, dst, sent, got, peer):
        return pltpu.make_async_remote_copy(
            src_ref=src,
            dst_ref=dst,
            send_sem=sent,
            recv_sem=got,
            device_id=peer,
            device_id_type=MESH,
        )

    def arrived(dst, got):
        copy(dst, dst, got, got, (g, me ^ 1)).wait_recv()

    def left(src, sent):
        copy(src, src, sent, sent, (g, me ^ 1)).wait_send()

    def cols(index):
        return slice(index * chunk, (index + 1) * chunk)

    def by_plane(values):
        chosen = jnp.int32(values[0])
        for index, value in enumerate(values[1:], 1):
            chosen = jnp.where(z == index, value, chosen)
        return chosen

    def send_info(src, plane, way, peer):
        copy(src, info_buf.at[plane], info_sent.at[way, plane], info_line.at[plane], peer).start()

    def send_row(src, index, plane, way, peer):
        dst = rows_buf.at[plane, :, cols(index)]
        copy(src, dst, row_sent.at[way, plane, index], row_line.at[plane, index], peer).start()

    def slots_of(info):
        at = lax.broadcasted_iota(jnp.int32, (near * cap, rows), 0) + z * (near * cap)
        at = at.astype(jnp.float32)
        return [at == info[rank : rank + 1, :] for rank in range(top_count)]

    def pick(plane, info, load, indices):
        chosen = functools.reduce(jnp.logical_or, slots_of(info))
        chosen = jnp.where(chosen, 1.0, 0.0).astype(jnp.bfloat16)
        for index in indices:
            part = jnp.dot(chosen, load(index), preferred_element_type=jnp.float32)
            picked[plane, :, :, cols(index)] = part.astype(jnp.bfloat16).reshape(near, cap, chunk)
            for mask in range(1, near):
                other = own ^ mask
                copy(
                    picked.at[plane, other, :, cols(index)],
                    inbox.at[plane, own, :, cols(index)],
                    in_sem_s.at[plane, other],
                    in_sem.at[plane, own],
                    (g, me ^ mask),
                ).start()
            inbox[plane, own, :, cols(index)] = picked[plane, own, :, cols(index)]

    def receive(plane, indices):
        way = (plane > z).astype(jnp.int32)
        onward = jnp.where(way == 0, planes - 1 - z, z) > 0
        peer = (g, me + near - 2 * near * way)
        if indices[0] == 0:
            arrived(info_buf.at[plane], info_line.at[plane])

            @pl.when(onward)
            def _():
                send_info(info_buf.at[plane], plane, way, peer)

        def load(index):
            block = rows_buf.at[plane, :, cols(index)]
            arrived(block, row_line.at[plane, index])

            @pl.when(onward)
            def _():
                send_row(block, index, plane, way, peer)

            return block[...]

        pick(plane, info_buf[plane], load, indices)

    def run_expert(plane):
        for mask in range(1, near):
            arrived(inbox.at[plane, own ^ mask], in_sem.at[plane, own ^ mask])
        inner = jnp.dot(
            inbox[plane].reshape(near * cap, model), w_in[...], preferred_element_type=jnp.float32
        )
        gate, value = inner[:, :hidden_width], inner[:, hidden_width:]
        hidden = (gate / (1.0 + jnp.exp(-gate)) * value).astype(jnp.bfloat16)
        for index in range(chunks):
            part = jnp.dot(hidden, w_down[:, cols(index)], preferred_element_type=jnp.float32)
            outbox[plane, :, :, cols(index)] = part.astype(jnp.bfloat16).reshape(near, cap, chunk)
            for mask in range(1, near):
                other = own ^ mask
                copy(
                    outbox.at[plane, other, :, cols(index)],
                    answer.at[plane, own, :, cols(index)],
                    ans_sem_s.at[plane, other],
                    ans_sem.at[plane, own],
                    (g, me ^ mask),
                ).start()
            answer[plane, own, :, cols(index)] = outbox[plane, own, :, cols(index)]

    def combine(plane, info, store):
        for mask in range(1, near):
            arrived(answer.at[plane, own ^ mask], ans_sem.at[plane, own ^ mask])
        gates = jnp.zeros((near * cap, rows), jnp.float32)
        for rank, here in enumerate(slots_of(info)):
            gates = jnp.where(here, info[top_count + rank : top_count + rank + 1, :], gates)
        high = gates.astype(jnp.bfloat16)
        low = (gates - high.astype(jnp.float32)).astype(jnp.bfloat16)
        for index in range(chunks):
            values = answer[plane, :, :, cols(index)].reshape(near * cap, chunk)
            total = jnp.zeros((rows, chunk), jnp.float32)
            for term in (high, low):
                total = total + lax.dot_general(
                    term, values, (((0,), (0,)), ((), ())), preferred_element_type=jnp.float32
                )
            store(index, total)

    def combine_far(plane):
        def store(index, total):
            dense[plane, :, cols(index)] = total

        combine(plane, info_buf[plane], store)

    def pass_sum(target, index):
        way = (target < z).astype(jnp.int32)
        has_in = jnp.where(way == 0, z, planes - 1 - z) > 0
        peer = (g, me + near - 2 * near * way)
        block = sums_in.at[way, target, :, cols(index)]
        at = (way, target, index)

        @pl.when(has_in)
        def _():
            arrived(block, sum_sem.at[at])
            sums_out[target, :, cols(index)] = (
                dense[target, :, cols(index)] + block[...].astype(jnp.float32)
            ).astype(jnp.bfloat16)

        @pl.when(jnp.logical_not(has_in))
        def _():
            sums_out[target, :, cols(index)] = dense[target, :, cols(index)].astype(jnp.bfloat16)

        copy(
            sums_out.at[target, :, cols(index)], block, sum_sem_s.at[at], sum_sem.at[at], peer
        ).start()

    def combine_own():
        def store(index, total):
            summed[:, cols(index)] = stream_ref[:, cols(index)] + total

        combine(z, info_ref[...], store)

    @pl.when(has_up)
    def _():
        send_info(info_ref, z, 0, up)

    @pl.when(has_down)
    def _():
        send_info(info_ref, z, 1, down)

    for index in range(chunks):
        block = normed_ref.at[:, cols(index)]

        @pl.when(has_up)
        def _():
            send_row(block, index, z, 0, up)

        @pl.when(has_down)
        def _():
            send_row(block, index, z, 1, down)

    own_at = visit_order.index(tuple(range(planes)))
    plane_at = [by_plane(values) for values in visit_order]
    target_at = [by_plane(values) for values in return_order]

    def perform(segment):
        for word in segment:
            first = int(word[1])
            if word[0] == "P":
                indices = range(int(word[2]), int(word[3]) + 1)
                if first == own_at:
                    pick(z, info_ref[...], lambda index: normed_ref[:, cols(index)], indices)
                else:
                    receive(plane_at[first], indices)
            elif word[0] == "E" and first == own_at:
                combine_own()
            elif word[0] == "E":
                combine_far(plane_at[first])
            else:
                pass_sum(target_at[first], int(word[2]))

    def step_body(step, carry):
        for number, segment in enumerate(expert_order[:-1]):

            @pl.when(step == number)
            def _():
                perform(segment)

        plane = plane_at[0]
        for number, value in enumerate(plane_at[1:], 1):
            plane = jnp.where(step == number, value, plane)
        run_expert(plane)
        return carry

    lax.fori_loop(0, planes, step_body, 0)
    perform(expert_order[-1])

    for index in range(chunks):

        @pl.when(has_down)
        def _():
            block = sums_in.at[0, z, :, cols(index)]
            arrived(block, sum_sem.at[0, z, index])
            summed[:, cols(index)] = summed[:, cols(index)] + block[...].astype(jnp.float32)

        @pl.when(has_up)
        def _():
            block = sums_in.at[1, z, :, cols(index)]
            arrived(block, sum_sem.at[1, z, index])
            summed[:, cols(index)] = summed[:, cols(index)] + block[...].astype(jnp.float32)

        out_ref[:, cols(index)] = summed[:, cols(index)].astype(out_ref.dtype)

    def drain(plane, carry):
        @pl.when((plane <= z) & has_up)
        def _():
            left(info_buf.at[plane], info_sent.at[0, plane])
            for index in range(chunks):
                left(rows_buf.at[plane, :, cols(index)], row_sent.at[0, plane, index])

        @pl.when((plane >= z) & has_down)
        def _():
            left(info_buf.at[plane], info_sent.at[1, plane])
            for index in range(chunks):
                left(rows_buf.at[plane, :, cols(index)], row_sent.at[1, plane, index])

        for mask in range(1, near):
            left(picked.at[plane, own ^ mask], in_sem_s.at[plane, own ^ mask])
            left(outbox.at[plane, own ^ mask], ans_sem_s.at[plane, own ^ mask])

        for index in range(chunks):

            @pl.when(plane > z)
            def _():
                left(sums_out.at[plane, :, cols(index)], sum_sem_s.at[0, plane, index])

            @pl.when(plane < z)
            def _():
                left(sums_out.at[plane, :, cols(index)], sum_sem_s.at[1, plane, index])

        return carry

    lax.fori_loop(0, planes, drain, 0)


def layer_kernel(*refs, top_count, experts, cap, front_count):
    inputs, out_ref, rest = refs[:10], refs[10], refs[11:]
    ids_ref, gates_ref, w_in_ref, w_down_ref = inputs[6:]
    stream, normed, info, w_in, w_down, load_sem = rest[:6]
    front_scratch, expert_scratch = rest[6 : 6 + front_count], rest[6 + front_count :]

    def route():
        rows = ids_ref.shape[1]
        ids = ids_ref[...].astype(jnp.float32)
        named = lax.broadcasted_iota(jnp.int32, (experts, rows), 0).astype(jnp.float32)
        hits = [named == ids[rank : rank + 1] for rank in range(top_count)]
        onehot = sum(jnp.where(hit, 1.0, 0.0) for hit in hits).astype(jnp.bfloat16)
        first = lax.broadcasted_iota(jnp.int32, (rows, rows), 0)
        second = lax.broadcasted_iota(jnp.int32, (rows, rows), 1)
        before = jnp.where(first < second, 1.0, 0.0).astype(jnp.bfloat16)
        earlier = jnp.dot(onehot, before, preferred_element_type=jnp.float32)
        info[...] = jnp.zeros(info.shape, info.dtype)
        for rank, hit in enumerate(hits):
            place = jnp.sum(jnp.where(hit, earlier, 0.0), 0, keepdims=True)
            info[rank : rank + 1] = ids[rank : rank + 1] * cap + place
        info[top_count : 2 * top_count] = gates_ref[...]

    loads = (
        pltpu.make_async_copy(w_in_ref, w_in, load_sem.at[0]),
        pltpu.make_async_copy(w_down_ref, w_down, load_sem.at[1]),
    )
    for load in loads:
        load.start()
    front_body(*inputs[:6], stream, normed, route, *front_scratch)
    for load in loads:
        load.wait()
    expert_body(normed, stream, info, out_ref, top_count, w_in, w_down, *expert_scratch)


def layer(queries, pairs, cached, w_out, resid, gain, ids, gates, w_in, w_down, axis_count):
    rows, heads, width = queries.shape
    top_count = ids.shape[0]
    cap = 2 * rows * top_count // axis_count
    lines = -(-2 * top_count // 8) * 8
    group = heads // 2
    near = 4
    planes = axis_count // near
    model = w_out.shape[2]
    slice_rows = w_out.shape[1]
    page = cached.shape[0]
    pieces = 4
    chunks = 4
    dma = pltpu.SemaphoreType.DMA
    anywhere = pl.BlockSpec(memory_space=pl.ANY)
    inside = pl.BlockSpec(memory_space=pltpu.VMEM)

    def half(*shape):
        return pltpu.VMEM(shape, jnp.bfloat16)

    def full(*shape):
        return pltpu.VMEM(shape, jnp.float32)

    front_scratch = [
        half(rows, heads, width),
        half(2, group, rows, width),
        half(rows, 2, 2 * width),
        half(2, rows, 2 * width),
        half(2, group, rows, width),
        half(2, planes, 2, 2, rows, 2 * width),
        half(planes, 2, 2, page, 2 * width),
        half(group, planes, 2, 2, slice_rows, model),
        full(2, group, rows, width),
        full(2, group, rows, 128),
        full(2, group, rows, 128),
        half(2, rows, group * width),
        half(rows, model),
        half(rows, model),
        dma((4,)),
        dma((2,)),
        dma((planes,)),
        dma((planes,)),
        dma((planes,)),
        dma((planes,)),
        dma((planes, 2)),
        dma((planes, 2)),
        dma((planes,)),
        dma((planes,)),
        dma((planes,)),
        dma((planes,)),
        dma((planes,)),
        dma((planes, 2)),
        dma((planes, 2)),
        dma((pieces, planes, 2)),
        dma((pieces, planes, 2)),
        dma((pieces, planes, 2)),
        dma((pieces,)),
        dma((pieces,)),
        dma((pieces, planes, 2)),
        dma((pieces, planes, 2)),
        dma((pieces, planes, 2, 2)),
        dma((pieces, planes, 2, 2)),
        dma((2 * pieces,)),
        dma((2 * pieces,)),
    ]
    expert_scratch = [
        half(planes, rows, model),
        full(planes, lines, rows),
        half(planes, near, cap, model),
        half(planes, near, cap, model),
        half(planes, near, cap, model),
        half(planes, near, cap, model),
        full(planes, rows, model),
        full(rows, model),
        half(2, planes, rows, model),
        half(planes, rows, model),
        dma((planes, chunks)),
        dma((2, planes, chunks)),
        dma((planes,)),
        dma((2, planes)),
        dma((planes, near)),
        dma((planes, near)),
        dma((planes, near)),
        dma((planes, near)),
        dma((2, planes, chunks)),
        dma((2, planes, chunks)),
    ]
    return pl.pallas_call(
        functools.partial(
            layer_kernel,
            top_count=top_count,
            experts=axis_count,
            cap=cap,
            front_count=len(front_scratch),
        ),
        out_shape=jax.ShapeDtypeStruct((rows, model), jnp.bfloat16),
        in_specs=[anywhere] * 4 + [inside] * 4 + [anywhere] * 2,
        out_specs=inside,
        scratch_shapes=[
            full(rows, model),
            half(rows, model),
            full(lines, rows),
            half(*w_in.shape),
            half(*w_down.shape),
            dma((2,)),
            *front_scratch,
            *expert_scratch,
        ],
        compiler_params=pltpu.CompilerParams(
            collective_id=0, has_side_effects=True, vmem_limit_bytes=60 * 2**20
        ),
        cost_estimate=pl.CostEstimate(
            flops=4 * 2 * group * rows * width * 4 * axis_count * rows
            + 4 * rows * group * width * model
            + 6 * planes * near * cap * model * w_down.shape[0],
            bytes_accessed=12 * 2**20,
            transcendentals=2 * group * rows * axis_count * rows,
        ),
    )(queries, pairs, cached, w_out, resid, gain, ids, gates, w_in, w_down)


def experts(stream, normed, expert_ids, expert_gates, w_in, w_down):
    row_count, model_width = stream.shape
    axis_count = lax.axis_size("head")
    top_count = expert_ids.shape[2]
    flat_ids = expert_ids.reshape(-1)
    local_experts = w_in.shape[0]
    experts = local_experts * axis_count
    capacity = max(2, 2 * row_count * top_count // experts)
    onehot = (flat_ids[:, None] == jnp.arange(experts, dtype=jnp.int32)[None, :]).astype(jnp.int32)
    before = jnp.tri(flat_ids.shape[0], k=-1, dtype=jnp.bfloat16)
    earlier = jnp.dot(
        before, onehot.astype(jnp.bfloat16), preferred_element_type=jnp.float32
    ).astype(jnp.int32)
    slot_rank = jnp.sum(earlier * onehot, 1)
    target = flat_ids * capacity + slot_rank
    target = target.reshape(row_count, top_count)
    places = jnp.arange(experts * capacity, dtype=jnp.int32)
    chosen = jnp.zeros((experts * capacity, row_count), jnp.bool_)
    gate_of = jnp.zeros((row_count, experts * capacity), jnp.float32)
    gates = expert_gates.reshape(row_count, top_count)
    for rank in range(top_count):
        chosen = chosen | (places[:, None] == target[None, :, rank])
        gate_of = jnp.where(
            target[:, rank, None] == places[None, :], gates[:, rank, None], gate_of
        )
    outgoing = jnp.dot(
        chosen.astype(jnp.bfloat16), normed, preferred_element_type=jnp.float32
    ).astype(jnp.bfloat16)
    outgoing = outgoing.reshape(axis_count, local_experts, capacity, model_width)
    hidden_width = w_down.shape[1]
    inner_act = jnp.einsum(
        "semd,edf->semf",
        lax.all_to_all(outgoing, "head", split_axis=0, concat_axis=0, tiled=True),
        w_in,
        preferred_element_type=jnp.float32,
    )
    hidden = (jax.nn.silu(inner_act[..., :hidden_width]) * inner_act[..., hidden_width:]).astype(
        jnp.bfloat16
    )
    answered = jnp.einsum(
        "semf,efd->semd", hidden, w_down, preferred_element_type=jnp.float32
    ).astype(jnp.bfloat16)
    returned_rows = lax.all_to_all(answered, "head", split_axis=0, concat_axis=0, tiled=True)
    picked = returned_rows.reshape(experts * capacity, model_width)
    expert_sum = jnp.zeros((row_count, model_width), jnp.float32)
    rest = gate_of
    for _ in range(3):
        term = lax.reduce_precision(rest, 8, 7)
        rest = rest - term
        expert_sum = expert_sum + jnp.dot(
            term.astype(jnp.bfloat16), picked, preferred_element_type=jnp.float32
        )
    return (stream + expert_sum).astype(jnp.bfloat16)


def local(queries, new_kv, cache, resid, w_out, norm_gain, expert_ids, expert_gates, w_in, w_down):
    axis_count = lax.axis_size("head")
    local_rows, seq_count, head_count, head_width = queries.shape
    pair_heads = new_kv.shape[2]
    fits = (
        seq_count == 1
        and pair_heads == 2
        and lax.axis_size("grp") == 2
        and axis_count == 4 * (len(front_order[1]) + 1)
        and w_out.shape[2] % 1024 == 0
        and cache.shape[0] == 1
        and w_out.shape[1] * axis_count == head_width
        and w_out.shape[1] % 16 == 0
        and local_rows % 32 == 0
        and cache.shape[1] * 2 % 128 == 0
        and head_count % 4 == 0
    )
    top_count = expert_ids.shape[2]
    experts_count = w_in.shape[0] * axis_count
    row_count = local_rows * seq_count
    fits = (
        fits
        and w_in.shape[0] == 1
        and row_count % 128 == 0
        and (row_count * top_count * 2) % (16 * experts_count) == 0
    )
    if fits:
        out = layer(
            queries.reshape(local_rows, head_count, head_width),
            new_kv.reshape(local_rows, pair_heads, 2 * head_width),
            cache[0],
            w_out,
            resid.reshape(local_rows, -1),
            norm_gain.reshape(1, -1),
            expert_ids.reshape(local_rows, top_count).T,
            expert_gates.reshape(local_rows, top_count).T,
            w_in[0],
            w_down[0],
            axis_count,
        )
    else:
        stream, normed = front_general(queries, new_kv, cache, resid, w_out, norm_gain)
        out = experts(stream, normed, expert_ids, expert_gates, w_in, w_down)
    return out.reshape(resid.shape)


def solution(mesh):
    return jax.shard_map(
        local,
        mesh=mesh,
        in_specs=(
            P("head", "grp", None, None),
            P("head", "grp", None, None),
            P(("grp", "head"), None, None),
            P("head", "grp", None),
            P(None, "head", None),
            P(),
            P("head", "grp", None),
            P("head", "grp", None),
            P("head", None, None),
            P("head", None, None),
        ),
        out_specs=P("head", "grp", None),
        check_vma=False,
    )
```
